32 devices in a mesh: mem: 8 (over y, x, core), band: 4 (over z).
Axes of the slice: x: 2, y: 2, z: 4, core: 2. Of those that a mesh axis runs over, the one named last changes fastest.
Arguments:
- ensemble: bfloat16 [256, 3, 240, 160], P('mem', None, 'band'), may hold values from -8 to 8, as said below
- layer_depth: float32 [240, 160], P('band'), may hold values from 0.5 to 2
- observed_cell: int32 [8, 8, 512], P('mem', 'band'), may hold values from 0 to 1799
- observed_value: float32 [8, 8, 512], P('mem', 'band'), may hold values from -6 to 6
- error_variance: float32 [8, 8, 512], P('mem', 'band'), may hold values from 4 to 64
- observed_count: int32 [8, 8], P('mem', 'band'), may hold values from 256 to 512, as said below
Outputs:
- analysis: bfloat16 [256, 3, 240, 160], P('mem', None, 'band')
The draws below stay inside these ranges and needn't reach their ends.
Inputs may be any that keep to these rules, and one draw needn't show every extreme that they name: `ensemble`: the forecast members scatter around a common state. `observed_count`: some tile holds 512 observations; the slots from the count on are unused.
All inputs are finite; a program needn't handle non-finite values.
Results may differ from the reference program's by a relative error of at most 0.0051.
The reference program's roundings to bfloat16 on the way count: a program that leaves them out, or rounds other values in their place, can miss the bound.
Values may be sent and summed in bfloat16 or wider, within the bound.
No kernel may reach another device: no remote copies, remote signals or barrier semaphores. Data moves between devices by JAX's collectives and lax.ppermute only.
A program may use at most 128 MiB of HBM per device.

```python
import math
import jax
import jax.numpy as jnp
from jax import lax

MODEL_RUN_COUNT = 256
PATCH_SPAN = 30
PARALLEL_LINES = 20
OBS_MAX = 512
SWEEPS = 5
PATCH_TOTAL = 8
COLUMNS = 240
ROWS = 160
N_MEM = 8


def draw_ensemble(key, part):
    key_base, key_member = jax.random.split(key, 2)
    common = jnp.clip(jax.random.normal(key_base, (1, 3, COLUMNS, ROWS), jnp.float32), -4.0, 4.0)
    member_part = jnp.clip(jax.random.normal(key_member, (MODEL_RUN_COUNT, 3, COLUMNS, ROWS), jnp.float32), -4.0, 4.0)
    return (common + member_part).astype(jnp.bfloat16)


def draw_observed_count(key, part):
    key_counts, key_chosen = jax.random.split(key)
    counts = jax.random.randint(key_counts, (N_MEM * PATCH_TOTAL,), OBS_MAX // 2, OBS_MAX + 1)
    chosen = jax.random.randint(key_chosen, (), 0, N_MEM * PATCH_TOTAL)
    counts = jnp.where(jnp.arange(N_MEM * PATCH_TOTAL) == chosen, OBS_MAX, counts)
    return counts.reshape(N_MEM, PATCH_TOTAL).astype(jnp.int32)


def place_ends(values, stream_key, smallest, top_value):
    longest = values.shape.index(max(values.shape))
    spots = []
    for shift in (0, 1):
        where = [jax.random.randint(jax.random.fold_in(stream_key, axis), (), 0, length) for axis, length in enumerate(values.shape)]
        where[longest] = (where[longest] + shift) % values.shape[longest]
        spots.append(tuple(where))
    return values.at[spots[0]].set(smallest).at[spots[1]].set(top_value)


def level_of(key, dims, shards, smallest, high):
    level = 1.0
    for dim, parts in shards:
        steps = jax.random.uniform(jax.random.fold_in(jax.random.fold_in(key, 6), dim), (parts,), jnp.float32, smallest / len(shards), high / len(shards))
        level = level * jnp.repeat(jnp.exp(steps), dims[dim] // parts).reshape((-1,) + (1,) * (len(dims) - 1 - dim))
    return level


def noise(rng, dims, scale, limit, shards=(), kind=jnp.bfloat16):
    array = jax.random.normal(rng, dims, jnp.float32) * scale
    if len(shards) > 0:
        array = level_of(rng, dims, shards, -0.22, 0.18) * array
    return jnp.clip(array, min=-limit, max=limit).astype(kind)


def setup_inputs(seed: int = 0) -> dict:
    key_list = jax.random.split(jax.random.key(seed), 7)
    ensemble = draw_ensemble(jax.random.fold_in(key_list[6], 71), 0)
    layer_depth = jnp.clip(jnp.exp(math.log(2.0) - 1.3862944 * jax.random.uniform(key_list[1], (COLUMNS, ROWS), jnp.float32) ** level_of(key_list[1], (COLUMNS, ROWS), ((0, 4),), -0.2, 0.2)), 0.5, 2.0)
    observed_cell = place_ends(jax.random.randint(key_list[2], (N_MEM, PATCH_TOTAL, OBS_MAX), 0, 3 * PATCH_SPAN * PARALLEL_LINES), jax.random.fold_in(key_list[2], 1), 0, (3 * PATCH_SPAN * PARALLEL_LINES) - 1).astype(jnp.int32)
    observed_value = noise(key_list[3], (N_MEM, PATCH_TOTAL, OBS_MAX), 1.5, 6.0, ((0, 8), (1, 4)), jnp.float32)
    error_variance = jnp.clip(jnp.exp(math.log(64.0) - 2.7725887 * jax.random.uniform(key_list[4], (N_MEM, PATCH_TOTAL, OBS_MAX), jnp.float32) ** level_of(key_list[4], (N_MEM, PATCH_TOTAL, OBS_MAX), ((0, 8), (1, 4)), -0.2, 0.2)), 4.0, 64.0)
    observed_count = draw_observed_count(jax.random.fold_in(key_list[6], 71), 0)
    return {"ensemble": ensemble, "layer_depth": layer_depth, "observed_cell": observed_cell, "observed_value": observed_value, "error_variance": error_variance, "observed_count": observed_count}


half_step = 0.1
coriolis_scale = 0.3
neighbour_weight = 0.75

def north_south(source):
    widths = [(0, 0)] * (source.ndim - 1) + [(1, 1)]
    padded = jnp.pad(source, widths)
    return padded[..., 2:] - padded[..., :-2]

def coriolis(latitudes):
    position = jnp.arange(latitudes, dtype=jnp.float32)
    return coriolis_scale * jnp.sin(math.pi * ((position + 0.5) / latitudes - 0.5))

def newton_schulz(starting):
    identity = jnp.eye(starting.shape[-1], dtype=starting.dtype)
    root_part = starting
    inverse_root = jnp.broadcast_to(identity, starting.shape)
    for sweep_index in range(SWEEPS):
        product = jnp.einsum('tij,tjk->tik', inverse_root, root_part, precision=lax.Precision.HIGHEST)
        middle = 1.5 * identity - 0.5 * product
        root_part = jnp.einsum('tij,tjk->tik', root_part, middle, precision=lax.Precision.HIGHEST)
        inverse_root = jnp.einsum('tij,tjk->tik', middle, inverse_root, precision=lax.Precision.HIGHEST)
    return inverse_root

def reference(ensemble, layer_depth, observed_cell, observed_value, error_variance, observed_count):
    height = ensemble[:, 0].astype(jnp.float32)
    eastward = ensemble[:, 1].astype(jnp.float32)
    northward = ensemble[:, 2].astype(jnp.float32)
    flux_east = lax.optimization_barrier((layer_depth * eastward).astype(jnp.bfloat16)).astype(jnp.float32)
    flux_north = lax.optimization_barrier((layer_depth * northward).astype(jnp.bfloat16)).astype(jnp.float32)
    east_west = jnp.roll(flux_east, -1, axis=1) - jnp.roll(flux_east, 1, axis=1)
    raised = height - half_step * (east_west + north_south(flux_north))
    surface_elevation_cast = lax.optimization_barrier(raised.astype(jnp.bfloat16))
    height_wide = surface_elevation_cast.astype(jnp.float32)
    turning = coriolis(ROWS)
    revised_zonal_velocity = eastward + turning * northward - half_step * (jnp.roll(height_wide, -1, axis=1) - jnp.roll(height_wide, 1, axis=1))
    revised_meridional_velocity = northward - turning * eastward - half_step * north_south(height_wide)
    advance_dynamics = jnp.stack([surface_elevation_cast, revised_zonal_velocity.astype(jnp.bfloat16), revised_meridional_velocity.astype(jnp.bfloat16)], axis=1)
    unrolled_realizations = advance_dynamics.reshape(MODEL_RUN_COUNT, -1)
    variable = observed_cell // (PATCH_SPAN * PARALLEL_LINES)
    column = observed_cell // PARALLEL_LINES % PATCH_SPAN
    row_index = observed_cell % PARALLEL_LINES
    strip_index = jnp.arange(N_MEM, dtype=jnp.int32)[:, None, None]
    tile_index = jnp.arange(PATCH_TOTAL, dtype=jnp.int32)[None, :, None]
    flat_index = (variable * (COLUMNS * ROWS) + (tile_index * PATCH_SPAN + column) * ROWS + strip_index * PARALLEL_LINES + row_index).astype(jnp.int32)
    slot_index = jnp.arange(OBS_MAX, dtype=jnp.int32)
    live_slots = slot_index[None, None, :] < observed_count[:, :, None]
    root_weight = jnp.sqrt(jnp.where(live_slots, 1.0 / error_variance, 0.0))

    def strip_stats(pieces):
        index_strip, root_strip, value_strip = pieces
        values = jnp.take(unrolled_realizations, index_strip.reshape(-1), axis=1).reshape(MODEL_RUN_COUNT, PATCH_TOTAL, OBS_MAX)
        observed_mean = lax.optimization_barrier(jnp.sum(values, axis=0, dtype=jnp.float32)) / MODEL_RUN_COUNT
        spread = (root_strip[None] * (values.astype(jnp.float32) - observed_mean[None])).astype(jnp.bfloat16)
        misfit = (root_strip * (value_strip - observed_mean)).astype(jnp.bfloat16)
        spread_wide = spread.astype(jnp.float32)
        misfit_wide = misfit.astype(jnp.float32)
        gram = jnp.einsum('kgo,lgo->gkl', spread_wide, spread_wide)
        pull = jnp.einsum('kgo,go->gk', spread_wide, misfit_wide)
        return (gram, pull)
    gram_blocks, pull_blocks = lax.map(strip_stats, (flat_index, root_weight, observed_value))
    padded_gram = jnp.pad(gram_blocks, ((1, 1), (0, 0), (0, 0), (0, 0)))
    padded_pull = jnp.pad(pull_blocks, ((1, 1), (0, 0), (0, 0)))
    total_gram = jnp.zeros(gram_blocks.shape, jnp.float32)
    total_pull = jnp.zeros(pull_blocks.shape, jnp.float32)
    for offset_lat in range(3):
        for offset_lon in range(3):
            factor = neighbour_weight ** (abs(offset_lat - 1) + abs(offset_lon - 1))
            total_gram = total_gram + factor * jnp.roll(padded_gram[offset_lat:offset_lat + N_MEM], 1 - offset_lon, axis=1)
            total_pull = total_pull + factor * jnp.roll(padded_pull[offset_lat:offset_lat + N_MEM], 1 - offset_lon, axis=1)
    first_band_piece = jnp.moveaxis(advance_dynamics.reshape(MODEL_RUN_COUNT, 3, PATCH_TOTAL, PATCH_SPAN, N_MEM, PARALLEL_LINES), 4, 0)
    first_band_piece = first_band_piece.reshape(N_MEM, MODEL_RUN_COUNT, 3, PATCH_TOTAL, PATCH_SPAN * PARALLEL_LINES)

    def strip_update(pieces):
        tile_values, gram, pull = pieces
        system = (MODEL_RUN_COUNT - 1) * jnp.eye(MODEL_RUN_COUNT, dtype=jnp.float32)[None] + gram
        frobenius = jnp.sqrt(lax.optimization_barrier(jnp.sum(system * system, axis=(1, 2))))
        inverse_root = newton_schulz(system / frobenius[:, None, None])
        spread_map = inverse_root * (math.sqrt(MODEL_RUN_COUNT - 1) / jnp.sqrt(frobenius))[:, None, None]
        half_pull = jnp.einsum('tij,tj->ti', inverse_root, pull, precision=lax.Precision.HIGHEST)
        shift_weights = jnp.einsum('tij,tj->ti', inverse_root, half_pull, precision=lax.Precision.HIGHEST) / frobenius[:, None]
        weights = (spread_map + shift_weights[:, :, None]).astype(jnp.bfloat16)
        state_mean = lax.optimization_barrier(jnp.sum(tile_values, axis=0, dtype=jnp.float32)) / MODEL_RUN_COUNT
        anomaly = (tile_values.astype(jnp.float32) - state_mean[None]).astype(jnp.bfloat16)
        update = jnp.einsum('gjk,jvgc->kvgc', weights.astype(jnp.float32), anomaly.astype(jnp.float32))
        return (state_mean[None] + update).astype(jnp.bfloat16)
    analysed = lax.map(strip_update, (first_band_piece, total_gram, total_pull))
    analysed = analysed.reshape(N_MEM, MODEL_RUN_COUNT, 3, PATCH_TOTAL, PATCH_SPAN, PARALLEL_LINES)
    return jnp.moveaxis(analysed, 0, 4).reshape(MODEL_RUN_COUNT, 3, COLUMNS, ROWS)
```

```python
import math

import jax
import jax.numpy as jnp
from jax import lax
from jax.experimental import pallas as pl
from jax.experimental.pallas import tpu as pltpu
from jax.sharding import PartitionSpec as P

SWEEPS = 5


half_step = 0.1
coriolis_scale = 0.3
neighbour_weight = 0.75


def padded_2(cells, sides, width):
    for axis, dim in sides:
        count = lax.axis_size(axis)
        head = lax.slice_in_dim(cells, 0, width, axis=dim)
        tail = lax.slice_in_dim(cells, cells.shape[dim] - width, cells.shape[dim], axis=dim)
        cells = jnp.concatenate(
            [
                lax.ppermute(tail, axis, [(i, (i + 1) % count) for i in range(count)]),
                cells,
                lax.ppermute(head, axis, [((i + 1) % count, i) for i in range(count)]),
            ],
            axis=dim,
        )
    return cells


def north_south(source):
    widths = [(0, 0)] * (source.ndim - 1) + [(1, 1)]
    padded = jnp.pad(source, widths)
    return padded[..., 2:] - padded[..., :-2]


def coriolis(latitudes):
    position = jnp.arange(latitudes, dtype=jnp.float32)
    return coriolis_scale * jnp.sin(math.pi * ((position + 0.5) / latitudes - 0.5))


def newton_schulz(starting):
    identity = jnp.eye(starting.shape[-1], dtype=starting.dtype)
    root_part = starting
    inverse_root = jnp.broadcast_to(identity, starting.shape)
    for sweep_index in range(SWEEPS):
        product = jnp.einsum(
            "tij,tjk->tik", inverse_root, root_part, precision=lax.Precision.HIGHEST
        )
        middle = 1.5 * identity - 0.5 * product
        root_part = jnp.einsum("tij,tjk->tik", root_part, middle, precision=lax.Precision.HIGHEST)
        inverse_root = jnp.einsum(
            "tij,tjk->tik", middle, inverse_root, precision=lax.Precision.HIGHEST
        )
    return inverse_root


def on_device(ensemble, layer_depth, observed_cell, observed_value, error_variance, observed_count):
    block_members = ensemble.shape[0]
    columns = ensemble.shape[2]
    latitudes = ensemble.shape[3]
    strips = lax.axis_size("mem")
    members = block_members * strips
    strip_rows = latitudes // strips
    tile_count = observed_cell.shape[1]
    tile_columns = columns // tile_count
    slot_count = observed_cell.shape[2]
    tile_cells = 3 * tile_columns * strip_rows
    height = ensemble[:, 0].astype(jnp.float32)
    eastward = ensemble[:, 1].astype(jnp.float32)
    northward = ensemble[:, 2].astype(jnp.float32)
    turning = coriolis(latitudes)
    flux_east = (layer_depth * eastward).astype(jnp.bfloat16)
    flux_north = (layer_depth * northward).astype(jnp.bfloat16)
    east_margin = padded_2(flux_east, (("band", 1),), 1)
    east_west = east_margin[:, 2:].astype(jnp.float32) - east_margin[:, :-2].astype(jnp.float32)
    north_local = lax.optimization_barrier(flux_north).astype(jnp.float32)
    raised = height - half_step * (east_west + north_south(north_local))
    surface_elevation_cast = raised.astype(jnp.bfloat16)
    height_margin = padded_2(surface_elevation_cast, (("band", 1),), 1)
    margin_wide = height_margin.astype(jnp.float32)
    height_inner = margin_wide[:, 1:-1]
    revised_zonal_velocity = (
        eastward + turning * northward - half_step * (margin_wide[:, 2:] - margin_wide[:, :-2])
    )
    revised_meridional_velocity = (
        northward - turning * eastward - half_step * north_south(height_inner)
    )
    advance_dynamics = jnp.stack(
        [
            surface_elevation_cast,
            revised_zonal_velocity.astype(jnp.bfloat16),
            revised_meridional_velocity.astype(jnp.bfloat16),
        ],
        axis=1,
    )
    reordered = advance_dynamics.reshape(
        block_members, 3, tile_count, tile_columns, strips, strip_rows
    )
    reordered = jnp.transpose(reordered, (4, 2, 0, 1, 3, 5)).reshape(
        strips, tile_count, block_members, tile_cells
    )
    tile_block = lax.all_to_all(reordered, "mem", split_axis=0, concat_axis=2, tiled=True)[0]
    cells_here = observed_cell[0]
    values = jnp.take_along_axis(tile_block, cells_here[:, None, :], axis=2)
    observed_mean = jnp.sum(values, axis=1, dtype=jnp.float32) / members
    slot_index = jnp.arange(slot_count, dtype=jnp.int32)[None, :]
    live_slots = slot_index < observed_count[0][:, None]
    root_weight = jnp.sqrt(jnp.where(live_slots, 1.0 / error_variance[0], 0.0))
    spread = (
        root_weight[:, None, :] * (values.astype(jnp.float32) - observed_mean[:, None, :])
    ).astype(jnp.bfloat16)
    misfit = (root_weight * (observed_value[0] - observed_mean)).astype(jnp.bfloat16)
    spread_margin, misfit_margin = (
        padded_2(spread[None], (("mem", 0), ("band", 1)), 1),
        padded_2(misfit[None], (("mem", 0), ("band", 1)), 1),
    )
    gram_margin = jnp.einsum(
        "atko,atlo->atkl", spread_margin, spread_margin, preferred_element_type=jnp.float32
    )
    pull_margin = jnp.einsum(
        "atko,ato->atk", spread_margin, misfit_margin, preferred_element_type=jnp.float32
    )
    strip_here = lax.axis_index("mem")
    lower_valid = (strip_here > 0).astype(jnp.float32)
    upper_valid = (strip_here < strips - 1).astype(jnp.float32)
    strip_mask = (lower_valid, 1.0, upper_valid)
    total_gram = jnp.zeros((tile_count, members, members), jnp.float32)
    total_pull = jnp.zeros((tile_count, members), jnp.float32)
    for offset_lat in range(3):
        for offset_lon in range(3):
            factor = (
                neighbour_weight ** (abs(offset_lat - 1) + abs(offset_lon - 1))
                * strip_mask[offset_lat]
            )
            total_gram = (
                total_gram + factor * gram_margin[offset_lat, offset_lon : offset_lon + tile_count]
            )
            total_pull = (
                total_pull + factor * pull_margin[offset_lat, offset_lon : offset_lon + tile_count]
            )
    system = (members - 1) * jnp.eye(members, dtype=jnp.float32)[None] + total_gram
    frobenius = jnp.sqrt(jnp.sum(system * system, axis=(1, 2)))
    inverse_root = newton_schulz(system / frobenius[:, None, None])
    spread_map = inverse_root * (math.sqrt(members - 1) / jnp.sqrt(frobenius))[:, None, None]
    half_pull = jnp.einsum("tij,tj->ti", inverse_root, total_pull, precision=lax.Precision.HIGHEST)
    shift_weights = (
        jnp.einsum("tij,tj->ti", inverse_root, half_pull, precision=lax.Precision.HIGHEST)
        / frobenius[:, None]
    )
    weights = (spread_map + shift_weights[:, :, None]).astype(jnp.bfloat16)
    state_mean = jnp.sum(tile_block, axis=1, dtype=jnp.float32) / members
    anomaly = (tile_block.astype(jnp.float32) - state_mean[:, None, :]).astype(jnp.bfloat16)
    update = jnp.einsum("tjk,tjc->tkc", weights, anomaly, preferred_element_type=jnp.float32)
    analysed = (state_mean[:, None, :] + update).astype(jnp.bfloat16)
    returned = lax.all_to_all(analysed[None], "mem", split_axis=2, concat_axis=0, tiled=True)
    returned = returned.reshape(strips, tile_count, block_members, 3, tile_columns, strip_rows)
    return jnp.transpose(returned, (2, 3, 1, 4, 0, 5)).reshape(block_members, 3, columns, latitudes)


LANES = 128
PAIRS = 8
GROUPS = 23
F32 = jnp.float32
BF16 = jnp.bfloat16
VMEM_BYTES = 56 * 1024 * 1024


def params():
    return pltpu.CompilerParams(vmem_limit_bytes=VMEM_BYTES)


def identity(size, dtype):
    row = lax.broadcasted_iota(jnp.int32, (size, size), 0)
    column = lax.broadcasted_iota(jnp.int32, (size, size), 1)
    return (row == column).astype(F32).astype(dtype)


def dot_nt(left, right):
    return lax.dot_general(left, right, (((1,), (1,)), ((), ())), preferred_element_type=F32)


def dot_nn(left, right):
    return lax.dot_general(left, right, (((1,), (0,)), ((), ())), preferred_element_type=F32)


def split(value):
    high = value.astype(BF16)
    return high, (value - high.astype(F32)).astype(BF16)


def dot_3(left, right):
    return dot_nn(left[0], right[0]) + (dot_nn(left[0], right[1]) + dot_nn(left[1], right[0]))


def exchange_lanes(blocks, lane):
    blocks = list(blocks)
    for bit in range(3):
        step = 1 << bit
        odd = (lane & step) != 0
        for q in range(8):
            if q & step:
                continue
            low, high = blocks[q], blocks[q | step]
            blocks[q] = jnp.where(odd, pltpu.roll(high, step, 1), low)
            blocks[q | step] = jnp.where(odd, high, pltpu.roll(low, LANES - step, 1))
    return blocks


def group_of(variable, index):
    return variable * 7 + index


def forecast_kernel(
    ens, left, right, depth, turn, out, wide, flux, height, deep, fields, staged
):
    members = ens.shape[0]
    batch = wide.shape[0]
    latitudes = ens.shape[3]
    rows = latitudes // 8
    wide[...] = jnp.zeros(wide.shape, F32)
    flux[...] = jnp.zeros(flux.shape, F32)
    height[...] = jnp.zeros(height.shape, F32)
    deep[...] = jnp.zeros(deep.shape, F32)
    deep[8:68, :] = depth[...]
    deep[6:8, :] = (left[96].astype(F32) + left[97].astype(F32)) + left[98].astype(F32)
    deep[68:70, :] = (right[96].astype(F32) + right[97].astype(F32)) + right[98].astype(F32)
    source = lax.broadcasted_iota(jnp.int32, (latitudes, latitudes), 0)
    target = lax.broadcasted_iota(jnp.int32, (latitudes, latitudes), 1)
    shift = (source == target + 1).astype(F32) - (source == target - 1).astype(F32)
    shift = shift.astype(BF16)
    turning = turn[0:1, :][None]

    def rows_apart(value):
        flat = value.reshape(batch * 80, latitudes)
        return dot_nn(flat, shift).reshape(batch, 80, latitudes)

    def step(index, carry):
        first = index * batch
        for k in range(batch):
            for v in range(3):
                wide[k, v, 8:68, :] = ens[first + k, v].astype(F32)
                wide[k, v, 6:8, :] = left[(first + k) * 3 + v].astype(F32)
                wide[k, v, 68:70, :] = right[(first + k) * 3 + v].astype(F32)
        depths = deep[...][None]
        flux[:, 8:88, :] = (depths * wide[:, 1]).astype(BF16).astype(F32)
        flux_north = (depths * wide[:, 2]).astype(BF16)
        east_west = flux[:, 9:89, :] - flux[:, 7:87, :]
        raised = wide[:, 0] - half_step * (east_west + rows_apart(flux_north))
        rounded = raised.astype(BF16)
        height[:, 8:88, :] = rounded.astype(F32)
        steps_north = rows_apart(rounded)[:, 8:72]
        steps_east = height[:, 17:81, :] - height[:, 15:79, :]
        east = wide[:, 1, 8:72, :]
        north = wide[:, 2, 8:72, :]
        new_east = east + turning * north - half_step * steps_east
        new_north = north - turning * east - half_step * steps_north
        here = pl.ds(first, batch)
        fields[0, here] = height[:, 16:80, :]
        fields[1, here] = new_east
        fields[2, here] = new_north
        fields[0, here, 60:64, :] = new_east[:, 56:60]
        fields[2, here, 60:64, :] = jnp.zeros((batch, 4, latitudes), F32)
        return carry

    lax.fori_loop(0, members // batch, step, 0)
    eye = identity(latitudes, BF16)
    staged[:, 460:464, :] = jnp.zeros((8, 4, 256), F32)

    def turn_group(v, first, g):
        block = fields[v, :, first : first + 8, :].reshape(256, latitudes).astype(BF16)
        turned = dot_nt(eye, block)
        for s in range(8):
            staged[s, rows * g : rows * (g + 1), :] = turned[rows * s : rows * (s + 1)]

    for v in range(3):
        for index in range(7):
            turn_group(v, 8 * index, group_of(v, index))
    turn_group(0, 56, 21)
    turn_group(2, 56, 22)
    out[...] = staged[...].astype(BF16)


def observe_kernel(cells, got, weight, target, held, gram, wide, seen):
    lane = lax.broadcasted_iota(jnp.int32, (16, LANES), 1)

    def spread_out(index, carry):
        here = pl.ds(pl.multiple_of(index * 16, 16), 16)
        for h in range(2):
            span = slice(h * LANES, (h + 1) * LANES)
            blocks = exchange_lanes([got[q, here, span].astype(F32) for q in range(8)], lane)
            for q in range(8):
                to = pl.ds(pl.multiple_of(q * 464 + index * 16, 16), 16)
                wide[h, to, :] = blocks[q]
                held[q, here, span] = blocks[q].astype(BF16)
        return carry

    lax.fori_loop(0, 29, spread_out, 0)
    ones = jnp.full((256, 256), 1.0, BF16)
    eye = identity(256, BF16)
    slots = seen.shape[2]
    unroll = 8

    def pick(index, carry):
        for t in range(2):
            for k in range(unroll):
                slot = index * unroll + k
                row = cells[t, slot]
                for h in range(2):
                    seen[t, h, pl.ds(slot, 1), :] = wide[h, pl.ds(row, 1), :]
        return carry

    lax.fori_loop(0, slots // unroll, pick, 0)
    for t in range(2):
        values = jnp.concatenate([seen[t, 0], seen[t, 1]], axis=1)
        mean = dot_nn(values.astype(BF16), ones) * (1.0 / 256)
        root = jnp.concatenate([weight[t], weight[t]], axis=1)
        goal = jnp.concatenate([target[t], target[t]], axis=1)
        spread = (root * (values - mean)).astype(BF16)
        misfit = (root * (goal - mean)).astype(BF16).astype(F32)
        pull = jnp.sum(spread.astype(F32) * misfit, axis=0, keepdims=True)
        turned = dot_nt(eye, spread).astype(BF16)
        gram[t, 0:256, :] = dot_nt(turned, turned)
        gram[t, 256:264, :] = jnp.broadcast_to(pull, (8, 256))
        gram[t, 264:272, :] = jnp.zeros((8, 256), F32)


def analyse_kernel(held, here, below, above, out, results):
    size = 256
    eye = identity(size, F32)
    maps = []
    for t in range(2):
        total = here[t] + neighbour_weight * (below[t].astype(F32) + above[t].astype(F32))
        system = (size - 1) * eye + total[0:256]
        pull = total[256:264]
        square = jnp.sum(jnp.sum(system * system, axis=0, keepdims=True), axis=1, keepdims=True)
        frobenius = jnp.sqrt(square)
        root_part = system / frobenius
        inverse_root = None
        for sweep in range(SWEEPS):
            if sweep == 0:
                middle = 1.5 * eye - 0.5 * root_part
                inverse_root = middle
                root_part = dot_3(split(root_part), split(middle))
            else:
                inverse_parts, root_parts = split(inverse_root), split(root_part)
                middle = 1.5 * eye - 0.5 * dot_3(inverse_parts, root_parts)
                middle_parts = split(middle)
                if sweep < SWEEPS - 1:
                    root_part = dot_3(root_parts, middle_parts)
                inverse_root = dot_3(middle_parts, inverse_parts)
        inverse_parts = split(inverse_root)
        half_pull = dot_3(split(pull), inverse_parts)
        shift = dot_3(split(half_pull), inverse_parts) / frobenius
        scale = math.sqrt(size - 1) / jnp.sqrt(frobenius)
        maps.append((inverse_root * scale + shift[0:1]).astype(BF16))
    average = jnp.full((size, size), 1.0 / size, BF16)
    row = lax.broadcasted_iota(jnp.int32, (464, size), 0)
    group = row // 20
    for q in range(8):
        cells = held[q]
        mean = dot_nn(cells, average)
        anomaly = (cells.astype(F32) - mean).astype(BF16)
        first = dot_nt(anomaly, maps[0])
        second = dot_nt(anomaly, maps[1])
        position = group - (group // 7) * 7
        is_first = (position < (4 if q < 6 else 3)) & (group < 21)
        results[q] = mean + jnp.where(is_first, first, second)
    lane = lax.broadcasted_iota(jnp.int32, (16, LANES), 1)

    def gather_in(index, carry):
        span16 = pl.ds(pl.multiple_of(index * 16, 16), 16)
        for h in range(2):
            span = slice(h * LANES, (h + 1) * LANES)
            blocks = exchange_lanes([results[q, span16, span] for q in range(8)], lane)
            for q in range(8):
                out[q, span16, span] = blocks[q].astype(BF16)
        return carry

    lax.fori_loop(0, 29, gather_in, 0)


def return_kernel(got, out, wide, turned):
    members = out.shape[0]
    latitudes = out.shape[3]
    rows = latitudes // 8
    wide[...] = got[...].astype(F32)
    eye = identity(256, BF16)

    def turn_group(g):
        for s in range(8):
            turned[g, rows * s : rows * (s + 1), :] = wide[s, rows * g : rows * (g + 1), :]
        block = dot_nt(eye, turned[g].astype(BF16))
        return block.reshape(members, 8, latitudes)

    mixed = turn_group(21)
    last = (mixed[:, 0:4], mixed[:, 4:8], turn_group(22)[:, 0:4])
    for v in range(3):
        for index in range(3):
            pair = [turn_group(group_of(v, 2 * index + k)) for k in range(2)]
            both = jnp.concatenate(pair, axis=1).astype(BF16)
            out[:, v, 16 * index : 16 * (index + 1), :] = both
        both = jnp.concatenate([turn_group(group_of(v, 6)), last[v]], axis=1).astype(BF16)
        out[:, v, 48:60, :] = both


def edges(ensemble, depth, first):
    part = lax.slice_in_dim(ensemble, first, first + 2, axis=2)
    part = part.reshape(-1, 2, ensemble.shape[3])
    deep = lax.slice_in_dim(depth, first, first + 2, axis=0)
    pieces = []
    for _ in range(3):
        piece = lax.reduce_precision(deep, 8, 7)
        pieces.append(piece.astype(BF16))
        deep = deep - piece
    return jnp.concatenate([part, jnp.stack(pieces)], axis=0)


def around(value, axis, step):
    count = lax.axis_size(axis)
    return lax.ppermute(value, axis, [(i, (i + step) % count) for i in range(count)])


def along(value, axis, step):
    count = lax.axis_size(axis)
    pairs = [(i, i + step) for i in range(count) if 0 <= i + step < count]
    return lax.ppermute(value, axis, pairs)


def swap(value):
    return lax.all_to_all(value, "mem", split_axis=0, concat_axis=0, tiled=True)


def on_device_fast(
    ensemble, layer_depth, observed_cell, observed_value, error_variance, observed_count
):
    members, _, columns, latitudes = ensemble.shape
    slots = observed_cell.shape[2]
    left = around(edges(ensemble, layer_depth, columns - 2), "band", 1)
    right = around(edges(ensemble, layer_depth, 0), "band", -1)
    turning = jnp.broadcast_to(coriolis(latitudes)[None], (8, latitudes))
    sent = pl.pallas_call(
        forecast_kernel,
        out_shape=jax.ShapeDtypeStruct((8, 464, 256), BF16),
        scratch_shapes=[
            pltpu.VMEM((4, 3, 80, latitudes), F32),
            pltpu.VMEM((4, 96, latitudes), F32),
            pltpu.VMEM((4, 96, latitudes), F32),
            pltpu.VMEM((80, latitudes), F32),
            pltpu.VMEM((3, members, 64, latitudes), F32),
            pltpu.VMEM((8, 464, 256), F32),
        ],
        compiler_params=params(),
        name="forecast",
    )(ensemble, left, right, layer_depth, turning)
    got = swap(sent)

    cell = observed_cell[0]
    variable = cell // 600
    tile = jnp.arange(2, dtype=jnp.int32)[:, None]
    column = tile * 30 + cell // 20 % 30
    group = variable * 7 + column // 8
    place = column % 8
    is_last = column >= 56
    group = jnp.where(is_last, 21 + variable // 2, group)
    place = jnp.where(is_last, column - 56 + 4 * (variable % 2), place)
    rows = place * 464 + group * 20 + cell % 20
    live = jnp.arange(slots, dtype=jnp.int32)[None, :] < observed_count[0][:, None]
    root = jnp.sqrt(jnp.where(live, 1.0 / error_variance[0], 0.0))
    root = jnp.broadcast_to(root[:, :, None], (2, slots, LANES))
    goal = jnp.broadcast_to(observed_value[0][:, :, None], (2, slots, LANES))
    vmem = pl.BlockSpec(memory_space=pltpu.VMEM)
    held, gram = pl.pallas_call(
        observe_kernel,
        out_shape=(
            jax.ShapeDtypeStruct((8, 464, 256), BF16),
            jax.ShapeDtypeStruct((2, 272, 256), F32),
        ),
        in_specs=[pl.BlockSpec(memory_space=pltpu.SMEM), vmem, vmem, vmem],
        scratch_shapes=[
            pltpu.VMEM((2, 8 * 464, LANES), F32),
            pltpu.VMEM((2, 2, slots, LANES), F32),
        ],
        compiler_params=params(),
        name="observe",
    )(rows, got, root, goal)

    short = gram.astype(BF16)
    west = around(short[1], "band", 1).astype(F32)
    east = around(short[0], "band", -1).astype(F32)
    across = jnp.stack(
        [
            gram[0] + neighbour_weight * (west + gram[1]),
            gram[1] + neighbour_weight * (gram[0] + east),
        ]
    )
    short = across.astype(BF16)
    below = along(short, "mem", 1)
    above = along(short, "mem", -1)
    back = pl.pallas_call(
        analyse_kernel,
        out_shape=jax.ShapeDtypeStruct((8, 464, 256), BF16),
        scratch_shapes=[pltpu.VMEM((8, 464, 256), F32)],
        compiler_params=params(),
        name="analyse",
    )(held, across, below, above)
    returned = swap(back)
    return pl.pallas_call(
        return_kernel,
        out_shape=jax.ShapeDtypeStruct(ensemble.shape, BF16),
        scratch_shapes=[
            pltpu.VMEM((8, 464, 256), F32),
            pltpu.VMEM((GROUPS, latitudes, 256), F32),
        ],
        compiler_params=params(),
        name="come_back",
    )(returned)


def choose(ensemble, layer_depth, observed_cell, *rest):
    shape = (lax.axis_size("mem"), ensemble.shape, observed_cell.shape[1])
    fits = shape == (8, (32, 3, 60, 160), 2) and observed_cell.shape[2] % 16 == 0
    chosen = on_device_fast if fits else on_device
    return chosen(ensemble, layer_depth, observed_cell, *rest)


def solution(mesh):
    in_specs = (
        P("mem", None, "band", None),
        P("band", None),
        P("mem", "band", None),
        P("mem", "band", None),
        P("mem", "band", None),
        P("mem", "band"),
    )
    out_specs = P("mem", None, "band", None)
    return jax.shard_map(
        choose, mesh=mesh, in_specs=in_specs, out_specs=out_specs, check_vma=False
    )
```

```python
import math

import jax
import jax.numpy as jnp
from jax import lax
from jax.experimental import pallas as pl
from jax.experimental.pallas import tpu as pltpu
from jax.sharding import PartitionSpec as P

SWEEPS = 5


half_step = 0.1
coriolis_scale = 0.3
neighbour_weight = 0.75


def padded_2(cells, sides, width):
    for axis, dim in sides:
        count = lax.axis_size(axis)
        head = lax.slice_in_dim(cells, 0, width, axis=dim)
        tail = lax.slice_in_dim(cells, cells.shape[dim] - width, cells.shape[dim], axis=dim)
        cells = jnp.concatenate(
            [
                lax.ppermute(tail, axis, [(i, (i + 1) % count) for i in range(count)]),
                cells,
                lax.ppermute(head, axis, [((i + 1) % count, i) for i in range(count)]),
            ],
            axis=dim,
        )
    return cells


def north_south(source):
    widths = [(0, 0)] * (source.ndim - 1) + [(1, 1)]
    padded = jnp.pad(source, widths)
    return padded[..., 2:] - padded[..., :-2]


def coriolis(latitudes):
    position = jnp.arange(latitudes, dtype=jnp.float32)
    return coriolis_scale * jnp.sin(math.pi * ((position + 0.5) / latitudes - 0.5))


def newton_schulz(starting):
    identity = jnp.eye(starting.shape[-1], dtype=starting.dtype)
    root_part = starting
    inverse_root = jnp.broadcast_to(identity, starting.shape)
    for sweep_index in range(SWEEPS):
        product = jnp.einsum(
            "tij,tjk->tik", inverse_root, root_part, precision=lax.Precision.HIGHEST
        )
        middle = 1.5 * identity - 0.5 * product
        root_part = jnp.einsum("tij,tjk->tik", root_part, middle, precision=lax.Precision.HIGHEST)
        inverse_root = jnp.einsum(
            "tij,tjk->tik", middle, inverse_root, precision=lax.Precision.HIGHEST
        )
    return inverse_root


def on_device(ensemble, layer_depth, observed_cell, observed_value, error_variance, observed_count):
    block_members = ensemble.shape[0]
    columns = ensemble.shape[2]
    latitudes = ensemble.shape[3]
    strips = lax.axis_size("mem")
    members = block_members * strips
    strip_rows = latitudes // strips
    tile_count = observed_cell.shape[1]
    tile_columns = columns // tile_count
    slot_count = observed_cell.shape[2]
    tile_cells = 3 * tile_columns * strip_rows
    height = ensemble[:, 0].astype(jnp.float32)
    eastward = ensemble[:, 1].astype(jnp.float32)
    northward = ensemble[:, 2].astype(jnp.float32)
    turning = coriolis(latitudes)
    flux_east = (layer_depth * eastward).astype(jnp.bfloat16)
    flux_north = (layer_depth * northward).astype(jnp.bfloat16)
    east_margin = padded_2(flux_east, (("band", 1),), 1)
    east_west = east_margin[:, 2:].astype(jnp.float32) - east_margin[:, :-2].astype(jnp.float32)
    north_local = lax.optimization_barrier(flux_north).astype(jnp.float32)
    raised = height - half_step * (east_west + north_south(north_local))
    surface_elevation_cast = raised.astype(jnp.bfloat16)
    height_margin = padded_2(surface_elevation_cast, (("band", 1),), 1)
    margin_wide = height_margin.astype(jnp.float32)
    height_inner = margin_wide[:, 1:-1]
    revised_zonal_velocity = (
        eastward + turning * northward - half_step * (margin_wide[:, 2:] - margin_wide[:, :-2])
    )
    revised_meridional_velocity = (
        northward - turning * eastward - half_step * north_south(height_inner)
    )
    advance_dynamics = jnp.stack(
        [
            surface_elevation_cast,
            revised_zonal_velocity.astype(jnp.bfloat16),
            revised_meridional_velocity.astype(jnp.bfloat16),
        ],
        axis=1,
    )
    reordered = advance_dynamics.reshape(
        block_members, 3, tile_count, tile_columns, strips, strip_rows
    )
    reordered = jnp.transpose(reordered, (4, 2, 0, 1, 3, 5)).reshape(
        strips, tile_count, block_members, tile_cells
    )
    tile_block = lax.all_to_all(reordered, "mem", split_axis=0, concat_axis=2, tiled=True)[0]
    cells_here = observed_cell[0]
    values = jnp.take_along_axis(tile_block, cells_here[:, None, :], axis=2)
    observed_mean = jnp.sum(values, axis=1, dtype=jnp.float32) / members
    slot_index = jnp.arange(slot_count, dtype=jnp.int32)[None, :]
    live_slots = slot_index < observed_count[0][:, None]
    root_weight = jnp.sqrt(jnp.where(live_slots, 1.0 / error_variance[0], 0.0))
    spread = (
        root_weight[:, None, :] * (values.astype(jnp.float32) - observed_mean[:, None, :])
    ).astype(jnp.bfloat16)
    misfit = (root_weight * (observed_value[0] - observed_mean)).astype(jnp.bfloat16)
    spread_margin, misfit_margin = (
        padded_2(spread[None], (("mem", 0), ("band", 1)), 1),
        padded_2(misfit[None], (("mem", 0), ("band", 1)), 1),
    )
    gram_margin = jnp.einsum(
        "atko,atlo->atkl", spread_margin, spread_margin, preferred_element_type=jnp.float32
    )
    pull_margin = jnp.einsum(
        "atko,ato->atk", spread_margin, misfit_margin, preferred_element_type=jnp.float32
    )
    strip_here = lax.axis_index("mem")
    lower_valid = (strip_here > 0).astype(jnp.float32)
    upper_valid = (strip_here < strips - 1).astype(jnp.float32)
    strip_mask = (lower_valid, 1.0, upper_valid)
    total_gram = jnp.zeros((tile_count, members, members), jnp.float32)
    total_pull = jnp.zeros((tile_count, members), jnp.float32)
    for offset_lat in range(3):
        for offset_lon in range(3):
            factor = (
                neighbour_weight ** (abs(offset_lat - 1) + abs(offset_lon - 1))
                * strip_mask[offset_lat]
            )
            total_gram = (
                total_gram + factor * gram_margin[offset_lat, offset_lon : offset_lon + tile_count]
            )
            total_pull = (
                total_pull + factor * pull_margin[offset_lat, offset_lon : offset_lon + tile_count]
            )
    system = (members - 1) * jnp.eye(members, dtype=jnp.float32)[None] + total_gram
    frobenius = jnp.sqrt(jnp.sum(system * system, axis=(1, 2)))
    inverse_root = newton_schulz(system / frobenius[:, None, None])
    spread_map = inverse_root * (math.sqrt(members - 1) / jnp.sqrt(frobenius))[:, None, None]
    half_pull = jnp.einsum("tij,tj->ti", inverse_root, total_pull, precision=lax.Precision.HIGHEST)
    shift_weights = (
        jnp.einsum("tij,tj->ti", inverse_root, half_pull, precision=lax.Precision.HIGHEST)
        / frobenius[:, None]
    )
    weights = (spread_map + shift_weights[:, :, None]).astype(jnp.bfloat16)
    state_mean = jnp.sum(tile_block, axis=1, dtype=jnp.float32) / members
    anomaly = (tile_block.astype(jnp.float32) - state_mean[:, None, :]).astype(jnp.bfloat16)
    update = jnp.einsum("tjk,tjc->tkc", weights, anomaly, preferred_element_type=jnp.float32)
    analysed = (state_mean[:, None, :] + update).astype(jnp.bfloat16)
    returned = lax.all_to_all(analysed[None], "mem", split_axis=2, concat_axis=0, tiled=True)
    returned = returned.reshape(strips, tile_count, block_members, 3, tile_columns, strip_rows)
    return jnp.transpose(returned, (2, 3, 1, 4, 0, 5)).reshape(block_members, 3, columns, latitudes)


LANES = 128
GROUPS = 23
CELLS = 464
F32 = jnp.float32
BF16 = jnp.bfloat16
VMEM_BYTES = 56 * 1024 * 1024


def params():
    return pltpu.CompilerParams(vmem_limit_bytes=VMEM_BYTES)


def identity(size, dtype):
    row = lax.broadcasted_iota(jnp.int32, (size, size), 0)
    column = lax.broadcasted_iota(jnp.int32, (size, size), 1)
    return (row == column).astype(F32).astype(dtype)


def dot_nt(left, right):
    return lax.dot_general(left, right, (((1,), (1,)), ((), ())), preferred_element_type=F32)


def dot_nn(left, right):
    return lax.dot_general(left, right, (((1,), (0,)), ((), ())), preferred_element_type=F32)


def split(value):
    high = value.astype(BF16)
    return high, (value - high.astype(F32)).astype(BF16)


def dot_3(left, right):
    return dot_nn(left[0], right[0]) + (dot_nn(left[0], right[1]) + dot_nn(left[1], right[0]))


def exchange_lanes(blocks, lane):
    blocks = [list(pair) for pair in blocks]
    for q in range(4):
        low, high = blocks[q], blocks[q + 4]
        blocks[q], blocks[q + 4] = [low[0], high[0]], [low[1], high[1]]
    for bit in range(2):
        step = 32 << bit
        odd = (lane & step) != 0
        for q in range(8):
            if q & (1 << bit):
                continue
            for h in range(2):
                low, high = blocks[q][h], blocks[q | (1 << bit)][h]
                blocks[q][h] = jnp.where(odd, pltpu.roll(high, step, 1), low)
                blocks[q | (1 << bit)][h] = jnp.where(odd, high, pltpu.roll(low, LANES - step, 1))
    return blocks


def group_of(variable, index):
    if index < 3:
        return variable * 3 + index
    return 9 + variable if index == 3 else 12 + variable * 3 + index - 4


def edge_kernel(first, last, depth, to_west, to_east):
    for out, block, columns, near in ((to_west, first, (0, 1), 0), (to_east, last, (58, 59), 1)):
        far = 1 - near
        out[0] = block[0, near]
        for plane, v, k in ((1, 2, near), (2, 1, near), (3, 1, far)):
            deep = depth[columns[k] : columns[k] + 1, :]
            out[plane] = (deep * block[v, k].astype(F32)).astype(BF16)


def forecast_kernel(ens, left, right, depth, turn, out, deep, flux, height, staged):
    columns, members, latitudes = ens.shape[1:]
    rows = latitudes // 8
    source = lax.broadcasted_iota(jnp.int32, (latitudes, latitudes), 0)
    target = lax.broadcasted_iota(jnp.int32, (latitudes, latitudes), 1)
    shift = (source == target + 1).astype(F32) - (source == target - 1).astype(F32)
    shift = shift.astype(BF16)
    turning = turn[0:1, :][None]

    def rows_apart(value):
        flat = value.reshape(-1, latitudes)
        return dot_nn(flat, shift).reshape(value.shape)

    for c in range(columns):
        deep[c] = jnp.broadcast_to(depth[c : c + 1, :], (members, latitudes))
    flux[0] = left[3].astype(F32)
    flux[1] = left[2].astype(F32)
    flux[columns + 2] = right[2].astype(F32)
    flux[columns + 3] = right[3].astype(F32)
    batch = 12

    def fluxes(index, carry):
        first = index * batch
        east = ens[1, pl.ds(first, batch)].astype(F32)
        flux[pl.ds(first + 2, batch)] = (deep[pl.ds(first, batch)] * east).astype(BF16).astype(F32)
        return carry

    lax.fori_loop(0, columns // batch, fluxes, 0)

    def heights(index, carry):
        first = index * batch
        here = pl.ds(first, batch)
        flux_north = (deep[here] * ens[2, here].astype(F32)).astype(BF16)
        east_west = flux[pl.ds(first + 3, batch)] - flux[pl.ds(first + 1, batch)]
        raised = ens[0, here].astype(F32) - half_step * (east_west + rows_apart(flux_north))
        height[pl.ds(first + 1, batch)] = raised.astype(BF16)
        return carry

    lax.fori_loop(0, columns // batch, heights, 0)
    for edge, at in ((left, 0), (right, columns + 1)):
        east_west = flux[at + 2] - flux[at]
        raised = edge[0].astype(F32) - half_step * (east_west + rows_apart(edge[1]))
        height[at] = raised.astype(BF16)

    eye = identity(latitudes, BF16)
    staged[:, 460:464, :] = jnp.zeros((8, 4, 256), F32)

    def put(block, g):
        turned = dot_nt(eye, block.reshape(256, latitudes))
        for s in range(8):
            staged[s, rows * g : rows * (g + 1), :] = turned[rows * s : rows * (s + 1)]

    def new_fields(first, count):
        here = slice(first, first + count)
        new_height = height[first + 1 : first + 1 + count]
        east = ens[1, here].astype(F32)
        north = ens[2, here].astype(F32)
        ahead = height[first + 2 : first + 2 + count].astype(F32)
        behind = height[first : first + count].astype(F32)
        new_east = east + turning * north - half_step * (ahead - behind)
        new_north = north - turning * east - half_step * rows_apart(new_height)
        return new_height, new_east.astype(BF16), new_north.astype(BF16)

    for index in range(7):
        for v, field in enumerate(new_fields(8 * index, 8)):
            put(field, group_of(v, index))
    ends = new_fields(56, 4)
    put(jnp.concatenate([ends[0], ends[1]], axis=0), 21)
    put(jnp.concatenate([ends[2], jnp.zeros_like(ends[2])], axis=0), 22)
    out[...] = staged[...].astype(BF16)


def observe_kernel(cells, got, weight, target, held, gram, short, wide, seen):
    lane = lax.broadcasted_iota(jnp.int32, (16, LANES), 1)

    def spread_out(index, carry):
        here = pl.ds(pl.multiple_of(index * 16, 16), 16)
        spans = [slice(h * LANES, (h + 1) * LANES) for h in range(2)]
        blocks = [[got[q, here, span].astype(F32) for span in spans] for q in range(8)]
        blocks = exchange_lanes(blocks, lane)
        for q in range(8):
            to = pl.ds(pl.multiple_of(q * CELLS + index * 16, 16), 16)
            for h in range(2):
                wide[h, to, :] = blocks[q][h]
                held[q, here, spans[h]] = blocks[q][h].astype(BF16)
        return carry

    lax.fori_loop(0, CELLS // 16, spread_out, 0)
    slots = seen.shape[2]
    unroll = 16

    def pick(index, carry):
        for t in range(2):
            for k in range(unroll):
                slot = index * unroll + k
                row = cells[t, slot]
                for h in range(2):
                    seen[t, h, pl.ds(slot, 1), :] = wide[h, pl.ds(row, 1), :]
        return carry

    lax.fori_loop(0, slots // unroll, pick, 0)
    eye = identity(256, BF16)
    for t in range(2):
        values = jnp.concatenate([seen[t, 0], seen[t, 1]], axis=1).astype(BF16)
        turned = dot_nt(eye, values)
        mean = jnp.sum(turned, axis=0, keepdims=True) * (1.0 / 256)
        root = weight[t : t + 1, :]
        spread = (root * (turned - mean)).astype(BF16)
        misfit = (root * (target[t : t + 1, :] - mean)).astype(BF16)
        block = dot_nt(spread, spread)
        pull = dot_nt(jnp.broadcast_to(misfit, (16, slots)), spread)
        gram[t, 0:256, :] = block
        gram[t, 256:272, :] = pull
        short[t, 0:256, :] = block.astype(BF16)
        short[t, 256:272, :] = pull.astype(BF16)


def analyse_kernel(held, gram, west, east, below, above, out, results):
    size = 256
    eye = identity(size, F32)
    maps = []
    for t in range(2):
        beside = west[...].astype(F32) + gram[1] if t == 0 else gram[0] + east[...].astype(F32)
        total = gram[t] + neighbour_weight * beside
        total = total + neighbour_weight * (below[t].astype(F32) + above[t].astype(F32))
        system = (size - 1) * eye + total[0:256]
        pull = total[256:272]
        square = jnp.sum(jnp.sum(system * system, axis=0, keepdims=True), axis=1, keepdims=True)
        frobenius = jnp.sqrt(square)
        root_part = system / frobenius
        inverse_root = None
        for sweep in range(SWEEPS):
            if sweep == 0:
                middle = 1.5 * eye - 0.5 * root_part
                inverse_root = middle
                root_part = dot_3(split(root_part), split(middle))
            else:
                inverse_parts, root_parts = split(inverse_root), split(root_part)
                middle = 1.5 * eye - 0.5 * dot_3(inverse_parts, root_parts)
                middle_parts = split(middle)
                if sweep < SWEEPS - 1:
                    root_part = dot_3(root_parts, middle_parts)
                inverse_root = dot_3(middle_parts, inverse_parts)
        inverse_parts = split(inverse_root)
        half_pull = dot_3(split(pull), inverse_parts)
        shift = dot_3(split(half_pull), inverse_parts) / frobenius
        scale = math.sqrt(size - 1) / jnp.sqrt(frobenius)
        maps.append((inverse_root * scale + shift[0:1]).astype(BF16))
    average = jnp.full((size, size), 1.0 / size, BF16)
    near = lax.broadcasted_iota(jnp.int32, (16, size), 0) < 4

    for q in range(8):
        cells = held[q]
        mean = dot_nn(cells, average)
        anomaly = (cells.astype(F32) - mean).astype(BF16)
        if q < 6:
            results[q, 0:240] = mean[0:240] + dot_nt(anomaly[0:240], maps[0])
            results[q, 240:464] = mean[240:464] + dot_nt(anomaly[240:464], maps[1])
        else:
            first = dot_nt(anomaly[0:192], maps[0])
            second = dot_nt(anomaly[176:464], maps[1])
            results[q, 0:176] = mean[0:176] + first[0:176]
            results[q, 176:192] = mean[176:192] + jnp.where(near, first[176:192], second[0:16])
            results[q, 192:464] = mean[192:464] + second[16:288]
    lane = lax.broadcasted_iota(jnp.int32, (16, LANES), 1)

    def gather_in(index, carry):
        here = pl.ds(pl.multiple_of(index * 16, 16), 16)
        spans = [slice(h * LANES, (h + 1) * LANES) for h in range(2)]
        blocks = [[results[q, here, span] for span in spans] for q in range(8)]
        blocks = exchange_lanes(blocks, lane)
        for q in range(8):
            for h in range(2):
                out[q, here, spans[h]] = blocks[q][h].astype(BF16)
        return carry

    lax.fori_loop(0, CELLS // 16, gather_in, 0)


def return_kernel(got, out, wide, turned):
    members, latitudes = out.shape[2:]
    rows = latitudes // 8
    wide[...] = got[...].astype(F32)
    eye = identity(256, BF16)

    def take(g):
        for s in range(8):
            turned[g, rows * s : rows * (s + 1), :] = wide[s, rows * g : rows * (g + 1), :]
        block = dot_nt(eye, turned[g].astype(BF16)).astype(BF16)
        return block.reshape(8, members, latitudes)

    for v in range(3):
        for index in range(7):
            out[v, 8 * index : 8 * index + 8] = take(group_of(v, index))
    mixed = take(21)
    out[0, 56:60] = mixed[0:4]
    out[1, 56:60] = mixed[4:8]
    out[2, 56:60] = take(22)[0:4]


def around(value, axis, step):
    count = lax.axis_size(axis)
    return lax.ppermute(value, axis, [(i, (i + step) % count) for i in range(count)])


def along(value, axis, step):
    count = lax.axis_size(axis)
    pairs = [(i, i + step) for i in range(count) if 0 <= i + step < count]
    return lax.ppermute(value, axis, pairs)


def swap(value):
    return lax.all_to_all(value, "mem", split_axis=0, concat_axis=0, tiled=True)


def cell_rows(cell):
    variable = cell // 600
    tile = jnp.arange(2, dtype=jnp.int32)[:, None]
    column = tile * 30 + cell // 20 % 30
    index = column // 8
    place = column % 8
    group = jnp.where(index < 3, variable * 3 + index, 8 + variable * 3 + index)
    group = jnp.where(index == 3, 9 + variable, group)
    is_last = column >= 56
    group = jnp.where(is_last, 21 + variable // 2, group)
    place = jnp.where(is_last, column - 56 + 4 * (variable % 2), place)
    return place * CELLS + group * 20 + cell % 20


def on_device_fast(
    ensemble, layer_depth, observed_cell, observed_value, error_variance, observed_count
):
    members, _, columns, latitudes = ensemble.shape
    slots = observed_cell.shape[2]
    planes = jnp.transpose(ensemble, (1, 2, 0, 3))
    edge = jax.ShapeDtypeStruct((4, members, latitudes), BF16)
    pair = (3, 2, members, latitudes)
    whole = pl.BlockSpec((4, members, latitudes), lambda i: (0, 0, 0))
    to_west, to_east = pl.pallas_call(
        edge_kernel,
        grid=(1,),
        out_shape=(edge, edge),
        in_specs=[
            pl.BlockSpec(pair, lambda i: (0, 0, 0, 0)),
            pl.BlockSpec(pair, lambda i: (0, columns // 2 - 1, 0, 0)),
            pl.BlockSpec((columns, latitudes), lambda i: (0, 0)),
        ],
        out_specs=(whole, whole),
        compiler_params=params(),
        name="edges",
    )(planes, planes, layer_depth)
    left = around(to_east, "band", 1)
    right = around(to_west, "band", -1)
    turning = jnp.broadcast_to(coriolis(latitudes)[None], (8, latitudes))
    sent = pl.pallas_call(
        forecast_kernel,
        out_shape=jax.ShapeDtypeStruct((8, CELLS, 256), BF16),
        scratch_shapes=[
            pltpu.VMEM((columns, members, latitudes), F32),
            pltpu.VMEM((columns + 4, members, latitudes), F32),
            pltpu.VMEM((columns + 2, members, latitudes), BF16),
            pltpu.VMEM((8, CELLS, 256), F32),
        ],
        compiler_params=params(),
        name="forecast",
    )(planes, left, right, layer_depth, turning)
    got = swap(sent)

    rows = cell_rows(observed_cell[0])
    live = jnp.arange(slots, dtype=jnp.int32)[None, :] < observed_count[0][:, None]
    root = jnp.sqrt(jnp.where(live, 1.0 / error_variance[0], 0.0))
    vmem = pl.BlockSpec(memory_space=pltpu.VMEM)
    held, gram, short = pl.pallas_call(
        observe_kernel,
        out_shape=(
            jax.ShapeDtypeStruct((8, CELLS, 256), BF16),
            jax.ShapeDtypeStruct((2, 272, 256), F32),
            jax.ShapeDtypeStruct((2, 272, 256), BF16),
        ),
        in_specs=[pl.BlockSpec(memory_space=pltpu.SMEM), vmem, vmem, vmem],
        scratch_shapes=[
            pltpu.VMEM((2, 8 * CELLS, LANES), F32),
            pltpu.VMEM((2, 2, slots, LANES), F32),
        ],
        compiler_params=params(),
        name="observe",
    )(rows, got, root, observed_value[0])

    west = around(short[1], "band", 1)
    east = around(short[0], "band", -1)
    beside = jnp.stack([west.astype(F32) + gram[1], gram[0] + east.astype(F32)])
    short = (gram + neighbour_weight * beside).astype(BF16)
    below = along(short, "mem", 1)
    above = along(short, "mem", -1)
    back = pl.pallas_call(
        analyse_kernel,
        out_shape=jax.ShapeDtypeStruct((8, CELLS, 256), BF16),
        scratch_shapes=[pltpu.VMEM((8, CELLS, 256), F32)],
        compiler_params=params(),
        name="analyse",
    )(held, gram, west, east, below, above)
    returned = swap(back)
    planes = pl.pallas_call(
        return_kernel,
        out_shape=jax.ShapeDtypeStruct(planes.shape, BF16),
        scratch_shapes=[
            pltpu.VMEM((8, CELLS, 256), F32),
            pltpu.VMEM((GROUPS, latitudes, 256), F32),
        ],
        compiler_params=params(),
        name="come_back",
    )(returned)
    return jnp.transpose(planes, (2, 0, 1, 3))


def choose(ensemble, layer_depth, observed_cell, *rest):
    shape = (lax.axis_size("mem"), ensemble.shape, observed_cell.shape[1])
    fits = shape == (8, (32, 3, 60, 160), 2) and observed_cell.shape[2] % 16 == 0
    chosen = on_device_fast if fits else on_device
    return chosen(ensemble, layer_depth, observed_cell, *rest)


def solution(mesh):
    in_specs = (
        P("mem", None, "band", None),
        P("band", None),
        P("mem", "band", None),
        P("mem", "band", None),
        P("mem", "band", None),
        P("mem", "band"),
    )
    out_specs = P("mem", None, "band", None)
    return jax.shard_map(
        choose, mesh=mesh, in_specs=in_specs, out_specs=out_specs, check_vma=False
    )
```

```python
import math

import jax
import jax.numpy as jnp
import numpy as np
from jax import lax
from jax.experimental import pallas as pl
from jax.experimental.pallas import tpu as pltpu
from jax.sharding import PartitionSpec as P

SWEEPS = 5


half_step = 0.1
coriolis_scale = 0.3
neighbour_weight = 0.75


def padded_2(cells, sides, width):
    for axis, dim in sides:
        count = lax.axis_size(axis)
        head = lax.slice_in_dim(cells, 0, width, axis=dim)
        tail = lax.slice_in_dim(cells, cells.shape[dim] - width, cells.shape[dim], axis=dim)
        cells = jnp.concatenate(
            [
                lax.ppermute(tail, axis, [(i, (i + 1) % count) for i in range(count)]),
                cells,
                lax.ppermute(head, axis, [((i + 1) % count, i) for i in range(count)]),
            ],
            axis=dim,
        )
    return cells


def north_south(source):
    widths = [(0, 0)] * (source.ndim - 1) + [(1, 1)]
    padded = jnp.pad(source, widths)
    return padded[..., 2:] - padded[..., :-2]


def coriolis(latitudes):
    position = jnp.arange(latitudes, dtype=jnp.float32)
    return coriolis_scale * jnp.sin(math.pi * ((position + 0.5) / latitudes - 0.5))


def newton_schulz(starting):
    identity = jnp.eye(starting.shape[-1], dtype=starting.dtype)
    root_part = starting
    inverse_root = jnp.broadcast_to(identity, starting.shape)
    for sweep_index in range(SWEEPS):
        product = jnp.einsum(
            "tij,tjk->tik", inverse_root, root_part, precision=lax.Precision.HIGHEST
        )
        middle = 1.5 * identity - 0.5 * product
        root_part = jnp.einsum("tij,tjk->tik", root_part, middle, precision=lax.Precision.HIGHEST)
        inverse_root = jnp.einsum(
            "tij,tjk->tik", middle, inverse_root, precision=lax.Precision.HIGHEST
        )
    return inverse_root


def on_device(ensemble, layer_depth, observed_cell, observed_value, error_variance, observed_count):
    block_members = ensemble.shape[0]
    columns = ensemble.shape[2]
    latitudes = ensemble.shape[3]
    strips = lax.axis_size("mem")
    members = block_members * strips
    strip_rows = latitudes // strips
    tile_count = observed_cell.shape[1]
    tile_columns = columns // tile_count
    slot_count = observed_cell.shape[2]
    tile_cells = 3 * tile_columns * strip_rows
    height = ensemble[:, 0].astype(jnp.float32)
    eastward = ensemble[:, 1].astype(jnp.float32)
    northward = ensemble[:, 2].astype(jnp.float32)
    turning = coriolis(latitudes)
    flux_east = (layer_depth * eastward).astype(jnp.bfloat16)
    flux_north = (layer_depth * northward).astype(jnp.bfloat16)
    east_margin = padded_2(flux_east, (("band", 1),), 1)
    east_west = east_margin[:, 2:].astype(jnp.float32) - east_margin[:, :-2].astype(jnp.float32)
    north_local = lax.optimization_barrier(flux_north).astype(jnp.float32)
    raised = height - half_step * (east_west + north_south(north_local))
    surface_elevation_cast = raised.astype(jnp.bfloat16)
    height_margin = padded_2(surface_elevation_cast, (("band", 1),), 1)
    margin_wide = height_margin.astype(jnp.float32)
    height_inner = margin_wide[:, 1:-1]
    revised_zonal_velocity = (
        eastward + turning * northward - half_step * (margin_wide[:, 2:] - margin_wide[:, :-2])
    )
    revised_meridional_velocity = (
        northward - turning * eastward - half_step * north_south(height_inner)
    )
    advance_dynamics = jnp.stack(
        [
            surface_elevation_cast,
            revised_zonal_velocity.astype(jnp.bfloat16),
            revised_meridional_velocity.astype(jnp.bfloat16),
        ],
        axis=1,
    )
    reordered = advance_dynamics.reshape(
        block_members, 3, tile_count, tile_columns, strips, strip_rows
    )
    reordered = jnp.transpose(reordered, (4, 2, 0, 1, 3, 5)).reshape(
        strips, tile_count, block_members, tile_cells
    )
    tile_block = lax.all_to_all(reordered, "mem", split_axis=0, concat_axis=2, tiled=True)[0]
    cells_here = observed_cell[0]
    values = jnp.take_along_axis(tile_block, cells_here[:, None, :], axis=2)
    observed_mean = jnp.sum(values, axis=1, dtype=jnp.float32) / members
    slot_index = jnp.arange(slot_count, dtype=jnp.int32)[None, :]
    live_slots = slot_index < observed_count[0][:, None]
    root_weight = jnp.sqrt(jnp.where(live_slots, 1.0 / error_variance[0], 0.0))
    spread = (
        root_weight[:, None, :] * (values.astype(jnp.float32) - observed_mean[:, None, :])
    ).astype(jnp.bfloat16)
    misfit = (root_weight * (observed_value[0] - observed_mean)).astype(jnp.bfloat16)
    spread_margin, misfit_margin = (
        padded_2(spread[None], (("mem", 0), ("band", 1)), 1),
        padded_2(misfit[None], (("mem", 0), ("band", 1)), 1),
    )
    gram_margin = jnp.einsum(
        "atko,atlo->atkl", spread_margin, spread_margin, preferred_element_type=jnp.float32
    )
    pull_margin = jnp.einsum(
        "atko,ato->atk", spread_margin, misfit_margin, preferred_element_type=jnp.float32
    )
    strip_here = lax.axis_index("mem")
    lower_valid = (strip_here > 0).astype(jnp.float32)
    upper_valid = (strip_here < strips - 1).astype(jnp.float32)
    strip_mask = (lower_valid, 1.0, upper_valid)
    total_gram = jnp.zeros((tile_count, members, members), jnp.float32)
    total_pull = jnp.zeros((tile_count, members), jnp.float32)
    for offset_lat in range(3):
        for offset_lon in range(3):
            factor = (
                neighbour_weight ** (abs(offset_lat - 1) + abs(offset_lon - 1))
                * strip_mask[offset_lat]
            )
            total_gram = (
                total_gram + factor * gram_margin[offset_lat, offset_lon : offset_lon + tile_count]
            )
            total_pull = (
                total_pull + factor * pull_margin[offset_lat, offset_lon : offset_lon + tile_count]
            )
    system = (members - 1) * jnp.eye(members, dtype=jnp.float32)[None] + total_gram
    frobenius = jnp.sqrt(jnp.sum(system * system, axis=(1, 2)))
    inverse_root = newton_schulz(system / frobenius[:, None, None])
    spread_map = inverse_root * (math.sqrt(members - 1) / jnp.sqrt(frobenius))[:, None, None]
    half_pull = jnp.einsum("tij,tj->ti", inverse_root, total_pull, precision=lax.Precision.HIGHEST)
    shift_weights = (
        jnp.einsum("tij,tj->ti", inverse_root, half_pull, precision=lax.Precision.HIGHEST)
        / frobenius[:, None]
    )
    weights = (spread_map + shift_weights[:, :, None]).astype(jnp.bfloat16)
    state_mean = jnp.sum(tile_block, axis=1, dtype=jnp.float32) / members
    anomaly = (tile_block.astype(jnp.float32) - state_mean[:, None, :]).astype(jnp.bfloat16)
    update = jnp.einsum("tjk,tjc->tkc", weights, anomaly, preferred_element_type=jnp.float32)
    analysed = (state_mean[:, None, :] + update).astype(jnp.bfloat16)
    returned = lax.all_to_all(analysed[None], "mem", split_axis=2, concat_axis=0, tiled=True)
    returned = returned.reshape(strips, tile_count, block_members, 3, tile_columns, strip_rows)
    return jnp.transpose(returned, (2, 3, 1, 4, 0, 5)).reshape(block_members, 3, columns, latitudes)


LANES = 128
GROUPS = 23
CELLS = 464
F32 = jnp.float32
BF16 = jnp.bfloat16
PACKED = 144
MIB = 1024 * 1024


def params(size):
    return pltpu.CompilerParams(vmem_limit_bytes=size * MIB)


def identity(size, dtype):
    row = lax.broadcasted_iota(jnp.int32, (size, size), 0)
    column = lax.broadcasted_iota(jnp.int32, (size, size), 1)
    return (row == column).astype(F32).astype(dtype)


def dot_nt(left, right):
    return lax.dot_general(left, right, (((1,), (1,)), ((), ())), preferred_element_type=F32)


def dot_nn(left, right):
    return lax.dot_general(left, right, (((1,), (0,)), ((), ())), preferred_element_type=F32)


def split(value):
    high = value.astype(BF16)
    return high, (value - high.astype(F32)).astype(BF16)


def left_3(parts):
    return jnp.concatenate([parts[0], parts[0], parts[1]], axis=1)


def right_3(parts):
    return jnp.concatenate([parts[0], parts[1], parts[0]], axis=0)


def triangle(size):
    row = lax.broadcasted_iota(jnp.int32, (size, size), 0)
    column = lax.broadcasted_iota(jnp.int32, (size, size), 1)
    return row, column


def packed(block, pull):
    row, column = triangle(128)
    last = block[128:256, 128:256]
    corner = jnp.where(row >= column, block[0:128, 0:128], last)
    middle = jnp.sum(jnp.where(row == column, last, 0.0), axis=0, keepdims=True)
    middle = jnp.concatenate([jnp.zeros_like(middle), middle], axis=1)
    top = jnp.concatenate([block[128:256, 0:128], corner], axis=1)
    return jnp.concatenate([top, pull, jnp.broadcast_to(middle, (8, 256))], axis=0)


def unpacked(value):
    row, column = triangle(128)
    low, corner = value[0:128, 0:128], value[0:128, 128:256]
    other = jnp.transpose(corner)
    first = jnp.where(row >= column, corner, other)
    last = jnp.where(row < column, corner, other)
    last = jnp.where(row == column, value[136:137, 128:256], last)
    top = jnp.concatenate([first, jnp.transpose(low)], axis=1)
    return jnp.concatenate([top, jnp.concatenate([low, last], axis=1)], axis=0), value[128:136]


def exchange_lanes(blocks, lane):
    blocks = [list(pair) for pair in blocks]
    for q in range(4):
        low, high = blocks[q], blocks[q + 4]
        blocks[q], blocks[q + 4] = [low[0], high[0]], [low[1], high[1]]
    for bit in range(2):
        step = 32 << bit
        odd = (lane & step) != 0
        for q in range(8):
            if q & (1 << bit):
                continue
            for h in range(2):
                low, high = blocks[q][h], blocks[q | (1 << bit)][h]
                blocks[q][h] = jnp.where(odd, pltpu.roll(high, step, 1), low)
                blocks[q | (1 << bit)][h] = jnp.where(odd, high, pltpu.roll(low, LANES - step, 1))
    return blocks


def group_of(variable, index):
    if index < 3:
        return variable * 3 + index
    return 9 + variable if index == 3 else 12 + variable * 3 + index - 4


def edge_kernel(first, last, depth, to_west, to_east):
    for out, block, columns, near in ((to_west, first, (0, 1), 0), (to_east, last, (58, 59), 1)):
        far = 1 - near
        out[0] = block[0, near]
        for plane, v, k in ((1, 2, near), (2, 1, near), (3, 1, far)):
            deep = depth[columns[k] : columns[k] + 1, :]
            out[plane] = (deep * block[v, k].astype(F32)).astype(BF16)


def forecast_kernel(ens, left, right, depth, turn, out, deep, flux, height, staged):
    columns, members, latitudes = ens.shape[1:]
    rows = latitudes // 8
    source = lax.broadcasted_iota(jnp.int32, (latitudes, latitudes), 0)
    target = lax.broadcasted_iota(jnp.int32, (latitudes, latitudes), 1)
    shift = (source == target + 1).astype(F32) - (source == target - 1).astype(F32)
    shift = shift.astype(BF16)
    turning = turn[0:1, :][None]

    def rows_apart(value):
        flat = value.reshape(-1, latitudes)
        return dot_nn(flat, shift).reshape(value.shape)

    for c in range(columns):
        deep[c] = jnp.broadcast_to(depth[c : c + 1, :], (members, latitudes))
    flux[0] = left[3].astype(F32)
    flux[1] = left[2].astype(F32)
    flux[columns + 2] = right[2].astype(F32)
    flux[columns + 3] = right[3].astype(F32)
    batch = 12

    def fluxes(index, carry):
        first = index * batch
        east = ens[1, pl.ds(first, batch)].astype(F32)
        flux[pl.ds(first + 2, batch)] = (deep[pl.ds(first, batch)] * east).astype(BF16).astype(F32)
        return carry

    lax.fori_loop(0, columns // batch, fluxes, 0)

    def heights(index, carry):
        first = index * batch
        here = pl.ds(first, batch)
        flux_north = (deep[here] * ens[2, here].astype(F32)).astype(BF16)
        east_west = flux[pl.ds(first + 3, batch)] - flux[pl.ds(first + 1, batch)]
        raised = ens[0, here].astype(F32) - half_step * (east_west + rows_apart(flux_north))
        height[pl.ds(first + 1, batch)] = raised.astype(BF16)
        return carry

    lax.fori_loop(0, columns // batch, heights, 0)
    for edge, at in ((left, 0), (right, columns + 1)):
        east_west = flux[at + 2] - flux[at]
        raised = edge[0].astype(F32) - half_step * (east_west + rows_apart(edge[1]))
        height[at] = raised.astype(BF16)

    eye = identity(latitudes, BF16)
    staged[:, 460:464, :] = jnp.zeros((8, 4, 256), F32)

    def put(block, g):
        turned = dot_nt(eye, block.reshape(256, latitudes))
        for s in range(8):
            staged[s, rows * g : rows * (g + 1), :] = turned[rows * s : rows * (s + 1)]

    def new_fields(first, count):
        here = slice(first, first + count)
        new_height = height[first + 1 : first + 1 + count]
        east = ens[1, here].astype(F32)
        north = ens[2, here].astype(F32)
        ahead = height[first + 2 : first + 2 + count].astype(F32)
        behind = height[first : first + count].astype(F32)
        new_east = east + turning * north - half_step * (ahead - behind)
        new_north = north - turning * east - half_step * rows_apart(new_height)
        return new_height, new_east.astype(BF16), new_north.astype(BF16)

    for index in range(7):
        for v, field in enumerate(new_fields(8 * index, 8)):
            put(field, group_of(v, index))
    ends = new_fields(56, 4)
    put(jnp.concatenate([ends[0], ends[1]], axis=0), 21)
    put(jnp.concatenate([ends[2], jnp.zeros_like(ends[2])], axis=0), 22)
    out[...] = staged[...].astype(BF16)


def observe_kernel(cells, got, weight, target, held, gram, short, wide, seen):
    lane = lax.broadcasted_iota(jnp.int32, (16, LANES), 1)

    def spread_out(index, carry):
        here = pl.ds(pl.multiple_of(index * 16, 16), 16)
        spans = [slice(h * LANES, (h + 1) * LANES) for h in range(2)]
        blocks = [[got[q, here, span] for span in spans] for q in range(8)]
        blocks = exchange_lanes(blocks, lane)
        for q in range(8):
            to = pl.ds(pl.multiple_of(q * CELLS + index * 16, 16), 16)
            for h in range(2):
                wide[h, to, :] = blocks[q][h].astype(F32)
                held[q, here, spans[h]] = blocks[q][h]
        return carry

    lax.fori_loop(0, CELLS // 16, spread_out, 0, unroll=4)
    slots = seen.shape[2]
    unroll = 16

    def pick(index, carry):
        for t in range(2):
            for k in range(unroll):
                slot = index * unroll + k
                row = cells[t, slot]
                for h in range(2):
                    seen[t, h, pl.ds(slot, 1), :] = wide[h, pl.ds(row, 1), :]
        return carry

    lax.fori_loop(0, slots // unroll, pick, 0)
    eye = identity(256, BF16)
    for t in range(2):
        values = jnp.concatenate([seen[t, 0], seen[t, 1]], axis=1).astype(BF16)
        turned = dot_nt(eye, values)
        mean = jnp.sum(turned, axis=0, keepdims=True) * (1.0 / 256)
        root = weight[t : t + 1, :]
        spread = (root * (turned - mean)).astype(BF16)
        misfit = (root * (target[t : t + 1, :] - mean)).astype(BF16)
        block = dot_nt(spread, spread)
        pull = dot_nt(jnp.broadcast_to(misfit, (16, slots)), spread)
        whole = packed(block, pull[0:8])
        gram[t] = whole
        short[t] = whole.astype(BF16)


def combine_kernel(gram, below, above, column, to_west, to_east):
    total = gram[...] + neighbour_weight * (below[...].astype(F32) + above[...].astype(F32))
    column[...] = total
    to_west[...] = total[0].astype(BF16)
    to_east[...] = total[1].astype(BF16)


def analyse_kernel(held, column, west, east, out, results):
    size = 256
    eye = identity(size, F32)
    beside = (west[...].astype(F32) + column[1], column[0] + east[...].astype(F32))
    norms, pulls, roots, inverses = [], [], [], []
    for t in range(2):
        block, pull = unpacked(column[t] + neighbour_weight * beside[t])
        system = (size - 1) * eye + block
        square = jnp.sum(jnp.sum(system * system, axis=0, keepdims=True), axis=1, keepdims=True)
        norms.append(jnp.sqrt(square))
        pulls.append(pull)
        roots.append(system / norms[t])
    for sweep in range(SWEEPS):
        rights = [right_3(split(root)) for root in roots]
        if sweep == 0:
            inverses = [1.5 * eye - 0.5 * root for root in roots]
            lefts = [left_3(split(inverse)) for inverse in inverses]
            roots = [dot_nn(left, right) for left, right in zip(lefts, rights)]
            continue
        parts = [split(inverse) for inverse in inverses]
        products = [dot_nn(left_3(part), right) for part, right in zip(parts, rights)]
        middles = [left_3(split(1.5 * eye - 0.5 * product)) for product in products]
        if sweep < SWEEPS - 1:
            roots = [dot_nn(middle, right) for middle, right in zip(middles, rights)]
        inverses = [dot_nn(middle, right_3(part)) for middle, part in zip(middles, parts)]
    maps = []
    for t in range(2):
        right = right_3(split(inverses[t]))
        half_pull = dot_nn(left_3(split(pulls[t])), right)
        shift = dot_nn(left_3(split(half_pull)), right) / norms[t]
        scale = math.sqrt(size - 1) / jnp.sqrt(norms[t])
        maps.append((inverses[t] * scale + shift[0:1]).astype(BF16))
    average = jnp.full((size, size), 1.0 / size, BF16)
    near = lax.broadcasted_iota(jnp.int32, (16, size), 0) < 4

    for q in range(8):
        cells = held[q]
        mean = dot_nn(cells, average)
        anomaly = (cells.astype(F32) - mean).astype(BF16)
        if q < 6:
            first = mean[0:240] + dot_nt(anomaly[0:240], maps[0])
            second = mean[240:464] + dot_nt(anomaly[240:464], maps[1])
            results[q, 0:240] = first.astype(BF16)
            results[q, 240:464] = second.astype(BF16)
        else:
            first = mean[0:192] + dot_nt(anomaly[0:192], maps[0])
            second = mean[176:464] + dot_nt(anomaly[176:464], maps[1])
            results[q, 0:176] = first[0:176].astype(BF16)
            results[q, 176:192] = jnp.where(near, first[176:192], second[0:16]).astype(BF16)
            results[q, 192:464] = second[16:288].astype(BF16)
    lane = lax.broadcasted_iota(jnp.int32, (16, LANES), 1)

    def gather_in(index, carry):
        here = pl.ds(pl.multiple_of(index * 16, 16), 16)
        spans = [slice(h * LANES, (h + 1) * LANES) for h in range(2)]
        blocks = [[results[q, here, span] for span in spans] for q in range(8)]
        blocks = exchange_lanes(blocks, lane)
        for q in range(8):
            for h in range(2):
                out[q, here, spans[h]] = blocks[q][h]
        return carry

    lax.fori_loop(0, CELLS // 16, gather_in, 0, unroll=4)


def return_kernel(got, out, wide, turned):
    members, latitudes = out.shape[2:]
    rows = latitudes // 8
    wide[...] = got[...].astype(F32)
    eye = identity(256, BF16)

    def take(g):
        for s in range(8):
            turned[g, rows * s : rows * (s + 1), :] = wide[s, rows * g : rows * (g + 1), :]
        block = dot_nt(eye, turned[g].astype(BF16)).astype(BF16)
        return block.reshape(8, members, latitudes)

    for v in range(3):
        for index in range(7):
            out[v, 8 * index : 8 * index + 8] = take(group_of(v, index))
    mixed = take(21)
    out[0, 56:60] = mixed[0:4]
    out[1, 56:60] = mixed[4:8]
    out[2, 56:60] = take(22)[0:4]


def around(value, axis, step):
    count = lax.axis_size(axis)
    return lax.ppermute(value, axis, [(i, (i + step) % count) for i in range(count)])


def along(value, axis, step):
    count = lax.axis_size(axis)
    pairs = [(i, i + step) for i in range(count) if 0 <= i + step < count]
    return lax.ppermute(value, axis, pairs)


def swap(value):
    return lax.all_to_all(value, "mem", split_axis=0, concat_axis=0, tiled=True)


def cell_rows(cell):
    variable = cell // 600
    tile = jnp.arange(2, dtype=jnp.int32)[:, None]
    column = tile * 30 + cell // 20 % 30
    index = column // 8
    place = column % 8
    group = jnp.where(index < 3, variable * 3 + index, 8 + variable * 3 + index)
    group = jnp.where(index == 3, 9 + variable, group)
    is_last = column >= 56
    group = jnp.where(is_last, 21 + variable // 2, group)
    place = jnp.where(is_last, column - 56 + 4 * (variable % 2), place)
    return place * CELLS + group * 20 + cell % 20


def on_device_fast(
    ensemble, layer_depth, observed_cell, observed_value, error_variance, observed_count
):
    members, _, columns, latitudes = ensemble.shape
    slots = observed_cell.shape[2]
    planes = jnp.transpose(ensemble, (1, 2, 0, 3))
    edge = jax.ShapeDtypeStruct((4, members, latitudes), BF16)
    pair = (3, 2, members, latitudes)
    whole = pl.BlockSpec((4, members, latitudes), lambda i: (0, 0, 0))
    to_west, to_east = pl.pallas_call(
        edge_kernel,
        grid=(1,),
        out_shape=(edge, edge),
        in_specs=[
            pl.BlockSpec(pair, lambda i: (0, 0, 0, 0)),
            pl.BlockSpec(pair, lambda i: (0, columns // 2 - 1, 0, 0)),
            pl.BlockSpec((columns, latitudes), lambda i: (0, 0)),
        ],
        out_specs=(whole, whole),
        compiler_params=params(8),
        name="edges",
    )(planes, planes, layer_depth)
    left = around(to_east, "band", 1)
    right = around(to_west, "band", -1)
    position = (np.arange(latitudes) + 0.5) / latitudes - 0.5
    turning = coriolis_scale * np.sin(math.pi * position)
    turning = jnp.asarray(np.broadcast_to(turning.astype(np.float32), (8, latitudes)))
    sent = pl.pallas_call(
        forecast_kernel,
        out_shape=jax.ShapeDtypeStruct((8, CELLS, 256), BF16),
        scratch_shapes=[
            pltpu.VMEM((columns, members, latitudes), F32),
            pltpu.VMEM((columns + 4, members, latitudes), F32),
            pltpu.VMEM((columns + 2, members, latitudes), BF16),
            pltpu.VMEM((8, CELLS, 256), F32),
        ],
        compiler_params=params(24),
        name="forecast",
    )(planes, left, right, layer_depth, turning)
    got = swap(sent)

    rows = cell_rows(observed_cell[0])
    live = jnp.arange(slots, dtype=jnp.int32)[None, :] < observed_count[0][:, None]
    root = jnp.sqrt(jnp.where(live, 1.0 / error_variance[0], 0.0))
    vmem = pl.BlockSpec(memory_space=pltpu.VMEM)
    held, gram, short = pl.pallas_call(
        observe_kernel,
        out_shape=(
            jax.ShapeDtypeStruct((8, CELLS, 256), BF16),
            jax.ShapeDtypeStruct((2, PACKED, 256), F32),
            jax.ShapeDtypeStruct((2, PACKED, 256), BF16),
        ),
        in_specs=[pl.BlockSpec(memory_space=pltpu.SMEM), vmem, vmem, vmem],
        scratch_shapes=[
            pltpu.VMEM((2, 8 * CELLS, LANES), F32),
            pltpu.VMEM((2, 2, slots, LANES), F32),
        ],
        compiler_params=params(20),
        name="observe",
    )(rows, got, root, observed_value[0])

    below = along(short, "mem", 1)
    above = along(short, "mem", -1)
    one_tile = jax.ShapeDtypeStruct((PACKED, 256), BF16)
    column, to_west, to_east = pl.pallas_call(
        combine_kernel,
        out_shape=(jax.ShapeDtypeStruct(gram.shape, F32), one_tile, one_tile),
        compiler_params=params(8),
        name="combine",
    )(gram, below, above)
    west = around(to_east, "band", 1)
    east = around(to_west, "band", -1)
    back = pl.pallas_call(
        analyse_kernel,
        out_shape=jax.ShapeDtypeStruct((8, CELLS, 256), BF16),
        scratch_shapes=[pltpu.VMEM((8, CELLS, 256), BF16)],
        compiler_params=params(20),
        name="analyse",
    )(held, column, west, east)
    returned = swap(back)
    planes = pl.pallas_call(
        return_kernel,
        out_shape=jax.ShapeDtypeStruct(planes.shape, BF16),
        scratch_shapes=[
            pltpu.VMEM((8, CELLS, 256), F32),
            pltpu.VMEM((GROUPS, latitudes, 256), F32),
        ],
        compiler_params=params(24),
        name="come_back",
    )(returned)
    return jnp.transpose(planes, (2, 0, 1, 3))


def choose(ensemble, layer_depth, observed_cell, *rest):
    shape = (lax.axis_size("mem"), ensemble.shape, observed_cell.shape[1])
    fits = shape == (8, (32, 3, 60, 160), 2) and observed_cell.shape[2] % 16 == 0
    chosen = on_device_fast if fits else on_device
    return chosen(ensemble, layer_depth, observed_cell, *rest)


def solution(mesh):
    in_specs = (
        P("mem", None, "band", None),
        P("band", None),
        P("mem", "band", None),
        P("mem", "band", None),
        P("mem", "band", None),
        P("mem", "band"),
    )
    out_specs = P("mem", None, "band", None)
    return jax.shard_map(
        choose, mesh=mesh, in_specs=in_specs, out_specs=out_specs, check_vma=False
    )
```

```python
import math

import jax
import jax.numpy as jnp
import numpy as np
from jax import lax
from jax.experimental import pallas as pl
from jax.experimental.pallas import tpu as pltpu
from jax.sharding import PartitionSpec as P

SWEEPS = 5


half_step = 0.1
coriolis_scale = 0.3
neighbour_weight = 0.75


def padded_2(cells, sides, width):
    for axis, dim in sides:
        count = lax.axis_size(axis)
        head = lax.slice_in_dim(cells, 0, width, axis=dim)
        tail = lax.slice_in_dim(cells, cells.shape[dim] - width, cells.shape[dim], axis=dim)
        cells = jnp.concatenate(
            [
                lax.ppermute(tail, axis, [(i, (i + 1) % count) for i in range(count)]),
                cells,
                lax.ppermute(head, axis, [((i + 1) % count, i) for i in range(count)]),
            ],
            axis=dim,
        )
    return cells


def north_south(source):
    widths = [(0, 0)] * (source.ndim - 1) + [(1, 1)]
    padded = jnp.pad(source, widths)
    return padded[..., 2:] - padded[..., :-2]


def coriolis(latitudes):
    position = jnp.arange(latitudes, dtype=jnp.float32)
    return coriolis_scale * jnp.sin(math.pi * ((position + 0.5) / latitudes - 0.5))


def newton_schulz(starting):
    identity = jnp.eye(starting.shape[-1], dtype=starting.dtype)
    root_part = starting
    inverse_root = jnp.broadcast_to(identity, starting.shape)
    for sweep_index in range(SWEEPS):
        product = jnp.einsum(
            "tij,tjk->tik", inverse_root, root_part, precision=lax.Precision.HIGHEST
        )
        middle = 1.5 * identity - 0.5 * product
        root_part = jnp.einsum("tij,tjk->tik", root_part, middle, precision=lax.Precision.HIGHEST)
        inverse_root = jnp.einsum(
            "tij,tjk->tik", middle, inverse_root, precision=lax.Precision.HIGHEST
        )
    return inverse_root


def on_device(ensemble, layer_depth, observed_cell, observed_value, error_variance, observed_count):
    block_members = ensemble.shape[0]
    columns = ensemble.shape[2]
    latitudes = ensemble.shape[3]
    strips = lax.axis_size("mem")
    members = block_members * strips
    strip_rows = latitudes // strips
    tile_count = observed_cell.shape[1]
    tile_columns = columns // tile_count
    slot_count = observed_cell.shape[2]
    tile_cells = 3 * tile_columns * strip_rows
    height = ensemble[:, 0].astype(jnp.float32)
    eastward = ensemble[:, 1].astype(jnp.float32)
    northward = ensemble[:, 2].astype(jnp.float32)
    turning = coriolis(latitudes)
    flux_east = (layer_depth * eastward).astype(jnp.bfloat16)
    flux_north = (layer_depth * northward).astype(jnp.bfloat16)
    east_margin = padded_2(flux_east, (("band", 1),), 1)
    east_west = east_margin[:, 2:].astype(jnp.float32) - east_margin[:, :-2].astype(jnp.float32)
    north_local = lax.optimization_barrier(flux_north).astype(jnp.float32)
    raised = height - half_step * (east_west + north_south(north_local))
    surface_elevation_cast = raised.astype(jnp.bfloat16)
    height_margin = padded_2(surface_elevation_cast, (("band", 1),), 1)
    margin_wide = height_margin.astype(jnp.float32)
    height_inner = margin_wide[:, 1:-1]
    revised_zonal_velocity = (
        eastward + turning * northward - half_step * (margin_wide[:, 2:] - margin_wide[:, :-2])
    )
    revised_meridional_velocity = (
        northward - turning * eastward - half_step * north_south(height_inner)
    )
    advance_dynamics = jnp.stack(
        [
            surface_elevation_cast,
            revised_zonal_velocity.astype(jnp.bfloat16),
            revised_meridional_velocity.astype(jnp.bfloat16),
        ],
        axis=1,
    )
    reordered = advance_dynamics.reshape(
        block_members, 3, tile_count, tile_columns, strips, strip_rows
    )
    reordered = jnp.transpose(reordered, (4, 2, 0, 1, 3, 5)).reshape(
        strips, tile_count, block_members, tile_cells
    )
    tile_block = lax.all_to_all(reordered, "mem", split_axis=0, concat_axis=2, tiled=True)[0]
    cells_here = observed_cell[0]
    values = jnp.take_along_axis(tile_block, cells_here[:, None, :], axis=2)
    observed_mean = jnp.sum(values, axis=1, dtype=jnp.float32) / members
    slot_index = jnp.arange(slot_count, dtype=jnp.int32)[None, :]
    live_slots = slot_index < observed_count[0][:, None]
    root_weight = jnp.sqrt(jnp.where(live_slots, 1.0 / error_variance[0], 0.0))
    spread = (
        root_weight[:, None, :] * (values.astype(jnp.float32) - observed_mean[:, None, :])
    ).astype(jnp.bfloat16)
    misfit = (root_weight * (observed_value[0] - observed_mean)).astype(jnp.bfloat16)
    spread_margin, misfit_margin = (
        padded_2(spread[None], (("mem", 0), ("band", 1)), 1),
        padded_2(misfit[None], (("mem", 0), ("band", 1)), 1),
    )
    gram_margin = jnp.einsum(
        "atko,atlo->atkl", spread_margin, spread_margin, preferred_element_type=jnp.float32
    )
    pull_margin = jnp.einsum(
        "atko,ato->atk", spread_margin, misfit_margin, preferred_element_type=jnp.float32
    )
    strip_here = lax.axis_index("mem")
    lower_valid = (strip_here > 0).astype(jnp.float32)
    upper_valid = (strip_here < strips - 1).astype(jnp.float32)
    strip_mask = (lower_valid, 1.0, upper_valid)
    total_gram = jnp.zeros((tile_count, members, members), jnp.float32)
    total_pull = jnp.zeros((tile_count, members), jnp.float32)
    for offset_lat in range(3):
        for offset_lon in range(3):
            factor = (
                neighbour_weight ** (abs(offset_lat - 1) + abs(offset_lon - 1))
                * strip_mask[offset_lat]
            )
            total_gram = (
                total_gram + factor * gram_margin[offset_lat, offset_lon : offset_lon + tile_count]
            )
            total_pull = (
                total_pull + factor * pull_margin[offset_lat, offset_lon : offset_lon + tile_count]
            )
    system = (members - 1) * jnp.eye(members, dtype=jnp.float32)[None] + total_gram
    frobenius = jnp.sqrt(jnp.sum(system * system, axis=(1, 2)))
    inverse_root = newton_schulz(system / frobenius[:, None, None])
    spread_map = inverse_root * (math.sqrt(members - 1) / jnp.sqrt(frobenius))[:, None, None]
    half_pull = jnp.einsum("tij,tj->ti", inverse_root, total_pull, precision=lax.Precision.HIGHEST)
    shift_weights = (
        jnp.einsum("tij,tj->ti", inverse_root, half_pull, precision=lax.Precision.HIGHEST)
        / frobenius[:, None]
    )
    weights = (spread_map + shift_weights[:, :, None]).astype(jnp.bfloat16)
    state_mean = jnp.sum(tile_block, axis=1, dtype=jnp.float32) / members
    anomaly = (tile_block.astype(jnp.float32) - state_mean[:, None, :]).astype(jnp.bfloat16)
    update = jnp.einsum("tjk,tjc->tkc", weights, anomaly, preferred_element_type=jnp.float32)
    analysed = (state_mean[:, None, :] + update).astype(jnp.bfloat16)
    returned = lax.all_to_all(analysed[None], "mem", split_axis=2, concat_axis=0, tiled=True)
    returned = returned.reshape(strips, tile_count, block_members, 3, tile_columns, strip_rows)
    return jnp.transpose(returned, (2, 3, 1, 4, 0, 5)).reshape(block_members, 3, columns, latitudes)


LANES = 128
GROUPS = 23
CELLS = 464
INNER = 360
OUTER = 104
F32 = jnp.float32
BF16 = jnp.bfloat16
PACKED = 144
MIB = 1024 * 1024


def params(size):
    return pltpu.CompilerParams(vmem_limit_bytes=size * MIB)


def identity(size, dtype):
    row = lax.broadcasted_iota(jnp.int32, (size, size), 0)
    column = lax.broadcasted_iota(jnp.int32, (size, size), 1)
    return (row == column).astype(F32).astype(dtype)


def dot_nt(left, right):
    return lax.dot_general(left, right, (((1,), (1,)), ((), ())), preferred_element_type=F32)


def dot_nn(left, right):
    return lax.dot_general(left, right, (((1,), (0,)), ((), ())), preferred_element_type=F32)


def split(value):
    high = value.astype(BF16)
    return high, (value - high.astype(F32)).astype(BF16)


def left_3(parts):
    return jnp.concatenate([parts[0], parts[0], parts[1]], axis=1)


def right_3(parts):
    return jnp.concatenate([parts[0], parts[1], parts[0]], axis=0)


def triangle(size):
    row = lax.broadcasted_iota(jnp.int32, (size, size), 0)
    column = lax.broadcasted_iota(jnp.int32, (size, size), 1)
    return row, column


def packed(block, pull):
    row, column = triangle(128)
    last = block[128:256, 128:256]
    corner = jnp.where(row >= column, block[0:128, 0:128], last)
    middle = jnp.sum(jnp.where(row == column, last, 0.0), axis=0, keepdims=True)
    middle = jnp.concatenate([jnp.zeros_like(middle), middle], axis=1)
    top = jnp.concatenate([block[128:256, 0:128], corner], axis=1)
    return jnp.concatenate([top, pull, jnp.broadcast_to(middle, (8, 256))], axis=0)


def unpacked(value):
    row, column = triangle(128)
    low, corner = value[0:128, 0:128], value[0:128, 128:256]
    other = jnp.transpose(corner)
    first = jnp.where(row >= column, corner, other)
    last = jnp.where(row < column, corner, other)
    last = jnp.where(row == column, value[136:137, 128:256], last)
    top = jnp.concatenate([first, jnp.transpose(low)], axis=1)
    return jnp.concatenate([top, jnp.concatenate([low, last], axis=1)], axis=0), value[128:136]


def exchange_lanes(blocks, lane):
    blocks = [list(pair) for pair in blocks]
    for q in range(4):
        low, high = blocks[q], blocks[q + 4]
        blocks[q], blocks[q + 4] = [low[0], high[0]], [low[1], high[1]]
    for bit in range(2):
        step = 32 << bit
        odd = (lane & step) != 0
        for q in range(8):
            if q & (1 << bit):
                continue
            for h in range(2):
                low, high = blocks[q][h], blocks[q | (1 << bit)][h]
                blocks[q][h] = jnp.where(odd, pltpu.roll(high, step, 1), low)
                blocks[q | (1 << bit)][h] = jnp.where(odd, high, pltpu.roll(low, LANES - step, 1))
    return blocks


def group_of(variable, index):
    if index == 0:
        return 18 + variable
    if index == 3:
        return 9 + variable
    return variable * 3 + index - 4 if index > 3 else 12 + variable * 2 + index - 1


def edge_kernel(first, last, depth, to_west, to_east):
    for out, block, columns, near in ((to_west, first, (0, 1), 0), (to_east, last, (58, 59), 1)):
        far = 1 - near
        out[0] = block[0, near]
        for plane, v, k in ((1, 2, near), (2, 1, near), (3, 1, far)):
            deep = depth[columns[k] : columns[k] + 1, :]
            out[plane] = (deep * block[v, k].astype(F32)).astype(BF16)


def difference(latitudes):
    source = lax.broadcasted_iota(jnp.int32, (latitudes, latitudes), 0)
    target = lax.broadcasted_iota(jnp.int32, (latitudes, latitudes), 1)
    shift = (source == target + 1).astype(F32) - (source == target - 1).astype(F32)
    return shift.astype(BF16)


def rows_apart(value, shift):
    flat = value.reshape(-1, value.shape[-1])
    return dot_nn(flat, shift).reshape(value.shape)


def fluxes(east, deep):
    return (deep * east.astype(F32)).astype(BF16).astype(F32)


def heights(field, north, deep, ahead, behind, shift):
    flux_north = (deep * north.astype(F32)).astype(BF16)
    raised = field.astype(F32) - half_step * ((ahead - behind) + rows_apart(flux_north, shift))
    return raised.astype(BF16)


def velocities(east, north, here, ahead, behind, turning, shift):
    east, north = east.astype(F32), north.astype(F32)
    apart = ahead.astype(F32) - behind.astype(F32)
    new_east = east + turning * north - half_step * apart
    new_north = north - turning * east - half_step * rows_apart(here, shift)
    return new_east.astype(BF16), new_north.astype(BF16)


def put_group(staged, block, eye, first):
    latitudes = eye.shape[0]
    rows = latitudes // 8
    turned = dot_nt(eye, block.reshape(256, latitudes))
    for s in range(8):
        staged[s, first : first + rows, :] = turned[rows * s : rows * (s + 1)]


def inner_kernel(ens, depth, turn, out, deep, flux, height, staged):
    members, latitudes = ens.shape[2:]
    shift = difference(latitudes)
    turning = turn[0:1, :][None]
    for c in range(6, 58):
        deep[c - 6] = jnp.broadcast_to(depth[c : c + 1, :], (members, latitudes))

    def flux_step(index, carry):
        here = pl.ds(index * 13, 13)
        flux[here] = fluxes(ens[1, pl.ds(index * 13 + 6, 13)], deep[here])
        return carry

    lax.fori_loop(0, 4, flux_step, 0)

    def height_step(index, carry):
        first = index * 10
        at = pl.ds(first + 7, 10)
        ahead, behind = flux[pl.ds(first + 2, 10)], flux[pl.ds(first, 10)]
        here = pl.ds(first + 1, 10)
        height[here] = heights(ens[0, at], ens[2, at], deep[here], ahead, behind, shift)
        return carry

    lax.fori_loop(0, 5, height_step, 0)
    eye = identity(latitudes, BF16)
    for index in range(1, 7):
        first = 8 * index
        at = slice(first, first + 8)
        here = height[first - 6 : first + 2]
        ahead, behind = height[first - 5 : first + 3], height[first - 7 : first + 1]
        new = velocities(ens[1, at], ens[2, at], here, ahead, behind, turning, shift)
        for v, field in enumerate((here,) + new):
            put_group(staged, field, eye, 20 * group_of(v, index))
    out[...] = staged[...].astype(BF16)


def outer_kernel(ens, left, right, depth, turn, *refs):
    outs, (flux, height, staged) = refs[:8], refs[8:]
    members, latitudes = ens.shape[2:]
    shift = difference(latitudes)
    turning = turn[0:1, :][None]
    eye = identity(latitudes, BF16)

    def depths(first, count):
        return jnp.stack(
            [
                jnp.broadcast_to(depth[c : c + 1, :], (members, latitudes))
                for c in range(first, first + count)
            ]
        )

    def window(edge, first, count, low, high):
        is_left = low == 0
        base = 2 if is_left else 0
        flux[base : base + count] = fluxes(ens[1, first : first + count], depths(first, count))
        at = 0 if is_left else count
        near, far = (1, 0) if is_left else (at, at + 1)
        flux[near] = edge[2].astype(F32)
        flux[far] = edge[3].astype(F32)
        wide = high - low + 1
        skip = 0 if is_left else 1
        columns = slice(first + skip, first + skip + wide)
        new = heights(
            ens[0, columns],
            ens[2, columns],
            depths(first + skip, wide),
            flux[base + skip + 1 : base + skip + 1 + wide],
            flux[base + skip - 1 : base + skip - 1 + wide],
            shift,
        )
        start = 1 if is_left else 0
        height[start : start + wide] = new
        place = 0 if is_left else wide
        middle = near
        east_west = flux[middle + 1] - flux[middle - 1]
        raised = edge[0].astype(F32) - half_step * (east_west + rows_apart(edge[1], shift))
        height[place] = raised.astype(BF16)
        count = high - low
        here = height[1 : 1 + count]
        ahead, behind = height[2 : 2 + count], height[0:count]
        at = slice(low, high)
        return (here,) + velocities(ens[1, at], ens[2, at], here, ahead, behind, turning, shift)

    staged[:, 100:104, :] = jnp.zeros((8, 4, 256), F32)
    for v, field in enumerate(window(left, 0, 10, 0, 8)):
        put_group(staged, field, eye, 20 * v)
    ends = window(right, 54, 6, 56, 60)
    put_group(staged, jnp.concatenate([ends[0], ends[1]], axis=0), eye, 60)
    put_group(staged, jnp.concatenate([ends[2], jnp.zeros_like(ends[2])], axis=0), eye, 80)
    me = lax.axis_index("mem")
    for d in range(8):
        outs[d][...] = staged[me ^ d].astype(BF16)


def observe_kernel(cells, weight, target, got, *refs):
    edges, (held, gram, short, joined, wide, seen) = refs[:8], refs[8:]
    lane = lax.broadcasted_iota(jnp.int32, (16, LANES), 1)
    me = lax.axis_index("mem")
    for d in range(8):
        joined[me ^ d, 8:112, :] = edges[d][...]
    joined[:, 0:8, :] = got[:, 352:360, :]
    spans = [slice(h * LANES, (h + 1) * LANES) for h in range(2)]

    def spread_out(source, offset):
        def step(index, carry):
            here = pl.ds(pl.multiple_of(index * 16, 16), 16)
            blocks = [[source[q, here, span] for span in spans] for q in range(8)]
            blocks = exchange_lanes(blocks, lane)
            there = pl.ds(pl.multiple_of(index * 16 + offset, 16), 16)
            for q in range(8):
                to = pl.ds(pl.multiple_of(q * CELLS + index * 16 + offset, 16), 16)
                for h in range(2):
                    wide[h, to, :] = blocks[q][h].astype(F32)
                    held[q, there, spans[h]] = blocks[q][h]
            return carry

        return step

    lax.fori_loop(0, 22, spread_out(got, 0), 0, unroll=4)
    lax.fori_loop(0, 7, spread_out(joined, 352), 0, unroll=4)
    slots = seen.shape[2]
    unroll = 16

    def pick(index, carry):
        for t in range(2):
            for k in range(unroll):
                slot = index * unroll + k
                row = cells[t, slot]
                for h in range(2):
                    seen[t, h, pl.ds(slot, 1), :] = wide[h, pl.ds(row, 1), :]
        return carry

    lax.fori_loop(0, slots // unroll, pick, 0)
    eye = identity(256, BF16)
    for t in range(2):
        values = jnp.concatenate([seen[t, 0], seen[t, 1]], axis=1).astype(BF16)
        turned = dot_nt(eye, values)
        mean = jnp.sum(turned, axis=0, keepdims=True) * (1.0 / 256)
        root = weight[t : t + 1, :]
        spread = (root * (turned - mean)).astype(BF16)
        misfit = (root * (target[t : t + 1, :] - mean)).astype(BF16)
        block = dot_nt(spread, spread)
        pull = dot_nt(jnp.broadcast_to(misfit, (16, slots)), spread)
        whole = packed(block, pull[0:8])
        gram[t] = whole
        short[t] = whole.astype(BF16)


def combine_kernel(gram, below, above, column, to_west, to_east):
    total = gram[...] + neighbour_weight * (below[...].astype(F32) + above[...].astype(F32))
    column[...] = total
    to_west[...] = total[0].astype(BF16)
    to_east[...] = total[1].astype(BF16)


def analyse_kernel(held, column, west, east, out, results):
    size = 256
    eye = identity(size, F32)
    beside = (west[...].astype(F32) + column[1], column[0] + east[...].astype(F32))
    norms, pulls, roots, inverses = [], [], [], []
    for t in range(2):
        block, pull = unpacked(column[t] + neighbour_weight * beside[t])
        system = (size - 1) * eye + block
        square = jnp.sum(jnp.sum(system * system, axis=0, keepdims=True), axis=1, keepdims=True)
        norms.append(jnp.sqrt(square))
        pulls.append(pull)
        roots.append(system / norms[t])
    for sweep in range(SWEEPS):
        rights = [right_3(split(root)) for root in roots]
        if sweep == 0:
            inverses = [1.5 * eye - 0.5 * root for root in roots]
            lefts = [left_3(split(inverse)) for inverse in inverses]
            roots = [dot_nn(left, right) for left, right in zip(lefts, rights)]
            continue
        parts = [split(inverse) for inverse in inverses]
        products = [dot_nn(left_3(part), right) for part, right in zip(parts, rights)]
        middles = [left_3(split(1.5 * eye - 0.5 * product)) for product in products]
        if sweep < SWEEPS - 1:
            roots = [dot_nn(middle, right) for middle, right in zip(middles, rights)]
        inverses = [dot_nn(middle, right_3(part)) for middle, part in zip(middles, parts)]
    maps = []
    for t in range(2):
        right = right_3(split(inverses[t]))
        half_pull = dot_nn(left_3(split(pulls[t])), right)
        shift = dot_nn(left_3(split(half_pull)), right) / norms[t]
        scale = math.sqrt(size - 1) / jnp.sqrt(norms[t])
        maps.append((inverses[t] * scale + shift[0:1]).astype(BF16))
    average = jnp.full((size, size), 1.0 / size, BF16)
    near = lax.broadcasted_iota(jnp.int32, (16, size), 0) < 4

    for q in range(8):
        cells = held[q]
        mean = dot_nn(cells, average)
        anomaly = (cells.astype(F32) - mean).astype(BF16)
        edge = 180 if q < 6 else 240
        low, high = edge // 16 * 16, (edge + 15) // 16 * 16
        second = mean[0:high] + dot_nt(anomaly[0:high], maps[1])
        first = mean[low:432] + dot_nt(anomaly[low:432], maps[0])
        last = mean[416:464] + dot_nt(anomaly[416:464], maps[1])
        results[q, 0:low] = second[0:low].astype(BF16)
        if low < high:
            both = jnp.where(near, second[low:high], first[0:16])
            results[q, low:high] = both.astype(BF16)
        results[q, high:416] = first[high - low : 416 - low].astype(BF16)
        both = jnp.where(near, first[416 - low : 432 - low], last[0:16])
        results[q, 416:432] = both.astype(BF16)
        results[q, 432:464] = last[16:48].astype(BF16)
    lane = lax.broadcasted_iota(jnp.int32, (16, LANES), 1)

    def gather_in(index, carry):
        here = pl.ds(pl.multiple_of(index * 16, 16), 16)
        spans = [slice(h * LANES, (h + 1) * LANES) for h in range(2)]
        blocks = [[results[q, here, span] for span in spans] for q in range(8)]
        blocks = exchange_lanes(blocks, lane)
        for q in range(8):
            for h in range(2):
                out[q, here, spans[h]] = blocks[q][h]
        return carry

    lax.fori_loop(0, CELLS // 16, gather_in, 0, unroll=4)


def return_kernel(got, out, wide, turned):
    members, latitudes = out.shape[2:]
    rows = latitudes // 8
    wide[...] = got[...].astype(F32)
    eye = identity(256, BF16)

    def take(g):
        for s in range(8):
            turned[g, rows * s : rows * (s + 1), :] = wide[s, rows * g : rows * (g + 1), :]
        block = dot_nt(eye, turned[g].astype(BF16)).astype(BF16)
        return block.reshape(8, members, latitudes)

    for v in range(3):
        for index in range(7):
            out[v, 8 * index : 8 * index + 8] = take(group_of(v, index))
    mixed = take(21)
    out[0, 56:60] = mixed[0:4]
    out[1, 56:60] = mixed[4:8]
    out[2, 56:60] = take(22)[0:4]


def around(value, axis, step):
    count = lax.axis_size(axis)
    return lax.ppermute(value, axis, [(i, (i + step) % count) for i in range(count)])


def along(value, axis, step):
    count = lax.axis_size(axis)
    pairs = [(i, i + step) for i in range(count) if 0 <= i + step < count]
    return lax.ppermute(value, axis, pairs)


def swap(value):
    return lax.all_to_all(value, "mem", split_axis=0, concat_axis=0, tiled=True)


def cell_rows(cell):
    variable = cell // 600
    tile = jnp.arange(2, dtype=jnp.int32)[:, None]
    column = tile * 30 + cell // 20 % 30
    index = column // 8
    place = column % 8
    group = jnp.where(index > 3, variable * 3 + index - 4, 11 + variable * 2 + index)
    group = jnp.where(index == 3, 9 + variable, group)
    group = jnp.where(index == 0, 18 + variable, group)
    is_last = column >= 56
    group = jnp.where(is_last, 21 + variable // 2, group)
    place = jnp.where(is_last, column - 56 + 4 * (variable % 2), place)
    return place * CELLS + group * 20 + cell % 20


def on_device_fast(
    ensemble, layer_depth, observed_cell, observed_value, error_variance, observed_count
):
    members, _, columns, latitudes = ensemble.shape
    slots = observed_cell.shape[2]
    planes = jnp.transpose(ensemble, (1, 2, 0, 3))
    edge = jax.ShapeDtypeStruct((4, members, latitudes), BF16)
    pair = (3, 2, members, latitudes)
    whole = pl.BlockSpec((4, members, latitudes), lambda i: (0, 0, 0))
    to_west, to_east = pl.pallas_call(
        edge_kernel,
        grid=(1,),
        out_shape=(edge, edge),
        in_specs=[
            pl.BlockSpec(pair, lambda i: (0, 0, 0, 0)),
            pl.BlockSpec(pair, lambda i: (0, columns // 2 - 1, 0, 0)),
            pl.BlockSpec((columns, latitudes), lambda i: (0, 0)),
        ],
        out_specs=(whole, whole),
        compiler_params=params(60),
        name="edges",
    )(planes, planes, layer_depth)
    left = around(to_east, "band", 1)
    right = around(to_west, "band", -1)
    position = (np.arange(latitudes) + 0.5) / latitudes - 0.5
    turning = coriolis_scale * np.sin(math.pi * position)
    turning = jnp.asarray(np.broadcast_to(turning.astype(np.float32), (8, latitudes)))
    sent = pl.pallas_call(
        inner_kernel,
        out_shape=jax.ShapeDtypeStruct((8, INNER, 256), BF16),
        scratch_shapes=[
            pltpu.VMEM((52, members, latitudes), F32),
            pltpu.VMEM((52, members, latitudes), F32),
            pltpu.VMEM((52, members, latitudes), BF16),
            pltpu.VMEM((8, INNER, 256), F32),
        ],
        compiler_params=params(24),
        name="inner",
    )(planes, layer_depth, turning)
    got = swap(sent)
    sent = pl.pallas_call(
        outer_kernel,
        out_shape=(jax.ShapeDtypeStruct((OUTER, 256), BF16),) * 8,
        scratch_shapes=[
            pltpu.VMEM((12, members, latitudes), F32),
            pltpu.VMEM((10, members, latitudes), BF16),
            pltpu.VMEM((8, OUTER, 256), F32),
        ],
        compiler_params=params(16),
        name="outer",
    )(planes, left, right, layer_depth, turning)
    got_edges = [sent[0]]
    for d in range(1, 8):
        got_edges.append(lax.ppermute(sent[d], "mem", [(i, i ^ d) for i in range(8)]))

    rows = cell_rows(observed_cell[0])
    live = jnp.arange(slots, dtype=jnp.int32)[None, :] < observed_count[0][:, None]
    root = jnp.sqrt(jnp.where(live, 1.0 / error_variance[0], 0.0))
    vmem = pl.BlockSpec(memory_space=pltpu.VMEM)
    held, gram, short = pl.pallas_call(
        observe_kernel,
        out_shape=(
            jax.ShapeDtypeStruct((8, CELLS, 256), BF16),
            jax.ShapeDtypeStruct((2, PACKED, 256), F32),
            jax.ShapeDtypeStruct((2, PACKED, 256), BF16),
        ),
        in_specs=[pl.BlockSpec(memory_space=pltpu.SMEM)] + [vmem] * 11,
        scratch_shapes=[
            pltpu.VMEM((8, 112, 256), BF16),
            pltpu.VMEM((2, 8 * CELLS, LANES), F32),
            pltpu.VMEM((2, 2, slots, LANES), F32),
        ],
        compiler_params=params(20),
        name="observe",
    )(rows, root, observed_value[0], got, *got_edges)

    below = along(short, "mem", 1)
    above = along(short, "mem", -1)
    one_tile = jax.ShapeDtypeStruct((PACKED, 256), BF16)
    column, to_west, to_east = pl.pallas_call(
        combine_kernel,
        out_shape=(jax.ShapeDtypeStruct(gram.shape, F32), one_tile, one_tile),
        compiler_params=params(8),
        name="combine",
    )(gram, below, above)
    west = around(to_east, "band", 1)
    east = around(to_west, "band", -1)
    back = pl.pallas_call(
        analyse_kernel,
        out_shape=jax.ShapeDtypeStruct((8, CELLS, 256), BF16),
        scratch_shapes=[pltpu.VMEM((8, CELLS, 256), BF16)],
        compiler_params=params(20),
        name="analyse",
    )(held, column, west, east)
    returned = swap(back)
    planes = pl.pallas_call(
        return_kernel,
        out_shape=jax.ShapeDtypeStruct(planes.shape, BF16),
        scratch_shapes=[
            pltpu.VMEM((8, CELLS, 256), F32),
            pltpu.VMEM((GROUPS, latitudes, 256), F32),
        ],
        compiler_params=params(24),
        name="come_back",
    )(returned)
    return jnp.transpose(planes, (2, 0, 1, 3))


def choose(ensemble, layer_depth, observed_cell, *rest):
    shape = (lax.axis_size("mem"), ensemble.shape, observed_cell.shape[1])
    fits = shape == (8, (32, 3, 60, 160), 2) and observed_cell.shape[2] % 16 == 0
    chosen = on_device_fast if fits else on_device
    return chosen(ensemble, layer_depth, observed_cell, *rest)


def solution(mesh):
    in_specs = (
        P("mem", None, "band", None),
        P("band", None),
        P("mem", "band", None),
        P("mem", "band", None),
        P("mem", "band", None),
        P("mem", "band"),
    )
    out_specs = P("mem", None, "band", None)
    return jax.shard_map(
        choose, mesh=mesh, in_specs=in_specs, out_specs=out_specs, check_vma=False
    )
```

```python
import math

import jax
import jax.numpy as jnp
import numpy as np
from jax import lax
from jax.experimental import pallas as pl
from jax.experimental.pallas import tpu as pltpu
from jax.sharding import PartitionSpec as P

SWEEPS = 5


half_step = 0.1
coriolis_scale = 0.3
neighbour_weight = 0.75


def padded_2(cells, sides, width):
    for axis, dim in sides:
        count = lax.axis_size(axis)
        head = lax.slice_in_dim(cells, 0, width, axis=dim)
        tail = lax.slice_in_dim(cells, cells.shape[dim] - width, cells.shape[dim], axis=dim)
        cells = jnp.concatenate(
            [
                lax.ppermute(tail, axis, [(i, (i + 1) % count) for i in range(count)]),
                cells,
                lax.ppermute(head, axis, [((i + 1) % count, i) for i in range(count)]),
            ],
            axis=dim,
        )
    return cells


def north_south(source):
    widths = [(0, 0)] * (source.ndim - 1) + [(1, 1)]
    padded = jnp.pad(source, widths)
    return padded[..., 2:] - padded[..., :-2]


def coriolis(latitudes):
    position = jnp.arange(latitudes, dtype=jnp.float32)
    return coriolis_scale * jnp.sin(math.pi * ((position + 0.5) / latitudes - 0.5))


def newton_schulz(starting):
    identity = jnp.eye(starting.shape[-1], dtype=starting.dtype)
    root_part = starting
    inverse_root = jnp.broadcast_to(identity, starting.shape)
    for sweep_index in range(SWEEPS):
        product = jnp.einsum(
            "tij,tjk->tik", inverse_root, root_part, precision=lax.Precision.HIGHEST
        )
        middle = 1.5 * identity - 0.5 * product
        root_part = jnp.einsum("tij,tjk->tik", root_part, middle, precision=lax.Precision.HIGHEST)
        inverse_root = jnp.einsum(
            "tij,tjk->tik", middle, inverse_root, precision=lax.Precision.HIGHEST
        )
    return inverse_root


def on_device(ensemble, layer_depth, observed_cell, observed_value, error_variance, observed_count):
    block_members = ensemble.shape[0]
    columns = ensemble.shape[2]
    latitudes = ensemble.shape[3]
    strips = lax.axis_size("mem")
    members = block_members * strips
    strip_rows = latitudes // strips
    tile_count = observed_cell.shape[1]
    tile_columns = columns // tile_count
    slot_count = observed_cell.shape[2]
    tile_cells = 3 * tile_columns * strip_rows
    height = ensemble[:, 0].astype(jnp.float32)
    eastward = ensemble[:, 1].astype(jnp.float32)
    northward = ensemble[:, 2].astype(jnp.float32)
    turning = coriolis(latitudes)
    flux_east = (layer_depth * eastward).astype(jnp.bfloat16)
    flux_north = (layer_depth * northward).astype(jnp.bfloat16)
    east_margin = padded_2(flux_east, (("band", 1),), 1)
    east_west = east_margin[:, 2:].astype(jnp.float32) - east_margin[:, :-2].astype(jnp.float32)
    north_local = lax.optimization_barrier(flux_north).astype(jnp.float32)
    raised = height - half_step * (east_west + north_south(north_local))
    surface_elevation_cast = raised.astype(jnp.bfloat16)
    height_margin = padded_2(surface_elevation_cast, (("band", 1),), 1)
    margin_wide = height_margin.astype(jnp.float32)
    height_inner = margin_wide[:, 1:-1]
    revised_zonal_velocity = (
        eastward + turning * northward - half_step * (margin_wide[:, 2:] - margin_wide[:, :-2])
    )
    revised_meridional_velocity = (
        northward - turning * eastward - half_step * north_south(height_inner)
    )
    advance_dynamics = jnp.stack(
        [
            surface_elevation_cast,
            revised_zonal_velocity.astype(jnp.bfloat16),
            revised_meridional_velocity.astype(jnp.bfloat16),
        ],
        axis=1,
    )
    reordered = advance_dynamics.reshape(
        block_members, 3, tile_count, tile_columns, strips, strip_rows
    )
    reordered = jnp.transpose(reordered, (4, 2, 0, 1, 3, 5)).reshape(
        strips, tile_count, block_members, tile_cells
    )
    tile_block = lax.all_to_all(reordered, "mem", split_axis=0, concat_axis=2, tiled=True)[0]
    cells_here = observed_cell[0]
    values = jnp.take_along_axis(tile_block, cells_here[:, None, :], axis=2)
    observed_mean = jnp.sum(values, axis=1, dtype=jnp.float32) / members
    slot_index = jnp.arange(slot_count, dtype=jnp.int32)[None, :]
    live_slots = slot_index < observed_count[0][:, None]
    root_weight = jnp.sqrt(jnp.where(live_slots, 1.0 / error_variance[0], 0.0))
    spread = (
        root_weight[:, None, :] * (values.astype(jnp.float32) - observed_mean[:, None, :])
    ).astype(jnp.bfloat16)
    misfit = (root_weight * (observed_value[0] - observed_mean)).astype(jnp.bfloat16)
    spread_margin, misfit_margin = (
        padded_2(spread[None], (("mem", 0), ("band", 1)), 1),
        padded_2(misfit[None], (("mem", 0), ("band", 1)), 1),
    )
    gram_margin = jnp.einsum(
        "atko,atlo->atkl", spread_margin, spread_margin, preferred_element_type=jnp.float32
    )
    pull_margin = jnp.einsum(
        "atko,ato->atk", spread_margin, misfit_margin, preferred_element_type=jnp.float32
    )
    strip_here = lax.axis_index("mem")
    lower_valid = (strip_here > 0).astype(jnp.float32)
    upper_valid = (strip_here < strips - 1).astype(jnp.float32)
    strip_mask = (lower_valid, 1.0, upper_valid)
    total_gram = jnp.zeros((tile_count, members, members), jnp.float32)
    total_pull = jnp.zeros((tile_count, members), jnp.float32)
    for offset_lat in range(3):
        for offset_lon in range(3):
            factor = (
                neighbour_weight ** (abs(offset_lat - 1) + abs(offset_lon - 1))
                * strip_mask[offset_lat]
            )
            total_gram = (
                total_gram + factor * gram_margin[offset_lat, offset_lon : offset_lon + tile_count]
            )
            total_pull = (
                total_pull + factor * pull_margin[offset_lat, offset_lon : offset_lon + tile_count]
            )
    system = (members - 1) * jnp.eye(members, dtype=jnp.float32)[None] + total_gram
    frobenius = jnp.sqrt(jnp.sum(system * system, axis=(1, 2)))
    inverse_root = newton_schulz(system / frobenius[:, None, None])
    spread_map = inverse_root * (math.sqrt(members - 1) / jnp.sqrt(frobenius))[:, None, None]
    half_pull = jnp.einsum("tij,tj->ti", inverse_root, total_pull, precision=lax.Precision.HIGHEST)
    shift_weights = (
        jnp.einsum("tij,tj->ti", inverse_root, half_pull, precision=lax.Precision.HIGHEST)
        / frobenius[:, None]
    )
    weights = (spread_map + shift_weights[:, :, None]).astype(jnp.bfloat16)
    state_mean = jnp.sum(tile_block, axis=1, dtype=jnp.float32) / members
    anomaly = (tile_block.astype(jnp.float32) - state_mean[:, None, :]).astype(jnp.bfloat16)
    update = jnp.einsum("tjk,tjc->tkc", weights, anomaly, preferred_element_type=jnp.float32)
    analysed = (state_mean[:, None, :] + update).astype(jnp.bfloat16)
    returned = lax.all_to_all(analysed[None], "mem", split_axis=2, concat_axis=0, tiled=True)
    returned = returned.reshape(strips, tile_count, block_members, 3, tile_columns, strip_rows)
    return jnp.transpose(returned, (2, 3, 1, 4, 0, 5)).reshape(block_members, 3, columns, latitudes)


LANES = 128
GROUPS = 23
CELLS = 464
INNER = 360
OUTER = 104
F32 = jnp.float32
BF16 = jnp.bfloat16
PACKED = 144
MIB = 1024 * 1024


def params(size):
    return pltpu.CompilerParams(vmem_limit_bytes=size * MIB)


def identity(size, dtype):
    row = lax.broadcasted_iota(jnp.int32, (size, size), 0)
    column = lax.broadcasted_iota(jnp.int32, (size, size), 1)
    return (row == column).astype(F32).astype(dtype)


def dot_nt(left, right):
    return lax.dot_general(left, right, (((1,), (1,)), ((), ())), preferred_element_type=F32)


def dot_nn(left, right):
    return lax.dot_general(left, right, (((1,), (0,)), ((), ())), preferred_element_type=F32)


def split(value):
    high = value.astype(BF16)
    return high, (value - high.astype(F32)).astype(BF16)


def left_3(parts):
    return jnp.concatenate([parts[0], parts[0], parts[1]], axis=1)


def right_3(parts):
    return jnp.concatenate([parts[0], parts[1], parts[0]], axis=0)


def triangle(size):
    row = lax.broadcasted_iota(jnp.int32, (size, size), 0)
    column = lax.broadcasted_iota(jnp.int32, (size, size), 1)
    return row, column


def packed(block, pull):
    row, column = triangle(128)
    last = block[128:256, 128:256]
    corner = jnp.where(row >= column, block[0:128, 0:128], last)
    middle = jnp.sum(jnp.where(row == column, last, 0.0), axis=0, keepdims=True)
    middle = jnp.concatenate([jnp.zeros_like(middle), middle], axis=1)
    top = jnp.concatenate([block[128:256, 0:128], corner], axis=1)
    return jnp.concatenate([top, pull, jnp.broadcast_to(middle, (8, 256))], axis=0)


def unpacked(value):
    row, column = triangle(128)
    low, corner = value[0:128, 0:128], value[0:128, 128:256]
    other = jnp.transpose(corner)
    first = jnp.where(row >= column, corner, other)
    last = jnp.where(row < column, corner, other)
    last = jnp.where(row == column, value[136:137, 128:256], last)
    top = jnp.concatenate([first, jnp.transpose(low)], axis=1)
    return jnp.concatenate([top, jnp.concatenate([low, last], axis=1)], axis=0), value[128:136]


def exchange_lanes(blocks, lane):
    blocks = [list(pair) for pair in blocks]
    for q in range(4):
        low, high = blocks[q], blocks[q + 4]
        blocks[q], blocks[q + 4] = [low[0], high[0]], [low[1], high[1]]
    for bit in range(2):
        step = 32 << bit
        odd = (lane & step) != 0
        for q in range(8):
            if q & (1 << bit):
                continue
            for h in range(2):
                low, high = blocks[q][h], blocks[q | (1 << bit)][h]
                blocks[q][h] = jnp.where(odd, pltpu.roll(high, step, 1), low)
                blocks[q | (1 << bit)][h] = jnp.where(odd, high, pltpu.roll(low, LANES - step, 1))
    return blocks


def group_of(variable, index):
    if index == 0:
        return 18 + variable
    if index == 3:
        return 9 + variable
    return variable * 3 + index - 4 if index > 3 else 12 + variable * 2 + index - 1


def difference(latitudes):
    source = lax.broadcasted_iota(jnp.int32, (latitudes, latitudes), 0)
    target = lax.broadcasted_iota(jnp.int32, (latitudes, latitudes), 1)
    shift = (source == target + 1).astype(F32) - (source == target - 1).astype(F32)
    return shift.astype(BF16)


def rows_apart(value, shift):
    flat = value.reshape(-1, value.shape[-1])
    return dot_nn(flat, shift).reshape(value.shape)


def fluxes(east, deep):
    return (deep * east.astype(F32)).astype(BF16).astype(F32)


def heights(field, north, deep, ahead, behind, shift):
    flux_north = (deep * north.astype(F32)).astype(BF16)
    raised = field.astype(F32) - half_step * ((ahead - behind) + rows_apart(flux_north, shift))
    return raised.astype(BF16)


def velocities(east, north, here, ahead, behind, turning, shift):
    east, north = east.astype(F32), north.astype(F32)
    apart = ahead.astype(F32) - behind.astype(F32)
    new_east = east + turning * north - half_step * apart
    new_north = north - turning * east - half_step * rows_apart(here, shift)
    return new_east.astype(BF16), new_north.astype(BF16)


def put_group(staged, block, eye, first):
    latitudes = eye.shape[0]
    rows = latitudes // 8
    turned = dot_nt(eye, block.reshape(256, latitudes))
    for s in range(8):
        staged[s, first : first + rows, :] = turned[rows * s : rows * (s + 1)]


def turning_row(latitudes):
    position = lax.broadcasted_iota(jnp.int32, (8, latitudes), 1).astype(F32)
    turning = coriolis_scale * jnp.sin(math.pi * ((position + 0.5) / latitudes - 0.5))
    return turning[0:1, :][None]


def inner_kernel(ens, depth, out, to_west, to_east, here, deep, flux, height, staged, arrived):
    columns, members, latitudes = here.shape[1:]
    batch = columns // 5
    pieces = [pltpu.make_async_copy(depth, deep, arrived.at[5])]
    for k in range(5):
        span = pl.ds(k * batch, batch)
        piece = pltpu.make_async_copy(ens.at[:, span], here.at[:, span], arrived.at[k])
        pieces.append(piece)
    for piece in pieces:
        piece.start()
    shift = difference(latitudes)
    turning = turning_row(latitudes)
    eye = identity(latitudes, BF16)
    pieces[0].wait()

    def depths(first, count):
        rows = [deep[c : c + 1, :] for c in range(first, first + count)]
        return jnp.stack([jnp.broadcast_to(row, (members, latitudes)) for row in rows])

    def edge(to, near, far):
        to[0] = here[0, near]
        to[1] = (deep[near : near + 1, :] * here[2, near].astype(F32)).astype(BF16)
        to[2] = flux[near].astype(BF16)
        to[3] = flux[far].astype(BF16)

    done = 1
    for k in range(5):
        pieces[k + 1].wait()
        first = k * batch
        flux[first : first + batch] = fluxes(here[1, first : first + batch], depths(first, batch))
        if k == 0:
            edge(to_west, 0, 1)
        if k == 4:
            edge(to_east, columns - 1, columns - 2)
        low, high = max(first - 1, 1), first + batch - 1
        at = slice(low, high)
        ahead, behind = flux[low + 1 : high + 1], flux[low - 1 : high - 1]
        height[at] = heights(
            here[0, at], here[2, at], depths(low, high - low), ahead, behind, shift
        )
        while done < 7 and 8 * done + 9 <= high:
            first = 8 * done
            at = slice(first, first + 8)
            ahead, behind = height[first + 1 : first + 9], height[first - 1 : first + 7]
            new = velocities(here[1, at], here[2, at], height[at], ahead, behind, turning, shift)
            for v, field in enumerate((height[at],) + new):
                put_group(staged, field, eye, 20 * group_of(v, done))
            done += 1
    out[...] = staged[...].astype(BF16)


def outer_kernel(west_block, east_block, left, right, depth, *refs):
    outs, (flux, height, staged) = refs[:8], refs[8:]
    members, latitudes = west_block.shape[2:]
    shift = difference(latitudes)
    turning = turning_row(latitudes)
    eye = identity(latitudes, BF16)

    def depths(first, count):
        return jnp.stack(
            [
                jnp.broadcast_to(depth[c : c + 1, :], (members, latitudes))
                for c in range(first, first + count)
            ]
        )

    def window(ens, edge, first, count, low, high):
        is_left = low == 0
        base = 2 if is_left else 0
        flux[base : base + count] = fluxes(ens[1, 0:count], depths(first, count))
        at = 0 if is_left else count
        near, far = (1, 0) if is_left else (at, at + 1)
        flux[near] = edge[2].astype(F32)
        flux[far] = edge[3].astype(F32)
        wide = high - low + 1
        skip = 0 if is_left else 1
        columns = slice(skip, skip + wide)
        new = heights(
            ens[0, columns],
            ens[2, columns],
            depths(first + skip, wide),
            flux[base + skip + 1 : base + skip + 1 + wide],
            flux[base + skip - 1 : base + skip - 1 + wide],
            shift,
        )
        start = 1 if is_left else 0
        height[start : start + wide] = new
        place = 0 if is_left else wide
        middle = near
        east_west = flux[middle + 1] - flux[middle - 1]
        raised = edge[0].astype(F32) - half_step * (east_west + rows_apart(edge[1], shift))
        height[place] = raised.astype(BF16)
        count = high - low
        here = height[1 : 1 + count]
        ahead, behind = height[2 : 2 + count], height[0:count]
        at = slice(low - first, high - first)
        return (here,) + velocities(ens[1, at], ens[2, at], here, ahead, behind, turning, shift)

    staged[:, 100:104, :] = jnp.zeros((8, 4, 256), F32)
    for v, field in enumerate(window(west_block, left, 0, 10, 0, 8)):
        put_group(staged, field, eye, 20 * v)
    ends = window(east_block, right, 54, 6, 56, 60)
    put_group(staged, jnp.concatenate([ends[0], ends[1]], axis=0), eye, 60)
    put_group(staged, jnp.concatenate([ends[2], jnp.zeros_like(ends[2])], axis=0), eye, 80)
    me = lax.axis_index("mem")
    for d in range(8):
        outs[d][...] = staged[me ^ d].astype(BF16)


def observe_kernel(cells, weight, target, got, *refs):
    edges, (held, gram, short, joined, wide, seen) = refs[:8], refs[8:]
    lane = lax.broadcasted_iota(jnp.int32, (16, LANES), 1)
    me = lax.axis_index("mem")
    for d in range(8):
        joined[me ^ d, 8:112, :] = edges[d][...]
    joined[:, 0:8, :] = got[:, 352:360, :]
    spans = [slice(h * LANES, (h + 1) * LANES) for h in range(2)]

    def spread_out(source, offset):
        def step(index, carry):
            here = pl.ds(pl.multiple_of(index * 16, 16), 16)
            blocks = [[source[q, here, span] for span in spans] for q in range(8)]
            blocks = exchange_lanes(blocks, lane)
            there = pl.ds(pl.multiple_of(index * 16 + offset, 16), 16)
            for q in range(8):
                to = pl.ds(pl.multiple_of(q * CELLS + index * 16 + offset, 16), 16)
                for h in range(2):
                    wide[h, to, :] = blocks[q][h].astype(F32)
                    held[q, there, spans[h]] = blocks[q][h]
            return carry

        return step

    lax.fori_loop(0, 22, spread_out(got, 0), 0, unroll=4)
    lax.fori_loop(0, 7, spread_out(joined, 352), 0, unroll=4)
    slots = seen.shape[2]
    unroll = 16

    def pick(index, carry):
        for t in range(2):
            for k in range(unroll):
                slot = index * unroll + k
                row = cells[t, slot]
                for h in range(2):
                    seen[t, h, pl.ds(slot, 1), :] = wide[h, pl.ds(row, 1), :]
        return carry

    lax.fori_loop(0, slots // unroll, pick, 0)
    eye = identity(256, BF16)
    for t in range(2):
        values = jnp.concatenate([seen[t, 0], seen[t, 1]], axis=1).astype(BF16)
        turned = dot_nt(eye, values)
        mean = jnp.sum(turned, axis=0, keepdims=True) * (1.0 / 256)
        root = weight[t : t + 1, :]
        spread = (root * (turned - mean)).astype(BF16)
        misfit = (root * (target[t : t + 1, :] - mean)).astype(BF16)
        block = dot_nt(spread, spread)
        pull = dot_nt(jnp.broadcast_to(misfit, (16, slots)), spread)
        whole = packed(block, pull[0:8])
        gram[t] = whole
        short[t] = whole.astype(BF16)


def combine_kernel(gram, below, above, column, to_west, to_east):
    total = gram[...] + neighbour_weight * (below[...].astype(F32) + above[...].astype(F32))
    column[...] = total
    to_west[...] = total[0].astype(BF16)
    to_east[...] = total[1].astype(BF16)


def analyse_kernel(held, column, west, east, *refs):
    outs, (results, ordered) = refs[:8], refs[8:]
    size = 256
    eye = identity(size, F32)
    beside = (west[...].astype(F32) + column[1], column[0] + east[...].astype(F32))
    norms, pulls, roots, inverses = [], [], [], []
    for t in range(2):
        block, pull = unpacked(column[t] + neighbour_weight * beside[t])
        system = (size - 1) * eye + block
        square = jnp.sum(jnp.sum(system * system, axis=0, keepdims=True), axis=1, keepdims=True)
        norms.append(jnp.sqrt(square))
        pulls.append(pull)
        roots.append(system / norms[t])
    for sweep in range(SWEEPS):
        rights = [right_3(split(root)) for root in roots]
        if sweep == 0:
            inverses = [1.5 * eye - 0.5 * root for root in roots]
            lefts = [left_3(split(inverse)) for inverse in inverses]
            roots = [dot_nn(left, right) for left, right in zip(lefts, rights)]
            continue
        parts = [split(inverse) for inverse in inverses]
        products = [dot_nn(left_3(part), right) for part, right in zip(parts, rights)]
        middles = [left_3(split(1.5 * eye - 0.5 * product)) for product in products]
        if sweep < SWEEPS - 1:
            roots = [dot_nn(middle, right) for middle, right in zip(middles, rights)]
        inverses = [dot_nn(middle, right_3(part)) for middle, part in zip(middles, parts)]
    maps = []
    for t in range(2):
        right = right_3(split(inverses[t]))
        half_pull = dot_nn(left_3(split(pulls[t])), right)
        shift = dot_nn(left_3(split(half_pull)), right) / norms[t]
        scale = math.sqrt(size - 1) / jnp.sqrt(norms[t])
        ordered[t] = (inverses[t] * scale + shift[0:1]).astype(BF16).reshape(8, 32, size)
    me = lax.axis_index("mem")
    for t in range(2):
        maps.append(jnp.concatenate([ordered[t, me ^ d] for d in range(8)], axis=0))
    average = jnp.full((size, size), 1.0 / size, BF16)
    near = lax.broadcasted_iota(jnp.int32, (16, size), 0) < 4

    for q in range(8):
        cells = held[q]
        mean = dot_nn(cells, average)
        anomaly = (cells.astype(F32) - mean).astype(BF16)
        edge = 180 if q < 6 else 240
        low, high = edge // 16 * 16, (edge + 15) // 16 * 16
        second = mean[0:high] + dot_nt(anomaly[0:high], maps[1])
        first = mean[low:432] + dot_nt(anomaly[low:432], maps[0])
        last = mean[416:464] + dot_nt(anomaly[416:464], maps[1])
        results[q, 0:low] = second[0:low].astype(BF16)
        if low < high:
            both = jnp.where(near, second[low:high], first[0:16])
            results[q, low:high] = both.astype(BF16)
        results[q, high:416] = first[high - low : 416 - low].astype(BF16)
        both = jnp.where(near, first[416 - low : 432 - low], last[0:16])
        results[q, 416:432] = both.astype(BF16)
        results[q, 432:464] = last[16:48].astype(BF16)
    lane = lax.broadcasted_iota(jnp.int32, (16, LANES), 1)

    def gather_in(index, carry):
        here = pl.ds(pl.multiple_of(index * 16, 16), 16)
        spans = [slice(h * LANES, (h + 1) * LANES) for h in range(2)]
        blocks = [[results[q, here, span] for span in spans] for q in range(8)]
        blocks = exchange_lanes(blocks, lane)
        for q in range(8):
            for h in range(2):
                outs[q][here, spans[h]] = blocks[q][h]
        return carry

    lax.fori_loop(0, CELLS // 16, gather_in, 0, unroll=4)


def return_kernel(*refs):
    got, (out, wide, turned, planes, sent) = refs[:8], refs[8:]
    members, latitudes = planes.shape[2:]
    rows = latitudes // 8
    me = lax.axis_index("mem")
    for d in range(8):
        wide[me ^ d] = got[d][...].astype(F32)
    eye = identity(256, BF16)

    def take(g):
        for s in range(8):
            turned[g, rows * s : rows * (s + 1), :] = wide[s, rows * g : rows * (g + 1), :]
        block = dot_nt(eye, turned[g].astype(BF16)).astype(BF16)
        return block.reshape(8, members, latitudes)

    mixed = take(21)
    planes[0, 56:60] = mixed[0:4]
    planes[1, 56:60] = mixed[4:8]
    planes[2, 56:60] = take(22)[0:4]
    copies = []
    for v in range(3):
        for index in range(7):
            planes[v, 8 * index : 8 * index + 8] = take(group_of(v, index))
        copies.append(pltpu.make_async_copy(planes.at[v], out.at[v], sent.at[v]))
        copies[v].start()
    for copy in copies:
        copy.wait()


def around(value, axis, step):
    count = lax.axis_size(axis)
    return lax.ppermute(value, axis, [(i, (i + step) % count) for i in range(count)])


def along(value, axis, step):
    count = lax.axis_size(axis)
    pairs = [(i, i + step) for i in range(count) if 0 <= i + step < count]
    return lax.ppermute(value, axis, pairs)


def partners(values):
    count = len(values)
    pairs = [[(i, i ^ d) for i in range(count)] for d in range(count)]
    return [values[0]] + [lax.ppermute(values[d], "mem", pairs[d]) for d in range(1, count)]


def swap(value):
    return lax.all_to_all(value, "mem", split_axis=0, concat_axis=0, tiled=True)


def cell_rows(cell):
    variable = cell // 600
    tile = jnp.arange(2, dtype=jnp.int32)[:, None]
    column = tile * 30 + cell // 20 % 30
    index = column // 8
    place = column % 8
    group = jnp.where(index > 3, variable * 3 + index - 4, 11 + variable * 2 + index)
    group = jnp.where(index == 3, 9 + variable, group)
    group = jnp.where(index == 0, 18 + variable, group)
    is_last = column >= 56
    group = jnp.where(is_last, 21 + variable // 2, group)
    place = jnp.where(is_last, column - 56 + 4 * (variable % 2), place)
    return place * CELLS + group * 20 + cell % 20


def on_device_fast(
    ensemble, layer_depth, observed_cell, observed_value, error_variance, observed_count
):
    members, _, columns, latitudes = ensemble.shape
    slots = observed_cell.shape[2]
    planes = jnp.transpose(ensemble, (1, 2, 0, 3))
    edge = jax.ShapeDtypeStruct((4, members, latitudes), BF16)
    far = pl.BlockSpec(memory_space=pltpu.HBM)
    sent, to_west, to_east = pl.pallas_call(
        inner_kernel,
        out_shape=(jax.ShapeDtypeStruct((8, INNER, 256), BF16), edge, edge),
        in_specs=[far, far],
        scratch_shapes=[
            pltpu.VMEM(planes.shape, BF16),
            pltpu.VMEM((columns, latitudes), F32),
            pltpu.VMEM((columns, members, latitudes), F32),
            pltpu.VMEM((columns, members, latitudes), BF16),
            pltpu.VMEM((8, INNER, 256), F32),
            pltpu.SemaphoreType.DMA((6,)),
        ],
        compiler_params=params(60),
        name="inner",
    )(planes, layer_depth)
    got = swap(sent)
    left = around(to_east, "band", 1)
    right = around(to_west, "band", -1)
    flat = pl.BlockSpec((4, members, latitudes), lambda i: (0, 0, 0))
    out_edge = jax.ShapeDtypeStruct((OUTER, 256), BF16)
    sent = pl.pallas_call(
        outer_kernel,
        grid=(1,),
        out_shape=(out_edge,) * 8,
        in_specs=[
            pl.BlockSpec((3, 10, members, latitudes), lambda i: (0, 0, 0, 0)),
            pl.BlockSpec((3, 6, members, latitudes), lambda i: (0, 9, 0, 0)),
            flat,
            flat,
            pl.BlockSpec((columns, latitudes), lambda i: (0, 0)),
        ],
        out_specs=(pl.BlockSpec((OUTER, 256), lambda i: (0, 0)),) * 8,
        scratch_shapes=[
            pltpu.VMEM((12, members, latitudes), F32),
            pltpu.VMEM((10, members, latitudes), BF16),
            pltpu.VMEM((8, OUTER, 256), F32),
        ],
        compiler_params=params(24),
        name="outer",
    )(planes, planes, left, right, layer_depth)
    got_edges = partners(sent)

    rows = cell_rows(observed_cell[0])
    live = jnp.arange(slots, dtype=jnp.int32)[None, :] < observed_count[0][:, None]
    root = jnp.sqrt(jnp.where(live, 1.0 / error_variance[0], 0.0))
    vmem = pl.BlockSpec(memory_space=pltpu.VMEM)
    held, gram, short = pl.pallas_call(
        observe_kernel,
        out_shape=(
            jax.ShapeDtypeStruct((8, CELLS, 256), BF16),
            jax.ShapeDtypeStruct((2, PACKED, 256), F32),
            jax.ShapeDtypeStruct((2, PACKED, 256), BF16),
        ),
        in_specs=[pl.BlockSpec(memory_space=pltpu.SMEM)] + [vmem] * 11,
        scratch_shapes=[
            pltpu.VMEM((8, 112, 256), BF16),
            pltpu.VMEM((2, 8 * CELLS, LANES), F32),
            pltpu.VMEM((2, 2, slots, LANES), F32),
        ],
        compiler_params=params(20),
        name="observe",
    )(rows, root, observed_value[0], got, *got_edges)

    below = along(short, "mem", 1)
    above = along(short, "mem", -1)
    one_tile = jax.ShapeDtypeStruct((PACKED, 256), BF16)
    column, to_west, to_east = pl.pallas_call(
        combine_kernel,
        out_shape=(jax.ShapeDtypeStruct(gram.shape, F32), one_tile, one_tile),
        compiler_params=params(8),
        name="combine",
    )(gram, below, above)
    west = around(to_east, "band", 1)
    east = around(to_west, "band", -1)
    back = pl.pallas_call(
        analyse_kernel,
        out_shape=(jax.ShapeDtypeStruct((CELLS, 256), BF16),) * 8,
        scratch_shapes=[pltpu.VMEM((8, CELLS, 256), BF16), pltpu.VMEM((2, 8, 32, 256), BF16)],
        compiler_params=params(20),
        name="analyse",
    )(held, column, west, east)
    returned = partners(back)
    planes = pl.pallas_call(
        return_kernel,
        out_shape=jax.ShapeDtypeStruct(planes.shape, BF16),
        out_specs=far,
        scratch_shapes=[
            pltpu.VMEM((8, CELLS, 256), F32),
            pltpu.VMEM((GROUPS, latitudes, 256), F32),
            pltpu.VMEM(planes.shape, BF16),
            pltpu.SemaphoreType.DMA((3,)),
        ],
        compiler_params=params(24),
        name="come_back",
    )(*returned)
    return jnp.transpose(planes, (2, 0, 1, 3))


def choose(ensemble, layer_depth, observed_cell, *rest):
    shape = (lax.axis_size("mem"), ensemble.shape, observed_cell.shape[1])
    fits = shape == (8, (32, 3, 60, 160), 2) and observed_cell.shape[2] % 16 == 0
    chosen = on_device_fast if fits else on_device
    return chosen(ensemble, layer_depth, observed_cell, *rest)


def solution(mesh):
    in_specs = (
        P("mem", None, "band", None),
        P("band", None),
        P("mem", "band", None),
        P("mem", "band", None),
        P("mem", "band", None),
        P("mem", "band"),
    )
    out_specs = P("mem", None, "band", None)
    return jax.shard_map(
        choose, mesh=mesh, in_specs=in_specs, out_specs=out_specs, check_vma=False
    )
```

```python
import math

import jax
import jax.numpy as jnp
import numpy as np
from jax import lax
from jax.experimental import pallas as pl
from jax.experimental.pallas import tpu as pltpu
from jax.sharding import PartitionSpec as P

SWEEPS = 5


half_step = 0.1
coriolis_scale = 0.3
neighbour_weight = 0.75


def padded_2(cells, sides, width):
    for axis, dim in sides:
        count = lax.axis_size(axis)
        head = lax.slice_in_dim(cells, 0, width, axis=dim)
        tail = lax.slice_in_dim(cells, cells.shape[dim] - width, cells.shape[dim], axis=dim)
        cells = jnp.concatenate(
            [
                lax.ppermute(tail, axis, [(i, (i + 1) % count) for i in range(count)]),
                cells,
                lax.ppermute(head, axis, [((i + 1) % count, i) for i in range(count)]),
            ],
            axis=dim,
        )
    return cells


def north_south(source):
    widths = [(0, 0)] * (source.ndim - 1) + [(1, 1)]
    padded = jnp.pad(source, widths)
    return padded[..., 2:] - padded[..., :-2]


def coriolis(latitudes):
    position = jnp.arange(latitudes, dtype=jnp.float32)
    return coriolis_scale * jnp.sin(math.pi * ((position + 0.5) / latitudes - 0.5))


def newton_schulz(starting):
    identity = jnp.eye(starting.shape[-1], dtype=starting.dtype)
    root_part = starting
    inverse_root = jnp.broadcast_to(identity, starting.shape)
    for sweep_index in range(SWEEPS):
        product = jnp.einsum(
            "tij,tjk->tik", inverse_root, root_part, precision=lax.Precision.HIGHEST
        )
        middle = 1.5 * identity - 0.5 * product
        root_part = jnp.einsum("tij,tjk->tik", root_part, middle, precision=lax.Precision.HIGHEST)
        inverse_root = jnp.einsum(
            "tij,tjk->tik", middle, inverse_root, precision=lax.Precision.HIGHEST
        )
    return inverse_root


def on_device(ensemble, layer_depth, observed_cell, observed_value, error_variance, observed_count):
    block_members = ensemble.shape[0]
    columns = ensemble.shape[2]
    latitudes = ensemble.shape[3]
    strips = lax.axis_size("mem")
    members = block_members * strips
    strip_rows = latitudes // strips
    tile_count = observed_cell.shape[1]
    tile_columns = columns // tile_count
    slot_count = observed_cell.shape[2]
    tile_cells = 3 * tile_columns * strip_rows
    height = ensemble[:, 0].astype(jnp.float32)
    eastward = ensemble[:, 1].astype(jnp.float32)
    northward = ensemble[:, 2].astype(jnp.float32)
    turning = coriolis(latitudes)
    flux_east = (layer_depth * eastward).astype(jnp.bfloat16)
    flux_north = (layer_depth * northward).astype(jnp.bfloat16)
    east_margin = padded_2(flux_east, (("band", 1),), 1)
    east_west = east_margin[:, 2:].astype(jnp.float32) - east_margin[:, :-2].astype(jnp.float32)
    north_local = lax.optimization_barrier(flux_north).astype(jnp.float32)
    raised = height - half_step * (east_west + north_south(north_local))
    surface_elevation_cast = raised.astype(jnp.bfloat16)
    height_margin = padded_2(surface_elevation_cast, (("band", 1),), 1)
    margin_wide = height_margin.astype(jnp.float32)
    height_inner = margin_wide[:, 1:-1]
    revised_zonal_velocity = (
        eastward + turning * northward - half_step * (margin_wide[:, 2:] - margin_wide[:, :-2])
    )
    revised_meridional_velocity = (
        northward - turning * eastward - half_step * north_south(height_inner)
    )
    advance_dynamics = jnp.stack(
        [
            surface_elevation_cast,
            revised_zonal_velocity.astype(jnp.bfloat16),
            revised_meridional_velocity.astype(jnp.bfloat16),
        ],
        axis=1,
    )
    reordered = advance_dynamics.reshape(
        block_members, 3, tile_count, tile_columns, strips, strip_rows
    )
    reordered = jnp.transpose(reordered, (4, 2, 0, 1, 3, 5)).reshape(
        strips, tile_count, block_members, tile_cells
    )
    tile_block = lax.all_to_all(reordered, "mem", split_axis=0, concat_axis=2, tiled=True)[0]
    cells_here = observed_cell[0]
    values = jnp.take_along_axis(tile_block, cells_here[:, None, :], axis=2)
    observed_mean = jnp.sum(values, axis=1, dtype=jnp.float32) / members
    slot_index = jnp.arange(slot_count, dtype=jnp.int32)[None, :]
    live_slots = slot_index < observed_count[0][:, None]
    root_weight = jnp.sqrt(jnp.where(live_slots, 1.0 / error_variance[0], 0.0))
    spread = (
        root_weight[:, None, :] * (values.astype(jnp.float32) - observed_mean[:, None, :])
    ).astype(jnp.bfloat16)
    misfit = (root_weight * (observed_value[0] - observed_mean)).astype(jnp.bfloat16)
    spread_margin, misfit_margin = (
        padded_2(spread[None], (("mem", 0), ("band", 1)), 1),
        padded_2(misfit[None], (("mem", 0), ("band", 1)), 1),
    )
    gram_margin = jnp.einsum(
        "atko,atlo->atkl", spread_margin, spread_margin, preferred_element_type=jnp.float32
    )
    pull_margin = jnp.einsum(
        "atko,ato->atk", spread_margin, misfit_margin, preferred_element_type=jnp.float32
    )
    strip_here = lax.axis_index("mem")
    lower_valid = (strip_here > 0).astype(jnp.float32)
    upper_valid = (strip_here < strips - 1).astype(jnp.float32)
    strip_mask = (lower_valid, 1.0, upper_valid)
    total_gram = jnp.zeros((tile_count, members, members), jnp.float32)
    total_pull = jnp.zeros((tile_count, members), jnp.float32)
    for offset_lat in range(3):
        for offset_lon in range(3):
            factor = (
                neighbour_weight ** (abs(offset_lat - 1) + abs(offset_lon - 1))
                * strip_mask[offset_lat]
            )
            total_gram = (
                total_gram + factor * gram_margin[offset_lat, offset_lon : offset_lon + tile_count]
            )
            total_pull = (
                total_pull + factor * pull_margin[offset_lat, offset_lon : offset_lon + tile_count]
            )
    system = (members - 1) * jnp.eye(members, dtype=jnp.float32)[None] + total_gram
    frobenius = jnp.sqrt(jnp.sum(system * system, axis=(1, 2)))
    inverse_root = newton_schulz(system / frobenius[:, None, None])
    spread_map = inverse_root * (math.sqrt(members - 1) / jnp.sqrt(frobenius))[:, None, None]
    half_pull = jnp.einsum("tij,tj->ti", inverse_root, total_pull, precision=lax.Precision.HIGHEST)
    shift_weights = (
        jnp.einsum("tij,tj->ti", inverse_root, half_pull, precision=lax.Precision.HIGHEST)
        / frobenius[:, None]
    )
    weights = (spread_map + shift_weights[:, :, None]).astype(jnp.bfloat16)
    state_mean = jnp.sum(tile_block, axis=1, dtype=jnp.float32) / members
    anomaly = (tile_block.astype(jnp.float32) - state_mean[:, None, :]).astype(jnp.bfloat16)
    update = jnp.einsum("tjk,tjc->tkc", weights, anomaly, preferred_element_type=jnp.float32)
    analysed = (state_mean[:, None, :] + update).astype(jnp.bfloat16)
    returned = lax.all_to_all(analysed[None], "mem", split_axis=2, concat_axis=0, tiled=True)
    returned = returned.reshape(strips, tile_count, block_members, 3, tile_columns, strip_rows)
    return jnp.transpose(returned, (2, 3, 1, 4, 0, 5)).reshape(block_members, 3, columns, latitudes)


LANES = 128
GROUPS = 23
INNER = 360
OUTER = 104
BLOCK = 112
FIRST = 240
SECOND = 224
F32 = jnp.float32
BF16 = jnp.bfloat16
PACKED = 144
ORDER = (6, 7, 2, 4, 3, 5, 1, 0)
MIB = 1024 * 1024


def params(size):
    return pltpu.CompilerParams(vmem_limit_bytes=size * MIB)


def cost(flops, moved):
    return pl.CostEstimate(flops=flops, bytes_accessed=moved, transcendentals=0)


def identity(size, dtype):
    row = lax.broadcasted_iota(jnp.int32, (size, size), 0)
    column = lax.broadcasted_iota(jnp.int32, (size, size), 1)
    return (row == column).astype(F32).astype(dtype)


def dot_nt(left, right):
    return lax.dot_general(left, right, (((1,), (1,)), ((), ())), preferred_element_type=F32)


def dot_nn(left, right):
    return lax.dot_general(left, right, (((1,), (0,)), ((), ())), preferred_element_type=F32)


def split(value):
    high = value.astype(BF16)
    return high, (value - high.astype(F32)).astype(BF16)


def left_3(parts):
    return jnp.concatenate([parts[0], parts[0], parts[1]], axis=1)


def right_3(parts):
    return jnp.concatenate([parts[0], parts[1], parts[0]], axis=0)


def triangle(size):
    row = lax.broadcasted_iota(jnp.int32, (size, size), 0)
    column = lax.broadcasted_iota(jnp.int32, (size, size), 1)
    return row, column


def packed(block, pull):
    row, column = triangle(128)
    last = block[128:256, 128:256]
    corner = jnp.where(row >= column, block[0:128, 0:128], last)
    middle = jnp.sum(jnp.where(row == column, last, 0.0), axis=0, keepdims=True)
    middle = jnp.concatenate([jnp.zeros_like(middle), middle], axis=1)
    top = jnp.concatenate([block[128:256, 0:128], corner], axis=1)
    return jnp.concatenate([top, pull, jnp.broadcast_to(middle, (8, 256))], axis=0)


def unpacked(value):
    row, column = triangle(128)
    low, corner = value[0:128, 0:128], value[0:128, 128:256]
    other = jnp.transpose(corner)
    first = jnp.where(row >= column, corner, other)
    last = jnp.where(row < column, corner, other)
    last = jnp.where(row == column, value[136:137, 128:256], last)
    top = jnp.concatenate([first, jnp.transpose(low)], axis=1)
    return jnp.concatenate([top, jnp.concatenate([low, last], axis=1)], axis=0), value[128:136]


def exchange_lanes(blocks, lane):
    blocks = [list(pair) for pair in blocks]
    for q in range(4):
        low, high = blocks[q], blocks[q + 4]
        blocks[q], blocks[q + 4] = [low[0], high[0]], [low[1], high[1]]
    for bit in range(2):
        step = 32 << bit
        odd = (lane & step) != 0
        for q in range(8):
            if q & (1 << bit):
                continue
            for h in range(2):
                low, high = blocks[q][h], blocks[q | (1 << bit)][h]
                blocks[q][h] = jnp.where(odd, pltpu.roll(high, step, 1), low)
                blocks[q | (1 << bit)][h] = jnp.where(odd, high, pltpu.roll(low, LANES - step, 1))
    return blocks


def group_of(variable, index):
    if index == 0:
        return 18 + variable
    if index == 3:
        return 9 + variable
    return variable * 3 + index - 4 if index > 3 else 12 + variable * 2 + index - 1


def difference(latitudes):
    source = lax.broadcasted_iota(jnp.int32, (latitudes, latitudes), 0)
    target = lax.broadcasted_iota(jnp.int32, (latitudes, latitudes), 1)
    shift = (source == target + 1).astype(F32) - (source == target - 1).astype(F32)
    return shift.astype(BF16)


def rows_apart(value, shift):
    flat = value.reshape(-1, value.shape[-1])
    return dot_nn(flat, shift).reshape(value.shape)


def fluxes(east, deep):
    return (deep * east.astype(F32)).astype(BF16).astype(F32)


def heights(field, north, deep, ahead, behind, shift):
    flux_north = (deep * north.astype(F32)).astype(BF16)
    raised = field.astype(F32) - half_step * ((ahead - behind) + rows_apart(flux_north, shift))
    return raised.astype(BF16)


def velocities(east, north, here, ahead, behind, turning, shift):
    east, north = east.astype(F32), north.astype(F32)
    apart = ahead.astype(F32) - behind.astype(F32)
    new_east = east + turning * north - half_step * apart
    new_north = north - turning * east - half_step * rows_apart(here, shift)
    return new_east.astype(BF16), new_north.astype(BF16)


def put_group(staged, block, eye, first):
    latitudes = eye.shape[0]
    rows = latitudes // 8
    turned = dot_nt(eye, block.reshape(256, latitudes))
    for s in range(8):
        staged[s, first : first + rows, :] = turned[rows * s : rows * (s + 1)]


def turning_row(latitudes):
    position = lax.broadcasted_iota(jnp.int32, (8, latitudes), 1).astype(F32)
    turning = coriolis_scale * jnp.sin(math.pi * ((position + 0.5) / latitudes - 0.5))
    return turning[0:1, :][None]


def inner_kernel(ens, depth, out, to_west, to_east, here, deep, flux, height, staged, arrived):
    columns, members, latitudes = here.shape[1:]
    batch = columns // 5
    pieces = [pltpu.make_async_copy(depth, deep, arrived.at[5])]
    for k in range(5):
        span = pl.ds(k * batch, batch)
        piece = pltpu.make_async_copy(ens.at[:, span], here.at[:, span], arrived.at[k])
        pieces.append(piece)
    for piece in pieces:
        piece.start()
    shift = difference(latitudes)
    turning = turning_row(latitudes)
    eye = identity(latitudes, BF16)
    pieces[0].wait()

    def depths(first, count):
        rows = [deep[c : c + 1, :] for c in range(first, first + count)]
        return jnp.stack([jnp.broadcast_to(row, (members, latitudes)) for row in rows])

    def edge(to, near, far):
        to[0] = here[0, near]
        to[1] = (deep[near : near + 1, :] * here[2, near].astype(F32)).astype(BF16)
        to[2] = flux[near].astype(BF16)
        to[3] = flux[far].astype(BF16)

    done = 1
    for k in range(5):
        pieces[k + 1].wait()
        first = k * batch
        flux[first : first + batch] = fluxes(here[1, first : first + batch], depths(first, batch))
        if k == 0:
            edge(to_west, 0, 1)
        if k == 4:
            edge(to_east, columns - 1, columns - 2)
        low, high = max(first - 1, 1), first + batch - 1
        at = slice(low, high)
        ahead, behind = flux[low + 1 : high + 1], flux[low - 1 : high - 1]
        height[at] = heights(
            here[0, at], here[2, at], depths(low, high - low), ahead, behind, shift
        )
        while done < 7 and 8 * done + 9 <= high:
            first = 8 * done
            at = slice(first, first + 8)
            ahead, behind = height[first + 1 : first + 9], height[first - 1 : first + 7]
            new = velocities(here[1, at], here[2, at], height[at], ahead, behind, turning, shift)
            for v, field in enumerate((height[at],) + new):
                put_group(staged, field, eye, 20 * group_of(v, done))
            done += 1
    out[...] = staged[...].astype(BF16)


def outer_kernel(west_block, east_block, left, right, depth, *refs):
    outs, (flux, height, staged) = refs[:8], refs[8:]
    members, latitudes = west_block.shape[2:]
    shift = difference(latitudes)
    turning = turning_row(latitudes)
    eye = identity(latitudes, BF16)

    def depths(first, count):
        return jnp.stack(
            [
                jnp.broadcast_to(depth[c : c + 1, :], (members, latitudes))
                for c in range(first, first + count)
            ]
        )

    def window(ens, edge, first, count, low, high):
        is_left = low == 0
        base = 2 if is_left else 0
        flux[base : base + count] = fluxes(ens[1, 0:count], depths(first, count))
        at = 0 if is_left else count
        near, far = (1, 0) if is_left else (at, at + 1)
        flux[near] = edge[2].astype(F32)
        flux[far] = edge[3].astype(F32)
        wide = high - low + 1
        skip = 0 if is_left else 1
        columns = slice(skip, skip + wide)
        new = heights(
            ens[0, columns],
            ens[2, columns],
            depths(first + skip, wide),
            flux[base + skip + 1 : base + skip + 1 + wide],
            flux[base + skip - 1 : base + skip - 1 + wide],
            shift,
        )
        start = 1 if is_left else 0
        height[start : start + wide] = new
        place = 0 if is_left else wide
        middle = near
        east_west = flux[middle + 1] - flux[middle - 1]
        raised = edge[0].astype(F32) - half_step * (east_west + rows_apart(edge[1], shift))
        height[place] = raised.astype(BF16)
        count = high - low
        here = height[1 : 1 + count]
        ahead, behind = height[2 : 2 + count], height[0:count]
        at = slice(low - first, high - first)
        return (here,) + velocities(ens[1, at], ens[2, at], here, ahead, behind, turning, shift)

    staged[:, 100:104, :] = jnp.zeros((8, 4, 256), F32)
    for v, field in enumerate(window(west_block, left, 0, 10, 0, 8)):
        put_group(staged, field, eye, 20 * v)
    ends = window(east_block, right, 54, 6, 56, 60)
    put_group(staged, jnp.concatenate([ends[0], ends[1]], axis=0), eye, 60)
    put_group(staged, jnp.concatenate([ends[2], jnp.zeros_like(ends[2])], axis=0), eye, 80)
    me = lax.axis_index("mem")
    for k, d in enumerate(ORDER):
        outs[k][...] = staged[me ^ d].astype(BF16)


def spread_block(source, held, wide, start, lane):
    spans = [slice(h * LANES, (h + 1) * LANES) for h in range(2)]
    count = source.shape[1]
    here = pl.ds(start, 16)
    blocks = exchange_lanes([[source[q, here, span] for span in spans] for q in range(8)], lane)
    for q in range(8):
        to = pl.ds(pl.multiple_of(q * count + start, 8), 16)
        for h in range(2):
            wide[h, to, :] = blocks[q][h].astype(F32)
            held[q, here, spans[h]] = blocks[q][h]


def spread_kernel(got, held, wide):
    lane = lax.broadcasted_iota(jnp.int32, (16, LANES), 1)

    def step(index, carry):
        spread_block(got, held, wide, pl.multiple_of(index * 16, 16), lane)
        return carry

    lax.fori_loop(0, 22, step, 0, unroll=4)
    spread_block(got, held, wide, INNER - 16, lane)


def observe_kernel(cells, weight, target, wide_inner, *refs):
    edges, (held, gram, short, joined, wide, seen) = refs[:8], refs[8:]
    lane = lax.broadcasted_iota(jnp.int32, (16, LANES), 1)
    me = lax.axis_index("mem")
    for k, d in enumerate(ORDER):
        joined[me ^ d, 0:OUTER, :] = edges[k][...]
    joined[:, OUTER:BLOCK, :] = jnp.zeros((8, BLOCK - OUTER, 256), BF16)
    for index in range(BLOCK // 16):
        spread_block(joined, held, wide, index * 16, lane)
    slots = seen.shape[2]
    unroll = 16

    def pick(index, carry):
        for t in range(2):
            for k in range(unroll):
                slot = index * unroll + k
                row = cells[t, slot]
                is_inner = row < 8 * INNER
                near = jnp.where(is_inner, row, 0)
                far = jnp.where(is_inner, 0, row - 8 * INNER)
                for h in range(2):
                    first = wide_inner[h, pl.ds(near, 1), :]
                    second = wide[h, pl.ds(far, 1), :]
                    seen[t, h, pl.ds(slot, 1), :] = jnp.where(is_inner, first, second)
        return carry

    lax.fori_loop(0, slots // unroll, pick, 0)
    eye = identity(256, BF16)
    for t in range(2):
        values = jnp.concatenate([seen[t, 0], seen[t, 1]], axis=1).astype(BF16)
        turned = dot_nt(eye, values)
        mean = jnp.sum(turned, axis=0, keepdims=True) * (1.0 / 256)
        root = weight[t : t + 1, :]
        spread = (root * (turned - mean)).astype(BF16)
        misfit = (root * (target[t : t + 1, :] - mean)).astype(BF16)
        block = dot_nt(spread, spread)
        pull = dot_nt(jnp.broadcast_to(misfit, (16, slots)), spread)
        whole = packed(block, pull[0:8])
        gram[t] = whole
        short[t] = whole.astype(BF16)


def combine_kernel(gram, below, above, column, to_west, to_east):
    total = gram[...] + neighbour_weight * (below[...].astype(F32) + above[...].astype(F32))
    column[...] = total
    to_west[...] = total[0].astype(BF16)
    to_east[...] = total[1].astype(BF16)


def prepare_kernel(inner, outer, *refs):
    average = jnp.full((256, LANES), 1.0 / 256, BF16)
    for q in range(8):
        pieces = (inner[q, 0:FIRST], jnp.concatenate([inner[q, FIRST:INNER], outer[q, 0:OUTER]], axis=0))
        for k, piece in enumerate(pieces):
            mean = dot_nn(piece, average)
            refs[2 * k + 1][q] = mean
            mean = jnp.concatenate([mean, mean], axis=1)
            refs[2 * k][q] = (piece.astype(F32) - mean).astype(BF16)


def send_back(results, outs):
    lane = lax.broadcasted_iota(jnp.int32, (16, LANES), 1)
    spans = [slice(h * LANES, (h + 1) * LANES) for h in range(2)]

    def step(index, carry):
        here = pl.ds(pl.multiple_of(index * 16, 16), 16)
        blocks = [[results[q, here, span] for span in spans] for q in range(8)]
        blocks = exchange_lanes(blocks, lane)
        for q in range(8):
            for h in range(2):
                outs[ORDER.index(q)][here, spans[h]] = blocks[q][h]
        return carry

    lax.fori_loop(0, results.shape[1] // 16, step, 0, unroll=4)


def apply_maps(anomaly, mean, maps, results, q, edge, order):
    count = results.shape[1]
    low, high = edge // 16 * 16, (edge + 15) // 16 * 16
    first = dot_nt(anomaly[q, 0:high], maps[order[0]])
    centre = jnp.concatenate([mean[q], mean[q]], axis=1)
    results[q, 0:low] = (centre[0:low] + first[0:low]).astype(BF16)
    if low == count:
        return
    second = dot_nt(anomaly[q, low:count], maps[order[1]])
    if low < high:
        near = lax.broadcasted_iota(jnp.int32, (16, 256), 0) < edge - low
        both = jnp.where(near, first[low:high], second[0:16])
        results[q, low:high] = (centre[low:high] + both).astype(BF16)
    results[q, high:count] = (centre[high:count] + second[high - low : count - low]).astype(BF16)


def second_kernel(maps, anomaly, mean, *refs):
    outs, results = refs[:8], refs[8]
    both = [maps[0], maps[1]]
    for q in range(8):
        apply_maps(anomaly, mean, both, results, q, 180, (0, 1))
    send_back(results, outs)


def analyse_kernel(column, west, east, anomaly, mean, *refs):
    outs, (kept, results, ordered) = refs[:8], refs[8:]
    size = 256
    eye = identity(size, F32)
    beside = (west[...].astype(F32) + column[1], column[0] + east[...].astype(F32))
    norms, pulls, roots, inverses = [], [], [], []
    for t in range(2):
        block, pull = unpacked(column[t] + neighbour_weight * beside[t])
        system = (size - 1) * eye + block
        square = jnp.sum(jnp.sum(system * system, axis=0, keepdims=True), axis=1, keepdims=True)
        norms.append(jnp.sqrt(square))
        pulls.append(pull)
        roots.append(system / norms[t])
    for sweep in range(SWEEPS):
        rights = [right_3(split(root)) for root in roots]
        if sweep == 0:
            inverses = [1.5 * eye - 0.5 * root for root in roots]
            lefts = [left_3(split(inverse)) for inverse in inverses]
            roots = [dot_nn(left, right) for left, right in zip(lefts, rights)]
            continue
        parts = [split(inverse) for inverse in inverses]
        products = [dot_nn(left_3(part), right) for part, right in zip(parts, rights)]
        middles = [left_3(split(1.5 * eye - 0.5 * product)) for product in products]
        if sweep < SWEEPS - 1:
            roots = [dot_nn(middle, right) for middle, right in zip(middles, rights)]
        inverses = [dot_nn(middle, right_3(part)) for middle, part in zip(middles, parts)]
    maps = []
    for t in range(2):
        right = right_3(split(inverses[t]))
        half_pull = dot_nn(left_3(split(pulls[t])), right)
        shift = dot_nn(left_3(split(half_pull)), right) / norms[t]
        scale = math.sqrt(size - 1) / jnp.sqrt(norms[t])
        ordered[t] = (inverses[t] * scale + shift[0:1]).astype(BF16).reshape(8, 32, size)
    me = lax.axis_index("mem")
    for t in range(2):
        maps.append(jnp.concatenate([ordered[t, me ^ d] for d in range(8)], axis=0))
        kept[t] = maps[t]
    for q in range(8):
        apply_maps(anomaly, mean, maps, results, q, 180 if q < 6 else FIRST, (1, 0))
    send_back(results, outs)


def spread_strips(got, wide):
    me = lax.axis_index("mem")
    for k, d in enumerate(ORDER):
        wide[me ^ d] = got[k][...].astype(F32)


def take_group(wide, turned, eye, g, shape):
    rows = shape[2] // 8
    for s in range(8):
        turned[g, rows * s : rows * (s + 1), :] = wide[s, rows * g : rows * (g + 1), :]
    return dot_nt(eye, turned[g].astype(BF16)).astype(BF16).reshape(shape)


def first_return_kernel(*refs):
    got, (out, wide, turned, planes, sent) = refs[:8], refs[8:]
    shape = (8,) + planes.shape[2:]
    spread_strips(got, wide)
    eye = identity(256, BF16)
    copies = []
    for v in range(3):
        for index in range(3, 7):
            at = 8 * (index - 3)
            planes[v, at : at + 8] = take_group(wide, turned, eye, group_of(v, index), shape)
        copies.append(pltpu.make_async_copy(planes.at[v], out.at[v, pl.ds(24, 32)], sent.at[v]))
        copies[v].start()
    for copy in copies:
        copy.wait()


def second_return_kernel(*refs):
    got, (_, out, wide, turned, planes, sent) = refs[:8], refs[8:]
    shape = (8,) + planes.shape[2:]
    spread_strips(got, wide)
    eye = identity(256, BF16)
    mixed = take_group(wide, turned, eye, 9, shape)
    planes[0, 24:28] = mixed[0:4]
    planes[1, 24:28] = mixed[4:8]
    planes[2, 24:28] = take_group(wide, turned, eye, 10, shape)[0:4]
    copies = []
    for v in range(3):
        for index in range(3):
            at = 8 * index
            block = take_group(wide, turned, eye, group_of(v, index) - 12, shape)
            planes[v, at : at + 8] = block
        for k, (at, to, count) in enumerate(((0, 0, 24), (24, 56, 4))):
            source, target = planes.at[v, pl.ds(at, count)], out.at[v, pl.ds(to, count)]
            copies.append(pltpu.make_async_copy(source, target, sent.at[2 * v + k]))
            copies[-1].start()
    for copy in copies:
        copy.wait()


def around(value, axis, step):
    count = lax.axis_size(axis)
    return lax.ppermute(value, axis, [(i, (i + step) % count) for i in range(count)])


def along(value, axis, step):
    count = lax.axis_size(axis)
    pairs = [(i, i + step) for i in range(count) if 0 <= i + step < count]
    return lax.ppermute(value, axis, pairs)


def partners(values):
    count = len(values)
    moved = []
    for d, value in zip(ORDER, values):
        pairs = [(i, i ^ d) for i in range(count)]
        moved.append(value if d == 0 else lax.ppermute(value, "mem", pairs))
    return moved


def swap(value):
    return lax.all_to_all(value, "mem", split_axis=0, concat_axis=0, tiled=True)


def cell_rows(cell):
    variable = cell // 600
    tile = jnp.arange(2, dtype=jnp.int32)[:, None]
    column = tile * 30 + cell // 20 % 30
    index = column // 8
    place = column % 8
    group = jnp.where(index > 3, variable * 3 + index - 4, 11 + variable * 2 + index)
    group = jnp.where(index == 3, 9 + variable, group)
    group = jnp.where(index == 0, 18 + variable, group)
    is_last = column >= 56
    group = jnp.where(is_last, 21 + variable // 2, group)
    place = jnp.where(is_last, column - 56 + 4 * (variable % 2), place)
    first = place * INNER + group * 20
    last = 8 * INNER + place * BLOCK + (group - 18) * 20
    return jnp.where(group < 18, first, last) + cell % 20


def on_device_fast(
    ensemble, layer_depth, observed_cell, observed_value, error_variance, observed_count
):
    members, _, columns, latitudes = ensemble.shape
    slots = observed_cell.shape[2]
    planes = jnp.transpose(ensemble, (1, 2, 0, 3))
    edge = jax.ShapeDtypeStruct((4, members, latitudes), BF16)
    far = pl.BlockSpec(memory_space=pltpu.HBM)
    sent, to_west, to_east = pl.pallas_call(
        inner_kernel,
        out_shape=(jax.ShapeDtypeStruct((8, INNER, 256), BF16), edge, edge),
        in_specs=[far, far],
        scratch_shapes=[
            pltpu.VMEM(planes.shape, BF16),
            pltpu.VMEM((columns, latitudes), F32),
            pltpu.VMEM((columns, members, latitudes), F32),
            pltpu.VMEM((columns, members, latitudes), BF16),
            pltpu.VMEM((8, INNER, 256), F32),
            pltpu.SemaphoreType.DMA((6,)),
        ],
        compiler_params=params(60),
        name="inner",
    )(planes, layer_depth)
    got = swap(sent)
    left = around(to_east, "band", 1)
    right = around(to_west, "band", -1)
    flat = pl.BlockSpec((4, members, latitudes), lambda i: (0, 0, 0))
    out_edge = jax.ShapeDtypeStruct((OUTER, 256), BF16)
    sent = pl.pallas_call(
        outer_kernel,
        grid=(1,),
        out_shape=(out_edge,) * 8,
        in_specs=[
            pl.BlockSpec((3, 10, members, latitudes), lambda i: (0, 0, 0, 0)),
            pl.BlockSpec((3, 6, members, latitudes), lambda i: (0, 9, 0, 0)),
            flat,
            flat,
            pl.BlockSpec((columns, latitudes), lambda i: (0, 0)),
        ],
        out_specs=(pl.BlockSpec((OUTER, 256), lambda i: (0, 0)),) * 8,
        scratch_shapes=[
            pltpu.VMEM((12, members, latitudes), F32),
            pltpu.VMEM((10, members, latitudes), BF16),
            pltpu.VMEM((8, OUTER, 256), F32),
        ],
        compiler_params=params(24),
        name="outer",
    )(planes, planes, left, right, layer_depth)
    got_edges = partners(sent)

    rows = cell_rows(observed_cell[0])
    live = jnp.arange(slots, dtype=jnp.int32)[None, :] < observed_count[0][:, None]
    root = jnp.sqrt(jnp.where(live, 1.0 / error_variance[0], 0.0))
    vmem = pl.BlockSpec(memory_space=pltpu.VMEM)
    held_inner, wide = pl.pallas_call(
        spread_kernel,
        out_shape=(
            jax.ShapeDtypeStruct((8, INNER, 256), BF16),
            jax.ShapeDtypeStruct((2, 8 * INNER, LANES), F32),
        ),
        compiler_params=params(8),
        cost_estimate=cost(1, 4 * MIB),
        name="spread",
    )(got)
    held_outer, gram, short = pl.pallas_call(
        observe_kernel,
        out_shape=(
            jax.ShapeDtypeStruct((8, BLOCK, 256), BF16),
            jax.ShapeDtypeStruct((2, PACKED, 256), F32),
            jax.ShapeDtypeStruct((2, PACKED, 256), BF16),
        ),
        in_specs=[pl.BlockSpec(memory_space=pltpu.SMEM)] + [vmem] * 11,
        scratch_shapes=[
            pltpu.VMEM((8, BLOCK, 256), BF16),
            pltpu.VMEM((2, 8 * BLOCK, LANES), F32),
            pltpu.VMEM((2, 2, slots, LANES), F32),
        ],
        compiler_params=params(16),
        name="observe",
    )(rows, root, observed_value[0], wide, *got_edges)
    anomaly_1, mean_1, anomaly_2, mean_2 = pl.pallas_call(
        prepare_kernel,
        out_shape=(
            jax.ShapeDtypeStruct((8, FIRST, 256), BF16),
            jax.ShapeDtypeStruct((8, FIRST, LANES), F32),
            jax.ShapeDtypeStruct((8, SECOND, 256), BF16),
            jax.ShapeDtypeStruct((8, SECOND, LANES), F32),
        ),
        compiler_params=params(12),
        cost_estimate=cost(1, 6 * MIB),
        name="prepare",
    )(held_inner, held_outer)

    below = along(short, "mem", 1)
    above = along(short, "mem", -1)
    one_tile = jax.ShapeDtypeStruct((PACKED, 256), BF16)
    column, to_west, to_east = pl.pallas_call(
        combine_kernel,
        out_shape=(jax.ShapeDtypeStruct(gram.shape, F32), one_tile, one_tile),
        compiler_params=params(8),
        name="combine",
    )(gram, below, above)
    west = around(to_east, "band", 1)
    east = around(to_west, "band", -1)
    *back, maps = pl.pallas_call(
        analyse_kernel,
        out_shape=(jax.ShapeDtypeStruct((FIRST, 256), BF16),) * 8
        + (jax.ShapeDtypeStruct((2, 256, 256), BF16),),
        scratch_shapes=[pltpu.VMEM((8, FIRST, 256), BF16), pltpu.VMEM((2, 8, 32, 256), BF16)],
        compiler_params=params(20),
        name="analyse",
    )(column, west, east, anomaly_1, mean_1)
    first = partners(back)
    back = pl.pallas_call(
        second_kernel,
        out_shape=(jax.ShapeDtypeStruct((SECOND, 256), BF16),) * 8,
        scratch_shapes=[pltpu.VMEM((8, SECOND, 256), BF16)],
        compiler_params=params(16),
        cost_estimate=cost(1, 6 * MIB),
        name="second",
    )(maps, anomaly_2, mean_2)
    second = partners(back)
    result = jax.ShapeDtypeStruct(planes.shape, BF16)
    half = pl.pallas_call(
        first_return_kernel,
        out_shape=result,
        out_specs=far,
        scratch_shapes=[
            pltpu.VMEM((8, FIRST, 256), F32),
            pltpu.VMEM((12, latitudes, 256), F32),
            pltpu.VMEM((3, 32, members, latitudes), BF16),
            pltpu.SemaphoreType.DMA((3,)),
        ],
        compiler_params=params(20),
        cost_estimate=cost(1, 4 * MIB),
        name="first_return",
    )(*first)
    planes = pl.pallas_call(
        second_return_kernel,
        out_shape=result,
        in_specs=[vmem] * 8 + [far],
        out_specs=far,
        scratch_shapes=[
            pltpu.VMEM((8, SECOND, 256), F32),
            pltpu.VMEM((11, latitudes, 256), F32),
            pltpu.VMEM((3, 28, members, latitudes), BF16),
            pltpu.SemaphoreType.DMA((6,)),
        ],
        input_output_aliases={8: 0},
        compiler_params=params(20),
        name="second_return",
    )(*second, half)
    return jnp.transpose(planes, (2, 0, 1, 3))


def choose(ensemble, layer_depth, observed_cell, *rest):
    shape = (lax.axis_size("mem"), ensemble.shape, observed_cell.shape[1])
    fits = shape == (8, (32, 3, 60, 160), 2) and observed_cell.shape[2] % 16 == 0
    chosen = on_device_fast if fits else on_device
    return chosen(ensemble, layer_depth, observed_cell, *rest)


def solution(mesh):
    in_specs = (
        P("mem", None, "band", None),
        P("band", None),
        P("mem", "band", None),
        P("mem", "band", None),
        P("mem", "band", None),
        P("mem", "band"),
    )
    out_specs = P("mem", None, "band", None)
    return jax.shard_map(
        choose, mesh=mesh, in_specs=in_specs, out_specs=out_specs, check_vma=False
    )
```

```python
import math

import jax
import jax.numpy as jnp
import numpy as np
from jax import lax
from jax.experimental import pallas as pl
from jax.experimental.pallas import tpu as pltpu
from jax.sharding import PartitionSpec as P

SWEEPS = 5


half_step = 0.1
coriolis_scale = 0.3
neighbour_weight = 0.75


def padded_2(cells, sides, width):
    for axis, dim in sides:
        count = lax.axis_size(axis)
        head = lax.slice_in_dim(cells, 0, width, axis=dim)
        tail = lax.slice_in_dim(cells, cells.shape[dim] - width, cells.shape[dim], axis=dim)
        cells = jnp.concatenate(
            [
                lax.ppermute(tail, axis, [(i, (i + 1) % count) for i in range(count)]),
                cells,
                lax.ppermute(head, axis, [((i + 1) % count, i) for i in range(count)]),
            ],
            axis=dim,
        )
    return cells


def north_south(source):
    widths = [(0, 0)] * (source.ndim - 1) + [(1, 1)]
    padded = jnp.pad(source, widths)
    return padded[..., 2:] - padded[..., :-2]


def coriolis(latitudes):
    position = jnp.arange(latitudes, dtype=jnp.float32)
    return coriolis_scale * jnp.sin(math.pi * ((position + 0.5) / latitudes - 0.5))


def newton_schulz(starting):
    identity = jnp.eye(starting.shape[-1], dtype=starting.dtype)
    root_part = starting
    inverse_root = jnp.broadcast_to(identity, starting.shape)
    for sweep_index in range(SWEEPS):
        product = jnp.einsum(
            "tij,tjk->tik", inverse_root, root_part, precision=lax.Precision.HIGHEST
        )
        middle = 1.5 * identity - 0.5 * product
        root_part = jnp.einsum("tij,tjk->tik", root_part, middle, precision=lax.Precision.HIGHEST)
        inverse_root = jnp.einsum(
            "tij,tjk->tik", middle, inverse_root, precision=lax.Precision.HIGHEST
        )
    return inverse_root


def on_device(ensemble, layer_depth, observed_cell, observed_value, error_variance, observed_count):
    block_members = ensemble.shape[0]
    columns = ensemble.shape[2]
    latitudes = ensemble.shape[3]
    strips = lax.axis_size("mem")
    members = block_members * strips
    strip_rows = latitudes // strips
    tile_count = observed_cell.shape[1]
    tile_columns = columns // tile_count
    slot_count = observed_cell.shape[2]
    tile_cells = 3 * tile_columns * strip_rows
    height = ensemble[:, 0].astype(jnp.float32)
    eastward = ensemble[:, 1].astype(jnp.float32)
    northward = ensemble[:, 2].astype(jnp.float32)
    turning = coriolis(latitudes)
    flux_east = (layer_depth * eastward).astype(jnp.bfloat16)
    flux_north = (layer_depth * northward).astype(jnp.bfloat16)
    east_margin = padded_2(flux_east, (("band", 1),), 1)
    east_west = east_margin[:, 2:].astype(jnp.float32) - east_margin[:, :-2].astype(jnp.float32)
    north_local = lax.optimization_barrier(flux_north).astype(jnp.float32)
    raised = height - half_step * (east_west + north_south(north_local))
    surface_elevation_cast = raised.astype(jnp.bfloat16)
    height_margin = padded_2(surface_elevation_cast, (("band", 1),), 1)
    margin_wide = height_margin.astype(jnp.float32)
    height_inner = margin_wide[:, 1:-1]
    revised_zonal_velocity = (
        eastward + turning * northward - half_step * (margin_wide[:, 2:] - margin_wide[:, :-2])
    )
    revised_meridional_velocity = (
        northward - turning * eastward - half_step * north_south(height_inner)
    )
    advance_dynamics = jnp.stack(
        [
            surface_elevation_cast,
            revised_zonal_velocity.astype(jnp.bfloat16),
            revised_meridional_velocity.astype(jnp.bfloat16),
        ],
        axis=1,
    )
    reordered = advance_dynamics.reshape(
        block_members, 3, tile_count, tile_columns, strips, strip_rows
    )
    reordered = jnp.transpose(reordered, (4, 2, 0, 1, 3, 5)).reshape(
        strips, tile_count, block_members, tile_cells
    )
    tile_block = lax.all_to_all(reordered, "mem", split_axis=0, concat_axis=2, tiled=True)[0]
    cells_here = observed_cell[0]
    values = jnp.take_along_axis(tile_block, cells_here[:, None, :], axis=2)
    observed_mean = jnp.sum(values, axis=1, dtype=jnp.float32) / members
    slot_index = jnp.arange(slot_count, dtype=jnp.int32)[None, :]
    live_slots = slot_index < observed_count[0][:, None]
    root_weight = jnp.sqrt(jnp.where(live_slots, 1.0 / error_variance[0], 0.0))
    spread = (
        root_weight[:, None, :] * (values.astype(jnp.float32) - observed_mean[:, None, :])
    ).astype(jnp.bfloat16)
    misfit = (root_weight * (observed_value[0] - observed_mean)).astype(jnp.bfloat16)
    spread_margin, misfit_margin = (
        padded_2(spread[None], (("mem", 0), ("band", 1)), 1),
        padded_2(misfit[None], (("mem", 0), ("band", 1)), 1),
    )
    gram_margin = jnp.einsum(
        "atko,atlo->atkl", spread_margin, spread_margin, preferred_element_type=jnp.float32
    )
    pull_margin = jnp.einsum(
        "atko,ato->atk", spread_margin, misfit_margin, preferred_element_type=jnp.float32
    )
    strip_here = lax.axis_index("mem")
    lower_valid = (strip_here > 0).astype(jnp.float32)
    upper_valid = (strip_here < strips - 1).astype(jnp.float32)
    strip_mask = (lower_valid, 1.0, upper_valid)
    total_gram = jnp.zeros((tile_count, members, members), jnp.float32)
    total_pull = jnp.zeros((tile_count, members), jnp.float32)
    for offset_lat in range(3):
        for offset_lon in range(3):
            factor = (
                neighbour_weight ** (abs(offset_lat - 1) + abs(offset_lon - 1))
                * strip_mask[offset_lat]
            )
            total_gram = (
                total_gram + factor * gram_margin[offset_lat, offset_lon : offset_lon + tile_count]
            )
            total_pull = (
                total_pull + factor * pull_margin[offset_lat, offset_lon : offset_lon + tile_count]
            )
    system = (members - 1) * jnp.eye(members, dtype=jnp.float32)[None] + total_gram
    frobenius = jnp.sqrt(jnp.sum(system * system, axis=(1, 2)))
    inverse_root = newton_schulz(system / frobenius[:, None, None])
    spread_map = inverse_root * (math.sqrt(members - 1) / jnp.sqrt(frobenius))[:, None, None]
    half_pull = jnp.einsum("tij,tj->ti", inverse_root, total_pull, precision=lax.Precision.HIGHEST)
    shift_weights = (
        jnp.einsum("tij,tj->ti", inverse_root, half_pull, precision=lax.Precision.HIGHEST)
        / frobenius[:, None]
    )
    weights = (spread_map + shift_weights[:, :, None]).astype(jnp.bfloat16)
    state_mean = jnp.sum(tile_block, axis=1, dtype=jnp.float32) / members
    anomaly = (tile_block.astype(jnp.float32) - state_mean[:, None, :]).astype(jnp.bfloat16)
    update = jnp.einsum("tjk,tjc->tkc", weights, anomaly, preferred_element_type=jnp.float32)
    analysed = (state_mean[:, None, :] + update).astype(jnp.bfloat16)
    returned = lax.all_to_all(analysed[None], "mem", split_axis=2, concat_axis=0, tiled=True)
    returned = returned.reshape(strips, tile_count, block_members, 3, tile_columns, strip_rows)
    return jnp.transpose(returned, (2, 3, 1, 4, 0, 5)).reshape(block_members, 3, columns, latitudes)


LANES = 128
GROUPS = 23
INNER = 360
OUTER = 104
BLOCK = 112
FIRST = 240
SECOND = 224
F32 = jnp.float32
BF16 = jnp.bfloat16
PACKED = 144
CHIPS = (0, 2, 4, 6)
ORDER = (6, 2, 4, 7, 1, 3, 5, 0)
MIB = 1024 * 1024


def params(size):
    return pltpu.CompilerParams(vmem_limit_bytes=size * MIB)


def cost(flops, moved):
    return pl.CostEstimate(flops=flops, bytes_accessed=moved, transcendentals=0)


def identity(size, dtype):
    row = lax.broadcasted_iota(jnp.int32, (size, size), 0)
    column = lax.broadcasted_iota(jnp.int32, (size, size), 1)
    return (row == column).astype(F32).astype(dtype)


def dot_nt(left, right):
    return lax.dot_general(left, right, (((1,), (1,)), ((), ())), preferred_element_type=F32)


def dot_nn(left, right):
    return lax.dot_general(left, right, (((1,), (0,)), ((), ())), preferred_element_type=F32)


def split(value):
    high = value.astype(BF16)
    return high, (value - high.astype(F32)).astype(BF16)


def left_3(parts):
    return jnp.concatenate([parts[0], parts[0], parts[1]], axis=1)


def right_3(parts):
    return jnp.concatenate([parts[0], parts[1], parts[0]], axis=0)


def triangle(size):
    row = lax.broadcasted_iota(jnp.int32, (size, size), 0)
    column = lax.broadcasted_iota(jnp.int32, (size, size), 1)
    return row, column


def packed(block, pull):
    row, column = triangle(128)
    last = block[128:256, 128:256]
    corner = jnp.where(row >= column, block[0:128, 0:128], last)
    middle = jnp.sum(jnp.where(row == column, last, 0.0), axis=0, keepdims=True)
    middle = jnp.concatenate([jnp.zeros_like(middle), middle], axis=1)
    top = jnp.concatenate([block[128:256, 0:128], corner], axis=1)
    return jnp.concatenate([top, pull, jnp.broadcast_to(middle, (8, 256))], axis=0)


def unpacked(value):
    row, column = triangle(128)
    low, corner = value[0:128, 0:128], value[0:128, 128:256]
    other = jnp.transpose(corner)
    first = jnp.where(row >= column, corner, other)
    last = jnp.where(row < column, corner, other)
    last = jnp.where(row == column, value[136:137, 128:256], last)
    top = jnp.concatenate([first, jnp.transpose(low)], axis=1)
    return jnp.concatenate([top, jnp.concatenate([low, last], axis=1)], axis=0), value[128:136]


def exchange_lanes(blocks, lane):
    blocks = [list(pair) for pair in blocks]
    for q in range(4):
        low, high = blocks[q], blocks[q + 4]
        blocks[q], blocks[q + 4] = [low[0], high[0]], [low[1], high[1]]
    for bit in range(2):
        step = 32 << bit
        odd = (lane & step) != 0
        for q in range(8):
            if q & (1 << bit):
                continue
            for h in range(2):
                low, high = blocks[q][h], blocks[q | (1 << bit)][h]
                blocks[q][h] = jnp.where(odd, pltpu.roll(high, step, 1), low)
                blocks[q | (1 << bit)][h] = jnp.where(odd, high, pltpu.roll(low, LANES - step, 1))
    return blocks


def group_of(variable, index):
    if index == 0:
        return 18 + variable
    if index == 3:
        return 9 + variable
    return variable * 3 + index - 4 if index > 3 else 12 + variable * 2 + index - 1


def difference(latitudes):
    source = lax.broadcasted_iota(jnp.int32, (latitudes, latitudes), 0)
    target = lax.broadcasted_iota(jnp.int32, (latitudes, latitudes), 1)
    shift = (source == target + 1).astype(F32) - (source == target - 1).astype(F32)
    return shift.astype(BF16)


def rows_apart(value, shift):
    flat = value.reshape(-1, value.shape[-1])
    return dot_nn(flat, shift).reshape(value.shape)


def fluxes(east, deep):
    return (deep * east.astype(F32)).astype(BF16).astype(F32)


def heights(field, north, deep, ahead, behind, shift):
    flux_north = (deep * north.astype(F32)).astype(BF16)
    raised = field.astype(F32) - half_step * ((ahead - behind) + rows_apart(flux_north, shift))
    return raised.astype(BF16)


def velocities(east, north, here, ahead, behind, turning, shift):
    east, north = east.astype(F32), north.astype(F32)
    apart = ahead.astype(F32) - behind.astype(F32)
    new_east = east + turning * north - half_step * apart
    new_north = north - turning * east - half_step * rows_apart(here, shift)
    return new_east.astype(BF16), new_north.astype(BF16)


def put_group(staged, block, eye, first):
    latitudes = eye.shape[0]
    rows = latitudes // 8
    turned = dot_nt(eye, block.reshape(256, latitudes))
    for s in range(8):
        staged[s, first : first + rows, :] = turned[rows * s : rows * (s + 1)]


def turning_row(latitudes):
    position = lax.broadcasted_iota(jnp.int32, (8, latitudes), 1).astype(F32)
    turning = coriolis_scale * jnp.sin(math.pi * ((position + 0.5) / latitudes - 0.5))
    return turning[0:1, :][None]


def inner_kernel(ens, depth, out, to_west, to_east, here, deep, flux, height, staged, arrived):
    columns, members, latitudes = here.shape[1:]
    batch = columns // 5
    pieces = [pltpu.make_async_copy(depth, deep, arrived.at[5])]
    for k in range(5):
        span = pl.ds(k * batch, batch)
        piece = pltpu.make_async_copy(ens.at[:, span], here.at[:, span], arrived.at[k])
        pieces.append(piece)
    for piece in pieces:
        piece.start()
    shift = difference(latitudes)
    turning = turning_row(latitudes)
    eye = identity(latitudes, BF16)
    pieces[0].wait()

    def depths(first, count):
        rows = [deep[c : c + 1, :] for c in range(first, first + count)]
        return jnp.stack([jnp.broadcast_to(row, (members, latitudes)) for row in rows])

    def edge(to, near, far):
        to[0] = here[0, near]
        to[1] = (deep[near : near + 1, :] * here[2, near].astype(F32)).astype(BF16)
        to[2] = flux[near].astype(BF16)
        to[3] = flux[far].astype(BF16)

    done = 1
    for k in range(5):
        pieces[k + 1].wait()
        first = k * batch
        flux[first : first + batch] = fluxes(here[1, first : first + batch], depths(first, batch))
        if k == 0:
            edge(to_west, 0, 1)
        if k == 4:
            edge(to_east, columns - 1, columns - 2)
        low, high = max(first - 1, 1), first + batch - 1
        at = slice(low, high)
        ahead, behind = flux[low + 1 : high + 1], flux[low - 1 : high - 1]
        height[at] = heights(
            here[0, at], here[2, at], depths(low, high - low), ahead, behind, shift
        )
        while done < 7 and 8 * done + 9 <= high:
            first = 8 * done
            at = slice(first, first + 8)
            ahead, behind = height[first + 1 : first + 9], height[first - 1 : first + 7]
            new = velocities(here[1, at], here[2, at], height[at], ahead, behind, turning, shift)
            for v, field in enumerate((height[at],) + new):
                put_group(staged, field, eye, 20 * group_of(v, done))
            done += 1
    out[...] = staged[...].astype(BF16)


def outer_kernel(
    west_block, east_block, left, right, depth, straight, cross, flux, height, staged
):
    members, latitudes = west_block.shape[2:]
    shift = difference(latitudes)
    turning = turning_row(latitudes)
    eye = identity(latitudes, BF16)

    def depths(first, count):
        return jnp.stack(
            [
                jnp.broadcast_to(depth[c : c + 1, :], (members, latitudes))
                for c in range(first, first + count)
            ]
        )

    def window(ens, edge, first, count, low, high):
        is_left = low == 0
        base = 2 if is_left else 0
        flux[base : base + count] = fluxes(ens[1, 0:count], depths(first, count))
        at = 0 if is_left else count
        near, far = (1, 0) if is_left else (at, at + 1)
        flux[near] = edge[2].astype(F32)
        flux[far] = edge[3].astype(F32)
        wide = high - low + 1
        skip = 0 if is_left else 1
        columns = slice(skip, skip + wide)
        new = heights(
            ens[0, columns],
            ens[2, columns],
            depths(first + skip, wide),
            flux[base + skip + 1 : base + skip + 1 + wide],
            flux[base + skip - 1 : base + skip - 1 + wide],
            shift,
        )
        start = 1 if is_left else 0
        height[start : start + wide] = new
        place = 0 if is_left else wide
        middle = near
        east_west = flux[middle + 1] - flux[middle - 1]
        raised = edge[0].astype(F32) - half_step * (east_west + rows_apart(edge[1], shift))
        height[place] = raised.astype(BF16)
        count = high - low
        here = height[1 : 1 + count]
        ahead, behind = height[2 : 2 + count], height[0:count]
        at = slice(low - first, high - first)
        return (here,) + velocities(ens[1, at], ens[2, at], here, ahead, behind, turning, shift)

    staged[:, 100:104, :] = jnp.zeros((8, 4, 256), F32)
    for v, field in enumerate(window(west_block, left, 0, 10, 0, 8)):
        put_group(staged, field, eye, 20 * v)
    ends = window(east_block, right, 54, 6, 56, 60)
    put_group(staged, jnp.concatenate([ends[0], ends[1]], axis=0), eye, 60)
    put_group(staged, jnp.concatenate([ends[2], jnp.zeros_like(ends[2])], axis=0), eye, 80)
    me = lax.axis_index("mem")
    for k, d in enumerate(CHIPS):
        straight[k] = staged[me ^ d].astype(BF16)
        cross[k] = staged[me ^ d ^ 1].astype(BF16)


def spread_block(source, held, wide, start, lane):
    spans = [slice(h * LANES, (h + 1) * LANES) for h in range(2)]
    count = source.shape[1]
    here = pl.ds(start, 16)
    blocks = exchange_lanes([[source[q, here, span] for span in spans] for q in range(8)], lane)
    for q in range(8):
        to = pl.ds(pl.multiple_of(q * count + start, 8), 16)
        for h in range(2):
            wide[h, to, :] = blocks[q][h].astype(F32)
            held[q, here, spans[h]] = blocks[q][h]


def spread_kernel(cells, got, held, seen, outer, wide):
    lane = lax.broadcasted_iota(jnp.int32, (16, LANES), 1)

    def step(index, carry):
        spread_block(got, held, wide, pl.multiple_of(index * 16, 16), lane)
        return carry

    lax.fori_loop(0, 22, step, 0, unroll=4)
    spread_block(got, held, wide, INNER - 16, lane)
    slots = seen.shape[2]
    unroll = 16

    def pick(index, counts):
        counts = list(counts)
        for t in range(2):
            for k in range(unroll):
                slot = index * unroll + k
                row = cells[t, slot]
                is_inner = row < 8 * INNER
                near = jnp.where(is_inner, row, 0)
                for h in range(2):
                    seen[t, h, pl.ds(slot, 1), :] = wide[h, pl.ds(near, 1), :]
                outer[t, counts[t]] = slot
                counts[t] = counts[t] + jnp.where(is_inner, 0, 1)
        return tuple(counts)

    counts = lax.fori_loop(0, slots // unroll, pick, (jnp.int32(0), jnp.int32(0)))
    for t in range(2):
        for k in range(8):
            outer[t, counts[t] + k] = slots
        outer[t, slots + LANES - 1] = counts[t]


def observe_kernel(cells, outer, weight, target, first, straight, cross, *refs):
    edges, (held, gram, short, joined, wide, seen) = refs[:3], refs[3:]
    lane = lax.broadcasted_iota(jnp.int32, (16, LANES), 1)
    me = lax.axis_index("mem")
    for k, d in enumerate(CHIPS):
        joined[me ^ d, 0:OUTER, :] = straight[0] if k == 0 else edges[k - 1][0]
        joined[me ^ d ^ 1, 0:OUTER, :] = cross[0] if k == 0 else edges[k - 1][1]
    joined[:, OUTER:BLOCK, :] = jnp.zeros((8, BLOCK - OUTER, 256), BF16)
    for index in range(BLOCK // 16):
        spread_block(joined, held, wide, index * 16, lane)
    slots = first.shape[2]
    seen[:, :, 0:slots, :] = first[...]
    for t in range(2):

        def pick(index, carry):
            for k in range(8):
                slot = outer[t, index * 8 + k]
                row = cells[t, slot] - 8 * INNER
                for h in range(2):
                    seen[t, h, pl.ds(slot, 1), :] = wide[h, pl.ds(row, 1), :]
            return carry

        lax.fori_loop(0, (outer[t, slots + LANES - 1] + 7) // 8, pick, 0)
    eye = identity(256, BF16)
    for t in range(2):
        values = jnp.concatenate([seen[t, h, 0:slots] for h in range(2)], axis=1).astype(BF16)
        turned = dot_nt(eye, values)
        mean = jnp.sum(turned, axis=0, keepdims=True) * (1.0 / 256)
        root = weight[t : t + 1, :]
        spread = (root * (turned - mean)).astype(BF16)
        misfit = (root * (target[t : t + 1, :] - mean)).astype(BF16)
        block = dot_nt(spread, spread)
        pull = dot_nt(jnp.broadcast_to(misfit, (16, slots)), spread)
        whole = packed(block, pull[0:8])
        gram[t] = whole
        short[t] = whole.astype(BF16)


def combine_kernel(gram, below, above, column, to_west, to_east):
    total = gram[...] + neighbour_weight * (below[...].astype(F32) + above[...].astype(F32))
    column[...] = total
    to_west[...] = total[0].astype(BF16)
    to_east[...] = total[1].astype(BF16)


def prepare_kernel(inner, outer, *refs):
    average = jnp.full((256, LANES), 1.0 / 256, BF16)
    for q in range(8):
        pieces = (inner[q, 0:FIRST], jnp.concatenate([inner[q, FIRST:INNER], outer[q, 0:OUTER]], axis=0))
        for k, piece in enumerate(pieces):
            mean = dot_nn(piece, average)
            refs[2 * k + 1][q] = mean
            mean = jnp.concatenate([mean, mean], axis=1)
            refs[2 * k][q] = (piece.astype(F32) - mean).astype(BF16)


def send_back(results, outs):
    lane = lax.broadcasted_iota(jnp.int32, (16, LANES), 1)
    spans = [slice(h * LANES, (h + 1) * LANES) for h in range(2)]

    def step(index, carry):
        here = pl.ds(pl.multiple_of(index * 16, 16), 16)
        blocks = [[results[q, here, span] for span in spans] for q in range(8)]
        blocks = exchange_lanes(blocks, lane)
        for q in range(8):
            for h in range(2):
                outs[ORDER.index(q)][here, spans[h]] = blocks[q][h]
        return carry

    lax.fori_loop(0, results.shape[1] // 16, step, 0, unroll=4)


def apply_maps(anomaly, mean, maps, results, q, edge, order):
    count = results.shape[1]
    low, high = edge // 16 * 16, (edge + 15) // 16 * 16
    first = dot_nt(anomaly[q, 0:high], maps[order[0]])
    centre = jnp.concatenate([mean[q], mean[q]], axis=1)
    results[q, 0:low] = (centre[0:low] + first[0:low]).astype(BF16)
    if low == count:
        return
    second = dot_nt(anomaly[q, low:count], maps[order[1]])
    if low < high:
        near = lax.broadcasted_iota(jnp.int32, (16, 256), 0) < edge - low
        both = jnp.where(near, first[low:high], second[0:16])
        results[q, low:high] = (centre[low:high] + both).astype(BF16)
    results[q, high:count] = (centre[high:count] + second[high - low : count - low]).astype(BF16)


def second_kernel(maps, anomaly, mean, *refs):
    outs, results = refs[:8], refs[8]
    both = [maps[0], maps[1]]
    for q in range(8):
        apply_maps(anomaly, mean, both, results, q, 180, (0, 1))
    send_back(results, outs)


def analyse_kernel(column, west, east, anomaly, mean, *refs):
    outs, (kept, results, ordered) = refs[:8], refs[8:]
    size = 256
    eye = identity(size, F32)
    beside = (west[...].astype(F32) + column[1], column[0] + east[...].astype(F32))
    norms, pulls, roots, inverses = [], [], [], []
    for t in range(2):
        block, pull = unpacked(column[t] + neighbour_weight * beside[t])
        system = (size - 1) * eye + block
        square = jnp.sum(jnp.sum(system * system, axis=0, keepdims=True), axis=1, keepdims=True)
        norms.append(jnp.sqrt(square))
        pulls.append(pull)
        roots.append(system / norms[t])
    for sweep in range(SWEEPS):
        rights = [right_3(split(root)) for root in roots]
        if sweep == 0:
            inverses = [1.5 * eye - 0.5 * root for root in roots]
            lefts = [left_3(split(inverse)) for inverse in inverses]
            roots = [dot_nn(left, right) for left, right in zip(lefts, rights)]
            continue
        parts = [split(inverse) for inverse in inverses]
        products = [dot_nn(left_3(part), right) for part, right in zip(parts, rights)]
        middles = [left_3(split(1.5 * eye - 0.5 * product)) for product in products]
        if sweep < SWEEPS - 1:
            roots = [dot_nn(middle, right) for middle, right in zip(middles, rights)]
        inverses = [dot_nn(middle, right_3(part)) for middle, part in zip(middles, parts)]
    maps = []
    for t in range(2):
        right = right_3(split(inverses[t]))
        half_pull = dot_nn(left_3(split(pulls[t])), right)
        shift = dot_nn(left_3(split(half_pull)), right) / norms[t]
        scale = math.sqrt(size - 1) / jnp.sqrt(norms[t])
        ordered[t] = (inverses[t] * scale + shift[0:1]).astype(BF16).reshape(8, 32, size)
    me = lax.axis_index("mem")
    for t in range(2):
        maps.append(jnp.concatenate([ordered[t, me ^ d] for d in range(8)], axis=0))
        kept[t] = maps[t]
    for q in range(8):
        apply_maps(anomaly, mean, maps, results, q, 180 if q < 6 else FIRST, (1, 0))
    send_back(results, outs)


def spread_strips(got, wide):
    me = lax.axis_index("mem")
    for k, d in enumerate(ORDER):
        wide[me ^ d] = got[k][...].astype(F32)


def take_group(wide, turned, eye, g, shape):
    rows = shape[2] // 8
    for s in range(8):
        turned[g, rows * s : rows * (s + 1), :] = wide[s, rows * g : rows * (g + 1), :]
    return dot_nt(eye, turned[g].astype(BF16)).astype(BF16).reshape(shape)


def first_return_kernel(*refs):
    got, (out, wide, turned, planes, sent) = refs[:8], refs[8:]
    shape = (8,) + planes.shape[2:]
    spread_strips(got, wide)
    eye = identity(256, BF16)
    copies = []
    for v in range(3):
        for index in range(3, 7):
            at = 8 * (index - 3)
            planes[v, at : at + 8] = take_group(wide, turned, eye, group_of(v, index), shape)
        copies.append(pltpu.make_async_copy(planes.at[v], out.at[v, pl.ds(24, 32)], sent.at[v]))
        copies[v].start()
    for copy in copies:
        copy.wait()


def second_return_kernel(*refs):
    got, (_, out, wide, turned, planes, sent) = refs[:8], refs[8:]
    shape = (8,) + planes.shape[2:]
    spread_strips(got, wide)
    eye = identity(256, BF16)
    mixed = take_group(wide, turned, eye, 9, shape)
    planes[0, 24:28] = mixed[0:4]
    planes[1, 24:28] = mixed[4:8]
    planes[2, 24:28] = take_group(wide, turned, eye, 10, shape)[0:4]
    copies = []
    for v in range(3):
        for index in range(3):
            at = 8 * index
            block = take_group(wide, turned, eye, group_of(v, index) - 12, shape)
            planes[v, at : at + 8] = block
        for k, (at, to, count) in enumerate(((0, 0, 24), (24, 56, 4))):
            source, target = planes.at[v, pl.ds(at, count)], out.at[v, pl.ds(to, count)]
            copies.append(pltpu.make_async_copy(source, target, sent.at[2 * v + k]))
            copies[-1].start()
    for copy in copies:
        copy.wait()


def around(value, axis, step):
    count = lax.axis_size(axis)
    return lax.ppermute(value, axis, [(i, (i + step) % count) for i in range(count)])


def along(value, axis, step):
    count = lax.axis_size(axis)
    pairs = [(i, i + step) for i in range(count) if 0 <= i + step < count]
    return lax.ppermute(value, axis, pairs)


def across(value, difference):
    return lax.ppermute(value, "mem", [(i, i ^ difference) for i in range(8)])


def partners(values):
    return [across(value, d) if d else value for d, value in zip(ORDER, values)]


def swap(value):
    return lax.all_to_all(value, "mem", split_axis=0, concat_axis=0, tiled=True)


def cell_rows(cell):
    variable = cell // 600
    tile = jnp.arange(2, dtype=jnp.int32)[:, None]
    column = tile * 30 + cell // 20 % 30
    index = column // 8
    place = column % 8
    group = jnp.where(index > 3, variable * 3 + index - 4, 11 + variable * 2 + index)
    group = jnp.where(index == 3, 9 + variable, group)
    group = jnp.where(index == 0, 18 + variable, group)
    is_last = column >= 56
    group = jnp.where(is_last, 21 + variable // 2, group)
    place = jnp.where(is_last, column - 56 + 4 * (variable % 2), place)
    first = place * INNER + group * 20
    last = 8 * INNER + place * BLOCK + (group - 18) * 20
    return jnp.where(group < 18, first, last) + cell % 20


def on_device_fast(
    ensemble, layer_depth, observed_cell, observed_value, error_variance, observed_count
):
    members, _, columns, latitudes = ensemble.shape
    slots = observed_cell.shape[2]
    planes = jnp.transpose(ensemble, (1, 2, 0, 3))
    edge = jax.ShapeDtypeStruct((4, members, latitudes), BF16)
    far = pl.BlockSpec(memory_space=pltpu.HBM)
    sent, to_west, to_east = pl.pallas_call(
        inner_kernel,
        out_shape=(jax.ShapeDtypeStruct((8, INNER, 256), BF16), edge, edge),
        in_specs=[far, far],
        scratch_shapes=[
            pltpu.VMEM(planes.shape, BF16),
            pltpu.VMEM((columns, latitudes), F32),
            pltpu.VMEM((columns, members, latitudes), F32),
            pltpu.VMEM((columns, members, latitudes), BF16),
            pltpu.VMEM((8, INNER, 256), F32),
            pltpu.SemaphoreType.DMA((6,)),
        ],
        compiler_params=params(60),
        name="inner",
    )(planes, layer_depth)
    got = swap(sent)
    left = around(to_east, "band", 1)
    right = around(to_west, "band", -1)
    flat = pl.BlockSpec((4, members, latitudes), lambda i: (0, 0, 0))
    straight, cross = pl.pallas_call(
        outer_kernel,
        grid=(1,),
        out_shape=(jax.ShapeDtypeStruct((4, OUTER, 256), BF16),) * 2,
        in_specs=[
            pl.BlockSpec((3, 10, members, latitudes), lambda i: (0, 0, 0, 0)),
            pl.BlockSpec((3, 6, members, latitudes), lambda i: (0, 9, 0, 0)),
            flat,
            flat,
            pl.BlockSpec((columns, latitudes), lambda i: (0, 0)),
        ],
        out_specs=(pl.BlockSpec((4, OUTER, 256), lambda i: (0, 0, 0)),) * 2,
        scratch_shapes=[
            pltpu.VMEM((12, members, latitudes), F32),
            pltpu.VMEM((10, members, latitudes), BF16),
            pltpu.VMEM((8, OUTER, 256), F32),
        ],
        compiler_params=params(24),
        name="outer",
    )(planes, planes, left, right, layer_depth)
    cross = across(cross, 1)
    got_edges = [across(jnp.stack([straight[k], cross[k]]), CHIPS[k]) for k in (3, 1, 2)]
    got_edges = got_edges[1:] + got_edges[:1]

    rows = cell_rows(observed_cell[0])
    live = jnp.arange(slots, dtype=jnp.int32)[None, :] < observed_count[0][:, None]
    root = jnp.sqrt(jnp.where(live, 1.0 / error_variance[0], 0.0))
    vmem = pl.BlockSpec(memory_space=pltpu.VMEM)
    rows = jnp.pad(rows, ((0, 0), (0, LANES)), constant_values=8 * INNER)
    smem = pl.BlockSpec(memory_space=pltpu.SMEM)
    held_inner, seen, outer = pl.pallas_call(
        spread_kernel,
        out_shape=(
            jax.ShapeDtypeStruct((8, INNER, 256), BF16),
            jax.ShapeDtypeStruct((2, 2, slots, LANES), F32),
            jax.ShapeDtypeStruct((2, slots + LANES), jnp.int32),
        ),
        in_specs=[smem, vmem],
        out_specs=(vmem, vmem, smem),
        scratch_shapes=[pltpu.VMEM((2, 8 * INNER, LANES), F32)],
        compiler_params=params(12),
        cost_estimate=cost(1, 8 * MIB),
        name="spread",
    )(rows, got)
    held_outer, gram, short = pl.pallas_call(
        observe_kernel,
        out_shape=(
            jax.ShapeDtypeStruct((8, BLOCK, 256), BF16),
            jax.ShapeDtypeStruct((2, PACKED, 256), F32),
            jax.ShapeDtypeStruct((2, PACKED, 256), BF16),
        ),
        in_specs=[smem, smem] + [vmem] * 8,
        scratch_shapes=[
            pltpu.VMEM((8, BLOCK, 256), BF16),
            pltpu.VMEM((2, 8 * BLOCK, LANES), F32),
            pltpu.VMEM((2, 2, slots + 8, LANES), F32),
        ],
        compiler_params=params(16),
        name="observe",
    )(rows, outer, root, observed_value[0], seen, straight, cross, *got_edges)
    anomaly_1, mean_1, anomaly_2, mean_2 = pl.pallas_call(
        prepare_kernel,
        out_shape=(
            jax.ShapeDtypeStruct((8, FIRST, 256), BF16),
            jax.ShapeDtypeStruct((8, FIRST, LANES), F32),
            jax.ShapeDtypeStruct((8, SECOND, 256), BF16),
            jax.ShapeDtypeStruct((8, SECOND, LANES), F32),
        ),
        compiler_params=params(12),
        cost_estimate=cost(1, 6 * MIB),
        name="prepare",
    )(held_inner, held_outer)

    below = along(short, "mem", 1)
    above = along(short, "mem", -1)
    one_tile = jax.ShapeDtypeStruct((PACKED, 256), BF16)
    column, to_west, to_east = pl.pallas_call(
        combine_kernel,
        out_shape=(jax.ShapeDtypeStruct(gram.shape, F32), one_tile, one_tile),
        compiler_params=params(8),
        name="combine",
    )(gram, below, above)
    west = around(to_east, "band", 1)
    east = around(to_west, "band", -1)
    *back, maps = pl.pallas_call(
        analyse_kernel,
        out_shape=(jax.ShapeDtypeStruct((FIRST, 256), BF16),) * 8
        + (jax.ShapeDtypeStruct((2, 256, 256), BF16),),
        scratch_shapes=[pltpu.VMEM((8, FIRST, 256), BF16), pltpu.VMEM((2, 8, 32, 256), BF16)],
        compiler_params=params(20),
        name="analyse",
    )(column, west, east, anomaly_1, mean_1)
    first = partners(back)
    maps, first[4] = lax.optimization_barrier((maps, first[4]))
    back = pl.pallas_call(
        second_kernel,
        out_shape=(jax.ShapeDtypeStruct((SECOND, 256), BF16),) * 8,
        scratch_shapes=[pltpu.VMEM((8, SECOND, 256), BF16)],
        compiler_params=params(16),
        cost_estimate=cost(1, 6 * MIB),
        name="second",
    )(maps, anomaly_2, mean_2)
    second = partners(back)
    result = jax.ShapeDtypeStruct(planes.shape, BF16)
    half = pl.pallas_call(
        first_return_kernel,
        out_shape=result,
        out_specs=far,
        scratch_shapes=[
            pltpu.VMEM((8, FIRST, 256), F32),
            pltpu.VMEM((12, latitudes, 256), F32),
            pltpu.VMEM((3, 32, members, latitudes), BF16),
            pltpu.SemaphoreType.DMA((3,)),
        ],
        compiler_params=params(20),
        cost_estimate=cost(1, 4 * MIB),
        name="first_return",
    )(*first)
    planes = pl.pallas_call(
        second_return_kernel,
        out_shape=result,
        in_specs=[vmem] * 8 + [far],
        out_specs=far,
        scratch_shapes=[
            pltpu.VMEM((8, SECOND, 256), F32),
            pltpu.VMEM((11, latitudes, 256), F32),
            pltpu.VMEM((3, 28, members, latitudes), BF16),
            pltpu.SemaphoreType.DMA((6,)),
        ],
        input_output_aliases={8: 0},
        compiler_params=params(20),
        name="second_return",
    )(*second, half)
    return jnp.transpose(planes, (2, 0, 1, 3))


def choose(ensemble, layer_depth, observed_cell, *rest):
    shape = (lax.axis_size("mem"), ensemble.shape, observed_cell.shape[1])
    fits = shape == (8, (32, 3, 60, 160), 2) and observed_cell.shape[2] % 16 == 0
    chosen = on_device_fast if fits else on_device
    return chosen(ensemble, layer_depth, observed_cell, *rest)


def solution(mesh):
    in_specs = (
        P("mem", None, "band", None),
        P("band", None),
        P("mem", "band", None),
        P("mem", "band", None),
        P("mem", "band", None),
        P("mem", "band"),
    )
    out_specs = P("mem", None, "band", None)
    return jax.shard_map(
        choose, mesh=mesh, in_specs=in_specs, out_specs=out_specs, check_vma=False
    )
```

```python
import math

import jax
import jax.numpy as jnp
import numpy as np
from jax import lax
from jax.experimental import pallas as pl
from jax.experimental.pallas import tpu as pltpu
from jax.sharding import PartitionSpec as P

SWEEPS = 5


half_step = 0.1
coriolis_scale = 0.3
neighbour_weight = 0.75


def padded_2(cells, sides, width):
    for axis, dim in sides:
        count = lax.axis_size(axis)
        head = lax.slice_in_dim(cells, 0, width, axis=dim)
        tail = lax.slice_in_dim(cells, cells.shape[dim] - width, cells.shape[dim], axis=dim)
        cells = jnp.concatenate(
            [
                lax.ppermute(tail, axis, [(i, (i + 1) % count) for i in range(count)]),
                cells,
                lax.ppermute(head, axis, [((i + 1) % count, i) for i in range(count)]),
            ],
            axis=dim,
        )
    return cells


def north_south(source):
    widths = [(0, 0)] * (source.ndim - 1) + [(1, 1)]
    padded = jnp.pad(source, widths)
    return padded[..., 2:] - padded[..., :-2]


def coriolis(latitudes):
    position = jnp.arange(latitudes, dtype=jnp.float32)
    return coriolis_scale * jnp.sin(math.pi * ((position + 0.5) / latitudes - 0.5))


def newton_schulz(starting):
    identity = jnp.eye(starting.shape[-1], dtype=starting.dtype)
    root_part = starting
    inverse_root = jnp.broadcast_to(identity, starting.shape)
    for sweep_index in range(SWEEPS):
        product = jnp.einsum(
            "tij,tjk->tik", inverse_root, root_part, precision=lax.Precision.HIGHEST
        )
        middle = 1.5 * identity - 0.5 * product
        root_part = jnp.einsum("tij,tjk->tik", root_part, middle, precision=lax.Precision.HIGHEST)
        inverse_root = jnp.einsum(
            "tij,tjk->tik", middle, inverse_root, precision=lax.Precision.HIGHEST
        )
    return inverse_root


def on_device(ensemble, layer_depth, observed_cell, observed_value, error_variance, observed_count):
    block_members = ensemble.shape[0]
    columns = ensemble.shape[2]
    latitudes = ensemble.shape[3]
    strips = lax.axis_size("mem")
    members = block_members * strips
    strip_rows = latitudes // strips
    tile_count = observed_cell.shape[1]
    tile_columns = columns // tile_count
    slot_count = observed_cell.shape[2]
    tile_cells = 3 * tile_columns * strip_rows
    height = ensemble[:, 0].astype(jnp.float32)
    eastward = ensemble[:, 1].astype(jnp.float32)
    northward = ensemble[:, 2].astype(jnp.float32)
    turning = coriolis(latitudes)
    flux_east = (layer_depth * eastward).astype(jnp.bfloat16)
    flux_north = (layer_depth * northward).astype(jnp.bfloat16)
    east_margin = padded_2(flux_east, (("band", 1),), 1)
    east_west = east_margin[:, 2:].astype(jnp.float32) - east_margin[:, :-2].astype(jnp.float32)
    north_local = lax.optimization_barrier(flux_north).astype(jnp.float32)
    raised = height - half_step * (east_west + north_south(north_local))
    surface_elevation_cast = raised.astype(jnp.bfloat16)
    height_margin = padded_2(surface_elevation_cast, (("band", 1),), 1)
    margin_wide = height_margin.astype(jnp.float32)
    height_inner = margin_wide[:, 1:-1]
    revised_zonal_velocity = (
        eastward + turning * northward - half_step * (margin_wide[:, 2:] - margin_wide[:, :-2])
    )
    revised_meridional_velocity = (
        northward - turning * eastward - half_step * north_south(height_inner)
    )
    advance_dynamics = jnp.stack(
        [
            surface_elevation_cast,
            revised_zonal_velocity.astype(jnp.bfloat16),
            revised_meridional_velocity.astype(jnp.bfloat16),
        ],
        axis=1,
    )
    reordered = advance_dynamics.reshape(
        block_members, 3, tile_count, tile_columns, strips, strip_rows
    )
    reordered = jnp.transpose(reordered, (4, 2, 0, 1, 3, 5)).reshape(
        strips, tile_count, block_members, tile_cells
    )
    tile_block = lax.all_to_all(reordered, "mem", split_axis=0, concat_axis=2, tiled=True)[0]
    cells_here = observed_cell[0]
    values = jnp.take_along_axis(tile_block, cells_here[:, None, :], axis=2)
    observed_mean = jnp.sum(values, axis=1, dtype=jnp.float32) / members
    slot_index = jnp.arange(slot_count, dtype=jnp.int32)[None, :]
    live_slots = slot_index < observed_count[0][:, None]
    root_weight = jnp.sqrt(jnp.where(live_slots, 1.0 / error_variance[0], 0.0))
    spread = (
        root_weight[:, None, :] * (values.astype(jnp.float32) - observed_mean[:, None, :])
    ).astype(jnp.bfloat16)
    misfit = (root_weight * (observed_value[0] - observed_mean)).astype(jnp.bfloat16)
    spread_margin, misfit_margin = (
        padded_2(spread[None], (("mem", 0), ("band", 1)), 1),
        padded_2(misfit[None], (("mem", 0), ("band", 1)), 1),
    )
    gram_margin = jnp.einsum(
        "atko,atlo->atkl", spread_margin, spread_margin, preferred_element_type=jnp.float32
    )
    pull_margin = jnp.einsum(
        "atko,ato->atk", spread_margin, misfit_margin, preferred_element_type=jnp.float32
    )
    strip_here = lax.axis_index("mem")
    lower_valid = (strip_here > 0).astype(jnp.float32)
    upper_valid = (strip_here < strips - 1).astype(jnp.float32)
    strip_mask = (lower_valid, 1.0, upper_valid)
    total_gram = jnp.zeros((tile_count, members, members), jnp.float32)
    total_pull = jnp.zeros((tile_count, members), jnp.float32)
    for offset_lat in range(3):
        for offset_lon in range(3):
            factor = (
                neighbour_weight ** (abs(offset_lat - 1) + abs(offset_lon - 1))
                * strip_mask[offset_lat]
            )
            total_gram = (
                total_gram + factor * gram_margin[offset_lat, offset_lon : offset_lon + tile_count]
            )
            total_pull = (
                total_pull + factor * pull_margin[offset_lat, offset_lon : offset_lon + tile_count]
            )
    system = (members - 1) * jnp.eye(members, dtype=jnp.float32)[None] + total_gram
    frobenius = jnp.sqrt(jnp.sum(system * system, axis=(1, 2)))
    inverse_root = newton_schulz(system / frobenius[:, None, None])
    spread_map = inverse_root * (math.sqrt(members - 1) / jnp.sqrt(frobenius))[:, None, None]
    half_pull = jnp.einsum("tij,tj->ti", inverse_root, total_pull, precision=lax.Precision.HIGHEST)
    shift_weights = (
        jnp.einsum("tij,tj->ti", inverse_root, half_pull, precision=lax.Precision.HIGHEST)
        / frobenius[:, None]
    )
    weights = (spread_map + shift_weights[:, :, None]).astype(jnp.bfloat16)
    state_mean = jnp.sum(tile_block, axis=1, dtype=jnp.float32) / members
    anomaly = (tile_block.astype(jnp.float32) - state_mean[:, None, :]).astype(jnp.bfloat16)
    update = jnp.einsum("tjk,tjc->tkc", weights, anomaly, preferred_element_type=jnp.float32)
    analysed = (state_mean[:, None, :] + update).astype(jnp.bfloat16)
    returned = lax.all_to_all(analysed[None], "mem", split_axis=2, concat_axis=0, tiled=True)
    returned = returned.reshape(strips, tile_count, block_members, 3, tile_columns, strip_rows)
    return jnp.transpose(returned, (2, 3, 1, 4, 0, 5)).reshape(block_members, 3, columns, latitudes)


LANES = 128
GROUPS = 23
INNER = 360
OUTER = 104
BLOCK = 112
FIRST = 240
SECOND = 224
F32 = jnp.float32
BF16 = jnp.bfloat16
PACKED = 144
CHIPS = (0, 2, 4, 6)
ORDER = (6, 2, 4, 7, 1, 3, 5, 0)
MIB = 1024 * 1024


def params(size):
    return pltpu.CompilerParams(vmem_limit_bytes=size * MIB)


def cost(flops, moved):
    return pl.CostEstimate(flops=flops, bytes_accessed=moved, transcendentals=0)


def identity(size, dtype):
    row = lax.broadcasted_iota(jnp.int32, (size, size), 0)
    column = lax.broadcasted_iota(jnp.int32, (size, size), 1)
    return (row == column).astype(F32).astype(dtype)


def dot_nt(left, right):
    return lax.dot_general(left, right, (((1,), (1,)), ((), ())), preferred_element_type=F32)


def dot_nn(left, right):
    return lax.dot_general(left, right, (((1,), (0,)), ((), ())), preferred_element_type=F32)


def split(value):
    high = value.astype(BF16)
    return high, (value - high.astype(F32)).astype(BF16)


def left_3(parts):
    return jnp.concatenate([parts[0], parts[0], parts[1]], axis=1)


def right_3(parts):
    return jnp.concatenate([parts[0], parts[1], parts[0]], axis=0)


def triangle(size):
    row = lax.broadcasted_iota(jnp.int32, (size, size), 0)
    column = lax.broadcasted_iota(jnp.int32, (size, size), 1)
    return row, column


def packed(block, pull):
    row, column = triangle(128)
    last = block[128:256, 128:256]
    corner = jnp.where(row >= column, block[0:128, 0:128], last)
    middle = jnp.sum(jnp.where(row == column, last, 0.0), axis=0, keepdims=True)
    middle = jnp.concatenate([jnp.zeros_like(middle), middle], axis=1)
    top = jnp.concatenate([block[128:256, 0:128], corner], axis=1)
    return jnp.concatenate([top, pull, jnp.broadcast_to(middle, (8, 256))], axis=0)


def unpacked(value):
    row, column = triangle(128)
    low, corner = value[0:128, 0:128], value[0:128, 128:256]
    other = jnp.transpose(corner)
    first = jnp.where(row >= column, corner, other)
    last = jnp.where(row < column, corner, other)
    last = jnp.where(row == column, value[136:137, 128:256], last)
    top = jnp.concatenate([first, jnp.transpose(low)], axis=1)
    return jnp.concatenate([top, jnp.concatenate([low, last], axis=1)], axis=0), value[128:136]


def exchange_lanes(blocks, lane):
    blocks = [list(pair) for pair in blocks]
    for q in range(4):
        low, high = blocks[q], blocks[q + 4]
        blocks[q], blocks[q + 4] = [low[0], high[0]], [low[1], high[1]]
    for bit in range(2):
        step = 32 << bit
        odd = (lane & step) != 0
        for q in range(8):
            if q & (1 << bit):
                continue
            for h in range(2):
                low, high = blocks[q][h], blocks[q | (1 << bit)][h]
                blocks[q][h] = jnp.where(odd, pltpu.roll(high, step, 1), low)
                blocks[q | (1 << bit)][h] = jnp.where(odd, high, pltpu.roll(low, LANES - step, 1))
    return blocks


def group_of(variable, index):
    if index == 0:
        return 18 + variable
    if index == 3:
        return 9 + variable
    return variable * 3 + index - 4 if index > 3 else 12 + variable * 2 + index - 1


def difference(latitudes):
    source = lax.broadcasted_iota(jnp.int32, (latitudes, latitudes), 0)
    target = lax.broadcasted_iota(jnp.int32, (latitudes, latitudes), 1)
    shift = (source == target + 1).astype(F32) - (source == target - 1).astype(F32)
    return shift.astype(BF16)


def rows_apart(value, shift):
    flat = value.reshape(-1, value.shape[-1])
    return dot_nn(flat, shift).reshape(value.shape)


def fluxes(east, deep):
    return (deep * east.astype(F32)).astype(BF16).astype(F32)


def heights(field, north, deep, ahead, behind, shift):
    flux_north = (deep * north.astype(F32)).astype(BF16)
    raised = field.astype(F32) - half_step * ((ahead - behind) + rows_apart(flux_north, shift))
    return raised.astype(BF16)


def velocities(east, north, here, ahead, behind, turning, shift):
    east, north = east.astype(F32), north.astype(F32)
    apart = ahead.astype(F32) - behind.astype(F32)
    new_east = east + turning * north - half_step * apart
    new_north = north - turning * east - half_step * rows_apart(here, shift)
    return new_east.astype(BF16), new_north.astype(BF16)


def put_group(staged, block, eye, first):
    latitudes = eye.shape[0]
    rows = latitudes // 8
    turned = dot_nt(eye, block.reshape(256, latitudes))
    for s in range(8):
        staged[s, first : first + rows, :] = turned[rows * s : rows * (s + 1)]


def turning_row(latitudes):
    position = lax.broadcasted_iota(jnp.int32, (8, latitudes), 1).astype(F32)
    turning = coriolis_scale * jnp.sin(math.pi * ((position + 0.5) / latitudes - 0.5))
    return turning[0:1, :][None]


def inner_kernel(
    ens, depth, out, to_first, to_second, here, deep, flux, height, staged, edges, arrived
):
    columns, members, latitudes = here.shape[1:]
    batch = columns // 5
    pieces = [pltpu.make_async_copy(depth, deep, arrived.at[5])]
    for k in range(5):
        span = pl.ds(k * batch, batch)
        piece = pltpu.make_async_copy(ens.at[:, span], here.at[:, span], arrived.at[k])
        pieces.append(piece)
    for piece in pieces:
        piece.start()
    shift = difference(latitudes)
    turning = turning_row(latitudes)
    eye = identity(latitudes, BF16)
    pieces[0].wait()

    def depths(first, count):
        rows = [deep[c : c + 1, :] for c in range(first, first + count)]
        return jnp.stack([jnp.broadcast_to(row, (members, latitudes)) for row in rows])

    def edge(side, near, far):
        edges[side, 0] = here[0, near]
        edges[side, 1] = (deep[near : near + 1, :] * here[2, near].astype(F32)).astype(BF16)
        edges[side, 2] = flux[near].astype(BF16)
        edges[side, 3] = flux[far].astype(BF16)

    done = 1
    for k in range(5):
        pieces[k + 1].wait()
        first = k * batch
        flux[first : first + batch] = fluxes(here[1, first : first + batch], depths(first, batch))
        if k == 0:
            edge(0, 0, 1)
        if k == 4:
            edge(1, columns - 1, columns - 2)
        low, high = max(first - 1, 1), first + batch - 1
        at = slice(low, high)
        ahead, behind = flux[low + 1 : high + 1], flux[low - 1 : high - 1]
        height[at] = heights(
            here[0, at], here[2, at], depths(low, high - low), ahead, behind, shift
        )
        while done < 7 and 8 * done + 9 <= high:
            first = 8 * done
            at = slice(first, first + 8)
            ahead, behind = height[first + 1 : first + 9], height[first - 1 : first + 7]
            new = velocities(here[1, at], here[2, at], height[at], ahead, behind, turning, shift)
            for v, field in enumerate((height[at],) + new):
                put_group(staged, field, eye, 20 * group_of(v, done))
            done += 1
    odd = lax.axis_index("band") & 1
    to_first[...] = edges[1 - odd]
    to_second[...] = edges[odd]
    out[...] = staged[...].astype(BF16)


def outer_kernel(
    west_block, east_block, first_swap, second_swap, depth, *refs
):
    straight, cross, flux, height, staged, swapped = refs
    odd = lax.axis_index("band") & 1
    for side, block in enumerate((first_swap, second_swap)):
        swapped[side] = block[...]
    left, right = swapped.at[1 - odd], swapped.at[odd]
    members, latitudes = west_block.shape[2:]
    shift = difference(latitudes)
    turning = turning_row(latitudes)
    eye = identity(latitudes, BF16)

    def depths(first, count):
        return jnp.stack(
            [
                jnp.broadcast_to(depth[c : c + 1, :], (members, latitudes))
                for c in range(first, first + count)
            ]
        )

    def window(ens, edge, first, count, low, high):
        is_left = low == 0
        base = 2 if is_left else 0
        flux[base : base + count] = fluxes(ens[1, 0:count], depths(first, count))
        at = 0 if is_left else count
        near, far = (1, 0) if is_left else (at, at + 1)
        flux[near] = edge[2].astype(F32)
        flux[far] = edge[3].astype(F32)
        wide = high - low + 1
        skip = 0 if is_left else 1
        columns = slice(skip, skip + wide)
        new = heights(
            ens[0, columns],
            ens[2, columns],
            depths(first + skip, wide),
            flux[base + skip + 1 : base + skip + 1 + wide],
            flux[base + skip - 1 : base + skip - 1 + wide],
            shift,
        )
        start = 1 if is_left else 0
        height[start : start + wide] = new
        place = 0 if is_left else wide
        middle = near
        east_west = flux[middle + 1] - flux[middle - 1]
        raised = edge[0].astype(F32) - half_step * (east_west + rows_apart(edge[1], shift))
        height[place] = raised.astype(BF16)
        count = high - low
        here = height[1 : 1 + count]
        ahead, behind = height[2 : 2 + count], height[0:count]
        at = slice(low - first, high - first)
        return (here,) + velocities(ens[1, at], ens[2, at], here, ahead, behind, turning, shift)

    staged[:, 100:104, :] = jnp.zeros((8, 4, 256), F32)
    for v, field in enumerate(window(west_block, left, 0, 10, 0, 8)):
        put_group(staged, field, eye, 20 * v)
    ends = window(east_block, right, 54, 6, 56, 60)
    put_group(staged, jnp.concatenate([ends[0], ends[1]], axis=0), eye, 60)
    put_group(staged, jnp.concatenate([ends[2], jnp.zeros_like(ends[2])], axis=0), eye, 80)
    me = lax.axis_index("mem")
    for k, d in enumerate(CHIPS):
        straight[k] = staged[me ^ d].astype(BF16)
        cross[k] = staged[me ^ d ^ 1].astype(BF16)


def spread_block(source, held, wide, start, lane):
    spans = [slice(h * LANES, (h + 1) * LANES) for h in range(2)]
    count = source.shape[1]
    here = pl.ds(start, 16)
    blocks = exchange_lanes([[source[q, here, span] for span in spans] for q in range(8)], lane)
    for q in range(8):
        to = pl.ds(pl.multiple_of(q * count + start, 8), 16)
        for h in range(2):
            wide[h, to, :] = blocks[q][h].astype(F32)
            held[q, here, spans[h]] = blocks[q][h]


def spread_kernel(cells, got, held, seen, wide):
    lane = lax.broadcasted_iota(jnp.int32, (16, LANES), 1)

    def step(index, carry):
        spread_block(got, held, wide, pl.multiple_of(index * 16, 16), lane)
        return carry

    lax.fori_loop(0, 22, step, 0, unroll=4)
    spread_block(got, held, wide, INNER - 16, lane)
    slots = seen.shape[2]
    unroll = 16

    def pick(index, carry):
        for t in range(2):
            for k in range(unroll):
                slot = index * unroll + k
                row = cells[t, slot]
                for h in range(2):
                    seen[t, h, pl.ds(slot, 1), :] = wide[h, pl.ds(row, 1), :]
        return carry

    lax.fori_loop(0, slots // unroll, pick, 0)


def observe_kernel(cells, outer, weight, target, first, straight, cross, *refs):
    edges, (held, gram, to_first, to_second, joined, wide, seen) = refs[:3], refs[3:]
    wholes = []
    lane = lax.broadcasted_iota(jnp.int32, (16, LANES), 1)
    me = lax.axis_index("mem")
    for k, d in enumerate(CHIPS):
        joined[me ^ d, 0:OUTER, :] = straight[0] if k == 0 else edges[k - 1][0]
        joined[me ^ d ^ 1, 0:OUTER, :] = cross[0] if k == 0 else edges[k - 1][1]
    joined[:, OUTER:BLOCK, :] = jnp.zeros((8, BLOCK - OUTER, 256), BF16)
    for index in range(BLOCK // 16):
        spread_block(joined, held, wide, index * 16, lane)
    slots = first.shape[2]
    seen[:, :, 0:slots, :] = first[...]
    for t in range(2):

        def pick(index, carry):
            for k in range(8):
                slot = outer[t, index * 8 + k]
                row = cells[t, slot] - 8 * INNER
                for h in range(2):
                    seen[t, h, pl.ds(slot, 1), :] = wide[h, pl.ds(row, 1), :]
            return carry

        lax.fori_loop(0, (outer[t, slots + LANES - 1] + 7) // 8, pick, 0)
    eye = identity(256, BF16)
    for t in range(2):
        values = jnp.concatenate([seen[t, h, 0:slots] for h in range(2)], axis=1).astype(BF16)
        turned = dot_nt(eye, values)
        mean = jnp.sum(turned, axis=0, keepdims=True) * (1.0 / 256)
        root = weight[t : t + 1, :]
        spread = (root * (turned - mean)).astype(BF16)
        misfit = (root * (target[t : t + 1, :] - mean)).astype(BF16)
        block = dot_nt(spread, spread)
        pull = dot_nt(jnp.broadcast_to(misfit, (16, slots)), spread)
        whole = packed(block, pull[0:8])
        gram[t] = whole
        wholes.append(whole.astype(BF16))
    odd = (lax.axis_index("band") & 1) == 1
    to_first[...] = jnp.where(odd, wholes[0], wholes[1])
    to_second[...] = jnp.where(odd, wholes[1], wholes[0])


def combine_kernel(gram, first_swap, second_swap, line, short):
    odd = (lax.axis_index("band") & 1) == 1
    first, second = first_swap[...].astype(F32), second_swap[...].astype(F32)
    west, east = jnp.where(odd, first, second), jnp.where(odd, second, first)
    for t, beside in enumerate((west + gram[1], gram[0] + east)):
        total = gram[t] + neighbour_weight * beside
        line[t] = total
        short[t] = total.astype(BF16)


def prepare_kernel(inner, outer, *refs):
    average = jnp.full((256, LANES), 1.0 / 256, BF16)
    for q in range(8):
        pieces = (inner[q, 0:FIRST], jnp.concatenate([inner[q, FIRST:INNER], outer[q, 0:OUTER]], axis=0))
        for k, piece in enumerate(pieces):
            mean = dot_nn(piece, average)
            refs[2 * k + 1][q] = mean
            mean = jnp.concatenate([mean, mean], axis=1)
            refs[2 * k][q] = (piece.astype(F32) - mean).astype(BF16)


def send_back(results, outs):
    lane = lax.broadcasted_iota(jnp.int32, (16, LANES), 1)
    spans = [slice(h * LANES, (h + 1) * LANES) for h in range(2)]

    def step(index, carry):
        here = pl.ds(pl.multiple_of(index * 16, 16), 16)
        blocks = [[results[q, here, span] for span in spans] for q in range(8)]
        blocks = exchange_lanes(blocks, lane)
        for q in range(8):
            for h in range(2):
                outs[ORDER.index(q)][here, spans[h]] = blocks[q][h]
        return carry

    lax.fori_loop(0, results.shape[1] // 16, step, 0, unroll=4)


def apply_maps(anomaly, mean, maps, results, q, edge, order):
    count = results.shape[1]
    low, high = edge // 16 * 16, (edge + 15) // 16 * 16
    first = dot_nt(anomaly[q, 0:high], maps[order[0]])
    centre = jnp.concatenate([mean[q], mean[q]], axis=1)
    results[q, 0:low] = (centre[0:low] + first[0:low]).astype(BF16)
    if low == count:
        return
    second = dot_nt(anomaly[q, low:count], maps[order[1]])
    if low < high:
        near = lax.broadcasted_iota(jnp.int32, (16, 256), 0) < edge - low
        both = jnp.where(near, first[low:high], second[0:16])
        results[q, low:high] = (centre[low:high] + both).astype(BF16)
    results[q, high:count] = (centre[high:count] + second[high - low : count - low]).astype(BF16)


def second_kernel(maps, anomaly, mean, *refs):
    outs, results = refs[:8], refs[8]
    both = [maps[0], maps[1]]
    for q in range(8):
        apply_maps(anomaly, mean, both, results, q, 180, (0, 1))
    send_back(results, outs)


def analyse_kernel(line, below, above, anomaly, mean, *refs):
    outs, (kept, results, ordered) = refs[:8], refs[8:]
    size = 256
    eye = identity(size, F32)
    norms, pulls, roots, inverses = [], [], [], []
    for t in range(2):
        beside = below[t].astype(F32) + above[t].astype(F32)
        block, pull = unpacked(line[t] + neighbour_weight * beside)
        system = (size - 1) * eye + block
        square = jnp.sum(jnp.sum(system * system, axis=0, keepdims=True), axis=1, keepdims=True)
        norms.append(jnp.sqrt(square))
        pulls.append(pull)
        roots.append(system / norms[t])
    for sweep in range(SWEEPS):
        rights = [right_3(split(root)) for root in roots]
        if sweep == 0:
            inverses = [1.5 * eye - 0.5 * root for root in roots]
            lefts = [left_3(split(inverse)) for inverse in inverses]
            roots = [dot_nn(left, right) for left, right in zip(lefts, rights)]
            continue
        parts = [split(inverse) for inverse in inverses]
        products = [dot_nn(left_3(part), right) for part, right in zip(parts, rights)]
        middles = [left_3(split(1.5 * eye - 0.5 * product)) for product in products]
        if sweep < SWEEPS - 1:
            roots = [dot_nn(middle, right) for middle, right in zip(middles, rights)]
        inverses = [dot_nn(middle, right_3(part)) for middle, part in zip(middles, parts)]
    maps = []
    for t in range(2):
        right = right_3(split(inverses[t]))
        half_pull = dot_nn(left_3(split(pulls[t])), right)
        shift = dot_nn(left_3(split(half_pull)), right) / norms[t]
        scale = math.sqrt(size - 1) / jnp.sqrt(norms[t])
        ordered[t] = (inverses[t] * scale + shift[0:1]).astype(BF16).reshape(8, 32, size)
    me = lax.axis_index("mem")
    for t in range(2):
        maps.append(jnp.concatenate([ordered[t, me ^ d] for d in range(8)], axis=0))
        kept[t] = maps[t]
    for q in range(8):
        apply_maps(anomaly, mean, maps, results, q, 180 if q < 6 else FIRST, (1, 0))
    send_back(results, outs)


def spread_strips(got, wide):
    me = lax.axis_index("mem")
    for k, d in enumerate(ORDER):
        wide[me ^ d] = got[k][...].astype(F32)


def take_group(wide, turned, eye, g, shape):
    rows = shape[2] // 8
    for s in range(8):
        turned[g, rows * s : rows * (s + 1), :] = wide[s, rows * g : rows * (g + 1), :]
    return dot_nt(eye, turned[g].astype(BF16)).astype(BF16).reshape(shape)


def first_return_kernel(*refs):
    got, (out, wide, turned, planes, sent) = refs[:8], refs[8:]
    shape = (8,) + planes.shape[2:]
    spread_strips(got, wide)
    eye = identity(256, BF16)
    copies = []
    for v in range(3):
        for index in range(3, 7):
            at = 8 * (index - 3)
            planes[v, at : at + 8] = take_group(wide, turned, eye, group_of(v, index), shape)
        copies.append(pltpu.make_async_copy(planes.at[v], out.at[v, pl.ds(24, 32)], sent.at[v]))
        copies[v].start()
    for copy in copies:
        copy.wait()


def second_return_kernel(*refs):
    got, (_, out, wide, turned, planes, sent) = refs[:8], refs[8:]
    shape = (8,) + planes.shape[2:]
    spread_strips(got, wide)
    eye = identity(256, BF16)
    mixed = take_group(wide, turned, eye, 9, shape)
    planes[0, 24:28] = mixed[0:4]
    planes[1, 24:28] = mixed[4:8]
    planes[2, 24:28] = take_group(wide, turned, eye, 10, shape)[0:4]
    copies = []
    for v in range(3):
        for index in range(3):
            at = 8 * index
            block = take_group(wide, turned, eye, group_of(v, index) - 12, shape)
            planes[v, at : at + 8] = block
        for k, (at, to, count) in enumerate(((0, 0, 24), (24, 56, 4))):
            source, target = planes.at[v, pl.ds(at, count)], out.at[v, pl.ds(to, count)]
            copies.append(pltpu.make_async_copy(source, target, sent.at[2 * v + k]))
            copies[-1].start()
    for copy in copies:
        copy.wait()


def swapped_pairs(values, axis, pairs):
    moved = []
    for value, some in zip(values, pairs):
        both = some + [(j, i) for i, j in some]
        moved.append(lax.ppermute(value, axis, both))
    return moved


def band_swaps(first, second):
    count = lax.axis_size("band")
    starts = range(0, count, 2)
    pairs = [[(i, i + 1) for i in starts], [(i + 1, (i + 2) % count) for i in starts]]
    return swapped_pairs((first, second), "band", pairs)


def mem_swaps(value):
    count = lax.axis_size("mem")
    pairs = [[(i, i + 1) for i in range(k, count - 1, 2)] for k in range(2)]
    return swapped_pairs((value, value), "mem", pairs)


def across(value, difference):
    return lax.ppermute(value, "mem", [(i, i ^ difference) for i in range(8)])


def partners(values):
    return [across(value, d) if d else value for d, value in zip(ORDER, values)]


def swap(value):
    return lax.all_to_all(value, "mem", split_axis=0, concat_axis=0, tiled=True)


def cell_rows(cell):
    variable = cell // 600
    tile = jnp.arange(2, dtype=jnp.int32)[:, None]
    column = tile * 30 + cell // 20 % 30
    index = column // 8
    place = column % 8
    group = jnp.where(index > 3, variable * 3 + index - 4, 11 + variable * 2 + index)
    group = jnp.where(index == 3, 9 + variable, group)
    group = jnp.where(index == 0, 18 + variable, group)
    is_last = column >= 56
    group = jnp.where(is_last, 21 + variable // 2, group)
    place = jnp.where(is_last, column - 56 + 4 * (variable % 2), place)
    first = place * INNER + group * 20
    last = 8 * INNER + place * BLOCK + (group - 18) * 20
    return jnp.where(group < 18, first, last) + cell % 20


def on_device_fast(
    ensemble, layer_depth, observed_cell, observed_value, error_variance, observed_count
):
    members, _, columns, latitudes = ensemble.shape
    slots = observed_cell.shape[2]
    planes = jnp.transpose(ensemble, (1, 2, 0, 3))
    edge = jax.ShapeDtypeStruct((4, members, latitudes), BF16)
    far = pl.BlockSpec(memory_space=pltpu.HBM)
    sent, to_first, to_second = pl.pallas_call(
        inner_kernel,
        out_shape=(jax.ShapeDtypeStruct((8, INNER, 256), BF16), edge, edge),
        in_specs=[far, far],
        scratch_shapes=[
            pltpu.VMEM(planes.shape, BF16),
            pltpu.VMEM((columns, latitudes), F32),
            pltpu.VMEM((columns, members, latitudes), F32),
            pltpu.VMEM((columns, members, latitudes), BF16),
            pltpu.VMEM((8, INNER, 256), F32),
            pltpu.VMEM((2, 4, members, latitudes), BF16),
            pltpu.SemaphoreType.DMA((6,)),
        ],
        compiler_params=params(60),
        name="inner",
    )(planes, layer_depth)
    got = swap(sent)
    swaps = band_swaps(to_first, to_second)
    flat = pl.BlockSpec((4, members, latitudes), lambda i: (0, 0, 0))
    straight, cross = pl.pallas_call(
        outer_kernel,
        grid=(1,),
        out_shape=(jax.ShapeDtypeStruct((4, OUTER, 256), BF16),) * 2,
        in_specs=[
            pl.BlockSpec((3, 10, members, latitudes), lambda i: (0, 0, 0, 0)),
            pl.BlockSpec((3, 6, members, latitudes), lambda i: (0, 9, 0, 0)),
            flat,
            flat,
            pl.BlockSpec((columns, latitudes), lambda i: (0, 0)),
        ],
        out_specs=(pl.BlockSpec((4, OUTER, 256), lambda i: (0, 0, 0)),) * 2,
        scratch_shapes=[
            pltpu.VMEM((12, members, latitudes), F32),
            pltpu.VMEM((10, members, latitudes), BF16),
            pltpu.VMEM((8, OUTER, 256), F32),
            pltpu.VMEM((2, 4, members, latitudes), BF16),
        ],
        compiler_params=params(24),
        name="outer",
    )(planes, planes, *swaps, layer_depth)
    cross = across(cross, 1)
    got_edges = [across(jnp.stack([straight[k], cross[k]]), CHIPS[k]) for k in (3, 1, 2)]
    got_edges = got_edges[1:] + got_edges[:1]

    rows = cell_rows(observed_cell[0])
    live = jnp.arange(slots, dtype=jnp.int32)[None, :] < observed_count[0][:, None]
    root = jnp.sqrt(jnp.where(live, 1.0 / error_variance[0], 0.0))
    vmem = pl.BlockSpec(memory_space=pltpu.VMEM)
    slot = jnp.arange(slots, dtype=jnp.int32)
    place = jnp.arange(slots + LANES, dtype=jnp.int32)
    is_outer = rows >= 8 * INNER
    near = jnp.where(is_outer, 0, rows)
    rank = jnp.sum(is_outer[:, None, :] & (slot[None, :] < slot[:, None])[None], axis=2)
    count = jnp.sum(is_outer, axis=1, keepdims=True)
    found = is_outer[:, None, :] & (rank[:, None, :] == place[None, :, None])
    outer = jnp.sum(jnp.where(found, slot, 0), axis=2)
    outer = jnp.where(place[None] < count, outer, slots)
    outer = jnp.where(place[None] == slots + LANES - 1, count, outer).astype(jnp.int32)
    rows = jnp.pad(rows, ((0, 0), (0, LANES)), constant_values=8 * INNER)
    smem = pl.BlockSpec(memory_space=pltpu.SMEM)
    held_inner, seen = pl.pallas_call(
        spread_kernel,
        out_shape=(
            jax.ShapeDtypeStruct((8, INNER, 256), BF16),
            jax.ShapeDtypeStruct((2, 2, slots, LANES), F32),
        ),
        in_specs=[smem, vmem],
        scratch_shapes=[pltpu.VMEM((2, 8 * INNER, LANES), F32)],
        compiler_params=params(12),
        cost_estimate=cost(1, 8 * MIB),
        name="spread",
    )(near, got)
    one_tile = jax.ShapeDtypeStruct((PACKED, 256), BF16)
    held_outer, gram, to_first, to_second = pl.pallas_call(
        observe_kernel,
        out_shape=(
            jax.ShapeDtypeStruct((8, BLOCK, 256), BF16),
            jax.ShapeDtypeStruct((2, PACKED, 256), F32),
            one_tile,
            one_tile,
        ),
        in_specs=[smem, smem] + [vmem] * 8,
        scratch_shapes=[
            pltpu.VMEM((8, BLOCK, 256), BF16),
            pltpu.VMEM((2, 8 * BLOCK, LANES), F32),
            pltpu.VMEM((2, 2, slots + 8, LANES), F32),
        ],
        compiler_params=params(16),
        name="observe",
    )(rows, outer, root, observed_value[0], seen, straight, cross, *got_edges)
    anomaly_1, mean_1, anomaly_2, mean_2 = pl.pallas_call(
        prepare_kernel,
        out_shape=(
            jax.ShapeDtypeStruct((8, FIRST, 256), BF16),
            jax.ShapeDtypeStruct((8, FIRST, LANES), F32),
            jax.ShapeDtypeStruct((8, SECOND, 256), BF16),
            jax.ShapeDtypeStruct((8, SECOND, LANES), F32),
        ),
        compiler_params=params(12),
        cost_estimate=cost(1, 6 * MIB),
        name="prepare",
    )(held_inner, held_outer)

    line, short = pl.pallas_call(
        combine_kernel,
        out_shape=(
            jax.ShapeDtypeStruct(gram.shape, F32),
            jax.ShapeDtypeStruct(gram.shape, BF16),
        ),
        compiler_params=params(8),
        name="combine",
    )(gram, *band_swaps(to_first, to_second))
    below, above = mem_swaps(short)
    *back, maps = pl.pallas_call(
        analyse_kernel,
        out_shape=(jax.ShapeDtypeStruct((FIRST, 256), BF16),) * 8
        + (jax.ShapeDtypeStruct((2, 256, 256), BF16),),
        scratch_shapes=[pltpu.VMEM((8, FIRST, 256), BF16), pltpu.VMEM((2, 8, 32, 256), BF16)],
        compiler_params=params(20),
        name="analyse",
    )(line, below, above, anomaly_1, mean_1)
    first = partners(back)
    maps, first[4] = lax.optimization_barrier((maps, first[4]))
    back = pl.pallas_call(
        second_kernel,
        out_shape=(jax.ShapeDtypeStruct((SECOND, 256), BF16),) * 8,
        scratch_shapes=[pltpu.VMEM((8, SECOND, 256), BF16)],
        compiler_params=params(16),
        cost_estimate=cost(1, 6 * MIB),
        name="second",
    )(maps, anomaly_2, mean_2)
    second = partners(back)
    result = jax.ShapeDtypeStruct(planes.shape, BF16)
    half = pl.pallas_call(
        first_return_kernel,
        out_shape=result,
        out_specs=far,
        scratch_shapes=[
            pltpu.VMEM((8, FIRST, 256), F32),
            pltpu.VMEM((12, latitudes, 256), F32),
            pltpu.VMEM((3, 32, members, latitudes), BF16),
            pltpu.SemaphoreType.DMA((3,)),
        ],
        compiler_params=params(20),
        cost_estimate=cost(1, 4 * MIB),
        name="first_return",
    )(*first)
    planes = pl.pallas_call(
        second_return_kernel,
        out_shape=result,
        in_specs=[vmem] * 8 + [far],
        out_specs=far,
        scratch_shapes=[
            pltpu.VMEM((8, SECOND, 256), F32),
            pltpu.VMEM((11, latitudes, 256), F32),
            pltpu.VMEM((3, 28, members, latitudes), BF16),
            pltpu.SemaphoreType.DMA((6,)),
        ],
        input_output_aliases={8: 0},
        compiler_params=params(20),
        name="second_return",
    )(*second, half)
    return jnp.transpose(planes, (2, 0, 1, 3))


def choose(ensemble, layer_depth, observed_cell, *rest):
    mesh_shape = (lax.axis_size("mem"), lax.axis_size("band"))
    shape = (mesh_shape, ensemble.shape, observed_cell.shape[1])
    fits = shape == ((8, 4), (32, 3, 60, 160), 2) and observed_cell.shape[2] % 16 == 0
    chosen = on_device_fast if fits else on_device
    return chosen(ensemble, layer_depth, observed_cell, *rest)


def solution(mesh):
    in_specs = (
        P("mem", None, "band", None),
        P("band", None),
        P("mem", "band", None),
        P("mem", "band", None),
        P("mem", "band", None),
        P("mem", "band"),
    )
    out_specs = P("mem", None, "band", None)
    return jax.shard_map(
        choose, mesh=mesh, in_specs=in_specs, out_specs=out_specs, check_vma=False
    )
```

```python
import math

import jax
import jax.numpy as jnp
import numpy as np
from jax import lax
from jax.experimental import pallas as pl
from jax.experimental.pallas import tpu as pltpu
from jax.sharding import PartitionSpec as P

SWEEPS = 5


half_step = 0.1
coriolis_scale = 0.3
neighbour_weight = 0.75


def padded_2(cells, sides, width):
    for axis, dim in sides:
        count = lax.axis_size(axis)
        head = lax.slice_in_dim(cells, 0, width, axis=dim)
        tail = lax.slice_in_dim(cells, cells.shape[dim] - width, cells.shape[dim], axis=dim)
        cells = jnp.concatenate(
            [
                lax.ppermute(tail, axis, [(i, (i + 1) % count) for i in range(count)]),
                cells,
                lax.ppermute(head, axis, [((i + 1) % count, i) for i in range(count)]),
            ],
            axis=dim,
        )
    return cells


def north_south(source):
    widths = [(0, 0)] * (source.ndim - 1) + [(1, 1)]
    padded = jnp.pad(source, widths)
    return padded[..., 2:] - padded[..., :-2]


def coriolis(latitudes):
    position = jnp.arange(latitudes, dtype=jnp.float32)
    return coriolis_scale * jnp.sin(math.pi * ((position + 0.5) / latitudes - 0.5))


def newton_schulz(starting):
    identity = jnp.eye(starting.shape[-1], dtype=starting.dtype)
    root_part = starting
    inverse_root = jnp.broadcast_to(identity, starting.shape)
    for sweep_index in range(SWEEPS):
        product = jnp.einsum(
            "tij,tjk->tik", inverse_root, root_part, precision=lax.Precision.HIGHEST
        )
        middle = 1.5 * identity - 0.5 * product
        root_part = jnp.einsum("tij,tjk->tik", root_part, middle, precision=lax.Precision.HIGHEST)
        inverse_root = jnp.einsum(
            "tij,tjk->tik", middle, inverse_root, precision=lax.Precision.HIGHEST
        )
    return inverse_root


def on_device(ensemble, layer_depth, observed_cell, observed_value, error_variance, observed_count):
    block_members = ensemble.shape[0]
    columns = ensemble.shape[2]
    latitudes = ensemble.shape[3]
    strips = lax.axis_size("mem")
    members = block_members * strips
    strip_rows = latitudes // strips
    tile_count = observed_cell.shape[1]
    tile_columns = columns // tile_count
    slot_count = observed_cell.shape[2]
    tile_cells = 3 * tile_columns * strip_rows
    height = ensemble[:, 0].astype(jnp.float32)
    eastward = ensemble[:, 1].astype(jnp.float32)
    northward = ensemble[:, 2].astype(jnp.float32)
    turning = coriolis(latitudes)
    flux_east = (layer_depth * eastward).astype(jnp.bfloat16)
    flux_north = (layer_depth * northward).astype(jnp.bfloat16)
    east_margin = padded_2(flux_east, (("band", 1),), 1)
    east_west = east_margin[:, 2:].astype(jnp.float32) - east_margin[:, :-2].astype(jnp.float32)
    north_local = lax.optimization_barrier(flux_north).astype(jnp.float32)
    raised = height - half_step * (east_west + north_south(north_local))
    surface_elevation_cast = raised.astype(jnp.bfloat16)
    height_margin = padded_2(surface_elevation_cast, (("band", 1),), 1)
    margin_wide = height_margin.astype(jnp.float32)
    height_inner = margin_wide[:, 1:-1]
    revised_zonal_velocity = (
        eastward + turning * northward - half_step * (margin_wide[:, 2:] - margin_wide[:, :-2])
    )
    revised_meridional_velocity = (
        northward - turning * eastward - half_step * north_south(height_inner)
    )
    advance_dynamics = jnp.stack(
        [
            surface_elevation_cast,
            revised_zonal_velocity.astype(jnp.bfloat16),
            revised_meridional_velocity.astype(jnp.bfloat16),
        ],
        axis=1,
    )
    reordered = advance_dynamics.reshape(
        block_members, 3, tile_count, tile_columns, strips, strip_rows
    )
    reordered = jnp.transpose(reordered, (4, 2, 0, 1, 3, 5)).reshape(
        strips, tile_count, block_members, tile_cells
    )
    tile_block = lax.all_to_all(reordered, "mem", split_axis=0, concat_axis=2, tiled=True)[0]
    cells_here = observed_cell[0]
    values = jnp.take_along_axis(tile_block, cells_here[:, None, :], axis=2)
    observed_mean = jnp.sum(values, axis=1, dtype=jnp.float32) / members
    slot_index = jnp.arange(slot_count, dtype=jnp.int32)[None, :]
    live_slots = slot_index < observed_count[0][:, None]
    root_weight = jnp.sqrt(jnp.where(live_slots, 1.0 / error_variance[0], 0.0))
    spread = (
        root_weight[:, None, :] * (values.astype(jnp.float32) - observed_mean[:, None, :])
    ).astype(jnp.bfloat16)
    misfit = (root_weight * (observed_value[0] - observed_mean)).astype(jnp.bfloat16)
    spread_margin, misfit_margin = (
        padded_2(spread[None], (("mem", 0), ("band", 1)), 1),
        padded_2(misfit[None], (("mem", 0), ("band", 1)), 1),
    )
    gram_margin = jnp.einsum(
        "atko,atlo->atkl", spread_margin, spread_margin, preferred_element_type=jnp.float32
    )
    pull_margin = jnp.einsum(
        "atko,ato->atk", spread_margin, misfit_margin, preferred_element_type=jnp.float32
    )
    strip_here = lax.axis_index("mem")
    lower_valid = (strip_here > 0).astype(jnp.float32)
    upper_valid = (strip_here < strips - 1).astype(jnp.float32)
    strip_mask = (lower_valid, 1.0, upper_valid)
    total_gram = jnp.zeros((tile_count, members, members), jnp.float32)
    total_pull = jnp.zeros((tile_count, members), jnp.float32)
    for offset_lat in range(3):
        for offset_lon in range(3):
            factor = (
                neighbour_weight ** (abs(offset_lat - 1) + abs(offset_lon - 1))
                * strip_mask[offset_lat]
            )
            total_gram = (
                total_gram + factor * gram_margin[offset_lat, offset_lon : offset_lon + tile_count]
            )
            total_pull = (
                total_pull + factor * pull_margin[offset_lat, offset_lon : offset_lon + tile_count]
            )
    system = (members - 1) * jnp.eye(members, dtype=jnp.float32)[None] + total_gram
    frobenius = jnp.sqrt(jnp.sum(system * system, axis=(1, 2)))
    inverse_root = newton_schulz(system / frobenius[:, None, None])
    spread_map = inverse_root * (math.sqrt(members - 1) / jnp.sqrt(frobenius))[:, None, None]
    half_pull = jnp.einsum("tij,tj->ti", inverse_root, total_pull, precision=lax.Precision.HIGHEST)
    shift_weights = (
        jnp.einsum("tij,tj->ti", inverse_root, half_pull, precision=lax.Precision.HIGHEST)
        / frobenius[:, None]
    )
    weights = (spread_map + shift_weights[:, :, None]).astype(jnp.bfloat16)
    state_mean = jnp.sum(tile_block, axis=1, dtype=jnp.float32) / members
    anomaly = (tile_block.astype(jnp.float32) - state_mean[:, None, :]).astype(jnp.bfloat16)
    update = jnp.einsum("tjk,tjc->tkc", weights, anomaly, preferred_element_type=jnp.float32)
    analysed = (state_mean[:, None, :] + update).astype(jnp.bfloat16)
    returned = lax.all_to_all(analysed[None], "mem", split_axis=2, concat_axis=0, tiled=True)
    returned = returned.reshape(strips, tile_count, block_members, 3, tile_columns, strip_rows)
    return jnp.transpose(returned, (2, 3, 1, 4, 0, 5)).reshape(block_members, 3, columns, latitudes)


LANES = 128
GROUPS = 23
INNER = 360
OUTER = 104
BLOCK = 112
FIRST = 240
SECOND = 224
F32 = jnp.float32
BF16 = jnp.bfloat16
PACKED = 144
CHIPS = (0, 2, 4, 6)
ORDER = (6, 7, 2, 4, 3, 5, 1, 0)
MIB = 1024 * 1024


def params(size):
    return pltpu.CompilerParams(vmem_limit_bytes=size * MIB)


def cost(flops, moved):
    return pl.CostEstimate(flops=flops, bytes_accessed=moved, transcendentals=0)


def identity(size, dtype):
    row = lax.broadcasted_iota(jnp.int32, (size, size), 0)
    column = lax.broadcasted_iota(jnp.int32, (size, size), 1)
    return (row == column).astype(F32).astype(dtype)


def dot_nt(left, right):
    return lax.dot_general(left, right, (((1,), (1,)), ((), ())), preferred_element_type=F32)


def dot_nn(left, right):
    return lax.dot_general(left, right, (((1,), (0,)), ((), ())), preferred_element_type=F32)


def split(value):
    high = value.astype(BF16)
    return high, (value - high.astype(F32)).astype(BF16)


def left_3(parts):
    return jnp.concatenate([parts[0], parts[0], parts[1]], axis=1)


def right_3(parts):
    return jnp.concatenate([parts[0], parts[1], parts[0]], axis=0)


def triangle(size):
    row = lax.broadcasted_iota(jnp.int32, (size, size), 0)
    column = lax.broadcasted_iota(jnp.int32, (size, size), 1)
    return row, column


def packed(block, pull):
    row, column = triangle(128)
    last = block[128:256, 128:256]
    corner = jnp.where(row >= column, block[0:128, 0:128], last)
    middle = jnp.sum(jnp.where(row == column, last, 0.0), axis=0, keepdims=True)
    middle = jnp.concatenate([jnp.zeros_like(middle), middle], axis=1)
    top = jnp.concatenate([block[128:256, 0:128], corner], axis=1)
    return jnp.concatenate([top, pull, jnp.broadcast_to(middle, (8, 256))], axis=0)


def unpacked(value):
    row, column = triangle(128)
    low, corner = value[0:128, 0:128], value[0:128, 128:256]
    other = jnp.transpose(corner)
    first = jnp.where(row >= column, corner, other)
    last = jnp.where(row < column, corner, other)
    last = jnp.where(row == column, value[136:137, 128:256], last)
    top = jnp.concatenate([first, jnp.transpose(low)], axis=1)
    return jnp.concatenate([top, jnp.concatenate([low, last], axis=1)], axis=0), value[128:136]


def exchange_lanes(blocks, lane):
    blocks = [list(pair) for pair in blocks]
    for q in range(4):
        low, high = blocks[q], blocks[q + 4]
        blocks[q], blocks[q + 4] = [low[0], high[0]], [low[1], high[1]]
    for bit in range(2):
        step = 32 << bit
        odd = (lane & step) != 0
        for q in range(8):
            if q & (1 << bit):
                continue
            for h in range(2):
                low, high = blocks[q][h], blocks[q | (1 << bit)][h]
                blocks[q][h] = jnp.where(odd, pltpu.roll(high, step, 1), low)
                blocks[q | (1 << bit)][h] = jnp.where(odd, high, pltpu.roll(low, LANES - step, 1))
    return blocks


def group_of(variable, index):
    if index == 0:
        return 18 + variable
    if index == 3:
        return 9 + variable
    return variable * 3 + index - 4 if index > 3 else 12 + variable * 2 + index - 1


def difference(latitudes):
    source = lax.broadcasted_iota(jnp.int32, (latitudes, latitudes), 0)
    target = lax.broadcasted_iota(jnp.int32, (latitudes, latitudes), 1)
    shift = (source == target + 1).astype(F32) - (source == target - 1).astype(F32)
    return shift.astype(BF16)


def rows_apart(value, shift):
    flat = value.reshape(-1, value.shape[-1])
    return dot_nn(flat, shift).reshape(value.shape)


def fluxes(east, deep):
    return (deep * east.astype(F32)).astype(BF16).astype(F32)


def heights(field, north, deep, ahead, behind, shift):
    flux_north = (deep * north.astype(F32)).astype(BF16)
    raised = field.astype(F32) - half_step * ((ahead - behind) + rows_apart(flux_north, shift))
    return raised.astype(BF16)


def velocities(east, north, here, ahead, behind, turning, shift):
    east, north = east.astype(F32), north.astype(F32)
    apart = ahead.astype(F32) - behind.astype(F32)
    new_east = east + turning * north - half_step * apart
    new_north = north - turning * east - half_step * rows_apart(here, shift)
    return new_east.astype(BF16), new_north.astype(BF16)


def put_group(staged, block, eye, first):
    latitudes = eye.shape[0]
    rows = latitudes // 8
    turned = dot_nt(eye, block.reshape(256, latitudes))
    for s in range(8):
        staged[s, first : first + rows, :] = turned[rows * s : rows * (s + 1)]


def turning_row(latitudes):
    position = lax.broadcasted_iota(jnp.int32, (8, latitudes), 1).astype(F32)
    turning = coriolis_scale * jnp.sin(math.pi * ((position + 0.5) / latitudes - 0.5))
    return turning[0:1, :][None]


def inner_kernel(
    ens, depth, out, to_first, to_second, here, deep, flux, height, staged, edges, arrived
):
    columns, members, latitudes = here.shape[1:]
    batch = columns // 5
    pieces = [pltpu.make_async_copy(depth, deep, arrived.at[5])]
    for k in range(5):
        span = pl.ds(k * batch, batch)
        piece = pltpu.make_async_copy(ens.at[:, span], here.at[:, span], arrived.at[k])
        pieces.append(piece)
    for piece in pieces:
        piece.start()
    shift = difference(latitudes)
    turning = turning_row(latitudes)
    eye = identity(latitudes, BF16)
    pieces[0].wait()

    def depths(first, count):
        rows = [deep[c : c + 1, :] for c in range(first, first + count)]
        return jnp.stack([jnp.broadcast_to(row, (members, latitudes)) for row in rows])

    def edge(side, near, far):
        edges[side, 0] = here[0, near]
        edges[side, 1] = (deep[near : near + 1, :] * here[2, near].astype(F32)).astype(BF16)
        edges[side, 2] = flux[near].astype(BF16)
        edges[side, 3] = flux[far].astype(BF16)

    done = 1
    for k in range(5):
        pieces[k + 1].wait()
        first = k * batch
        flux[first : first + batch] = fluxes(here[1, first : first + batch], depths(first, batch))
        if k == 0:
            edge(0, 0, 1)
        if k == 4:
            edge(1, columns - 1, columns - 2)
        low, high = max(first - 1, 1), first + batch - 1
        at = slice(low, high)
        ahead, behind = flux[low + 1 : high + 1], flux[low - 1 : high - 1]
        height[at] = heights(
            here[0, at], here[2, at], depths(low, high - low), ahead, behind, shift
        )
        while done < 7 and 8 * done + 9 <= high:
            first = 8 * done
            at = slice(first, first + 8)
            ahead, behind = height[first + 1 : first + 9], height[first - 1 : first + 7]
            new = velocities(here[1, at], here[2, at], height[at], ahead, behind, turning, shift)
            for v, field in enumerate((height[at],) + new):
                put_group(staged, field, eye, 20 * group_of(v, done))
            done += 1
    odd = lax.axis_index("band") & 1
    to_first[...] = edges[1 - odd]
    to_second[...] = edges[odd]
    out[...] = staged[...].astype(BF16)


def outer_kernel(
    west_block, east_block, first_swap, second_swap, depth, *refs
):
    straight, cross, flux, height, staged, swapped = refs
    odd = lax.axis_index("band") & 1
    for side, block in enumerate((first_swap, second_swap)):
        swapped[side] = block[...]
    left, right = swapped.at[1 - odd], swapped.at[odd]
    members, latitudes = west_block.shape[2:]
    shift = difference(latitudes)
    turning = turning_row(latitudes)
    eye = identity(latitudes, BF16)

    def depths(first, count):
        return jnp.stack(
            [
                jnp.broadcast_to(depth[c : c + 1, :], (members, latitudes))
                for c in range(first, first + count)
            ]
        )

    def window(ens, edge, first, count, low, high):
        is_left = low == 0
        base = 2 if is_left else 0
        flux[base : base + count] = fluxes(ens[1, 0:count], depths(first, count))
        at = 0 if is_left else count
        near, far = (1, 0) if is_left else (at, at + 1)
        flux[near] = edge[2].astype(F32)
        flux[far] = edge[3].astype(F32)
        wide = high - low + 1
        skip = 0 if is_left else 1
        columns = slice(skip, skip + wide)
        new = heights(
            ens[0, columns],
            ens[2, columns],
            depths(first + skip, wide),
            flux[base + skip + 1 : base + skip + 1 + wide],
            flux[base + skip - 1 : base + skip - 1 + wide],
            shift,
        )
        start = 1 if is_left else 0
        height[start : start + wide] = new
        place = 0 if is_left else wide
        middle = near
        east_west = flux[middle + 1] - flux[middle - 1]
        raised = edge[0].astype(F32) - half_step * (east_west + rows_apart(edge[1], shift))
        height[place] = raised.astype(BF16)
        count = high - low
        here = height[1 : 1 + count]
        ahead, behind = height[2 : 2 + count], height[0:count]
        at = slice(low - first, high - first)
        return (here,) + velocities(ens[1, at], ens[2, at], here, ahead, behind, turning, shift)

    staged[:, 100:104, :] = jnp.zeros((8, 4, 256), F32)
    for v, field in enumerate(window(west_block, left, 0, 10, 0, 8)):
        put_group(staged, field, eye, 20 * v)
    ends = window(east_block, right, 54, 6, 56, 60)
    put_group(staged, jnp.concatenate([ends[0], ends[1]], axis=0), eye, 60)
    put_group(staged, jnp.concatenate([ends[2], jnp.zeros_like(ends[2])], axis=0), eye, 80)
    me = lax.axis_index("mem")
    for k, d in enumerate(CHIPS):
        straight[k] = staged[me ^ d].astype(BF16)
        cross[k] = staged[me ^ d ^ 1].astype(BF16)


def spread_block(source, held, wide, start, lane):
    spans = [slice(h * LANES, (h + 1) * LANES) for h in range(2)]
    count = source.shape[1]
    here = pl.ds(start, 16)
    blocks = exchange_lanes([[source[q, here, span] for span in spans] for q in range(8)], lane)
    for q in range(8):
        to = pl.ds(pl.multiple_of(q * count + start, 8), 16)
        for h in range(2):
            wide[h, to, :] = blocks[q][h].astype(F32)
            held[q, here, spans[h]] = blocks[q][h]


def spread_kernel(cells, far, held, seen, wide, got, arrived):
    copies = []
    for k, (first, last) in enumerate(((0, 128), (128, 256), (256, INNER))):
        span = pl.ds(first, last - first)
        copies.append(pltpu.make_async_copy(far.at[:, span], got.at[:, span], arrived.at[k]))
    for copy in copies:
        copy.start()
    lane = lax.broadcasted_iota(jnp.int32, (16, LANES), 1)

    def step(index, carry):
        spread_block(got, held, wide, pl.multiple_of(index * 16, 16), lane)
        return carry

    for copy, (first, last) in zip(copies, ((0, 8), (8, 16), (16, 22))):
        copy.wait()
        lax.fori_loop(first, last, step, 0, unroll=4)
    spread_block(got, held, wide, INNER - 16, lane)
    slots = seen.shape[2]
    unroll = 16

    def pick(index, carry):
        for t in range(2):
            for k in range(unroll):
                slot = index * unroll + k
                row = cells[t, slot]
                for h in range(2):
                    seen[t, h, pl.ds(slot, 1), :] = wide[h, pl.ds(row, 1), :]
        return carry

    lax.fori_loop(0, slots // unroll, pick, 0)


def observe_kernel(cells, outer, weight, target, first, straight, cross, *refs):
    edges, (held, gram, to_first, to_second, joined, wide, seen) = refs[:3], refs[3:]
    wholes = []
    lane = lax.broadcasted_iota(jnp.int32, (16, LANES), 1)
    me = lax.axis_index("mem")
    for k, d in enumerate(CHIPS):
        joined[me ^ d, 0:OUTER, :] = straight[0] if k == 0 else edges[k - 1][0]
        joined[me ^ d ^ 1, 0:OUTER, :] = cross[0] if k == 0 else edges[k - 1][1]
    joined[:, OUTER:BLOCK, :] = jnp.zeros((8, BLOCK - OUTER, 256), BF16)
    for index in range(BLOCK // 16):
        spread_block(joined, held, wide, index * 16, lane)
    slots = first.shape[2]
    seen[:, :, 0:slots, :] = first[...]
    for t in range(2):

        def pick(index, carry):
            for k in range(8):
                slot = outer[t, index * 8 + k]
                row = cells[t, slot] - 8 * INNER
                for h in range(2):
                    seen[t, h, pl.ds(slot, 1), :] = wide[h, pl.ds(row, 1), :]
            return carry

        lax.fori_loop(0, (outer[t, slots + LANES - 1] + 7) // 8, pick, 0)
    eye = identity(256, BF16)
    for t in range(2):
        values = jnp.concatenate([seen[t, h, 0:slots] for h in range(2)], axis=1).astype(BF16)
        turned = dot_nt(eye, values)
        mean = jnp.sum(turned, axis=0, keepdims=True) * (1.0 / 256)
        root = weight[t : t + 1, :]
        spread = (root * (turned - mean)).astype(BF16)
        misfit = (root * (target[t : t + 1, :] - mean)).astype(BF16)
        block = dot_nt(spread, spread)
        pull = dot_nt(jnp.broadcast_to(misfit, (16, slots)), spread)
        whole = packed(block, pull[0:8])
        gram[t] = whole
        wholes.append(whole.astype(BF16))
    odd = (lax.axis_index("band") & 1) == 1
    to_first[...] = jnp.where(odd, wholes[0], wholes[1])
    to_second[...] = jnp.where(odd, wholes[1], wholes[0])


def combine_kernel(gram, first_swap, second_swap, line, short):
    odd = (lax.axis_index("band") & 1) == 1
    first, second = first_swap[...].astype(F32), second_swap[...].astype(F32)
    west, east = jnp.where(odd, first, second), jnp.where(odd, second, first)
    for t, beside in enumerate((west + gram[1], gram[0] + east)):
        total = gram[t] + neighbour_weight * beside
        line[t] = total
        short[t] = total.astype(BF16)


def prepare_kernel(inner, outer, *refs):
    average = jnp.full((256, LANES), 1.0 / 256, BF16)
    for q in range(8):
        pieces = (inner[q, 0:FIRST], jnp.concatenate([inner[q, FIRST:INNER], outer[q, 0:OUTER]], axis=0))
        for k, piece in enumerate(pieces):
            mean = dot_nn(piece, average)
            refs[2 * k + 1][q] = mean
            mean = jnp.concatenate([mean, mean], axis=1)
            refs[2 * k][q] = (piece.astype(F32) - mean).astype(BF16)


def send_back(results, outs):
    lane = lax.broadcasted_iota(jnp.int32, (16, LANES), 1)
    spans = [slice(h * LANES, (h + 1) * LANES) for h in range(2)]

    def step(index, carry):
        here = pl.ds(pl.multiple_of(index * 16, 16), 16)
        blocks = [[results[q, here, span] for span in spans] for q in range(8)]
        blocks = exchange_lanes(blocks, lane)
        for q in range(8):
            for h in range(2):
                outs[ORDER.index(q)][here, spans[h]] = blocks[q][h]
        return carry

    lax.fori_loop(0, results.shape[1] // 16, step, 0, unroll=4)


def apply_maps(anomaly, mean, maps, results, q, edge, order):
    count = results.shape[1]
    low, high = edge // 16 * 16, (edge + 15) // 16 * 16
    first = dot_nt(anomaly[q, 0:high], maps[order[0]])
    centre = jnp.concatenate([mean[q], mean[q]], axis=1)
    results[q, 0:low] = (centre[0:low] + first[0:low]).astype(BF16)
    if low == count:
        return
    second = dot_nt(anomaly[q, low:count], maps[order[1]])
    if low < high:
        near = lax.broadcasted_iota(jnp.int32, (16, 256), 0) < edge - low
        both = jnp.where(near, first[low:high], second[0:16])
        results[q, low:high] = (centre[low:high] + both).astype(BF16)
    results[q, high:count] = (centre[high:count] + second[high - low : count - low]).astype(BF16)


def second_kernel(maps, anomaly, mean, *refs):
    outs, results = refs[:8], refs[8]
    both = [maps[0], maps[1]]
    for q in range(8):
        apply_maps(anomaly, mean, both, results, q, 180, (0, 1))
    send_back(results, outs)


def analyse_kernel(line, below, above, anomaly, mean, *refs):
    outs, (kept, results, ordered) = refs[:8], refs[8:]
    size = 256
    eye = identity(size, F32)
    norms, pulls, roots, inverses = [], [], [], []
    for t in range(2):
        beside = below[t].astype(F32) + above[t].astype(F32)
        block, pull = unpacked(line[t] + neighbour_weight * beside)
        system = (size - 1) * eye + block
        square = jnp.sum(jnp.sum(system * system, axis=0, keepdims=True), axis=1, keepdims=True)
        norms.append(jnp.sqrt(square))
        pulls.append(pull)
        roots.append(system / norms[t])
    for sweep in range(SWEEPS):
        rights = [right_3(split(root)) for root in roots]
        if sweep == 0:
            inverses = [1.5 * eye - 0.5 * root for root in roots]
            lefts = [left_3(split(inverse)) for inverse in inverses]
            roots = [dot_nn(left, right) for left, right in zip(lefts, rights)]
            continue
        parts = [split(inverse) for inverse in inverses]
        products = [dot_nn(left_3(part), right) for part, right in zip(parts, rights)]
        middles = [left_3(split(1.5 * eye - 0.5 * product)) for product in products]
        if sweep < SWEEPS - 1:
            roots = [dot_nn(middle, right) for middle, right in zip(middles, rights)]
        inverses = [dot_nn(middle, right_3(part)) for middle, part in zip(middles, parts)]
    maps = []
    for t in range(2):
        right = right_3(split(inverses[t]))
        half_pull = dot_nn(left_3(split(pulls[t])), right)
        shift = dot_nn(left_3(split(half_pull)), right) / norms[t]
        scale = math.sqrt(size - 1) / jnp.sqrt(norms[t])
        ordered[t] = (inverses[t] * scale + shift[0:1]).astype(BF16).reshape(8, 32, size)
    me = lax.axis_index("mem")
    for t in range(2):
        maps.append(jnp.concatenate([ordered[t, me ^ d] for d in range(8)], axis=0))
        kept[t] = maps[t]
    for q in range(8):
        apply_maps(anomaly, mean, maps, results, q, 180 if q < 6 else FIRST, (1, 0))
    send_back(results, outs)


def spread_strips(got, wide):
    me = lax.axis_index("mem")
    for k, d in enumerate(ORDER):
        wide[me ^ d] = got[k][...].astype(F32)


def take_group(wide, turned, eye, g, shape):
    rows = shape[2] // 8
    for s in range(8):
        turned[g, rows * s : rows * (s + 1), :] = wide[s, rows * g : rows * (g + 1), :]
    return dot_nt(eye, turned[g].astype(BF16)).astype(BF16).reshape(shape)


def first_return_kernel(*refs):
    got, (out, wide, turned, planes, sent) = refs[:8], refs[8:]
    shape = (8,) + planes.shape[2:]
    spread_strips(got, wide)
    eye = identity(256, BF16)
    copies = []
    for v in range(3):
        for index in range(3, 7):
            at = 8 * (index - 3)
            planes[v, at : at + 8] = take_group(wide, turned, eye, group_of(v, index), shape)
        copies.append(pltpu.make_async_copy(planes.at[v], out.at[v, pl.ds(24, 32)], sent.at[v]))
        copies[v].start()
    for copy in copies:
        copy.wait()


def second_return_kernel(*refs):
    got, (_, out, wide, turned, planes, sent) = refs[:8], refs[8:]
    shape = (8,) + planes.shape[2:]
    spread_strips(got, wide)
    eye = identity(256, BF16)
    mixed = take_group(wide, turned, eye, 9, shape)
    planes[0, 24:28] = mixed[0:4]
    planes[1, 24:28] = mixed[4:8]
    planes[2, 24:28] = take_group(wide, turned, eye, 10, shape)[0:4]
    copies = []
    for v in range(3):
        for index in range(3):
            at = 8 * index
            block = take_group(wide, turned, eye, group_of(v, index) - 12, shape)
            planes[v, at : at + 8] = block
        for k, (at, to, count) in enumerate(((0, 0, 24), (24, 56, 4))):
            source, target = planes.at[v, pl.ds(at, count)], out.at[v, pl.ds(to, count)]
            copies.append(pltpu.make_async_copy(source, target, sent.at[2 * v + k]))
            copies[-1].start()
    for copy in copies:
        copy.wait()


def swapped_pairs(values, axis, pairs):
    moved = []
    for value, some in zip(values, pairs):
        both = some + [(j, i) for i, j in some]
        moved.append(lax.ppermute(value, axis, both))
    return moved


def band_swaps(first, second):
    count = lax.axis_size("band")
    starts = range(0, count, 2)
    pairs = [[(i, i + 1) for i in starts], [(i + 1, (i + 2) % count) for i in starts]]
    return swapped_pairs((first, second), "band", pairs)


def mem_swaps(value):
    count = lax.axis_size("mem")
    pairs = [[(i, i + 1) for i in range(k, count - 1, 2)] for k in range(2)]
    return swapped_pairs((value, value), "mem", pairs)


def across(value, difference):
    return lax.ppermute(value, "mem", [(i, i ^ difference) for i in range(8)])


def partners(values):
    return [across(value, d) if d else value for d, value in zip(ORDER, values)]


def swap(value):
    return lax.all_to_all(value, "mem", split_axis=0, concat_axis=0, tiled=True)


def cell_rows(cell):
    variable = cell // 600
    tile = jnp.arange(2, dtype=jnp.int32)[:, None]
    column = tile * 30 + cell // 20 % 30
    index = column // 8
    place = column % 8
    group = jnp.where(index > 3, variable * 3 + index - 4, 11 + variable * 2 + index)
    group = jnp.where(index == 3, 9 + variable, group)
    group = jnp.where(index == 0, 18 + variable, group)
    is_last = column >= 56
    group = jnp.where(is_last, 21 + variable // 2, group)
    place = jnp.where(is_last, column - 56 + 4 * (variable % 2), place)
    first = place * INNER + group * 20
    last = 8 * INNER + place * BLOCK + (group - 18) * 20
    return jnp.where(group < 18, first, last) + cell % 20


def on_device_fast(
    ensemble, layer_depth, observed_cell, observed_value, error_variance, observed_count
):
    members, _, columns, latitudes = ensemble.shape
    slots = observed_cell.shape[2]
    planes = jnp.transpose(ensemble, (1, 2, 0, 3))
    edge = jax.ShapeDtypeStruct((4, members, latitudes), BF16)
    far = pl.BlockSpec(memory_space=pltpu.HBM)
    sent, to_first, to_second = pl.pallas_call(
        inner_kernel,
        out_shape=(jax.ShapeDtypeStruct((8, INNER, 256), BF16), edge, edge),
        in_specs=[far, far],
        scratch_shapes=[
            pltpu.VMEM(planes.shape, BF16),
            pltpu.VMEM((columns, latitudes), F32),
            pltpu.VMEM((columns, members, latitudes), F32),
            pltpu.VMEM((columns, members, latitudes), BF16),
            pltpu.VMEM((8, INNER, 256), F32),
            pltpu.VMEM((2, 4, members, latitudes), BF16),
            pltpu.SemaphoreType.DMA((6,)),
        ],
        compiler_params=params(60),
        name="inner",
    )(planes, layer_depth)
    got = swap(sent)
    swaps = band_swaps(to_first, to_second)
    flat = pl.BlockSpec((4, members, latitudes), lambda i: (0, 0, 0))
    straight, cross = pl.pallas_call(
        outer_kernel,
        grid=(1,),
        out_shape=(jax.ShapeDtypeStruct((4, OUTER, 256), BF16),) * 2,
        in_specs=[
            pl.BlockSpec((3, 10, members, latitudes), lambda i: (0, 0, 0, 0)),
            pl.BlockSpec((3, 6, members, latitudes), lambda i: (0, 9, 0, 0)),
            flat,
            flat,
            pl.BlockSpec((columns, latitudes), lambda i: (0, 0)),
        ],
        out_specs=(pl.BlockSpec((4, OUTER, 256), lambda i: (0, 0, 0)),) * 2,
        scratch_shapes=[
            pltpu.VMEM((12, members, latitudes), F32),
            pltpu.VMEM((10, members, latitudes), BF16),
            pltpu.VMEM((8, OUTER, 256), F32),
            pltpu.VMEM((2, 4, members, latitudes), BF16),
        ],
        compiler_params=params(24),
        name="outer",
    )(planes, planes, *swaps, layer_depth)
    cross = across(cross, 1)
    got_edges = [across(jnp.stack([straight[k], cross[k]]), CHIPS[k]) for k in (3, 1, 2)]
    got_edges = got_edges[1:] + got_edges[:1]

    rows = cell_rows(observed_cell[0])
    live = jnp.arange(slots, dtype=jnp.int32)[None, :] < observed_count[0][:, None]
    root = jnp.sqrt(jnp.where(live, 1.0 / error_variance[0], 0.0))
    vmem = pl.BlockSpec(memory_space=pltpu.VMEM)
    slot = jnp.arange(slots, dtype=jnp.int32)
    place = jnp.arange(slots + LANES, dtype=jnp.int32)
    is_outer = rows >= 8 * INNER
    near = jnp.where(is_outer, 0, rows)
    rank = jnp.sum(is_outer[:, None, :] & (slot[None, :] < slot[:, None])[None], axis=2)
    count = jnp.sum(is_outer, axis=1, keepdims=True)
    found = is_outer[:, None, :] & (rank[:, None, :] == place[None, :, None])
    outer = jnp.sum(jnp.where(found, slot, 0), axis=2)
    outer = jnp.where(place[None] < count, outer, slots)
    outer = jnp.where(place[None] == slots + LANES - 1, count, outer).astype(jnp.int32)
    rows = jnp.pad(rows, ((0, 0), (0, LANES)), constant_values=8 * INNER)
    smem = pl.BlockSpec(memory_space=pltpu.SMEM)
    held_inner, seen = pl.pallas_call(
        spread_kernel,
        out_shape=(
            jax.ShapeDtypeStruct((8, INNER, 256), BF16),
            jax.ShapeDtypeStruct((2, 2, slots, LANES), F32),
        ),
        in_specs=[smem, far],
        scratch_shapes=[
            pltpu.VMEM((2, 8 * INNER, LANES), F32),
            pltpu.VMEM((8, INNER, 256), BF16),
            pltpu.SemaphoreType.DMA((3,)),
        ],
        compiler_params=params(16),
        cost_estimate=cost(1, 8 * MIB),
        name="spread",
    )(near, got)
    one_tile = jax.ShapeDtypeStruct((PACKED, 256), BF16)
    held_outer, gram, to_first, to_second = pl.pallas_call(
        observe_kernel,
        out_shape=(
            jax.ShapeDtypeStruct((8, BLOCK, 256), BF16),
            jax.ShapeDtypeStruct((2, PACKED, 256), F32),
            one_tile,
            one_tile,
        ),
        in_specs=[smem, smem] + [vmem] * 8,
        scratch_shapes=[
            pltpu.VMEM((8, BLOCK, 256), BF16),
            pltpu.VMEM((2, 8 * BLOCK, LANES), F32),
            pltpu.VMEM((2, 2, slots + 8, LANES), F32),
        ],
        compiler_params=params(16),
        name="observe",
    )(rows, outer, root, observed_value[0], seen, straight, cross, *got_edges)
    anomaly_1, mean_1, anomaly_2, mean_2 = pl.pallas_call(
        prepare_kernel,
        out_shape=(
            jax.ShapeDtypeStruct((8, FIRST, 256), BF16),
            jax.ShapeDtypeStruct((8, FIRST, LANES), F32),
            jax.ShapeDtypeStruct((8, SECOND, 256), BF16),
            jax.ShapeDtypeStruct((8, SECOND, LANES), F32),
        ),
        compiler_params=params(12),
        cost_estimate=cost(1, 6 * MIB),
        name="prepare",
    )(held_inner, held_outer)

    line, short = pl.pallas_call(
        combine_kernel,
        out_shape=(
            jax.ShapeDtypeStruct(gram.shape, F32),
            jax.ShapeDtypeStruct(gram.shape, BF16),
        ),
        compiler_params=params(8),
        name="combine",
    )(gram, *band_swaps(to_first, to_second))
    below, above = mem_swaps(short)
    *back, maps = pl.pallas_call(
        analyse_kernel,
        out_shape=(jax.ShapeDtypeStruct((FIRST, 256), BF16),) * 8
        + (jax.ShapeDtypeStruct((2, 256, 256), BF16),),
        scratch_shapes=[pltpu.VMEM((8, FIRST, 256), BF16), pltpu.VMEM((2, 8, 32, 256), BF16)],
        compiler_params=params(20),
        name="analyse",
    )(line, below, above, anomaly_1, mean_1)
    first = partners(back)
    maps, first[0] = lax.optimization_barrier((maps, first[0]))
    back = pl.pallas_call(
        second_kernel,
        out_shape=(jax.ShapeDtypeStruct((SECOND, 256), BF16),) * 8,
        scratch_shapes=[pltpu.VMEM((8, SECOND, 256), BF16)],
        compiler_params=params(16),
        cost_estimate=cost(1, 6 * MIB),
        name="second",
    )(maps, anomaly_2, mean_2)
    second = partners(back)
    result = jax.ShapeDtypeStruct(planes.shape, BF16)
    half = pl.pallas_call(
        first_return_kernel,
        out_shape=result,
        out_specs=far,
        scratch_shapes=[
            pltpu.VMEM((8, FIRST, 256), F32),
            pltpu.VMEM((12, latitudes, 256), F32),
            pltpu.VMEM((3, 32, members, latitudes), BF16),
            pltpu.SemaphoreType.DMA((3,)),
        ],
        compiler_params=params(20),
        cost_estimate=cost(1, 4 * MIB),
        name="first_return",
    )(*first)
    planes = pl.pallas_call(
        second_return_kernel,
        out_shape=result,
        in_specs=[vmem] * 8 + [far],
        out_specs=far,
        scratch_shapes=[
            pltpu.VMEM((8, SECOND, 256), F32),
            pltpu.VMEM((11, latitudes, 256), F32),
            pltpu.VMEM((3, 28, members, latitudes), BF16),
            pltpu.SemaphoreType.DMA((6,)),
        ],
        input_output_aliases={8: 0},
        compiler_params=params(20),
        name="second_return",
    )(*second, half)
    return jnp.transpose(planes, (2, 0, 1, 3))


def choose(ensemble, layer_depth, observed_cell, *rest):
    mesh_shape = (lax.axis_size("mem"), lax.axis_size("band"))
    shape = (mesh_shape, ensemble.shape, observed_cell.shape[1])
    fits = shape == ((8, 4), (32, 3, 60, 160), 2) and observed_cell.shape[2] % 16 == 0
    chosen = on_device_fast if fits else on_device
    return chosen(ensemble, layer_depth, observed_cell, *rest)


def solution(mesh):
    in_specs = (
        P("mem", None, "band", None),
        P("band", None),
        P("mem", "band", None),
        P("mem", "band", None),
        P("mem", "band", None),
        P("mem", "band"),
    )
    out_specs = P("mem", None, "band", None)
    return jax.shard_map(
        choose, mesh=mesh, in_specs=in_specs, out_specs=out_specs, check_vma=False
    )
```

```python
import math

import jax
import jax.numpy as jnp
import numpy as np
from jax import lax
from jax.experimental import pallas as pl
from jax.experimental.pallas import tpu as pltpu
from jax.sharding import PartitionSpec as P

SWEEPS = 5


half_step = 0.1
coriolis_scale = 0.3
neighbour_weight = 0.75


def padded_2(cells, sides, width):
    for axis, dim in sides:
        count = lax.axis_size(axis)
        head = lax.slice_in_dim(cells, 0, width, axis=dim)
        tail = lax.slice_in_dim(cells, cells.shape[dim] - width, cells.shape[dim], axis=dim)
        cells = jnp.concatenate(
            [
                lax.ppermute(tail, axis, [(i, (i + 1) % count) for i in range(count)]),
                cells,
                lax.ppermute(head, axis, [((i + 1) % count, i) for i in range(count)]),
            ],
            axis=dim,
        )
    return cells


def north_south(source):
    widths = [(0, 0)] * (source.ndim - 1) + [(1, 1)]
    padded = jnp.pad(source, widths)
    return padded[..., 2:] - padded[..., :-2]


def coriolis(latitudes):
    position = jnp.arange(latitudes, dtype=jnp.float32)
    return coriolis_scale * jnp.sin(math.pi * ((position + 0.5) / latitudes - 0.5))


def newton_schulz(starting):
    identity = jnp.eye(starting.shape[-1], dtype=starting.dtype)
    root_part = starting
    inverse_root = jnp.broadcast_to(identity, starting.shape)
    for sweep_index in range(SWEEPS):
        product = jnp.einsum(
            "tij,tjk->tik", inverse_root, root_part, precision=lax.Precision.HIGHEST
        )
        middle = 1.5 * identity - 0.5 * product
        root_part = jnp.einsum("tij,tjk->tik", root_part, middle, precision=lax.Precision.HIGHEST)
        inverse_root = jnp.einsum(
            "tij,tjk->tik", middle, inverse_root, precision=lax.Precision.HIGHEST
        )
    return inverse_root


def on_device(ensemble, layer_depth, observed_cell, observed_value, error_variance, observed_count):
    block_members = ensemble.shape[0]
    columns = ensemble.shape[2]
    latitudes = ensemble.shape[3]
    strips = lax.axis_size("mem")
    members = block_members * strips
    strip_rows = latitudes // strips
    tile_count = observed_cell.shape[1]
    tile_columns = columns // tile_count
    slot_count = observed_cell.shape[2]
    tile_cells = 3 * tile_columns * strip_rows
    height = ensemble[:, 0].astype(jnp.float32)
    eastward = ensemble[:, 1].astype(jnp.float32)
    northward = ensemble[:, 2].astype(jnp.float32)
    turning = coriolis(latitudes)
    flux_east = (layer_depth * eastward).astype(jnp.bfloat16)
    flux_north = (layer_depth * northward).astype(jnp.bfloat16)
    east_margin = padded_2(flux_east, (("band", 1),), 1)
    east_west = east_margin[:, 2:].astype(jnp.float32) - east_margin[:, :-2].astype(jnp.float32)
    north_local = lax.optimization_barrier(flux_north).astype(jnp.float32)
    raised = height - half_step * (east_west + north_south(north_local))
    surface_elevation_cast = raised.astype(jnp.bfloat16)
    height_margin = padded_2(surface_elevation_cast, (("band", 1),), 1)
    margin_wide = height_margin.astype(jnp.float32)
    height_inner = margin_wide[:, 1:-1]
    revised_zonal_velocity = (
        eastward + turning * northward - half_step * (margin_wide[:, 2:] - margin_wide[:, :-2])
    )
    revised_meridional_velocity = (
        northward - turning * eastward - half_step * north_south(height_inner)
    )
    advance_dynamics = jnp.stack(
        [
            surface_elevation_cast,
            revised_zonal_velocity.astype(jnp.bfloat16),
            revised_meridional_velocity.astype(jnp.bfloat16),
        ],
        axis=1,
    )
    reordered = advance_dynamics.reshape(
        block_members, 3, tile_count, tile_columns, strips, strip_rows
    )
    reordered = jnp.transpose(reordered, (4, 2, 0, 1, 3, 5)).reshape(
        strips, tile_count, block_members, tile_cells
    )
    tile_block = lax.all_to_all(reordered, "mem", split_axis=0, concat_axis=2, tiled=True)[0]
    cells_here = observed_cell[0]
    values = jnp.take_along_axis(tile_block, cells_here[:, None, :], axis=2)
    observed_mean = jnp.sum(values, axis=1, dtype=jnp.float32) / members
    slot_index = jnp.arange(slot_count, dtype=jnp.int32)[None, :]
    live_slots = slot_index < observed_count[0][:, None]
    root_weight = jnp.sqrt(jnp.where(live_slots, 1.0 / error_variance[0], 0.0))
    spread = (
        root_weight[:, None, :] * (values.astype(jnp.float32) - observed_mean[:, None, :])
    ).astype(jnp.bfloat16)
    misfit = (root_weight * (observed_value[0] - observed_mean)).astype(jnp.bfloat16)
    spread_margin, misfit_margin = (
        padded_2(spread[None], (("mem", 0), ("band", 1)), 1),
        padded_2(misfit[None], (("mem", 0), ("band", 1)), 1),
    )
    gram_margin = jnp.einsum(
        "atko,atlo->atkl", spread_margin, spread_margin, preferred_element_type=jnp.float32
    )
    pull_margin = jnp.einsum(
        "atko,ato->atk", spread_margin, misfit_margin, preferred_element_type=jnp.float32
    )
    strip_here = lax.axis_index("mem")
    lower_valid = (strip_here > 0).astype(jnp.float32)
    upper_valid = (strip_here < strips - 1).astype(jnp.float32)
    strip_mask = (lower_valid, 1.0, upper_valid)
    total_gram = jnp.zeros((tile_count, members, members), jnp.float32)
    total_pull = jnp.zeros((tile_count, members), jnp.float32)
    for offset_lat in range(3):
        for offset_lon in range(3):
            factor = (
                neighbour_weight ** (abs(offset_lat - 1) + abs(offset_lon - 1))
                * strip_mask[offset_lat]
            )
            total_gram = (
                total_gram + factor * gram_margin[offset_lat, offset_lon : offset_lon + tile_count]
            )
            total_pull = (
                total_pull + factor * pull_margin[offset_lat, offset_lon : offset_lon + tile_count]
            )
    system = (members - 1) * jnp.eye(members, dtype=jnp.float32)[None] + total_gram
    frobenius = jnp.sqrt(jnp.sum(system * system, axis=(1, 2)))
    inverse_root = newton_schulz(system / frobenius[:, None, None])
    spread_map = inverse_root * (math.sqrt(members - 1) / jnp.sqrt(frobenius))[:, None, None]
    half_pull = jnp.einsum("tij,tj->ti", inverse_root, total_pull, precision=lax.Precision.HIGHEST)
    shift_weights = (
        jnp.einsum("tij,tj->ti", inverse_root, half_pull, precision=lax.Precision.HIGHEST)
        / frobenius[:, None]
    )
    weights = (spread_map + shift_weights[:, :, None]).astype(jnp.bfloat16)
    state_mean = jnp.sum(tile_block, axis=1, dtype=jnp.float32) / members
    anomaly = (tile_block.astype(jnp.float32) - state_mean[:, None, :]).astype(jnp.bfloat16)
    update = jnp.einsum("tjk,tjc->tkc", weights, anomaly, preferred_element_type=jnp.float32)
    analysed = (state_mean[:, None, :] + update).astype(jnp.bfloat16)
    returned = lax.all_to_all(analysed[None], "mem", split_axis=2, concat_axis=0, tiled=True)
    returned = returned.reshape(strips, tile_count, block_members, 3, tile_columns, strip_rows)
    return jnp.transpose(returned, (2, 3, 1, 4, 0, 5)).reshape(block_members, 3, columns, latitudes)


LANES = 128
GROUPS = 23
INNER = 360
OUTER = 104
BLOCK = 112
FIRST = 240
SECOND = 224
F32 = jnp.float32
BF16 = jnp.bfloat16
PACKED = 144
CHIPS = (0, 2, 4, 6)
ORDER = (6, 2, 4, 7, 1, 3, 5, 0)
MIB = 1024 * 1024


def params(size):
    return pltpu.CompilerParams(vmem_limit_bytes=size * MIB)


def cost(flops, moved):
    return pl.CostEstimate(flops=flops, bytes_accessed=moved, transcendentals=0)


def identity(size, dtype):
    row = lax.broadcasted_iota(jnp.int32, (size, size), 0)
    column = lax.broadcasted_iota(jnp.int32, (size, size), 1)
    return (row == column).astype(F32).astype(dtype)


def dot_nt(left, right):
    return lax.dot_general(left, right, (((1,), (1,)), ((), ())), preferred_element_type=F32)


def dot_nn(left, right):
    return lax.dot_general(left, right, (((1,), (0,)), ((), ())), preferred_element_type=F32)


def split(value):
    high = value.astype(BF16)
    return high, (value - high.astype(F32)).astype(BF16)


def left_3(parts):
    return jnp.concatenate([parts[0], parts[0], parts[1]], axis=1)


def right_3(parts):
    return jnp.concatenate([parts[0], parts[1], parts[0]], axis=0)


def triangle(size):
    row = lax.broadcasted_iota(jnp.int32, (size, size), 0)
    column = lax.broadcasted_iota(jnp.int32, (size, size), 1)
    return row, column


def packed(block, pull):
    row, column = triangle(128)
    last = block[128:256, 128:256]
    corner = jnp.where(row >= column, block[0:128, 0:128], last)
    middle = jnp.sum(jnp.where(row == column, last, 0.0), axis=0, keepdims=True)
    middle = jnp.concatenate([jnp.zeros_like(middle), middle], axis=1)
    top = jnp.concatenate([block[128:256, 0:128], corner], axis=1)
    return jnp.concatenate([top, pull, jnp.broadcast_to(middle, (8, 256))], axis=0)


def unpacked(value):
    row, column = triangle(128)
    low, corner = value[0:128, 0:128], value[0:128, 128:256]
    other = jnp.transpose(corner)
    first = jnp.where(row >= column, corner, other)
    last = jnp.where(row < column, corner, other)
    last = jnp.where(row == column, value[136:137, 128:256], last)
    top = jnp.concatenate([first, jnp.transpose(low)], axis=1)
    return jnp.concatenate([top, jnp.concatenate([low, last], axis=1)], axis=0), value[128:136]


def exchange_lanes(blocks, lane):
    blocks = [list(pair) for pair in blocks]
    for q in range(4):
        low, high = blocks[q], blocks[q + 4]
        blocks[q], blocks[q + 4] = [low[0], high[0]], [low[1], high[1]]
    for bit in range(2):
        step = 32 << bit
        odd = (lane & step) != 0
        for q in range(8):
            if q & (1 << bit):
                continue
            for h in range(2):
                low, high = blocks[q][h], blocks[q | (1 << bit)][h]
                blocks[q][h] = jnp.where(odd, pltpu.roll(high, step, 1), low)
                blocks[q | (1 << bit)][h] = jnp.where(odd, high, pltpu.roll(low, LANES - step, 1))
    return blocks


def group_of(variable, index):
    if index == 0:
        return 18 + variable
    if index == 3:
        return 9 + variable
    return variable * 3 + index - 4 if index > 3 else 12 + variable * 2 + index - 1


def difference(latitudes):
    source = lax.broadcasted_iota(jnp.int32, (latitudes, latitudes), 0)
    target = lax.broadcasted_iota(jnp.int32, (latitudes, latitudes), 1)
    shift = (source == target + 1).astype(F32) - (source == target - 1).astype(F32)
    return shift.astype(BF16)


def rows_apart(value, shift):
    flat = value.reshape(-1, value.shape[-1])
    return dot_nn(flat, shift).reshape(value.shape)


def fluxes(east, deep):
    return (deep * east.astype(F32)).astype(BF16).astype(F32)


def heights(field, north, deep, ahead, behind, shift):
    flux_north = (deep * north.astype(F32)).astype(BF16)
    raised = field.astype(F32) - half_step * ((ahead - behind) + rows_apart(flux_north, shift))
    return raised.astype(BF16)


def velocities(east, north, here, ahead, behind, turning, shift):
    east, north = east.astype(F32), north.astype(F32)
    apart = ahead.astype(F32) - behind.astype(F32)
    new_east = east + turning * north - half_step * apart
    new_north = north - turning * east - half_step * rows_apart(here, shift)
    return new_east.astype(BF16), new_north.astype(BF16)


def put_group(staged, block, eye, first):
    latitudes = eye.shape[0]
    rows = latitudes // 8
    turned = dot_nt(eye, block.reshape(256, latitudes))
    for s in range(8):
        staged[s, first : first + rows, :] = turned[rows * s : rows * (s + 1)]


def turning_row(latitudes):
    position = lax.broadcasted_iota(jnp.int32, (8, latitudes), 1).astype(F32)
    turning = coriolis_scale * jnp.sin(math.pi * ((position + 0.5) / latitudes - 0.5))
    return turning[0:1, :][None]


def inner_kernel(
    ens, depth, out, to_second, to_first, here, deep, flux, height, staged, half, edges, arrived
):
    columns, members, latitudes = here.shape[1:]
    batch = columns // 5
    pieces = [pltpu.make_async_copy(depth, deep, arrived.at[5])]
    for k in range(5):
        span = pl.ds(k * batch, batch)
        piece = pltpu.make_async_copy(ens.at[:, span], here.at[:, span], arrived.at[k])
        pieces.append(piece)
    for piece in pieces:
        piece.start()
    shift = difference(latitudes)
    turning = turning_row(latitudes)
    eye = identity(latitudes, BF16)
    pieces[0].wait()

    def depths(first, count):
        rows = [deep[c : c + 1, :] for c in range(first, first + count)]
        return jnp.stack([jnp.broadcast_to(row, (members, latitudes)) for row in rows])

    def edge(side, near, far):
        edges[side, 0] = here[0, near]
        edges[side, 1] = (deep[near : near + 1, :] * here[2, near].astype(F32)).astype(BF16)
        edges[side, 2] = flux[near].astype(BF16)
        edges[side, 3] = flux[far].astype(BF16)

    done = 1
    for k in range(5):
        pieces[k + 1].wait()
        first = k * batch
        flux[first : first + batch] = fluxes(here[1, first : first + batch], depths(first, batch))
        if k == 0:
            edge(0, 0, 1)
        if k == 4:
            edge(1, columns - 1, columns - 2)
        low, high = max(first - 1, 1), first + batch - 1
        at = slice(low, high)
        ahead, behind = flux[low + 1 : high + 1], flux[low - 1 : high - 1]
        height[at] = heights(
            here[0, at], here[2, at], depths(low, high - low), ahead, behind, shift
        )
        while done < 7 and 8 * done + 9 <= high:
            first = 8 * done
            at = slice(first, first + 8)
            ahead, behind = height[first + 1 : first + 9], height[first - 1 : first + 7]
            new = velocities(here[1, at], here[2, at], height[at], ahead, behind, turning, shift)
            for v, field in enumerate((height[at],) + new):
                put_group(staged, field, eye, 20 * group_of(v, done))
            done += 1
        if k == 2:
            half[:, FIRST:INNER] = staged[:, FIRST:INNER].astype(BF16)
            span = pl.ds(FIRST, INNER - FIRST)
            leaving = pltpu.make_async_copy(half.at[:, span], out.at[:, span], arrived.at[6])
            leaving.start()
    odd = lax.axis_index("band") & 1
    to_first[...] = edges[1 - odd]
    to_second[...] = edges[odd]
    half[:, 0:FIRST] = staged[:, 0:FIRST].astype(BF16)
    span = pl.ds(0, FIRST)
    last = pltpu.make_async_copy(half.at[:, span], out.at[:, span], arrived.at[7])
    last.start()
    leaving.wait()
    last.wait()


def outer_kernel(
    west_block, east_block, second_swap, first_swap, depth, *refs
):
    straight, cross, flux, height, staged, swapped = refs
    odd = lax.axis_index("band") & 1
    for side, block in enumerate((first_swap, second_swap)):
        swapped[side] = block[...]
    left, right = swapped.at[1 - odd], swapped.at[odd]
    members, latitudes = west_block.shape[2:]
    shift = difference(latitudes)
    turning = turning_row(latitudes)
    eye = identity(latitudes, BF16)

    def depths(first, count):
        return jnp.stack(
            [
                jnp.broadcast_to(depth[c : c + 1, :], (members, latitudes))
                for c in range(first, first + count)
            ]
        )

    def window(ens, edge, first, count, low, high):
        is_left = low == 0
        base = 2 if is_left else 0
        flux[base : base + count] = fluxes(ens[1, 0:count], depths(first, count))
        at = 0 if is_left else count
        near, far = (1, 0) if is_left else (at, at + 1)
        flux[near] = edge[2].astype(F32)
        flux[far] = edge[3].astype(F32)
        wide = high - low + 1
        skip = 0 if is_left else 1
        columns = slice(skip, skip + wide)
        new = heights(
            ens[0, columns],
            ens[2, columns],
            depths(first + skip, wide),
            flux[base + skip + 1 : base + skip + 1 + wide],
            flux[base + skip - 1 : base + skip - 1 + wide],
            shift,
        )
        start = 1 if is_left else 0
        height[start : start + wide] = new
        place = 0 if is_left else wide
        middle = near
        east_west = flux[middle + 1] - flux[middle - 1]
        raised = edge[0].astype(F32) - half_step * (east_west + rows_apart(edge[1], shift))
        height[place] = raised.astype(BF16)
        count = high - low
        here = height[1 : 1 + count]
        ahead, behind = height[2 : 2 + count], height[0:count]
        at = slice(low - first, high - first)
        return (here,) + velocities(ens[1, at], ens[2, at], here, ahead, behind, turning, shift)

    staged[:, 100:104, :] = jnp.zeros((8, 4, 256), F32)
    for v, field in enumerate(window(west_block, left, 0, 10, 0, 8)):
        put_group(staged, field, eye, 20 * v)
    ends = window(east_block, right, 54, 6, 56, 60)
    put_group(staged, jnp.concatenate([ends[0], ends[1]], axis=0), eye, 60)
    put_group(staged, jnp.concatenate([ends[2], jnp.zeros_like(ends[2])], axis=0), eye, 80)
    me = lax.axis_index("mem")
    for k, d in enumerate(CHIPS):
        straight[k] = staged[me ^ d].astype(BF16)
        cross[k] = staged[me ^ d ^ 1].astype(BF16)


def spread_block(source, wide, start, lane):
    spans = [slice(h * LANES, (h + 1) * LANES) for h in range(2)]
    count = source.shape[1]
    here = pl.ds(start, 16)
    blocks = exchange_lanes([[source[q, here, span] for span in spans] for q in range(8)], lane)
    for q in range(8):
        to = pl.ds(pl.multiple_of(q * count + start, 8), 16)
        for h in range(2):
            wide[h, to, :] = blocks[q][h].astype(F32)


def spread_kernel(cells, got, wide, seen):
    lane = lax.broadcasted_iota(jnp.int32, (16, LANES), 1)

    def step(index, carry):
        spread_block(got, wide, pl.multiple_of(index * 16, 16), lane)
        return carry

    lax.fori_loop(0, 22, step, 0, unroll=4)
    spread_block(got, wide, INNER - 16, lane)
    slots = seen.shape[2]
    unroll = 16

    def pick(index, carry):
        for t in range(2):
            for k in range(unroll):
                slot = index * unroll + k
                row = cells[t, slot]
                for h in range(2):
                    seen[t, h, pl.ds(slot, 1), :] = wide[h, pl.ds(row, 1), :]
        return carry

    lax.fori_loop(0, slots // unroll, pick, 0)


def observe_kernel(cells, outer, weight, target, first, straight, cross, *refs):
    edges, (wide, gram, to_second, to_first, joined, seen) = refs[:3], refs[3:]
    wholes = []
    lane = lax.broadcasted_iota(jnp.int32, (16, LANES), 1)
    me = lax.axis_index("mem")
    for k, d in enumerate(CHIPS):
        joined[me ^ d, 0:OUTER, :] = straight[0] if k == 0 else edges[k - 1][0]
        joined[me ^ d ^ 1, 0:OUTER, :] = cross[0] if k == 0 else edges[k - 1][1]
    joined[:, OUTER:BLOCK, :] = jnp.zeros((8, BLOCK - OUTER, 256), BF16)
    for index in range(BLOCK // 16):
        spread_block(joined, wide, index * 16, lane)
    slots = first.shape[2]
    seen[:, :, 0:slots, :] = first[...]
    for t in range(2):

        def pick(index, carry):
            for k in range(8):
                slot = outer[t, index * 8 + k]
                row = cells[t, slot] - 8 * INNER
                for h in range(2):
                    seen[t, h, pl.ds(slot, 1), :] = wide[h, pl.ds(row, 1), :]
            return carry

        lax.fori_loop(0, (outer[t, slots + LANES - 1] + 7) // 8, pick, 0)
    eye = identity(256, BF16)
    for t in range(2):
        values = jnp.concatenate([seen[t, h, 0:slots] for h in range(2)], axis=1).astype(BF16)
        turned = dot_nt(eye, values)
        mean = jnp.sum(turned, axis=0, keepdims=True) * (1.0 / 256)
        root = weight[t : t + 1, :]
        spread = (root * (turned - mean)).astype(BF16)
        misfit = (root * (target[t : t + 1, :] - mean)).astype(BF16)
        block = dot_nt(spread, spread)
        pull = dot_nt(jnp.broadcast_to(misfit, (16, slots)), spread)
        whole = packed(block, pull[0:8])
        gram[t] = whole
        wholes.append(whole.astype(BF16))
    odd = (lax.axis_index("band") & 1) == 1
    to_first[...] = jnp.where(odd, wholes[0], wholes[1])
    to_second[...] = jnp.where(odd, wholes[1], wholes[0])


def combine_kernel(gram, second_swap, first_swap, line, short):
    odd = (lax.axis_index("band") & 1) == 1
    first, second = first_swap[...].astype(F32), second_swap[...].astype(F32)
    west, east = jnp.where(odd, first, second), jnp.where(odd, second, first)
    for t, beside in enumerate((west + gram[1], gram[0] + east)):
        total = gram[t] + neighbour_weight * beside
        line[t] = total
        short[t] = total.astype(BF16)


def prepare_kernel(inner, outer, *refs):
    average = jnp.full((256, LANES), 1.0 / 256, BF16)
    for q in range(8):
        cells = [inner[h, q * INNER : (q + 1) * INNER, :] for h in range(2)]
        rest = [outer[h, q * BLOCK : q * BLOCK + OUTER, :] for h in range(2)]
        cells, rest = jnp.concatenate(cells, axis=1), jnp.concatenate(rest, axis=1)
        pieces = (cells[0:FIRST], jnp.concatenate([cells[FIRST:INNER], rest], axis=0))
        for k, piece in enumerate(pieces):
            mean = dot_nn(piece.astype(BF16), average)
            refs[2 * k + 1][q] = mean
            mean = jnp.concatenate([mean, mean], axis=1)
            refs[2 * k][q] = (piece - mean).astype(BF16)


def send_back(results, outs):
    lane = lax.broadcasted_iota(jnp.int32, (16, LANES), 1)
    spans = [slice(h * LANES, (h + 1) * LANES) for h in range(2)]

    def step(index, carry):
        here = pl.ds(pl.multiple_of(index * 16, 16), 16)
        blocks = [[results[q, here, span] for span in spans] for q in range(8)]
        blocks = exchange_lanes(blocks, lane)
        for q in range(8):
            for h in range(2):
                outs[ORDER.index(q)][here, spans[h]] = blocks[q][h]
        return carry

    lax.fori_loop(0, results.shape[1] // 16, step, 0, unroll=4)


def apply_maps(anomaly, mean, maps, results, q, edge, order):
    count = results.shape[1]
    low, high = edge // 16 * 16, (edge + 15) // 16 * 16
    first = dot_nt(anomaly[q, 0:high], maps[order[0]])
    centre = jnp.concatenate([mean[q], mean[q]], axis=1)
    results[q, 0:low] = (centre[0:low] + first[0:low]).astype(BF16)
    if low == count:
        return
    second = dot_nt(anomaly[q, low:count], maps[order[1]])
    if low < high:
        near = lax.broadcasted_iota(jnp.int32, (16, 256), 0) < edge - low
        both = jnp.where(near, first[low:high], second[0:16])
        results[q, low:high] = (centre[low:high] + both).astype(BF16)
    results[q, high:count] = (centre[high:count] + second[high - low : count - low]).astype(BF16)


def second_kernel(maps, anomaly, mean, *refs):
    outs, results = refs[:8], refs[8]
    both = [maps[0], maps[1]]
    for q in range(8):
        apply_maps(anomaly, mean, both, results, q, 180, (0, 1))
    send_back(results, outs)


def analyse_kernel(line, below, above, anomaly, mean, *refs):
    outs, (kept, results, ordered) = refs[:8], refs[8:]
    size = 256
    eye = identity(size, F32)
    norms, pulls, roots, inverses = [], [], [], []
    for t in range(2):
        beside = below[t].astype(F32) + above[t].astype(F32)
        block, pull = unpacked(line[t] + neighbour_weight * beside)
        system = (size - 1) * eye + block
        square = jnp.sum(jnp.sum(system * system, axis=0, keepdims=True), axis=1, keepdims=True)
        norms.append(jnp.sqrt(square))
        pulls.append(pull)
        roots.append(system / norms[t])
    for sweep in range(SWEEPS):
        rights = [right_3(split(root)) for root in roots]
        if sweep == 0:
            inverses = [1.5 * eye - 0.5 * root for root in roots]
            lefts = [left_3(split(inverse)) for inverse in inverses]
            roots = [dot_nn(left, right) for left, right in zip(lefts, rights)]
            continue
        parts = [split(inverse) for inverse in inverses]
        products = [dot_nn(left_3(part), right) for part, right in zip(parts, rights)]
        middles = [left_3(split(1.5 * eye - 0.5 * product)) for product in products]
        if sweep < SWEEPS - 1:
            roots = [dot_nn(middle, right) for middle, right in zip(middles, rights)]
        inverses = [dot_nn(middle, right_3(part)) for middle, part in zip(middles, parts)]
    maps = []
    for t in range(2):
        right = right_3(split(inverses[t]))
        half_pull = dot_nn(left_3(split(pulls[t])), right)
        shift = dot_nn(left_3(split(half_pull)), right) / norms[t]
        scale = math.sqrt(size - 1) / jnp.sqrt(norms[t])
        ordered[t] = (inverses[t] * scale + shift[0:1]).astype(BF16).reshape(8, 32, size)
    me = lax.axis_index("mem")
    for t in range(2):
        maps.append(jnp.concatenate([ordered[t, me ^ d] for d in range(8)], axis=0))
        kept[t] = maps[t]
    for q in range(8):
        apply_maps(anomaly, mean, maps, results, q, 180 if q < 6 else FIRST, (1, 0))
    send_back(results, outs)


def spread_strips(got, wide):
    me = lax.axis_index("mem")
    for k, d in enumerate(ORDER):
        wide[me ^ d] = got[k][...].astype(F32)


def take_group(wide, turned, eye, g, shape):
    rows = shape[2] // 8
    for s in range(8):
        turned[g, rows * s : rows * (s + 1), :] = wide[s, rows * g : rows * (g + 1), :]
    return dot_nt(eye, turned[g].astype(BF16)).astype(BF16).reshape(shape)


def first_return_kernel(*refs):
    got, (out, wide, turned, planes, sent) = refs[:8], refs[8:]
    shape = (8,) + planes.shape[2:]
    spread_strips(got, wide)
    eye = identity(256, BF16)
    copies = []
    for v in range(3):
        for index in range(3, 7):
            at = 8 * (index - 3)
            planes[v, at : at + 8] = take_group(wide, turned, eye, group_of(v, index), shape)
        copies.append(pltpu.make_async_copy(planes.at[v], out.at[v, pl.ds(24, 32)], sent.at[v]))
        copies[v].start()
    for copy in copies:
        copy.wait()


def second_return_kernel(*refs):
    got, (_, out, wide, turned, planes, sent) = refs[:8], refs[8:]
    shape = (8,) + planes.shape[2:]
    spread_strips(got, wide)
    eye = identity(256, BF16)
    mixed = take_group(wide, turned, eye, 9, shape)
    planes[0, 24:28] = mixed[0:4]
    planes[1, 24:28] = mixed[4:8]
    planes[2, 24:28] = take_group(wide, turned, eye, 10, shape)[0:4]
    copies = []
    for v in range(3):
        for index in range(3):
            at = 8 * index
            block = take_group(wide, turned, eye, group_of(v, index) - 12, shape)
            planes[v, at : at + 8] = block
        for k, (at, to, count) in enumerate(((0, 0, 24), (24, 56, 4))):
            source, target = planes.at[v, pl.ds(at, count)], out.at[v, pl.ds(to, count)]
            copies.append(pltpu.make_async_copy(source, target, sent.at[2 * v + k]))
            copies[-1].start()
    for copy in copies:
        copy.wait()


def swapped_pairs(values, axis, pairs):
    moved = []
    for value, some in zip(values, pairs):
        both = some + [(j, i) for i, j in some]
        moved.append(lax.ppermute(value, axis, both))
    return moved


def band_swaps(first, second):
    count = lax.axis_size("band")
    starts = range(0, count, 2)
    pairs = [[(i, i + 1) for i in starts], [(i + 1, (i + 2) % count) for i in starts]]
    return swapped_pairs((second, first), "band", pairs[::-1])[::-1]


def mem_swaps(value):
    count = lax.axis_size("mem")
    pairs = [[(i, i + 1) for i in range(k, count - 1, 2)] for k in range(2)]
    return swapped_pairs((value, value), "mem", pairs)


def across(value, difference):
    return lax.ppermute(value, "mem", [(i, i ^ difference) for i in range(8)])


def partners(values):
    return [across(value, d) if d else value for d, value in zip(ORDER, values)]


def swap(value):
    return lax.all_to_all(value, "mem", split_axis=0, concat_axis=0, tiled=True)


def cell_rows(cell):
    variable = cell // 600
    tile = jnp.arange(2, dtype=jnp.int32)[:, None]
    column = tile * 30 + cell // 20 % 30
    index = column // 8
    place = column % 8
    group = jnp.where(index > 3, variable * 3 + index - 4, 11 + variable * 2 + index)
    group = jnp.where(index == 3, 9 + variable, group)
    group = jnp.where(index == 0, 18 + variable, group)
    is_last = column >= 56
    group = jnp.where(is_last, 21 + variable // 2, group)
    place = jnp.where(is_last, column - 56 + 4 * (variable % 2), place)
    first = place * INNER + group * 20
    last = 8 * INNER + place * BLOCK + (group - 18) * 20
    return jnp.where(group < 18, first, last) + cell % 20


def on_device_fast(
    ensemble, layer_depth, observed_cell, observed_value, error_variance, observed_count
):
    members, _, columns, latitudes = ensemble.shape
    slots = observed_cell.shape[2]
    planes = jnp.transpose(ensemble, (1, 2, 0, 3))
    edge = jax.ShapeDtypeStruct((4, members, latitudes), BF16)
    far = pl.BlockSpec(memory_space=pltpu.HBM)
    vmem = pl.BlockSpec(memory_space=pltpu.VMEM)
    sent, to_second, to_first = pl.pallas_call(
        inner_kernel,
        out_shape=(jax.ShapeDtypeStruct((8, INNER, 256), BF16), edge, edge),
        in_specs=[far, far],
        out_specs=(far, vmem, vmem),
        scratch_shapes=[
            pltpu.VMEM(planes.shape, BF16),
            pltpu.VMEM((columns, latitudes), F32),
            pltpu.VMEM((columns, members, latitudes), F32),
            pltpu.VMEM((columns, members, latitudes), BF16),
            pltpu.VMEM((8, INNER, 256), F32),
            pltpu.VMEM((8, INNER, 256), BF16),
            pltpu.VMEM((2, 4, members, latitudes), BF16),
            pltpu.SemaphoreType.DMA((8,)),
        ],
        compiler_params=params(60),
        name="inner",
    )(planes, layer_depth)
    got = swap(sent)
    swaps = band_swaps(to_first, to_second)
    flat = pl.BlockSpec((4, members, latitudes), lambda i: (0, 0, 0))
    straight, cross = pl.pallas_call(
        outer_kernel,
        grid=(1,),
        out_shape=(jax.ShapeDtypeStruct((4, OUTER, 256), BF16),) * 2,
        in_specs=[
            pl.BlockSpec((3, 10, members, latitudes), lambda i: (0, 0, 0, 0)),
            pl.BlockSpec((3, 6, members, latitudes), lambda i: (0, 9, 0, 0)),
            flat,
            flat,
            pl.BlockSpec((columns, latitudes), lambda i: (0, 0)),
        ],
        out_specs=(pl.BlockSpec((4, OUTER, 256), lambda i: (0, 0, 0)),) * 2,
        scratch_shapes=[
            pltpu.VMEM((12, members, latitudes), F32),
            pltpu.VMEM((10, members, latitudes), BF16),
            pltpu.VMEM((8, OUTER, 256), F32),
            pltpu.VMEM((2, 4, members, latitudes), BF16),
        ],
        compiler_params=params(24),
        name="outer",
    )(planes, planes, *swaps[::-1], layer_depth)
    cross = across(cross, 1)
    got_edges = [across(jnp.stack([straight[k], cross[k]]), CHIPS[k]) for k in (3, 1, 2)]
    got_edges = got_edges[1:] + got_edges[:1]

    rows = cell_rows(observed_cell[0])
    live = jnp.arange(slots, dtype=jnp.int32)[None, :] < observed_count[0][:, None]
    root = jnp.sqrt(jnp.where(live, 1.0 / error_variance[0], 0.0))
    slot = jnp.arange(slots, dtype=jnp.int32)
    place = jnp.arange(slots + LANES, dtype=jnp.int32)
    is_outer = rows >= 8 * INNER
    near = jnp.where(is_outer, 0, rows)
    rank = jnp.sum(is_outer[:, None, :] & (slot[None, :] < slot[:, None])[None], axis=2)
    count = jnp.sum(is_outer, axis=1, keepdims=True)
    found = is_outer[:, None, :] & (rank[:, None, :] == place[None, :, None])
    outer = jnp.sum(jnp.where(found, slot, 0), axis=2)
    outer = jnp.where(place[None] < count, outer, slots)
    outer = jnp.where(place[None] == slots + LANES - 1, count, outer).astype(jnp.int32)
    rows = jnp.pad(rows, ((0, 0), (0, LANES)), constant_values=8 * INNER)
    smem = pl.BlockSpec(memory_space=pltpu.SMEM)
    held_inner, seen = pl.pallas_call(
        spread_kernel,
        out_shape=(
            jax.ShapeDtypeStruct((2, 8 * INNER, LANES), F32),
            jax.ShapeDtypeStruct((2, 2, slots, LANES), F32),
        ),
        in_specs=[smem, vmem],
        compiler_params=params(12),
        cost_estimate=cost(1, 8 * MIB),
        name="spread",
    )(near, got)
    one_tile = jax.ShapeDtypeStruct((PACKED, 256), BF16)
    held_outer, gram, to_second, to_first = pl.pallas_call(
        observe_kernel,
        out_shape=(
            jax.ShapeDtypeStruct((2, 8 * BLOCK, LANES), F32),
            jax.ShapeDtypeStruct((2, PACKED, 256), F32),
            one_tile,
            one_tile,
        ),
        in_specs=[smem, smem] + [vmem] * 8,
        scratch_shapes=[
            pltpu.VMEM((8, BLOCK, 256), BF16),
            pltpu.VMEM((2, 2, slots + 8, LANES), F32),
        ],
        compiler_params=params(16),
        name="observe",
    )(rows, outer, root, observed_value[0], seen, straight, cross, *got_edges)
    anomaly_1, mean_1, anomaly_2, mean_2 = pl.pallas_call(
        prepare_kernel,
        out_shape=(
            jax.ShapeDtypeStruct((8, FIRST, 256), BF16),
            jax.ShapeDtypeStruct((8, FIRST, LANES), F32),
            jax.ShapeDtypeStruct((8, SECOND, 256), BF16),
            jax.ShapeDtypeStruct((8, SECOND, LANES), F32),
        ),
        compiler_params=params(12),
        cost_estimate=cost(1, 6 * MIB),
        name="prepare",
    )(held_inner, held_outer)

    line, short = pl.pallas_call(
        combine_kernel,
        out_shape=(
            jax.ShapeDtypeStruct(gram.shape, F32),
            jax.ShapeDtypeStruct(gram.shape, BF16),
        ),
        compiler_params=params(8),
        name="combine",
    )(gram, *band_swaps(to_first, to_second)[::-1])
    below, above = mem_swaps(short)
    *back, maps = pl.pallas_call(
        analyse_kernel,
        out_shape=(jax.ShapeDtypeStruct((FIRST, 256), BF16),) * 8
        + (jax.ShapeDtypeStruct((2, 256, 256), BF16),),
        scratch_shapes=[pltpu.VMEM((8, FIRST, 256), BF16), pltpu.VMEM((2, 8, 32, 256), BF16)],
        compiler_params=params(20),
        name="analyse",
    )(line, below, above, anomaly_1, mean_1)
    first = partners(back)
    maps, first[4] = lax.optimization_barrier((maps, first[4]))
    back = pl.pallas_call(
        second_kernel,
        out_shape=(jax.ShapeDtypeStruct((SECOND, 256), BF16),) * 8,
        scratch_shapes=[pltpu.VMEM((8, SECOND, 256), BF16)],
        compiler_params=params(16),
        cost_estimate=cost(1, 6 * MIB),
        name="second",
    )(maps, anomaly_2, mean_2)
    second = partners(back)
    result = jax.ShapeDtypeStruct(planes.shape, BF16)
    half = pl.pallas_call(
        first_return_kernel,
        out_shape=result,
        out_specs=far,
        scratch_shapes=[
            pltpu.VMEM((8, FIRST, 256), F32),
            pltpu.VMEM((12, latitudes, 256), F32),
            pltpu.VMEM((3, 32, members, latitudes), BF16),
            pltpu.SemaphoreType.DMA((3,)),
        ],
        compiler_params=params(20),
        cost_estimate=cost(1, 4 * MIB),
        name="first_return",
    )(*first)
    planes = pl.pallas_call(
        second_return_kernel,
        out_shape=result,
        in_specs=[vmem] * 8 + [far],
        out_specs=far,
        scratch_shapes=[
            pltpu.VMEM((8, SECOND, 256), F32),
            pltpu.VMEM((11, latitudes, 256), F32),
            pltpu.VMEM((3, 28, members, latitudes), BF16),
            pltpu.SemaphoreType.DMA((6,)),
        ],
        input_output_aliases={8: 0},
        compiler_params=params(20),
        name="second_return",
    )(*second, half)
    return jnp.transpose(planes, (2, 0, 1, 3))


def choose(ensemble, layer_depth, observed_cell, *rest):
    mesh_shape = (lax.axis_size("mem"), lax.axis_size("band"))
    shape = (mesh_shape, ensemble.shape, observed_cell.shape[1])
    fits = shape == ((8, 4), (32, 3, 60, 160), 2) and observed_cell.shape[2] % 16 == 0
    chosen = on_device_fast if fits else on_device
    return chosen(ensemble, layer_depth, observed_cell, *rest)


def solution(mesh):
    in_specs = (
        P("mem", None, "band", None),
        P("band", None),
        P("mem", "band", None),
        P("mem", "band", None),
        P("mem", "band", None),
        P("mem", "band"),
    )
    out_specs = P("mem", None, "band", None)
    return jax.shard_map(
        choose, mesh=mesh, in_specs=in_specs, out_specs=out_specs, check_vma=False
    )
```

```python
import math

import jax
import jax.numpy as jnp
import numpy as np
from jax import lax
from jax.experimental import pallas as pl
from jax.experimental.pallas import tpu as pltpu
from jax.sharding import PartitionSpec as P

SWEEPS = 5


half_step = 0.1
coriolis_scale = 0.3
neighbour_weight = 0.75


def padded_2(cells, sides, width):
    for axis, dim in sides:
        count = lax.axis_size(axis)
        head = lax.slice_in_dim(cells, 0, width, axis=dim)
        tail = lax.slice_in_dim(cells, cells.shape[dim] - width, cells.shape[dim], axis=dim)
        cells = jnp.concatenate(
            [
                lax.ppermute(tail, axis, [(i, (i + 1) % count) for i in range(count)]),
                cells,
                lax.ppermute(head, axis, [((i + 1) % count, i) for i in range(count)]),
            ],
            axis=dim,
        )
    return cells


def north_south(source):
    widths = [(0, 0)] * (source.ndim - 1) + [(1, 1)]
    padded = jnp.pad(source, widths)
    return padded[..., 2:] - padded[..., :-2]


def coriolis(latitudes):
    position = jnp.arange(latitudes, dtype=jnp.float32)
    return coriolis_scale * jnp.sin(math.pi * ((position + 0.5) / latitudes - 0.5))


def newton_schulz(starting):
    identity = jnp.eye(starting.shape[-1], dtype=starting.dtype)
    root_part = starting
    inverse_root = jnp.broadcast_to(identity, starting.shape)
    for sweep_index in range(SWEEPS):
        product = jnp.einsum(
            "tij,tjk->tik", inverse_root, root_part, precision=lax.Precision.HIGHEST
        )
        middle = 1.5 * identity - 0.5 * product
        root_part = jnp.einsum("tij,tjk->tik", root_part, middle, precision=lax.Precision.HIGHEST)
        inverse_root = jnp.einsum(
            "tij,tjk->tik", middle, inverse_root, precision=lax.Precision.HIGHEST
        )
    return inverse_root


def on_device(ensemble, layer_depth, observed_cell, observed_value, error_variance, observed_count):
    block_members = ensemble.shape[0]
    columns = ensemble.shape[2]
    latitudes = ensemble.shape[3]
    strips = lax.axis_size("mem")
    members = block_members * strips
    strip_rows = latitudes // strips
    tile_count = observed_cell.shape[1]
    tile_columns = columns // tile_count
    slot_count = observed_cell.shape[2]
    tile_cells = 3 * tile_columns * strip_rows
    height = ensemble[:, 0].astype(jnp.float32)
    eastward = ensemble[:, 1].astype(jnp.float32)
    northward = ensemble[:, 2].astype(jnp.float32)
    turning = coriolis(latitudes)
    flux_east = (layer_depth * eastward).astype(jnp.bfloat16)
    flux_north = (layer_depth * northward).astype(jnp.bfloat16)
    east_margin = padded_2(flux_east, (("band", 1),), 1)
    east_west = east_margin[:, 2:].astype(jnp.float32) - east_margin[:, :-2].astype(jnp.float32)
    north_local = lax.optimization_barrier(flux_north).astype(jnp.float32)
    raised = height - half_step * (east_west + north_south(north_local))
    surface_elevation_cast = raised.astype(jnp.bfloat16)
    height_margin = padded_2(surface_elevation_cast, (("band", 1),), 1)
    margin_wide = height_margin.astype(jnp.float32)
    height_inner = margin_wide[:, 1:-1]
    revised_zonal_velocity = (
        eastward + turning * northward - half_step * (margin_wide[:, 2:] - margin_wide[:, :-2])
    )
    revised_meridional_velocity = (
        northward - turning * eastward - half_step * north_south(height_inner)
    )
    advance_dynamics = jnp.stack(
        [
            surface_elevation_cast,
            revised_zonal_velocity.astype(jnp.bfloat16),
            revised_meridional_velocity.astype(jnp.bfloat16),
        ],
        axis=1,
    )
    reordered = advance_dynamics.reshape(
        block_members, 3, tile_count, tile_columns, strips, strip_rows
    )
    reordered = jnp.transpose(reordered, (4, 2, 0, 1, 3, 5)).reshape(
        strips, tile_count, block_members, tile_cells
    )
    tile_block = lax.all_to_all(reordered, "mem", split_axis=0, concat_axis=2, tiled=True)[0]
    cells_here = observed_cell[0]
    values = jnp.take_along_axis(tile_block, cells_here[:, None, :], axis=2)
    observed_mean = jnp.sum(values, axis=1, dtype=jnp.float32) / members
    slot_index = jnp.arange(slot_count, dtype=jnp.int32)[None, :]
    live_slots = slot_index < observed_count[0][:, None]
    root_weight = jnp.sqrt(jnp.where(live_slots, 1.0 / error_variance[0], 0.0))
    spread = (
        root_weight[:, None, :] * (values.astype(jnp.float32) - observed_mean[:, None, :])
    ).astype(jnp.bfloat16)
    misfit = (root_weight * (observed_value[0] - observed_mean)).astype(jnp.bfloat16)
    spread_margin, misfit_margin = (
        padded_2(spread[None], (("mem", 0), ("band", 1)), 1),
        padded_2(misfit[None], (("mem", 0), ("band", 1)), 1),
    )
    gram_margin = jnp.einsum(
        "atko,atlo->atkl", spread_margin, spread_margin, preferred_element_type=jnp.float32
    )
    pull_margin = jnp.einsum(
        "atko,ato->atk", spread_margin, misfit_margin, preferred_element_type=jnp.float32
    )
    strip_here = lax.axis_index("mem")
    lower_valid = (strip_here > 0).astype(jnp.float32)
    upper_valid = (strip_here < strips - 1).astype(jnp.float32)
    strip_mask = (lower_valid, 1.0, upper_valid)
    total_gram = jnp.zeros((tile_count, members, members), jnp.float32)
    total_pull = jnp.zeros((tile_count, members), jnp.float32)
    for offset_lat in range(3):
        for offset_lon in range(3):
            factor = (
                neighbour_weight ** (abs(offset_lat - 1) + abs(offset_lon - 1))
                * strip_mask[offset_lat]
            )
            total_gram = (
                total_gram + factor * gram_margin[offset_lat, offset_lon : offset_lon + tile_count]
            )
            total_pull = (
                total_pull + factor * pull_margin[offset_lat, offset_lon : offset_lon + tile_count]
            )
    system = (members - 1) * jnp.eye(members, dtype=jnp.float32)[None] + total_gram
    frobenius = jnp.sqrt(jnp.sum(system * system, axis=(1, 2)))
    inverse_root = newton_schulz(system / frobenius[:, None, None])
    spread_map = inverse_root * (math.sqrt(members - 1) / jnp.sqrt(frobenius))[:, None, None]
    half_pull = jnp.einsum("tij,tj->ti", inverse_root, total_pull, precision=lax.Precision.HIGHEST)
    shift_weights = (
        jnp.einsum("tij,tj->ti", inverse_root, half_pull, precision=lax.Precision.HIGHEST)
        / frobenius[:, None]
    )
    weights = (spread_map + shift_weights[:, :, None]).astype(jnp.bfloat16)
    state_mean = jnp.sum(tile_block, axis=1, dtype=jnp.float32) / members
    anomaly = (tile_block.astype(jnp.float32) - state_mean[:, None, :]).astype(jnp.bfloat16)
    update = jnp.einsum("tjk,tjc->tkc", weights, anomaly, preferred_element_type=jnp.float32)
    analysed = (state_mean[:, None, :] + update).astype(jnp.bfloat16)
    returned = lax.all_to_all(analysed[None], "mem", split_axis=2, concat_axis=0, tiled=True)
    returned = returned.reshape(strips, tile_count, block_members, 3, tile_columns, strip_rows)
    return jnp.transpose(returned, (2, 3, 1, 4, 0, 5)).reshape(block_members, 3, columns, latitudes)


LANES = 128
GROUPS = 23
INNER = 304
OUTER = 160
FIRST = 240
SECOND = 224
F32 = jnp.float32
BF16 = jnp.bfloat16
PACKED = 144
CHIPS = (0, 2, 4, 6)
ORDER = (6, 2, 4, 7, 1, 3, 5, 0)
MIB = 1024 * 1024


def params(size):
    return pltpu.CompilerParams(vmem_limit_bytes=size * MIB)


def cost(flops, moved):
    return pl.CostEstimate(flops=flops, bytes_accessed=moved, transcendentals=0)


def identity(size, dtype):
    row = lax.broadcasted_iota(jnp.int32, (size, size), 0)
    column = lax.broadcasted_iota(jnp.int32, (size, size), 1)
    return (row == column).astype(F32).astype(dtype)


def dot_nt(left, right):
    return lax.dot_general(left, right, (((1,), (1,)), ((), ())), preferred_element_type=F32)


def dot_nn(left, right):
    return lax.dot_general(left, right, (((1,), (0,)), ((), ())), preferred_element_type=F32)


def split(value):
    high = value.astype(BF16)
    return high, (value - high.astype(F32)).astype(BF16)


def left_3(parts):
    return jnp.concatenate([parts[0], parts[0], parts[1]], axis=1)


def right_3(parts):
    return jnp.concatenate([parts[0], parts[1], parts[0]], axis=0)


def triangle(size):
    row = lax.broadcasted_iota(jnp.int32, (size, size), 0)
    column = lax.broadcasted_iota(jnp.int32, (size, size), 1)
    return row, column


def packed(block, pull):
    row, column = triangle(128)
    last = block[128:256, 128:256]
    corner = jnp.where(row >= column, block[0:128, 0:128], last)
    middle = jnp.sum(jnp.where(row == column, last, 0.0), axis=0, keepdims=True)
    middle = jnp.concatenate([jnp.zeros_like(middle), middle], axis=1)
    top = jnp.concatenate([block[128:256, 0:128], corner], axis=1)
    return jnp.concatenate([top, pull, jnp.broadcast_to(middle, (8, 256))], axis=0)


def unpacked(value):
    row, column = triangle(128)
    low, corner = value[0:128, 0:128], value[0:128, 128:256]
    other = jnp.transpose(corner)
    first = jnp.where(row >= column, corner, other)
    last = jnp.where(row < column, corner, other)
    last = jnp.where(row == column, value[136:137, 128:256], last)
    top = jnp.concatenate([first, jnp.transpose(low)], axis=1)
    return jnp.concatenate([top, jnp.concatenate([low, last], axis=1)], axis=0), value[128:136]


def exchange_lanes(blocks, lane):
    blocks = [list(pair) for pair in blocks]
    for q in range(4):
        low, high = blocks[q], blocks[q + 4]
        blocks[q], blocks[q + 4] = [low[0], high[0]], [low[1], high[1]]
    for bit in range(2):
        step = 32 << bit
        odd = (lane & step) != 0
        for q in range(8):
            if q & (1 << bit):
                continue
            for h in range(2):
                low, high = blocks[q][h], blocks[q | (1 << bit)][h]
                blocks[q][h] = jnp.where(odd, pltpu.roll(high, step, 1), low)
                blocks[q | (1 << bit)][h] = jnp.where(odd, high, pltpu.roll(low, LANES - step, 1))
    return blocks


def group_of(variable, index):
    return variable + (variable * 2 + index - 4 if index > 3 else 18 - 3 * index)


def row_of(group):
    return 20 * group + (4 if group >= 15 else 0)


def difference(latitudes):
    source = lax.broadcasted_iota(jnp.int32, (latitudes, latitudes), 0)
    target = lax.broadcasted_iota(jnp.int32, (latitudes, latitudes), 1)
    shift = (source == target + 1).astype(F32) - (source == target - 1).astype(F32)
    return shift.astype(BF16)


def rows_apart(value, shift):
    flat = value.reshape(-1, value.shape[-1])
    return dot_nn(flat, shift).reshape(value.shape)


def fluxes(east, deep):
    return (deep * east.astype(F32)).astype(BF16).astype(F32)


def heights(field, north, deep, ahead, behind, shift):
    flux_north = (deep * north.astype(F32)).astype(BF16)
    raised = field.astype(F32) - half_step * ((ahead - behind) + rows_apart(flux_north, shift))
    return raised.astype(BF16)


def velocities(east, north, here, ahead, behind, turning, shift):
    east, north = east.astype(F32), north.astype(F32)
    apart = ahead.astype(F32) - behind.astype(F32)
    new_east = east + turning * north - half_step * apart
    new_north = north - turning * east - half_step * rows_apart(here, shift)
    return new_east.astype(BF16), new_north.astype(BF16)


def put_group(staged, block, eye, first):
    latitudes = eye.shape[0]
    rows = latitudes // 8
    turned = dot_nt(eye, block.reshape(256, latitudes))
    for s in range(8):
        staged[s, first : first + rows, :] = turned[rows * s : rows * (s + 1)]


def turning_row(latitudes):
    position = lax.broadcasted_iota(jnp.int32, (8, latitudes), 1).astype(F32)
    turning = coriolis_scale * jnp.sin(math.pi * ((position + 0.5) / latitudes - 0.5))
    return turning[0:1, :][None]


def inner_kernel(
    ens, depth, out, to_first, to_second, here, deep, flux, height, staged, edges, arrived
):
    columns, members, latitudes = here.shape[1:]
    batch = columns // 5
    pieces = [pltpu.make_async_copy(depth, deep, arrived.at[5])]
    for k in range(5):
        span = pl.ds(k * batch, batch)
        piece = pltpu.make_async_copy(ens.at[:, span], here.at[:, span], arrived.at[k])
        pieces.append(piece)
    for piece in pieces:
        piece.start()
    shift = difference(latitudes)
    turning = turning_row(latitudes)
    eye = identity(latitudes, BF16)
    pieces[0].wait()

    def depths(first, count):
        rows = [deep[c : c + 1, :] for c in range(first, first + count)]
        return jnp.stack([jnp.broadcast_to(row, (members, latitudes)) for row in rows])

    def edge(side, near, far):
        edges[side, 0] = here[0, near]
        edges[side, 1] = (deep[near : near + 1, :] * here[2, near].astype(F32)).astype(BF16)
        edges[side, 2] = flux[near].astype(BF16)
        edges[side, 3] = flux[far].astype(BF16)

    staged[:, 300:INNER, :] = jnp.zeros((8, INNER - 300, 256), F32)
    done = 2
    for k in range(5):
        pieces[k + 1].wait()
        first, count = k * batch, batch if k else 2
        flux[first : first + count] = fluxes(here[1, first : first + count], depths(first, count))
        if k == 0:
            edge(0, 0, 1)
            continue
        if k == 4:
            edge(1, columns - 1, columns - 2)
        low, high = max(first - 1, batch + 1), first + batch - 1
        at = slice(low, high)
        ahead, behind = flux[low + 1 : high + 1], flux[low - 1 : high - 1]
        height[at] = heights(
            here[0, at], here[2, at], depths(low, high - low), ahead, behind, shift
        )
        while done < 7 and 8 * done + 9 <= high:
            first = 8 * done
            at = slice(first, first + 8)
            ahead, behind = height[first + 1 : first + 9], height[first - 1 : first + 7]
            new = velocities(here[1, at], here[2, at], height[at], ahead, behind, turning, shift)
            for v, field in enumerate((height[at],) + new):
                put_group(staged, field, eye, row_of(group_of(v, done)))
            done += 1
    odd = lax.axis_index("band") & 1
    to_first[...] = edges[1 - odd]
    to_second[...] = edges[odd]
    out[...] = staged[...].astype(BF16)


def outer_kernel(
    west_block, east_block, first_swap, second_swap, depth, *refs
):
    straight, cross, flux, height, staged, swapped = refs
    odd = lax.axis_index("band") & 1
    for side, block in enumerate((first_swap, second_swap)):
        swapped[side] = block[...]
    left, right = swapped.at[1 - odd], swapped.at[odd]
    members, latitudes = west_block.shape[2:]
    shift = difference(latitudes)
    turning = turning_row(latitudes)
    eye = identity(latitudes, BF16)

    def depths(first, count):
        return jnp.stack(
            [
                jnp.broadcast_to(depth[c : c + 1, :], (members, latitudes))
                for c in range(first, first + count)
            ]
        )

    def window(ens, edge, first, count, low, high):
        is_left = low == 0
        base = 2 if is_left else 0
        flux[base : base + count] = fluxes(ens[1, 0:count], depths(first, count))
        at = 0 if is_left else count
        near, far = (1, 0) if is_left else (at, at + 1)
        flux[near] = edge[2].astype(F32)
        flux[far] = edge[3].astype(F32)
        wide = high - low + 1
        skip = 0 if is_left else 1
        columns = slice(skip, skip + wide)
        new = heights(
            ens[0, columns],
            ens[2, columns],
            depths(first + skip, wide),
            flux[base + skip + 1 : base + skip + 1 + wide],
            flux[base + skip - 1 : base + skip - 1 + wide],
            shift,
        )
        start = 1 if is_left else 0
        height[start : start + wide] = new
        place = 0 if is_left else wide
        middle = near
        east_west = flux[middle + 1] - flux[middle - 1]
        raised = edge[0].astype(F32) - half_step * (east_west + rows_apart(edge[1], shift))
        height[place] = raised.astype(BF16)
        count = high - low
        here = height[1 : 1 + count]
        ahead, behind = height[2 : 2 + count], height[0:count]
        at = slice(low - first, high - first)
        return (here,) + velocities(ens[1, at], ens[2, at], here, ahead, behind, turning, shift)

    for v, field in enumerate(window(west_block, left, 0, 18, 0, 16)):
        for index in range(2):
            at = row_of(group_of(v, index)) - INNER
            put_group(staged, field[8 * index : 8 * index + 8], eye, at)
    ends = window(east_block, right, 54, 6, 56, 60)
    put_group(staged, jnp.concatenate([ends[0], ends[1]], axis=0), eye, 120)
    put_group(staged, jnp.concatenate([ends[2], jnp.zeros_like(ends[2])], axis=0), eye, 140)
    me = lax.axis_index("mem")
    for k, d in enumerate(CHIPS):
        straight[k] = staged[me ^ d].astype(BF16)
        cross[k] = staged[me ^ d ^ 1].astype(BF16)


def spread_block(source, held, wide, start, lane):
    spans = [slice(h * LANES, (h + 1) * LANES) for h in range(2)]
    count = source.shape[1]
    here = pl.ds(start, 16)
    blocks = exchange_lanes([[source[q, here, span] for span in spans] for q in range(8)], lane)
    for q in range(8):
        to = pl.ds(pl.multiple_of(q * count + start, 8), 16)
        for h in range(2):
            wide[h, to, :] = blocks[q][h].astype(F32)
            held[q, here, spans[h]] = blocks[q][h]


def spread_kernel(cells, got, held, seen, wide):
    lane = lax.broadcasted_iota(jnp.int32, (16, LANES), 1)

    def step(index, carry):
        spread_block(got, held, wide, pl.multiple_of(index * 16, 16), lane)
        return carry

    lax.fori_loop(0, INNER // 16, step, 0, unroll=4)
    slots = seen.shape[2]
    unroll = 16

    def pick(index, carry):
        for t in range(2):
            for k in range(unroll):
                slot = index * unroll + k
                row = cells[t, slot]
                for h in range(2):
                    seen[t, h, pl.ds(slot, 1), :] = wide[h, pl.ds(row, 1), :]
        return carry

    lax.fori_loop(0, slots // unroll, pick, 0)


def observe_kernel(cells, outer, weight, target, first, straight, cross, *refs):
    edges, (held, gram, to_first, to_second, joined, wide, seen) = refs[:3], refs[3:]
    wholes = []
    lane = lax.broadcasted_iota(jnp.int32, (16, LANES), 1)
    me = lax.axis_index("mem")
    for k, d in enumerate(CHIPS):
        joined[me ^ d, 0:OUTER, :] = straight[0] if k == 0 else edges[k - 1][0]
        joined[me ^ d ^ 1, 0:OUTER, :] = cross[0] if k == 0 else edges[k - 1][1]
    for index in range(OUTER // 16):
        spread_block(joined, held, wide, index * 16, lane)
    slots = first.shape[2]
    seen[:, :, 0:slots, :] = first[...]
    for t in range(2):

        def pick(index, carry):
            for k in range(8):
                slot = outer[t, index * 8 + k]
                row = cells[t, slot] - 8 * INNER
                for h in range(2):
                    seen[t, h, pl.ds(slot, 1), :] = wide[h, pl.ds(row, 1), :]
            return carry

        lax.fori_loop(0, (outer[t, slots + LANES - 1] + 7) // 8, pick, 0)
    eye = identity(256, BF16)
    for t in range(2):
        values = jnp.concatenate([seen[t, h, 0:slots] for h in range(2)], axis=1).astype(BF16)
        turned = dot_nt(eye, values)
        mean = jnp.sum(turned, axis=0, keepdims=True) * (1.0 / 256)
        root = weight[t : t + 1, :]
        spread = (root * (turned - mean)).astype(BF16)
        misfit = (root * (target[t : t + 1, :] - mean)).astype(BF16)
        block = dot_nt(spread, spread)
        pull = dot_nt(jnp.broadcast_to(misfit, (16, slots)), spread)
        whole = packed(block, pull[0:8])
        gram[t] = whole
        wholes.append(whole.astype(BF16))
    odd = (lax.axis_index("band") & 1) == 1
    to_first[...] = jnp.where(odd, wholes[0], wholes[1])
    to_second[...] = jnp.where(odd, wholes[1], wholes[0])


def combine_kernel(gram, first_swap, second_swap, line, short):
    odd = (lax.axis_index("band") & 1) == 1
    first, second = first_swap[...].astype(F32), second_swap[...].astype(F32)
    west, east = jnp.where(odd, first, second), jnp.where(odd, second, first)
    for t, beside in enumerate((west + gram[1], gram[0] + east)):
        total = gram[t] + neighbour_weight * beside
        line[t] = total
        short[t] = total.astype(BF16)


def prepare_kernel(inner, outer, *refs):
    average = jnp.full((256, LANES), 1.0 / 256, BF16)
    for q in range(8):
        pieces = (inner[q, 0:FIRST], jnp.concatenate([inner[q, FIRST:INNER], outer[q, 0:OUTER]], axis=0))
        for k, piece in enumerate(pieces):
            mean = dot_nn(piece, average)
            refs[2 * k + 1][q] = mean
            mean = jnp.concatenate([mean, mean], axis=1)
            refs[2 * k][q] = (piece.astype(F32) - mean).astype(BF16)


def send_back(results, outs):
    lane = lax.broadcasted_iota(jnp.int32, (16, LANES), 1)
    spans = [slice(h * LANES, (h + 1) * LANES) for h in range(2)]

    def step(index, carry):
        here = pl.ds(pl.multiple_of(index * 16, 16), 16)
        blocks = [[results[q, here, span] for span in spans] for q in range(8)]
        blocks = exchange_lanes(blocks, lane)
        for q in range(8):
            for h in range(2):
                outs[ORDER.index(q)][here, spans[h]] = blocks[q][h]
        return carry

    lax.fori_loop(0, results.shape[1] // 16, step, 0, unroll=4)


def apply_maps(anomaly, mean, maps, results, q, edge, order):
    count = results.shape[1]
    low, high = edge // 16 * 16, (edge + 15) // 16 * 16
    first = dot_nt(anomaly[q, 0:high], maps[order[0]])
    centre = jnp.concatenate([mean[q], mean[q]], axis=1)
    results[q, 0:low] = (centre[0:low] + first[0:low]).astype(BF16)
    if low == count:
        return
    second = dot_nt(anomaly[q, low:count], maps[order[1]])
    if low < high:
        near = lax.broadcasted_iota(jnp.int32, (16, 256), 0) < edge - low
        both = jnp.where(near, first[low:high], second[0:16])
        results[q, low:high] = (centre[low:high] + both).astype(BF16)
    results[q, high:count] = (centre[high:count] + second[high - low : count - low]).astype(BF16)


def second_kernel(maps, anomaly, mean, *refs):
    outs, results = refs[:8], refs[8]
    both = [maps[0], maps[1]]
    for q in range(8):
        apply_maps(anomaly, mean, both, results, q, 184, (0, 1))
    send_back(results, outs)


def analyse_kernel(line, below, above, anomaly, mean, *refs):
    outs, (kept, results, ordered) = refs[:8], refs[8:]
    size = 256
    eye = identity(size, F32)
    norms, pulls, roots, inverses = [], [], [], []
    for t in range(2):
        beside = below[t].astype(F32) + above[t].astype(F32)
        block, pull = unpacked(line[t] + neighbour_weight * beside)
        system = (size - 1) * eye + block
        square = jnp.sum(jnp.sum(system * system, axis=0, keepdims=True), axis=1, keepdims=True)
        norms.append(jnp.sqrt(square))
        pulls.append(pull)
        roots.append(system / norms[t])
    for sweep in range(SWEEPS):
        rights = [right_3(split(root)) for root in roots]
        if sweep == 0:
            inverses = [1.5 * eye - 0.5 * root for root in roots]
            lefts = [left_3(split(inverse)) for inverse in inverses]
            roots = [dot_nn(left, right) for left, right in zip(lefts, rights)]
            continue
        parts = [split(inverse) for inverse in inverses]
        products = [dot_nn(left_3(part), right) for part, right in zip(parts, rights)]
        middles = [left_3(split(1.5 * eye - 0.5 * product)) for product in products]
        if sweep < SWEEPS - 1:
            roots = [dot_nn(middle, right) for middle, right in zip(middles, rights)]
        inverses = [dot_nn(middle, right_3(part)) for middle, part in zip(middles, parts)]
    maps = []
    for t in range(2):
        right = right_3(split(inverses[t]))
        half_pull = dot_nn(left_3(split(pulls[t])), right)
        shift = dot_nn(left_3(split(half_pull)), right) / norms[t]
        scale = math.sqrt(size - 1) / jnp.sqrt(norms[t])
        ordered[t] = (inverses[t] * scale + shift[0:1]).astype(BF16).reshape(8, 32, size)
    me = lax.axis_index("mem")
    for t in range(2):
        maps.append(jnp.concatenate([ordered[t, me ^ d] for d in range(8)], axis=0))
        kept[t] = maps[t]
    for q in range(8):
        apply_maps(anomaly, mean, maps, results, q, 180 if q < 6 else FIRST, (1, 0))
    send_back(results, outs)


def spread_strips(got, wide):
    me = lax.axis_index("mem")
    for k, d in enumerate(ORDER):
        wide[me ^ d] = got[k][...].astype(F32)


def take_group(wide, turned, eye, g, shape, skipped=0):
    rows = shape[2] // 8
    at = row_of(g) - row_of(skipped)
    g = g - skipped
    for s in range(8):
        turned[g, rows * s : rows * (s + 1), :] = wide[s, at : at + rows, :]
    return dot_nt(eye, turned[g].astype(BF16)).astype(BF16).reshape(shape)


def first_return_kernel(*refs):
    got, (out, wide, turned, planes, sent) = refs[:8], refs[8:]
    shape = (8,) + planes.shape[2:]
    spread_strips(got, wide)
    eye = identity(256, BF16)
    copies = []
    for v in range(3):
        for index in range(3, 7):
            at = 8 * (index - 3)
            planes[v, at : at + 8] = take_group(wide, turned, eye, group_of(v, index), shape)
        copies.append(pltpu.make_async_copy(planes.at[v], out.at[v, pl.ds(24, 32)], sent.at[v]))
        copies[v].start()
    for copy in copies:
        copy.wait()


def second_return_kernel(*refs):
    got, (_, out, wide, turned, planes, sent) = refs[:8], refs[8:]
    shape = (8,) + planes.shape[2:]
    spread_strips(got, wide)
    eye = identity(256, BF16)
    mixed = take_group(wide, turned, eye, 21, shape, 12)
    planes[0, 24:28] = mixed[0:4]
    planes[1, 24:28] = mixed[4:8]
    planes[2, 24:28] = take_group(wide, turned, eye, 22, shape, 12)[0:4]
    copies = []
    for v in range(3):
        for index in range(3):
            at = 8 * index
            block = take_group(wide, turned, eye, group_of(v, index), shape, 12)
            planes[v, at : at + 8] = block
        for k, (at, to, count) in enumerate(((0, 0, 24), (24, 56, 4))):
            source, target = planes.at[v, pl.ds(at, count)], out.at[v, pl.ds(to, count)]
            copies.append(pltpu.make_async_copy(source, target, sent.at[2 * v + k]))
            copies[-1].start()
    for copy in copies:
        copy.wait()


def swapped_pairs(values, axis, pairs):
    moved = []
    for value, some in zip(values, pairs):
        both = some + [(j, i) for i, j in some]
        moved.append(lax.ppermute(value, axis, both))
    return moved


def band_swaps(first, second):
    count = lax.axis_size("band")
    starts = range(0, count, 2)
    pairs = [[(i, i + 1) for i in starts], [(i + 1, (i + 2) % count) for i in starts]]
    return swapped_pairs((first, second), "band", pairs)


def mem_swaps(value):
    count = lax.axis_size("mem")
    pairs = [[(i, i + 1) for i in range(k, count - 1, 2)] for k in range(2)]
    return swapped_pairs((value, value), "mem", pairs)


def across(value, difference):
    return lax.ppermute(value, "mem", [(i, i ^ difference) for i in range(8)])


def partners(values):
    return [across(value, d) if d else value for d, value in zip(ORDER, values)]


def swap(value):
    return lax.all_to_all(value, "mem", split_axis=0, concat_axis=0, tiled=True)


def cell_rows(cell):
    variable = cell // 600
    tile = jnp.arange(2, dtype=jnp.int32)[:, None]
    column = tile * 30 + cell // 20 % 30
    index = column // 8
    place = column % 8
    group = variable + jnp.where(index > 3, variable * 2 + index - 4, 18 - 3 * index)
    is_last = column >= 56
    group = jnp.where(is_last, 21 + variable // 2, group)
    place = jnp.where(is_last, column - 56 + 4 * (variable % 2), place)
    first = place * INNER + group * 20
    last = 8 * INNER + place * OUTER + (group - 15) * 20
    return jnp.where(group < 15, first, last) + cell % 20


def on_device_fast(
    ensemble, layer_depth, observed_cell, observed_value, error_variance, observed_count
):
    members, _, columns, latitudes = ensemble.shape
    slots = observed_cell.shape[2]
    planes = jnp.transpose(ensemble, (1, 2, 0, 3))
    edge = jax.ShapeDtypeStruct((4, members, latitudes), BF16)
    far = pl.BlockSpec(memory_space=pltpu.HBM)
    sent, to_first, to_second = pl.pallas_call(
        inner_kernel,
        out_shape=(jax.ShapeDtypeStruct((8, INNER, 256), BF16), edge, edge),
        in_specs=[far, far],
        scratch_shapes=[
            pltpu.VMEM(planes.shape, BF16),
            pltpu.VMEM((columns, latitudes), F32),
            pltpu.VMEM((columns, members, latitudes), F32),
            pltpu.VMEM((columns, members, latitudes), BF16),
            pltpu.VMEM((8, INNER, 256), F32),
            pltpu.VMEM((2, 4, members, latitudes), BF16),
            pltpu.SemaphoreType.DMA((6,)),
        ],
        compiler_params=params(60),
        name="inner",
    )(planes, layer_depth)
    got = swap(sent)
    swaps = band_swaps(to_first, to_second)
    flat = pl.BlockSpec((4, members, latitudes), lambda i: (0, 0, 0))
    straight, cross = pl.pallas_call(
        outer_kernel,
        grid=(1,),
        out_shape=(jax.ShapeDtypeStruct((4, OUTER, 256), BF16),) * 2,
        in_specs=[
            pl.BlockSpec((3, 20, members, latitudes), lambda i: (0, 0, 0, 0)),
            pl.BlockSpec((3, 6, members, latitudes), lambda i: (0, 9, 0, 0)),
            flat,
            flat,
            pl.BlockSpec((columns, latitudes), lambda i: (0, 0)),
        ],
        out_specs=(pl.BlockSpec((4, OUTER, 256), lambda i: (0, 0, 0)),) * 2,
        scratch_shapes=[
            pltpu.VMEM((20, members, latitudes), F32),
            pltpu.VMEM((18, members, latitudes), BF16),
            pltpu.VMEM((8, OUTER, 256), F32),
            pltpu.VMEM((2, 4, members, latitudes), BF16),
        ],
        compiler_params=params(24),
        name="outer",
    )(planes, planes, *swaps, layer_depth)
    cross = across(cross, 1)
    got_edges = [across(jnp.stack([straight[k], cross[k]]), CHIPS[k]) for k in (3, 1, 2)]
    got_edges = got_edges[1:] + got_edges[:1]

    rows = cell_rows(observed_cell[0])
    live = jnp.arange(slots, dtype=jnp.int32)[None, :] < observed_count[0][:, None]
    root = jnp.sqrt(jnp.where(live, 1.0 / error_variance[0], 0.0))
    vmem = pl.BlockSpec(memory_space=pltpu.VMEM)
    slot = jnp.arange(slots, dtype=jnp.int32)
    place = jnp.arange(slots + LANES, dtype=jnp.int32)
    is_outer = rows >= 8 * INNER
    near = jnp.where(is_outer, 0, rows)
    rank = jnp.sum(is_outer[:, None, :] & (slot[None, :] < slot[:, None])[None], axis=2)
    count = jnp.sum(is_outer, axis=1, keepdims=True)
    found = is_outer[:, None, :] & (rank[:, None, :] == place[None, :, None])
    outer = jnp.sum(jnp.where(found, slot, 0), axis=2)
    outer = jnp.where(place[None] < count, outer, slots)
    outer = jnp.where(place[None] == slots + LANES - 1, count, outer).astype(jnp.int32)
    rows = jnp.pad(rows, ((0, 0), (0, LANES)), constant_values=8 * INNER)
    smem = pl.BlockSpec(memory_space=pltpu.SMEM)
    held_inner, seen = pl.pallas_call(
        spread_kernel,
        out_shape=(
            jax.ShapeDtypeStruct((8, INNER, 256), BF16),
            jax.ShapeDtypeStruct((2, 2, slots, LANES), F32),
        ),
        in_specs=[smem, vmem],
        scratch_shapes=[pltpu.VMEM((2, 8 * INNER, LANES), F32)],
        compiler_params=params(12),
        cost_estimate=cost(1, 8 * MIB),
        name="spread",
    )(near, got)
    one_tile = jax.ShapeDtypeStruct((PACKED, 256), BF16)
    held_outer, gram, to_first, to_second = pl.pallas_call(
        observe_kernel,
        out_shape=(
            jax.ShapeDtypeStruct((8, OUTER, 256), BF16),
            jax.ShapeDtypeStruct((2, PACKED, 256), F32),
            one_tile,
            one_tile,
        ),
        in_specs=[smem, smem] + [vmem] * 8,
        scratch_shapes=[
            pltpu.VMEM((8, OUTER, 256), BF16),
            pltpu.VMEM((2, 8 * OUTER, LANES), F32),
            pltpu.VMEM((2, 2, slots + 8, LANES), F32),
        ],
        compiler_params=params(16),
        name="observe",
    )(rows, outer, root, observed_value[0], seen, straight, cross, *got_edges)
    anomaly_1, mean_1, anomaly_2, mean_2 = pl.pallas_call(
        prepare_kernel,
        out_shape=(
            jax.ShapeDtypeStruct((8, FIRST, 256), BF16),
            jax.ShapeDtypeStruct((8, FIRST, LANES), F32),
            jax.ShapeDtypeStruct((8, SECOND, 256), BF16),
            jax.ShapeDtypeStruct((8, SECOND, LANES), F32),
        ),
        compiler_params=params(12),
        cost_estimate=cost(1, 6 * MIB),
        name="prepare",
    )(held_inner, held_outer)

    line, short = pl.pallas_call(
        combine_kernel,
        out_shape=(
            jax.ShapeDtypeStruct(gram.shape, F32),
            jax.ShapeDtypeStruct(gram.shape, BF16),
        ),
        compiler_params=params(8),
        name="combine",
    )(gram, *band_swaps(to_first, to_second))
    below, above = mem_swaps(short)
    *back, maps = pl.pallas_call(
        analyse_kernel,
        out_shape=(jax.ShapeDtypeStruct((FIRST, 256), BF16),) * 8
        + (jax.ShapeDtypeStruct((2, 256, 256), BF16),),
        scratch_shapes=[pltpu.VMEM((8, FIRST, 256), BF16), pltpu.VMEM((2, 8, 32, 256), BF16)],
        compiler_params=params(20),
        name="analyse",
    )(line, below, above, anomaly_1, mean_1)
    first = partners(back)
    maps, first[4] = lax.optimization_barrier((maps, first[4]))
    back = pl.pallas_call(
        second_kernel,
        out_shape=(jax.ShapeDtypeStruct((SECOND, 256), BF16),) * 8,
        scratch_shapes=[pltpu.VMEM((8, SECOND, 256), BF16)],
        compiler_params=params(16),
        cost_estimate=cost(1, 6 * MIB),
        name="second",
    )(maps, anomaly_2, mean_2)
    second = partners(back)
    result = jax.ShapeDtypeStruct(planes.shape, BF16)
    half = pl.pallas_call(
        first_return_kernel,
        out_shape=result,
        out_specs=far,
        scratch_shapes=[
            pltpu.VMEM((8, FIRST, 256), F32),
            pltpu.VMEM((12, latitudes, 256), F32),
            pltpu.VMEM((3, 32, members, latitudes), BF16),
            pltpu.SemaphoreType.DMA((3,)),
        ],
        compiler_params=params(20),
        cost_estimate=cost(1, 4 * MIB),
        name="first_return",
    )(*first)
    planes = pl.pallas_call(
        second_return_kernel,
        out_shape=result,
        in_specs=[vmem] * 8 + [far],
        out_specs=far,
        scratch_shapes=[
            pltpu.VMEM((8, SECOND, 256), F32),
            pltpu.VMEM((11, latitudes, 256), F32),
            pltpu.VMEM((3, 28, members, latitudes), BF16),
            pltpu.SemaphoreType.DMA((6,)),
        ],
        input_output_aliases={8: 0},
        compiler_params=params(20),
        name="second_return",
    )(*second, half)
    return jnp.transpose(planes, (2, 0, 1, 3))


def choose(ensemble, layer_depth, observed_cell, *rest):
    mesh_shape = (lax.axis_size("mem"), lax.axis_size("band"))
    shape = (mesh_shape, ensemble.shape, observed_cell.shape[1])
    fits = shape == ((8, 4), (32, 3, 60, 160), 2) and observed_cell.shape[2] % 16 == 0
    chosen = on_device_fast if fits else on_device
    return chosen(ensemble, layer_depth, observed_cell, *rest)


def solution(mesh):
    in_specs = (
        P("mem", None, "band", None),
        P("band", None),
        P("mem", "band", None),
        P("mem", "band", None),
        P("mem", "band", None),
        P("mem", "band"),
    )
    out_specs = P("mem", None, "band", None)
    return jax.shard_map(
        choose, mesh=mesh, in_specs=in_specs, out_specs=out_specs, check_vma=False
    )
```

```python
import math

import jax
import jax.numpy as jnp
import numpy as np
from jax import lax
from jax.experimental import pallas as pl
from jax.experimental.pallas import tpu as pltpu
from jax.sharding import PartitionSpec as P

SWEEPS = 5


half_step = 0.1
coriolis_scale = 0.3
neighbour_weight = 0.75


def padded_2(cells, sides, width):
    for axis, dim in sides:
        count = lax.axis_size(axis)
        head = lax.slice_in_dim(cells, 0, width, axis=dim)
        tail = lax.slice_in_dim(cells, cells.shape[dim] - width, cells.shape[dim], axis=dim)
        cells = jnp.concatenate(
            [
                lax.ppermute(tail, axis, [(i, (i + 1) % count) for i in range(count)]),
                cells,
                lax.ppermute(head, axis, [((i + 1) % count, i) for i in range(count)]),
            ],
            axis=dim,
        )
    return cells


def north_south(source):
    widths = [(0, 0)] * (source.ndim - 1) + [(1, 1)]
    padded = jnp.pad(source, widths)
    return padded[..., 2:] - padded[..., :-2]


def coriolis(latitudes):
    position = jnp.arange(latitudes, dtype=jnp.float32)
    return coriolis_scale * jnp.sin(math.pi * ((position + 0.5) / latitudes - 0.5))


def newton_schulz(starting):
    identity = jnp.eye(starting.shape[-1], dtype=starting.dtype)
    root_part = starting
    inverse_root = jnp.broadcast_to(identity, starting.shape)
    for sweep_index in range(SWEEPS):
        product = jnp.einsum(
            "tij,tjk->tik", inverse_root, root_part, precision=lax.Precision.HIGHEST
        )
        middle = 1.5 * identity - 0.5 * product
        root_part = jnp.einsum("tij,tjk->tik", root_part, middle, precision=lax.Precision.HIGHEST)
        inverse_root = jnp.einsum(
            "tij,tjk->tik", middle, inverse_root, precision=lax.Precision.HIGHEST
        )
    return inverse_root


def on_device(ensemble, layer_depth, observed_cell, observed_value, error_variance, observed_count):
    block_members = ensemble.shape[0]
    columns = ensemble.shape[2]
    latitudes = ensemble.shape[3]
    strips = lax.axis_size("mem")
    members = block_members * strips
    strip_rows = latitudes // strips
    tile_count = observed_cell.shape[1]
    tile_columns = columns // tile_count
    slot_count = observed_cell.shape[2]
    tile_cells = 3 * tile_columns * strip_rows
    height = ensemble[:, 0].astype(jnp.float32)
    eastward = ensemble[:, 1].astype(jnp.float32)
    northward = ensemble[:, 2].astype(jnp.float32)
    turning = coriolis(latitudes)
    flux_east = (layer_depth * eastward).astype(jnp.bfloat16)
    flux_north = (layer_depth * northward).astype(jnp.bfloat16)
    east_margin = padded_2(flux_east, (("band", 1),), 1)
    east_west = east_margin[:, 2:].astype(jnp.float32) - east_margin[:, :-2].astype(jnp.float32)
    north_local = lax.optimization_barrier(flux_north).astype(jnp.float32)
    raised = height - half_step * (east_west + north_south(north_local))
    surface_elevation_cast = raised.astype(jnp.bfloat16)
    height_margin = padded_2(surface_elevation_cast, (("band", 1),), 1)
    margin_wide = height_margin.astype(jnp.float32)
    height_inner = margin_wide[:, 1:-1]
    revised_zonal_velocity = (
        eastward + turning * northward - half_step * (margin_wide[:, 2:] - margin_wide[:, :-2])
    )
    revised_meridional_velocity = (
        northward - turning * eastward - half_step * north_south(height_inner)
    )
    advance_dynamics = jnp.stack(
        [
            surface_elevation_cast,
            revised_zonal_velocity.astype(jnp.bfloat16),
            revised_meridional_velocity.astype(jnp.bfloat16),
        ],
        axis=1,
    )
    reordered = advance_dynamics.reshape(
        block_members, 3, tile_count, tile_columns, strips, strip_rows
    )
    reordered = jnp.transpose(reordered, (4, 2, 0, 1, 3, 5)).reshape(
        strips, tile_count, block_members, tile_cells
    )
    tile_block = lax.all_to_all(reordered, "mem", split_axis=0, concat_axis=2, tiled=True)[0]
    cells_here = observed_cell[0]
    values = jnp.take_along_axis(tile_block, cells_here[:, None, :], axis=2)
    observed_mean = jnp.sum(values, axis=1, dtype=jnp.float32) / members
    slot_index = jnp.arange(slot_count, dtype=jnp.int32)[None, :]
    live_slots = slot_index < observed_count[0][:, None]
    root_weight = jnp.sqrt(jnp.where(live_slots, 1.0 / error_variance[0], 0.0))
    spread = (
        root_weight[:, None, :] * (values.astype(jnp.float32) - observed_mean[:, None, :])
    ).astype(jnp.bfloat16)
    misfit = (root_weight * (observed_value[0] - observed_mean)).astype(jnp.bfloat16)
    spread_margin, misfit_margin = (
        padded_2(spread[None], (("mem", 0), ("band", 1)), 1),
        padded_2(misfit[None], (("mem", 0), ("band", 1)), 1),
    )
    gram_margin = jnp.einsum(
        "atko,atlo->atkl", spread_margin, spread_margin, preferred_element_type=jnp.float32
    )
    pull_margin = jnp.einsum(
        "atko,ato->atk", spread_margin, misfit_margin, preferred_element_type=jnp.float32
    )
    strip_here = lax.axis_index("mem")
    lower_valid = (strip_here > 0).astype(jnp.float32)
    upper_valid = (strip_here < strips - 1).astype(jnp.float32)
    strip_mask = (lower_valid, 1.0, upper_valid)
    total_gram = jnp.zeros((tile_count, members, members), jnp.float32)
    total_pull = jnp.zeros((tile_count, members), jnp.float32)
    for offset_lat in range(3):
        for offset_lon in range(3):
            factor = (
                neighbour_weight ** (abs(offset_lat - 1) + abs(offset_lon - 1))
                * strip_mask[offset_lat]
            )
            total_gram = (
                total_gram + factor * gram_margin[offset_lat, offset_lon : offset_lon + tile_count]
            )
            total_pull = (
                total_pull + factor * pull_margin[offset_lat, offset_lon : offset_lon + tile_count]
            )
    system = (members - 1) * jnp.eye(members, dtype=jnp.float32)[None] + total_gram
    frobenius = jnp.sqrt(jnp.sum(system * system, axis=(1, 2)))
    inverse_root = newton_schulz(system / frobenius[:, None, None])
    spread_map = inverse_root * (math.sqrt(members - 1) / jnp.sqrt(frobenius))[:, None, None]
    half_pull = jnp.einsum("tij,tj->ti", inverse_root, total_pull, precision=lax.Precision.HIGHEST)
    shift_weights = (
        jnp.einsum("tij,tj->ti", inverse_root, half_pull, precision=lax.Precision.HIGHEST)
        / frobenius[:, None]
    )
    weights = (spread_map + shift_weights[:, :, None]).astype(jnp.bfloat16)
    state_mean = jnp.sum(tile_block, axis=1, dtype=jnp.float32) / members
    anomaly = (tile_block.astype(jnp.float32) - state_mean[:, None, :]).astype(jnp.bfloat16)
    update = jnp.einsum("tjk,tjc->tkc", weights, anomaly, preferred_element_type=jnp.float32)
    analysed = (state_mean[:, None, :] + update).astype(jnp.bfloat16)
    returned = lax.all_to_all(analysed[None], "mem", split_axis=2, concat_axis=0, tiled=True)
    returned = returned.reshape(strips, tile_count, block_members, 3, tile_columns, strip_rows)
    return jnp.transpose(returned, (2, 3, 1, 4, 0, 5)).reshape(block_members, 3, columns, latitudes)


LANES = 128
GROUPS = 23
INNER = 304
OUTER = 152
FIRST = 240
SECOND = 216
F32 = jnp.float32
BF16 = jnp.bfloat16
PACKED = 136
CHIPS = (0, 2, 4, 6)
ORDER = (6, 2, 4, 7, 1, 3, 5, 0)
MIB = 1024 * 1024


def params(size):
    return pltpu.CompilerParams(vmem_limit_bytes=size * MIB)


def cost(flops, moved):
    return pl.CostEstimate(flops=flops, bytes_accessed=moved, transcendentals=0)


def identity(size, dtype):
    row = lax.broadcasted_iota(jnp.int32, (size, size), 0)
    column = lax.broadcasted_iota(jnp.int32, (size, size), 1)
    return (row == column).astype(F32).astype(dtype)


def dot_nt(left, right):
    return lax.dot_general(left, right, (((1,), (1,)), ((), ())), preferred_element_type=F32)


def dot_nn(left, right):
    return lax.dot_general(left, right, (((1,), (0,)), ((), ())), preferred_element_type=F32)


def split(value):
    high = value.astype(BF16)
    return high, (value - high.astype(F32)).astype(BF16)


def left_3(parts):
    return jnp.concatenate([parts[0], parts[0], parts[1]], axis=1)


def right_3(parts):
    return jnp.concatenate([parts[0], parts[1], parts[0]], axis=0)


def triangle(size):
    row = lax.broadcasted_iota(jnp.int32, (size, size), 0)
    column = lax.broadcasted_iota(jnp.int32, (size, size), 1)
    return row, column


def packed(block, pull):
    row, column = triangle(128)
    last = block[128:256, 128:256]
    corner = jnp.where(row >= column, block[0:128, 0:128], last)
    middle = jnp.sum(jnp.where(row == column, last, 0.0), axis=0, keepdims=True)
    middle = jnp.concatenate([jnp.zeros_like(middle), middle], axis=1)
    top = jnp.concatenate([block[128:256, 0:128], corner], axis=1)
    tail = jnp.where(lax.broadcasted_iota(jnp.int32, (8, 256), 0) == 0, pull, middle)
    return jnp.concatenate([top, tail], axis=0)


def unpacked(value):
    row, column = triangle(128)
    low, corner = value[0:128, 0:128], value[0:128, 128:256]
    other = jnp.transpose(corner)
    first = jnp.where(row >= column, corner, other)
    last = jnp.where(row < column, corner, other)
    last = jnp.where(row == column, value[129:130, 128:256], last)
    top = jnp.concatenate([first, jnp.transpose(low)], axis=1)
    return jnp.concatenate([top, jnp.concatenate([low, last], axis=1)], axis=0), value[128:136]


def exchange_lanes(blocks, lane):
    blocks = [list(pair) for pair in blocks]
    for q in range(4):
        low, high = blocks[q], blocks[q + 4]
        blocks[q], blocks[q + 4] = [low[0], high[0]], [low[1], high[1]]
    for bit in range(2):
        step = 32 << bit
        odd = (lane & step) != 0
        for q in range(8):
            if q & (1 << bit):
                continue
            for h in range(2):
                low, high = blocks[q][h], blocks[q | (1 << bit)][h]
                blocks[q][h] = jnp.where(odd, pltpu.roll(high, step, 1), low)
                blocks[q | (1 << bit)][h] = jnp.where(odd, high, pltpu.roll(low, LANES - step, 1))
    return blocks


def group_of(variable, index):
    return variable + (variable * 2 + index - 4 if index > 3 else 18 - 3 * index)


def row_of(group):
    return 20 * group + (4 if group >= 15 else 0)


def difference(latitudes):
    source = lax.broadcasted_iota(jnp.int32, (latitudes, latitudes), 0)
    target = lax.broadcasted_iota(jnp.int32, (latitudes, latitudes), 1)
    shift = (source == target + 1).astype(F32) - (source == target - 1).astype(F32)
    return shift.astype(BF16)


def rows_apart(value, shift):
    flat = value.reshape(-1, value.shape[-1])
    return dot_nn(flat, shift).reshape(value.shape)


def fluxes(east, deep):
    return (deep * east.astype(F32)).astype(BF16).astype(F32)


def heights(field, north, deep, ahead, behind, shift):
    flux_north = (deep * north.astype(F32)).astype(BF16)
    raised = field.astype(F32) - half_step * ((ahead - behind) + rows_apart(flux_north, shift))
    return raised.astype(BF16)


def velocities(east, north, here, ahead, behind, turning, shift):
    east, north = east.astype(F32), north.astype(F32)
    apart = ahead.astype(F32) - behind.astype(F32)
    new_east = east + turning * north - half_step * apart
    new_north = north - turning * east - half_step * rows_apart(here, shift)
    return new_east.astype(BF16), new_north.astype(BF16)


def put_group(staged, block, eye, first):
    latitudes = eye.shape[0]
    rows = latitudes // 8
    turned = dot_nt(eye, block.reshape(256, latitudes))
    for s in range(8):
        staged[s, first : first + rows, :] = turned[rows * s : rows * (s + 1)]


def turning_row(latitudes):
    position = lax.broadcasted_iota(jnp.int32, (8, latitudes), 1).astype(F32)
    turning = coriolis_scale * jnp.sin(math.pi * ((position + 0.5) / latitudes - 0.5))
    return turning[0:1, :][None]


def inner_kernel(
    ens, depth, out, to_first, to_second, here, deep, flux, height, staged, edges, arrived
):
    columns, members, latitudes = here.shape[1:]
    batch = columns // 5
    pieces = [pltpu.make_async_copy(depth, deep, arrived.at[5])]
    for k in range(5):
        span = pl.ds(k * batch, batch)
        piece = pltpu.make_async_copy(ens.at[:, span], here.at[:, span], arrived.at[k])
        pieces.append(piece)
    for piece in pieces:
        piece.start()
    shift = difference(latitudes)
    turning = turning_row(latitudes)
    eye = identity(latitudes, BF16)
    pieces[0].wait()

    def depths(first, count):
        rows = [deep[c : c + 1, :] for c in range(first, first + count)]
        return jnp.stack([jnp.broadcast_to(row, (members, latitudes)) for row in rows])

    def edge(side, near, far):
        edges[side, 0] = here[0, near]
        edges[side, 1] = (deep[near : near + 1, :] * here[2, near].astype(F32)).astype(BF16)
        edges[side, 2] = flux[near].astype(BF16)
        edges[side, 3] = flux[far].astype(BF16)

    staged[:, 300:INNER, :] = jnp.zeros((8, INNER - 300, 256), F32)
    done = 2
    for k in range(5):
        pieces[k + 1].wait()
        first, count = k * batch, batch if k else 2
        flux[first : first + count] = fluxes(here[1, first : first + count], depths(first, count))
        if k == 0:
            edge(0, 0, 1)
            continue
        if k == 4:
            edge(1, columns - 1, columns - 2)
        low, high = max(first - 1, batch + 1), first + batch - 1
        at = slice(low, high)
        ahead, behind = flux[low + 1 : high + 1], flux[low - 1 : high - 1]
        height[at] = heights(
            here[0, at], here[2, at], depths(low, high - low), ahead, behind, shift
        )
        while done < 7 and 8 * done + 9 <= high:
            first = 8 * done
            at = slice(first, first + 8)
            ahead, behind = height[first + 1 : first + 9], height[first - 1 : first + 7]
            new = velocities(here[1, at], here[2, at], height[at], ahead, behind, turning, shift)
            for v, field in enumerate((height[at],) + new):
                put_group(staged, field, eye, row_of(group_of(v, done)))
            done += 1
    odd = lax.axis_index("band") & 1
    to_first[...] = edges[1 - odd]
    to_second[...] = edges[odd]
    out[...] = staged[...].astype(BF16)


def outer_kernel(
    west_block, east_block, first_swap, second_swap, depth, *refs
):
    straight, cross, flux, height, staged, swapped = refs
    odd = lax.axis_index("band") & 1
    for side, block in enumerate((first_swap, second_swap)):
        swapped[side] = block[...]
    left, right = swapped.at[1 - odd], swapped.at[odd]
    members, latitudes = west_block.shape[2:]
    shift = difference(latitudes)
    turning = turning_row(latitudes)
    eye = identity(latitudes, BF16)

    def depths(first, count):
        return jnp.stack(
            [
                jnp.broadcast_to(depth[c : c + 1, :], (members, latitudes))
                for c in range(first, first + count)
            ]
        )

    def window(ens, edge, first, count, low, high):
        is_left = low == 0
        base = 2 if is_left else 0
        flux[base : base + count] = fluxes(ens[1, 0:count], depths(first, count))
        at = 0 if is_left else count
        near, far = (1, 0) if is_left else (at, at + 1)
        flux[near] = edge[2].astype(F32)
        flux[far] = edge[3].astype(F32)
        wide = high - low + 1
        skip = 0 if is_left else 1
        columns = slice(skip, skip + wide)
        new = heights(
            ens[0, columns],
            ens[2, columns],
            depths(first + skip, wide),
            flux[base + skip + 1 : base + skip + 1 + wide],
            flux[base + skip - 1 : base + skip - 1 + wide],
            shift,
        )
        start = 1 if is_left else 0
        height[start : start + wide] = new
        place = 0 if is_left else wide
        middle = near
        east_west = flux[middle + 1] - flux[middle - 1]
        raised = edge[0].astype(F32) - half_step * (east_west + rows_apart(edge[1], shift))
        height[place] = raised.astype(BF16)
        count = high - low
        here = height[1 : 1 + count]
        ahead, behind = height[2 : 2 + count], height[0:count]
        at = slice(low - first, high - first)
        return (here,) + velocities(ens[1, at], ens[2, at], here, ahead, behind, turning, shift)

    for v, field in enumerate(window(west_block, left, 0, 18, 0, 16)):
        for index in range(2):
            at = row_of(group_of(v, index)) - INNER
            put_group(staged, field[8 * index : 8 * index + 8], eye, at)
    ends = window(east_block, right, 54, 6, 56, 60)
    put_group(staged, jnp.concatenate([ends[0], ends[1]], axis=0), eye, 120)
    block = jnp.concatenate([ends[2], ends[2]], axis=0).reshape(256, latitudes)
    turned = dot_nt(eye, block)
    lower = lax.broadcasted_iota(jnp.int32, (10, 256), 1) < LANES
    for s in range(8):
        rows = [turned[20 * s + 10 * k : 20 * s + 10 * k + 10] for k in range(2)]
        staged[s, 140:150, :] = jnp.where(lower, rows[0], rows[1])
    staged[:, 150:OUTER, :] = jnp.zeros((8, OUTER - 150, 256), F32)
    me = lax.axis_index("mem")
    for k, d in enumerate(CHIPS):
        straight[k] = staged[me ^ d].astype(BF16)
        cross[k] = staged[me ^ d ^ 1].astype(BF16)


def spread_block(source, held, wide, start, lane):
    spans = [slice(h * LANES, (h + 1) * LANES) for h in range(2)]
    count = source.shape[1]
    here = pl.ds(start, 16)
    blocks = exchange_lanes([[source[q, here, span] for span in spans] for q in range(8)], lane)
    for q in range(8):
        to = pl.ds(pl.multiple_of(q * count + start, 8), 16)
        for h in range(2):
            wide[h, to, :] = blocks[q][h].astype(F32)
            held[q, here, spans[h]] = blocks[q][h]


def spread_kernel(cells, got, held, seen, wide):
    lane = lax.broadcasted_iota(jnp.int32, (16, LANES), 1)

    def step(index, carry):
        spread_block(got, held, wide, pl.multiple_of(index * 16, 16), lane)
        return carry

    lax.fori_loop(0, INNER // 16, step, 0, unroll=4)
    slots = seen.shape[2]
    unroll = 16

    def pick(index, carry):
        for t in range(2):
            for k in range(unroll):
                slot = index * unroll + k
                row = cells[t, slot]
                for h in range(2):
                    seen[t, h, pl.ds(slot, 1), :] = wide[h, pl.ds(row, 1), :]
        return carry

    lax.fori_loop(0, slots // unroll, pick, 0)


def observe_kernel(cells, outer, weight, target, first, straight, cross, *refs):
    edges, (held, gram, to_first, to_second, joined, wide, seen) = refs[:3], refs[3:]
    wholes = []
    lane = lax.broadcasted_iota(jnp.int32, (16, LANES), 1)
    me = lax.axis_index("mem")
    for k, d in enumerate(CHIPS):
        joined[me ^ d, 0:OUTER, :] = straight[0] if k == 0 else edges[k - 1][0]
        joined[me ^ d ^ 1, 0:OUTER, :] = cross[0] if k == 0 else edges[k - 1][1]
    for start in (*range(0, OUTER - 16, 16), OUTER - 16):
        spread_block(joined, held, wide, start, lane)
    slots = first.shape[2]
    seen[:, :, 0:slots, :] = first[...]
    for t in range(2):

        def pick(index, carry):
            for k in range(8):
                slot = outer[t, index * 8 + k]
                row = cells[t, slot] - 8 * INNER
                for h in range(2):
                    seen[t, h, pl.ds(slot, 1), :] = wide[h, pl.ds(row, 1), :]
            return carry

        lax.fori_loop(0, (outer[t, slots + LANES - 1] + 7) // 8, pick, 0)
    eye = identity(256, BF16)
    for t in range(2):
        values = jnp.concatenate([seen[t, h, 0:slots] for h in range(2)], axis=1).astype(BF16)
        turned = dot_nt(eye, values)
        mean = jnp.sum(turned, axis=0, keepdims=True) * (1.0 / 256)
        root = weight[t : t + 1, :]
        spread = (root * (turned - mean)).astype(BF16)
        misfit = (root * (target[t : t + 1, :] - mean)).astype(BF16)
        block = dot_nt(spread, spread)
        pull = dot_nt(jnp.broadcast_to(misfit, (16, slots)), spread)
        whole = packed(block, pull[0:8])
        gram[t] = whole
        wholes.append(whole.astype(BF16))
    odd = (lax.axis_index("band") & 1) == 1
    to_first[...] = jnp.where(odd, wholes[0], wholes[1])
    to_second[...] = jnp.where(odd, wholes[1], wholes[0])


def combine_kernel(gram, first_swap, second_swap, line, short):
    odd = (lax.axis_index("band") & 1) == 1
    first, second = first_swap[...].astype(F32), second_swap[...].astype(F32)
    west, east = jnp.where(odd, first, second), jnp.where(odd, second, first)
    for t, beside in enumerate((west + gram[1], gram[0] + east)):
        total = gram[t] + neighbour_weight * beside
        line[t] = total
        short[t] = total.astype(BF16)


def prepare_kernel(inner, outer, *refs):
    average = jnp.full((256, LANES), 1.0 / 256, BF16)
    for q in range(8):
        pieces = (inner[q, 0:FIRST], jnp.concatenate([inner[q, FIRST:INNER], outer[q, 0:OUTER]], axis=0))
        for k, piece in enumerate(pieces):
            mean = dot_nn(piece, average)
            refs[2 * k + 1][q] = mean
            mean = jnp.concatenate([mean, mean], axis=1)
            refs[2 * k][q] = (piece.astype(F32) - mean).astype(BF16)


def send_back(results, outs):
    lane = lax.broadcasted_iota(jnp.int32, (16, LANES), 1)
    spans = [slice(h * LANES, (h + 1) * LANES) for h in range(2)]

    def move(start):
        here = pl.ds(start, 16)
        blocks = [[results[q, here, span] for span in spans] for q in range(8)]
        blocks = exchange_lanes(blocks, lane)
        for q in range(8):
            for h in range(2):
                outs[ORDER.index(q)][here, spans[h]] = blocks[q][h]

    def step(index, carry):
        move(pl.multiple_of(index * 16, 16))
        return carry

    count = results.shape[1]
    lax.fori_loop(0, count // 16, step, 0, unroll=4)
    if count % 16:
        move(count - 16)


def apply_maps(anomaly, mean, maps, results, q, edge, order):
    count = results.shape[1]
    low, high = edge // 16 * 16, (edge + 15) // 16 * 16
    first = dot_nt(anomaly[q, 0:high], maps[order[0]])
    centre = jnp.concatenate([mean[q], mean[q]], axis=1)
    results[q, 0:low] = (centre[0:low] + first[0:low]).astype(BF16)
    if low == count:
        return
    second = dot_nt(anomaly[q, low:count], maps[order[1]])
    if low < high:
        near = lax.broadcasted_iota(jnp.int32, (16, 256), 0) < edge - low
        both = jnp.where(near, first[low:high], second[0:16])
        results[q, low:high] = (centre[low:high] + both).astype(BF16)
    results[q, high:count] = (centre[high:count] + second[high - low : count - low]).astype(BF16)


def second_kernel(maps, anomaly, mean, *refs):
    outs, results = refs[:8], refs[8]
    both = [maps[0], maps[1]]
    for q in range(8):
        apply_maps(anomaly, mean, both, results, q, 184, (0, 1))
    send_back(results, outs)


def analyse_kernel(line, below, above, anomaly, mean, *refs):
    outs, (kept, results, ordered) = refs[:8], refs[8:]
    size = 256
    eye = identity(size, F32)
    norms, pulls, roots, inverses = [], [], [], []
    for t in range(2):
        beside = below[t].astype(F32) + above[t].astype(F32)
        block, pull = unpacked(line[t] + neighbour_weight * beside)
        system = (size - 1) * eye + block
        square = jnp.sum(jnp.sum(system * system, axis=0, keepdims=True), axis=1, keepdims=True)
        norms.append(jnp.sqrt(square))
        pulls.append(pull)
        roots.append(system / norms[t])
    for sweep in range(SWEEPS):
        rights = [right_3(split(root)) for root in roots]
        if sweep == 0:
            inverses = [1.5 * eye - 0.5 * root for root in roots]
            lefts = [left_3(split(inverse)) for inverse in inverses]
            roots = [dot_nn(left, right) for left, right in zip(lefts, rights)]
            continue
        parts = [split(inverse) for inverse in inverses]
        products = [dot_nn(left_3(part), right) for part, right in zip(parts, rights)]
        middles = [left_3(split(1.5 * eye - 0.5 * product)) for product in products]
        if sweep < SWEEPS - 1:
            roots = [dot_nn(middle, right) for middle, right in zip(middles, rights)]
        inverses = [dot_nn(middle, right_3(part)) for middle, part in zip(middles, parts)]
    maps = []
    for t in range(2):
        right = right_3(split(inverses[t]))
        half_pull = dot_nn(left_3(split(pulls[t])), right)
        shift = dot_nn(left_3(split(half_pull)), right) / norms[t]
        scale = math.sqrt(size - 1) / jnp.sqrt(norms[t])
        ordered[t] = (inverses[t] * scale + shift[0:1]).astype(BF16).reshape(8, 32, size)
    me = lax.axis_index("mem")
    for t in range(2):
        maps.append(jnp.concatenate([ordered[t, me ^ d] for d in range(8)], axis=0))
        kept[t] = maps[t]
    for q in range(8):
        apply_maps(anomaly, mean, maps, results, q, 180 if q < 6 else FIRST, (1, 0))
    send_back(results, outs)


def spread_strips(got, wide):
    me = lax.axis_index("mem")
    for k, d in enumerate(ORDER):
        wide[me ^ d] = got[k][...].astype(F32)


def take_group(wide, turned, eye, g, shape, skipped=0):
    rows = shape[2] // 8
    at = row_of(g) - row_of(skipped)
    g = g - skipped
    for s in range(8):
        turned[g, rows * s : rows * (s + 1), :] = wide[s, at : at + rows, :]
    return dot_nt(eye, turned[g].astype(BF16)).astype(BF16).reshape(shape)


def first_return_kernel(*refs):
    got, (out, wide, turned, planes, sent) = refs[:8], refs[8:]
    shape = (8,) + planes.shape[2:]
    spread_strips(got, wide)
    eye = identity(256, BF16)
    copies = []
    for v in range(3):
        for index in range(3, 7):
            at = 8 * (index - 3)
            planes[v, at : at + 8] = take_group(wide, turned, eye, group_of(v, index), shape)
        copies.append(pltpu.make_async_copy(planes.at[v], out.at[v, pl.ds(24, 32)], sent.at[v]))
        copies[v].start()
    for copy in copies:
        copy.wait()


def second_return_kernel(*refs):
    got, (_, out, wide, turned, planes, sent) = refs[:8], refs[8:]
    shape = (8,) + planes.shape[2:]
    spread_strips(got, wide)
    eye = identity(256, BF16)
    mixed = take_group(wide, turned, eye, 21, shape, 12)
    planes[0, 24:28] = mixed[0:4]
    planes[1, 24:28] = mixed[4:8]
    at = row_of(22) - row_of(12)
    turned[10] = jnp.zeros(turned.shape[1:], F32)
    for s in range(8):
        for k in range(2):
            to = 20 * s + 10 * k
            half = wide[s, at : at + 10, k * LANES : (k + 1) * LANES]
            turned[10, to : to + 10, 0:LANES] = half
    block = dot_nt(eye, turned[10].astype(BF16)).astype(BF16).reshape(shape)
    planes[2, 24:28] = block[0:4]
    copies = []
    for v in range(3):
        for index in range(3):
            at = 8 * index
            block = take_group(wide, turned, eye, group_of(v, index), shape, 12)
            planes[v, at : at + 8] = block
        for k, (at, to, count) in enumerate(((0, 0, 24), (24, 56, 4))):
            source, target = planes.at[v, pl.ds(at, count)], out.at[v, pl.ds(to, count)]
            copies.append(pltpu.make_async_copy(source, target, sent.at[2 * v + k]))
            copies[-1].start()
    for copy in copies:
        copy.wait()


def swapped_pairs(values, axis, pairs):
    moved = []
    for value, some in zip(values, pairs):
        both = some + [(j, i) for i, j in some]
        moved.append(lax.ppermute(value, axis, both))
    return moved


def band_swaps(first, second):
    count = lax.axis_size("band")
    starts = range(0, count, 2)
    pairs = [[(i, i + 1) for i in starts], [(i + 1, (i + 2) % count) for i in starts]]
    return swapped_pairs((first, second), "band", pairs)


def mem_swaps(value):
    count = lax.axis_size("mem")
    pairs = [[(i, i + 1) for i in range(k, count - 1, 2)] for k in range(2)]
    return swapped_pairs((value, value), "mem", pairs)


def across(value, difference):
    return lax.ppermute(value, "mem", [(i, i ^ difference) for i in range(8)])


def partners(values):
    return [across(value, d) if d else value for d, value in zip(ORDER, values)]


def swap(value):
    return lax.all_to_all(value, "mem", split_axis=0, concat_axis=0, tiled=True)


def cell_rows(cell):
    variable = cell // 600
    tile = jnp.arange(2, dtype=jnp.int32)[:, None]
    column = tile * 30 + cell // 20 % 30
    index = column // 8
    place = column % 8
    group = variable + jnp.where(index > 3, variable * 2 + index - 4, 18 - 3 * index)
    is_last = column >= 56
    group = jnp.where(is_last, 21 + variable // 2, group)
    place = jnp.where(is_last, column - 56 + 4 * (variable % 2), place)
    row = cell % 20
    place = jnp.where(group == 22, place + 4 * (row // 10), place)
    row = jnp.where(group == 22, row % 10, row)
    first = place * INNER + group * 20
    last = 8 * INNER + place * OUTER + (group - 15) * 20
    return jnp.where(group < 15, first, last) + row


def on_device_fast(
    ensemble, layer_depth, observed_cell, observed_value, error_variance, observed_count
):
    members, _, columns, latitudes = ensemble.shape
    slots = observed_cell.shape[2]
    planes = jnp.transpose(ensemble, (1, 2, 0, 3))
    edge = jax.ShapeDtypeStruct((4, members, latitudes), BF16)
    far = pl.BlockSpec(memory_space=pltpu.HBM)
    sent, to_first, to_second = pl.pallas_call(
        inner_kernel,
        out_shape=(jax.ShapeDtypeStruct((8, INNER, 256), BF16), edge, edge),
        in_specs=[far, far],
        scratch_shapes=[
            pltpu.VMEM(planes.shape, BF16),
            pltpu.VMEM((columns, latitudes), F32),
            pltpu.VMEM((columns, members, latitudes), F32),
            pltpu.VMEM((columns, members, latitudes), BF16),
            pltpu.VMEM((8, INNER, 256), F32),
            pltpu.VMEM((2, 4, members, latitudes), BF16),
            pltpu.SemaphoreType.DMA((6,)),
        ],
        compiler_params=params(60),
        name="inner",
    )(planes, layer_depth)
    got = swap(sent)
    swaps = band_swaps(to_first, to_second)
    flat = pl.BlockSpec((4, members, latitudes), lambda i: (0, 0, 0))
    straight, cross = pl.pallas_call(
        outer_kernel,
        grid=(1,),
        out_shape=(jax.ShapeDtypeStruct((4, OUTER, 256), BF16),) * 2,
        in_specs=[
            pl.BlockSpec((3, 20, members, latitudes), lambda i: (0, 0, 0, 0)),
            pl.BlockSpec((3, 6, members, latitudes), lambda i: (0, 9, 0, 0)),
            flat,
            flat,
            pl.BlockSpec((columns, latitudes), lambda i: (0, 0)),
        ],
        out_specs=(pl.BlockSpec((4, OUTER, 256), lambda i: (0, 0, 0)),) * 2,
        scratch_shapes=[
            pltpu.VMEM((20, members, latitudes), F32),
            pltpu.VMEM((18, members, latitudes), BF16),
            pltpu.VMEM((8, OUTER, 256), F32),
            pltpu.VMEM((2, 4, members, latitudes), BF16),
        ],
        compiler_params=params(24),
        name="outer",
    )(planes, planes, *swaps, layer_depth)
    cross = across(cross, 1)
    got_edges = [across(jnp.stack([straight[k], cross[k]]), CHIPS[k]) for k in (3, 1, 2)]
    got_edges = got_edges[1:] + got_edges[:1]

    rows = cell_rows(observed_cell[0])
    live = jnp.arange(slots, dtype=jnp.int32)[None, :] < observed_count[0][:, None]
    root = jnp.sqrt(jnp.where(live, 1.0 / error_variance[0], 0.0))
    vmem = pl.BlockSpec(memory_space=pltpu.VMEM)
    slot = jnp.arange(slots, dtype=jnp.int32)
    place = jnp.arange(slots + LANES, dtype=jnp.int32)
    is_outer = rows >= 8 * INNER
    near = jnp.where(is_outer, 0, rows)
    rank = jnp.sum(is_outer[:, None, :] & (slot[None, :] < slot[:, None])[None], axis=2)
    count = jnp.sum(is_outer, axis=1, keepdims=True)
    found = is_outer[:, None, :] & (rank[:, None, :] == place[None, :, None])
    outer = jnp.sum(jnp.where(found, slot, 0), axis=2)
    outer = jnp.where(place[None] < count, outer, slots)
    outer = jnp.where(place[None] == slots + LANES - 1, count, outer).astype(jnp.int32)
    rows = jnp.pad(rows, ((0, 0), (0, LANES)), constant_values=8 * INNER)
    smem = pl.BlockSpec(memory_space=pltpu.SMEM)
    held_inner, seen = pl.pallas_call(
        spread_kernel,
        out_shape=(
            jax.ShapeDtypeStruct((8, INNER, 256), BF16),
            jax.ShapeDtypeStruct((2, 2, slots, LANES), F32),
        ),
        in_specs=[smem, vmem],
        scratch_shapes=[pltpu.VMEM((2, 8 * INNER, LANES), F32)],
        compiler_params=params(12),
        cost_estimate=cost(1, 8 * MIB),
        name="spread",
    )(near, got)
    one_tile = jax.ShapeDtypeStruct((PACKED, 256), BF16)
    held_outer, gram, to_first, to_second = pl.pallas_call(
        observe_kernel,
        out_shape=(
            jax.ShapeDtypeStruct((8, OUTER, 256), BF16),
            jax.ShapeDtypeStruct((2, PACKED, 256), F32),
            one_tile,
            one_tile,
        ),
        in_specs=[smem, smem] + [vmem] * 8,
        scratch_shapes=[
            pltpu.VMEM((8, OUTER, 256), BF16),
            pltpu.VMEM((2, 8 * OUTER, LANES), F32),
            pltpu.VMEM((2, 2, slots + 8, LANES), F32),
        ],
        compiler_params=params(16),
        name="observe",
    )(rows, outer, root, observed_value[0], seen, straight, cross, *got_edges)
    anomaly_1, mean_1, anomaly_2, mean_2 = pl.pallas_call(
        prepare_kernel,
        out_shape=(
            jax.ShapeDtypeStruct((8, FIRST, 256), BF16),
            jax.ShapeDtypeStruct((8, FIRST, LANES), F32),
            jax.ShapeDtypeStruct((8, SECOND, 256), BF16),
            jax.ShapeDtypeStruct((8, SECOND, LANES), F32),
        ),
        compiler_params=params(12),
        cost_estimate=cost(1, 6 * MIB),
        name="prepare",
    )(held_inner, held_outer)

    line, short = pl.pallas_call(
        combine_kernel,
        out_shape=(
            jax.ShapeDtypeStruct(gram.shape, F32),
            jax.ShapeDtypeStruct(gram.shape, BF16),
        ),
        compiler_params=params(8),
        name="combine",
    )(gram, *band_swaps(to_first, to_second))
    below, above = mem_swaps(short)
    *back, maps = pl.pallas_call(
        analyse_kernel,
        out_shape=(jax.ShapeDtypeStruct((FIRST, 256), BF16),) * 8
        + (jax.ShapeDtypeStruct((2, 256, 256), BF16),),
        scratch_shapes=[pltpu.VMEM((8, FIRST, 256), BF16), pltpu.VMEM((2, 8, 32, 256), BF16)],
        compiler_params=params(20),
        name="analyse",
    )(line, below, above, anomaly_1, mean_1)
    first = partners(back)
    maps, first[4] = lax.optimization_barrier((maps, first[4]))
    back = pl.pallas_call(
        second_kernel,
        out_shape=(jax.ShapeDtypeStruct((SECOND, 256), BF16),) * 8,
        scratch_shapes=[pltpu.VMEM((8, SECOND, 256), BF16)],
        compiler_params=params(16),
        cost_estimate=cost(1, 6 * MIB),
        name="second",
    )(maps, anomaly_2, mean_2)
    second = partners(back)
    result = jax.ShapeDtypeStruct(planes.shape, BF16)
    half = pl.pallas_call(
        first_return_kernel,
        out_shape=result,
        out_specs=far,
        scratch_shapes=[
            pltpu.VMEM((8, FIRST, 256), F32),
            pltpu.VMEM((12, latitudes, 256), F32),
            pltpu.VMEM((3, 32, members, latitudes), BF16),
            pltpu.SemaphoreType.DMA((3,)),
        ],
        compiler_params=params(20),
        cost_estimate=cost(1, 4 * MIB),
        name="first_return",
    )(*first)
    planes = pl.pallas_call(
        second_return_kernel,
        out_shape=result,
        in_specs=[vmem] * 8 + [far],
        out_specs=far,
        scratch_shapes=[
            pltpu.VMEM((8, SECOND, 256), F32),
            pltpu.VMEM((11, latitudes, 256), F32),
            pltpu.VMEM((3, 28, members, latitudes), BF16),
            pltpu.SemaphoreType.DMA((6,)),
        ],
        input_output_aliases={8: 0},
        compiler_params=params(20),
        name="second_return",
    )(*second, half)
    return jnp.transpose(planes, (2, 0, 1, 3))


def choose(ensemble, layer_depth, observed_cell, *rest):
    mesh_shape = (lax.axis_size("mem"), lax.axis_size("band"))
    shape = (mesh_shape, ensemble.shape, observed_cell.shape[1])
    fits = shape == ((8, 4), (32, 3, 60, 160), 2) and observed_cell.shape[2] % 16 == 0
    chosen = on_device_fast if fits else on_device
    return chosen(ensemble, layer_depth, observed_cell, *rest)


def solution(mesh):
    in_specs = (
        P("mem", None, "band", None),
        P("band", None),
        P("mem", "band", None),
        P("mem", "band", None),
        P("mem", "band", None),
        P("mem", "band"),
    )
    out_specs = P("mem", None, "band", None)
    return jax.shard_map(
        choose, mesh=mesh, in_specs=in_specs, out_specs=out_specs, check_vma=False
    )
```

```python
import math

import jax
import jax.numpy as jnp
import numpy as np
from jax import lax
from jax.experimental import pallas as pl
from jax.experimental.pallas import tpu as pltpu
from jax.sharding import PartitionSpec as P

SWEEPS = 5


half_step = 0.1
coriolis_scale = 0.3
neighbour_weight = 0.75


def padded_2(cells, sides, width):
    for axis, dim in sides:
        count = lax.axis_size(axis)
        head = lax.slice_in_dim(cells, 0, width, axis=dim)
        tail = lax.slice_in_dim(cells, cells.shape[dim] - width, cells.shape[dim], axis=dim)
        cells = jnp.concatenate(
            [
                lax.ppermute(tail, axis, [(i, (i + 1) % count) for i in range(count)]),
                cells,
                lax.ppermute(head, axis, [((i + 1) % count, i) for i in range(count)]),
            ],
            axis=dim,
        )
    return cells


def north_south(source):
    widths = [(0, 0)] * (source.ndim - 1) + [(1, 1)]
    padded = jnp.pad(source, widths)
    return padded[..., 2:] - padded[..., :-2]


def coriolis(latitudes):
    position = jnp.arange(latitudes, dtype=jnp.float32)
    return coriolis_scale * jnp.sin(math.pi * ((position + 0.5) / latitudes - 0.5))


def newton_schulz(starting):
    identity = jnp.eye(starting.shape[-1], dtype=starting.dtype)
    root_part = starting
    inverse_root = jnp.broadcast_to(identity, starting.shape)
    for sweep_index in range(SWEEPS):
        product = jnp.einsum(
            "tij,tjk->tik", inverse_root, root_part, precision=lax.Precision.HIGHEST
        )
        middle = 1.5 * identity - 0.5 * product
        root_part = jnp.einsum("tij,tjk->tik", root_part, middle, precision=lax.Precision.HIGHEST)
        inverse_root = jnp.einsum(
            "tij,tjk->tik", middle, inverse_root, precision=lax.Precision.HIGHEST
        )
    return inverse_root


def on_device(ensemble, layer_depth, observed_cell, observed_value, error_variance, observed_count):
    block_members = ensemble.shape[0]
    columns = ensemble.shape[2]
    latitudes = ensemble.shape[3]
    strips = lax.axis_size("mem")
    members = block_members * strips
    strip_rows = latitudes // strips
    tile_count = observed_cell.shape[1]
    tile_columns = columns // tile_count
    slot_count = observed_cell.shape[2]
    tile_cells = 3 * tile_columns * strip_rows
    height = ensemble[:, 0].astype(jnp.float32)
    eastward = ensemble[:, 1].astype(jnp.float32)
    northward = ensemble[:, 2].astype(jnp.float32)
    turning = coriolis(latitudes)
    flux_east = (layer_depth * eastward).astype(jnp.bfloat16)
    flux_north = (layer_depth * northward).astype(jnp.bfloat16)
    east_margin = padded_2(flux_east, (("band", 1),), 1)
    east_west = east_margin[:, 2:].astype(jnp.float32) - east_margin[:, :-2].astype(jnp.float32)
    north_local = lax.optimization_barrier(flux_north).astype(jnp.float32)
    raised = height - half_step * (east_west + north_south(north_local))
    surface_elevation_cast = raised.astype(jnp.bfloat16)
    height_margin = padded_2(surface_elevation_cast, (("band", 1),), 1)
    margin_wide = height_margin.astype(jnp.float32)
    height_inner = margin_wide[:, 1:-1]
    revised_zonal_velocity = (
        eastward + turning * northward - half_step * (margin_wide[:, 2:] - margin_wide[:, :-2])
    )
    revised_meridional_velocity = (
        northward - turning * eastward - half_step * north_south(height_inner)
    )
    advance_dynamics = jnp.stack(
        [
            surface_elevation_cast,
            revised_zonal_velocity.astype(jnp.bfloat16),
            revised_meridional_velocity.astype(jnp.bfloat16),
        ],
        axis=1,
    )
    reordered = advance_dynamics.reshape(
        block_members, 3, tile_count, tile_columns, strips, strip_rows
    )
    reordered = jnp.transpose(reordered, (4, 2, 0, 1, 3, 5)).reshape(
        strips, tile_count, block_members, tile_cells
    )
    tile_block = lax.all_to_all(reordered, "mem", split_axis=0, concat_axis=2, tiled=True)[0]
    cells_here = observed_cell[0]
    values = jnp.take_along_axis(tile_block, cells_here[:, None, :], axis=2)
    observed_mean = jnp.sum(values, axis=1, dtype=jnp.float32) / members
    slot_index = jnp.arange(slot_count, dtype=jnp.int32)[None, :]
    live_slots = slot_index < observed_count[0][:, None]
    root_weight = jnp.sqrt(jnp.where(live_slots, 1.0 / error_variance[0], 0.0))
    spread = (
        root_weight[:, None, :] * (values.astype(jnp.float32) - observed_mean[:, None, :])
    ).astype(jnp.bfloat16)
    misfit = (root_weight * (observed_value[0] - observed_mean)).astype(jnp.bfloat16)
    spread_margin, misfit_margin = (
        padded_2(spread[None], (("mem", 0), ("band", 1)), 1),
        padded_2(misfit[None], (("mem", 0), ("band", 1)), 1),
    )
    gram_margin = jnp.einsum(
        "atko,atlo->atkl", spread_margin, spread_margin, preferred_element_type=jnp.float32
    )
    pull_margin = jnp.einsum(
        "atko,ato->atk", spread_margin, misfit_margin, preferred_element_type=jnp.float32
    )
    strip_here = lax.axis_index("mem")
    lower_valid = (strip_here > 0).astype(jnp.float32)
    upper_valid = (strip_here < strips - 1).astype(jnp.float32)
    strip_mask = (lower_valid, 1.0, upper_valid)
    total_gram = jnp.zeros((tile_count, members, members), jnp.float32)
    total_pull = jnp.zeros((tile_count, members), jnp.float32)
    for offset_lat in range(3):
        for offset_lon in range(3):
            factor = (
                neighbour_weight ** (abs(offset_lat - 1) + abs(offset_lon - 1))
                * strip_mask[offset_lat]
            )
            total_gram = (
                total_gram + factor * gram_margin[offset_lat, offset_lon : offset_lon + tile_count]
            )
            total_pull = (
                total_pull + factor * pull_margin[offset_lat, offset_lon : offset_lon + tile_count]
            )
    system = (members - 1) * jnp.eye(members, dtype=jnp.float32)[None] + total_gram
    frobenius = jnp.sqrt(jnp.sum(system * system, axis=(1, 2)))
    inverse_root = newton_schulz(system / frobenius[:, None, None])
    spread_map = inverse_root * (math.sqrt(members - 1) / jnp.sqrt(frobenius))[:, None, None]
    half_pull = jnp.einsum("tij,tj->ti", inverse_root, total_pull, precision=lax.Precision.HIGHEST)
    shift_weights = (
        jnp.einsum("tij,tj->ti", inverse_root, half_pull, precision=lax.Precision.HIGHEST)
        / frobenius[:, None]
    )
    weights = (spread_map + shift_weights[:, :, None]).astype(jnp.bfloat16)
    state_mean = jnp.sum(tile_block, axis=1, dtype=jnp.float32) / members
    anomaly = (tile_block.astype(jnp.float32) - state_mean[:, None, :]).astype(jnp.bfloat16)
    update = jnp.einsum("tjk,tjc->tkc", weights, anomaly, preferred_element_type=jnp.float32)
    analysed = (state_mean[:, None, :] + update).astype(jnp.bfloat16)
    returned = lax.all_to_all(analysed[None], "mem", split_axis=2, concat_axis=0, tiled=True)
    returned = returned.reshape(strips, tile_count, block_members, 3, tile_columns, strip_rows)
    return jnp.transpose(returned, (2, 3, 1, 4, 0, 5)).reshape(block_members, 3, columns, latitudes)


LANES = 128
GROUPS = 23
INNER = 304
OUTER = 152
FIRST = 240
SECOND = 216
F32 = jnp.float32
BF16 = jnp.bfloat16
PACKED = 136
CHIPS = (0, 2, 4, 6)
ORDER = (6, 2, 4, 7, 1, 3, 5, 0)
MIB = 1024 * 1024


def params(size):
    return pltpu.CompilerParams(vmem_limit_bytes=size * MIB)


def cost(flops, moved):
    return pl.CostEstimate(flops=flops, bytes_accessed=moved, transcendentals=0)


def identity(size, dtype):
    row = lax.broadcasted_iota(jnp.int32, (size, size), 0)
    column = lax.broadcasted_iota(jnp.int32, (size, size), 1)
    return (row == column).astype(F32).astype(dtype)


def dot_nt(left, right):
    return lax.dot_general(left, right, (((1,), (1,)), ((), ())), preferred_element_type=F32)


def dot_nn(left, right):
    return lax.dot_general(left, right, (((1,), (0,)), ((), ())), preferred_element_type=F32)


def split(value):
    high = value.astype(BF16)
    return high, (value - high.astype(F32)).astype(BF16)


def left_3(parts):
    return jnp.concatenate([parts[0], parts[0], parts[1]], axis=1)


def right_3(parts):
    return jnp.concatenate([parts[0], parts[1], parts[0]], axis=0)


def triangle(size):
    row = lax.broadcasted_iota(jnp.int32, (size, size), 0)
    column = lax.broadcasted_iota(jnp.int32, (size, size), 1)
    return row, column


def packed(block, pull):
    row, column = triangle(128)
    last = block[128:256, 128:256]
    corner = jnp.where(row >= column, block[0:128, 0:128], last)
    middle = jnp.sum(jnp.where(row == column, last, 0.0), axis=0, keepdims=True)
    middle = jnp.concatenate([jnp.zeros_like(middle), middle], axis=1)
    top = jnp.concatenate([block[128:256, 0:128], corner], axis=1)
    tail = jnp.where(lax.broadcasted_iota(jnp.int32, (8, 256), 0) == 0, pull, middle)
    return jnp.concatenate([top, tail], axis=0)


def unpacked(value):
    row, column = triangle(128)
    low, corner = value[0:128, 0:128], value[0:128, 128:256]
    other = jnp.transpose(corner)
    first = jnp.where(row >= column, corner, other)
    last = jnp.where(row < column, corner, other)
    last = jnp.where(row == column, value[129:130, 128:256], last)
    top = jnp.concatenate([first, jnp.transpose(low)], axis=1)
    return jnp.concatenate([top, jnp.concatenate([low, last], axis=1)], axis=0), value[128:136]


def exchange_lanes(blocks, lane):
    blocks = [list(pair) for pair in blocks]
    for q in range(4):
        low, high = blocks[q], blocks[q + 4]
        blocks[q], blocks[q + 4] = [low[0], high[0]], [low[1], high[1]]
    for bit in range(2):
        step = 32 << bit
        odd = (lane & step) != 0
        for q in range(8):
            if q & (1 << bit):
                continue
            for h in range(2):
                low, high = blocks[q][h], blocks[q | (1 << bit)][h]
                blocks[q][h] = jnp.where(odd, pltpu.roll(high, step, 1), low)
                blocks[q | (1 << bit)][h] = jnp.where(odd, high, pltpu.roll(low, LANES - step, 1))
    return blocks


def group_of(variable, index):
    return variable + (variable * 2 + index - 4 if index > 3 else 18 - 3 * index)


def row_of(group):
    return 20 * group + (4 if group >= 15 else 0)


def difference(latitudes):
    source = lax.broadcasted_iota(jnp.int32, (latitudes, latitudes), 0)
    target = lax.broadcasted_iota(jnp.int32, (latitudes, latitudes), 1)
    shift = (source == target + 1).astype(F32) - (source == target - 1).astype(F32)
    return shift.astype(BF16)


def rows_apart(value, shift):
    flat = value.reshape(-1, value.shape[-1])
    return dot_nn(flat, shift).reshape(value.shape)


def fluxes(east, deep):
    return (deep * east.astype(F32)).astype(BF16).astype(F32)


def heights(field, north, deep, ahead, behind, shift):
    flux_north = (deep * north.astype(F32)).astype(BF16)
    raised = field.astype(F32) - half_step * ((ahead - behind) + rows_apart(flux_north, shift))
    return raised.astype(BF16)


def velocities(east, north, here, ahead, behind, turning, shift):
    east, north = east.astype(F32), north.astype(F32)
    apart = ahead.astype(F32) - behind.astype(F32)
    new_east = east + turning * north - half_step * apart
    new_north = north - turning * east - half_step * rows_apart(here, shift)
    return new_east.astype(BF16), new_north.astype(BF16)


def put_group(staged, block, eye, first):
    latitudes = eye.shape[0]
    rows = latitudes // 8
    turned = dot_nt(eye, block.reshape(256, latitudes))
    for s in range(8):
        staged[s, first : first + rows, :] = turned[rows * s : rows * (s + 1)]


def turning_row(latitudes):
    position = lax.broadcasted_iota(jnp.int32, (8, latitudes), 1).astype(F32)
    turning = coriolis_scale * jnp.sin(math.pi * ((position + 0.5) / latitudes - 0.5))
    return turning[0:1, :][None]


def inner_kernel(
    ens, depth, out, to_first, to_second, here, deep, flux, height, staged, edges, arrived
):
    columns, members, latitudes = here.shape[1:]
    batch = columns // 5
    pieces = [pltpu.make_async_copy(depth, deep, arrived.at[5])]
    for k in range(5):
        span = pl.ds(k * batch, batch)
        piece = pltpu.make_async_copy(ens.at[:, span], here.at[:, span], arrived.at[k])
        pieces.append(piece)
    for piece in pieces:
        piece.start()
    shift = difference(latitudes)
    turning = turning_row(latitudes)
    eye = identity(latitudes, BF16)
    pieces[0].wait()

    def depths(first, count):
        rows = [deep[c : c + 1, :] for c in range(first, first + count)]
        return jnp.stack([jnp.broadcast_to(row, (members, latitudes)) for row in rows])

    def edge(side, near, far):
        edges[side, 0] = here[0, near]
        edges[side, 1] = (deep[near : near + 1, :] * here[2, near].astype(F32)).astype(BF16)
        edges[side, 2] = flux[near].astype(BF16)
        edges[side, 3] = flux[far].astype(BF16)

    staged[:, 300:INNER, :] = jnp.zeros((8, INNER - 300, 256), F32)
    done = 2
    for k in range(5):
        pieces[k + 1].wait()
        first, count = k * batch, batch if k else 2
        flux[first : first + count] = fluxes(here[1, first : first + count], depths(first, count))
        if k == 0:
            edge(0, 0, 1)
            continue
        if k == 4:
            edge(1, columns - 1, columns - 2)
        low, high = max(first - 1, batch + 1), first + batch - 1
        at = slice(low, high)
        ahead, behind = flux[low + 1 : high + 1], flux[low - 1 : high - 1]
        height[at] = heights(
            here[0, at], here[2, at], depths(low, high - low), ahead, behind, shift
        )
        while done < 7 and 8 * done + 9 <= high:
            first = 8 * done
            at = slice(first, first + 8)
            ahead, behind = height[first + 1 : first + 9], height[first - 1 : first + 7]
            new = velocities(here[1, at], here[2, at], height[at], ahead, behind, turning, shift)
            for v, field in enumerate((height[at],) + new):
                put_group(staged, field, eye, row_of(group_of(v, done)))
            done += 1
    odd = lax.axis_index("band") & 1
    to_first[...] = edges[1 - odd]
    to_second[...] = edges[odd]
    out[...] = staged[...].astype(BF16)


def outer_kernel(
    west_block, east_block, first_swap, second_swap, depth, *refs
):
    straight, cross, flux, height, staged, swapped = refs
    odd = lax.axis_index("band") & 1
    for side, block in enumerate((first_swap, second_swap)):
        swapped[side] = block[...]
    left, right = swapped.at[1 - odd], swapped.at[odd]
    members, latitudes = west_block.shape[2:]
    shift = difference(latitudes)
    turning = turning_row(latitudes)
    eye = identity(latitudes, BF16)

    def depths(first, count):
        return jnp.stack(
            [
                jnp.broadcast_to(depth[c : c + 1, :], (members, latitudes))
                for c in range(first, first + count)
            ]
        )

    def window(ens, edge, first, count, low, high):
        is_left = low == 0
        base = 2 if is_left else 0
        flux[base : base + count] = fluxes(ens[1, 0:count], depths(first, count))
        at = 0 if is_left else count
        near, far = (1, 0) if is_left else (at, at + 1)
        flux[near] = edge[2].astype(F32)
        flux[far] = edge[3].astype(F32)
        wide = high - low + 1
        skip = 0 if is_left else 1
        columns = slice(skip, skip + wide)
        new = heights(
            ens[0, columns],
            ens[2, columns],
            depths(first + skip, wide),
            flux[base + skip + 1 : base + skip + 1 + wide],
            flux[base + skip - 1 : base + skip - 1 + wide],
            shift,
        )
        start = 1 if is_left else 0
        height[start : start + wide] = new
        place = 0 if is_left else wide
        middle = near
        east_west = flux[middle + 1] - flux[middle - 1]
        raised = edge[0].astype(F32) - half_step * (east_west + rows_apart(edge[1], shift))
        height[place] = raised.astype(BF16)
        count = high - low
        here = height[1 : 1 + count]
        ahead, behind = height[2 : 2 + count], height[0:count]
        at = slice(low - first, high - first)
        return (here,) + velocities(ens[1, at], ens[2, at], here, ahead, behind, turning, shift)

    for v, field in enumerate(window(west_block, left, 0, 18, 0, 16)):
        for index in range(2):
            at = row_of(group_of(v, index)) - INNER
            put_group(staged, field[8 * index : 8 * index + 8], eye, at)
    ends = window(east_block, right, 54, 6, 56, 60)
    put_group(staged, jnp.concatenate([ends[0], ends[1]], axis=0), eye, 120)
    block = jnp.concatenate([ends[2], ends[2]], axis=0).reshape(256, latitudes)
    turned = dot_nt(eye, block)
    lower = lax.broadcasted_iota(jnp.int32, (10, 256), 1) < LANES
    for s in range(8):
        rows = [turned[20 * s + 10 * k : 20 * s + 10 * k + 10] for k in range(2)]
        staged[s, 140:150, :] = jnp.where(lower, rows[0], rows[1])
    staged[:, 150:OUTER, :] = jnp.zeros((8, OUTER - 150, 256), F32)
    me = lax.axis_index("mem")
    for k, d in enumerate(CHIPS):
        straight[k] = staged[me ^ d].astype(BF16)
        cross[k] = staged[me ^ d ^ 1].astype(BF16)


def spread_block(source, held, wide, start, lane):
    spans = [slice(h * LANES, (h + 1) * LANES) for h in range(2)]
    count = source.shape[1]
    here = pl.ds(start, 16)
    blocks = exchange_lanes([[source[q, here, span] for span in spans] for q in range(8)], lane)
    for q in range(8):
        to = pl.ds(pl.multiple_of(q * count + start, 8), 16)
        for h in range(2):
            wide[h, to, :] = blocks[q][h].astype(F32)
            held[q, here, spans[h]] = blocks[q][h]


def spread_kernel(cells, got, held, seen, wide):
    lane = lax.broadcasted_iota(jnp.int32, (16, LANES), 1)

    def step(index, carry):
        spread_block(got, held, wide, pl.multiple_of(index * 16, 16), lane)
        return carry

    lax.fori_loop(0, INNER // 16, step, 0, unroll=4)
    slots = seen.shape[2]
    unroll = 16

    def pick(index, carry):
        for t in range(2):
            for k in range(unroll):
                slot = index * unroll + k
                row = cells[t, slot]
                for h in range(2):
                    seen[t, h, pl.ds(slot, 1), :] = wide[h, pl.ds(row, 1), :]
        return carry

    lax.fori_loop(0, slots // unroll, pick, 0)


def observe_kernel(cells, outer, weight, target, first, straight, cross, *refs):
    edges, (held, gram, to_first, to_second, joined, wide, seen) = refs[:3], refs[3:]
    wholes = []
    lane = lax.broadcasted_iota(jnp.int32, (16, LANES), 1)
    me = lax.axis_index("mem")
    for k, d in enumerate(CHIPS):
        joined[me ^ d, 0:OUTER, :] = straight[0] if k == 0 else edges[k - 1][0]
        joined[me ^ d ^ 1, 0:OUTER, :] = cross[0] if k == 0 else edges[k - 1][1]
    for start in (*range(0, OUTER - 16, 16), OUTER - 16):
        spread_block(joined, held, wide, start, lane)
    slots = first.shape[2]
    seen[:, :, 0:slots, :] = first[...]

    def pick(index, carry):
        for k in range(8):
            for t in range(2):
                slot = outer[t, index * 8 + k]
                row = cells[t, index * 8 + k]
                for h in range(2):
                    seen[t, h, pl.ds(slot, 1), :] = wide[h, pl.ds(row, 1), :]
        return carry

    last = slots + LANES - 1
    most = jnp.maximum(outer[0, last], outer[1, last])
    lax.fori_loop(0, (most + 7) // 8, pick, 0)
    eye = identity(256, BF16)
    for t in range(2):
        values = jnp.concatenate([seen[t, h, 0:slots] for h in range(2)], axis=1).astype(BF16)
        turned = dot_nt(eye, values)
        mean = jnp.sum(turned, axis=0, keepdims=True) * (1.0 / 256)
        root = weight[t : t + 1, :]
        spread = (root * (turned - mean)).astype(BF16)
        misfit = (root * (target[t : t + 1, :] - mean)).astype(BF16)
        block = dot_nt(spread, spread)
        pull = dot_nt(jnp.broadcast_to(misfit, (16, slots)), spread)
        whole = packed(block, pull[0:8])
        gram[t] = whole
        wholes.append(whole.astype(BF16))
    odd = (lax.axis_index("band") & 1) == 1
    to_first[...] = jnp.where(odd, wholes[0], wholes[1])
    to_second[...] = jnp.where(odd, wholes[1], wholes[0])


def combine_kernel(gram, first_swap, second_swap, line, short):
    odd = (lax.axis_index("band") & 1) == 1
    first, second = first_swap[...].astype(F32), second_swap[...].astype(F32)
    west, east = jnp.where(odd, first, second), jnp.where(odd, second, first)
    for t, beside in enumerate((west + gram[1], gram[0] + east)):
        total = gram[t] + neighbour_weight * beside
        line[t] = total
        short[t] = total.astype(BF16)


def prepare_kernel(inner, outer, *refs):
    average = jnp.full((256, LANES), 1.0 / 256, BF16)
    for q in range(8):
        pieces = (inner[q, 0:FIRST], jnp.concatenate([inner[q, FIRST:INNER], outer[q, 0:OUTER]], axis=0))
        for k, piece in enumerate(pieces):
            mean = dot_nn(piece, average)
            refs[2 * k + 1][q] = mean
            mean = jnp.concatenate([mean, mean], axis=1)
            refs[2 * k][q] = (piece.astype(F32) - mean).astype(BF16)


def send_back(results, outs):
    lane = lax.broadcasted_iota(jnp.int32, (16, LANES), 1)
    spans = [slice(h * LANES, (h + 1) * LANES) for h in range(2)]

    def move(start):
        here = pl.ds(start, 16)
        blocks = [[results[q, here, span] for span in spans] for q in range(8)]
        blocks = exchange_lanes(blocks, lane)
        for q in range(8):
            for h in range(2):
                outs[ORDER.index(q)][here, spans[h]] = blocks[q][h]

    def step(index, carry):
        move(pl.multiple_of(index * 16, 16))
        return carry

    count = results.shape[1]
    lax.fori_loop(0, count // 16, step, 0, unroll=4)
    if count % 16:
        move(count - 16)


def apply_maps(anomaly, mean, maps, results, q, edge, order):
    count = results.shape[1]
    low, high = edge // 16 * 16, (edge + 15) // 16 * 16
    first = dot_nt(anomaly[q, 0:high], maps[order[0]])
    centre = jnp.concatenate([mean[q], mean[q]], axis=1)
    results[q, 0:low] = (centre[0:low] + first[0:low]).astype(BF16)
    if low == count:
        return
    second = dot_nt(anomaly[q, low:count], maps[order[1]])
    if low < high:
        near = lax.broadcasted_iota(jnp.int32, (16, 256), 0) < edge - low
        both = jnp.where(near, first[low:high], second[0:16])
        results[q, low:high] = (centre[low:high] + both).astype(BF16)
    results[q, high:count] = (centre[high:count] + second[high - low : count - low]).astype(BF16)


def second_kernel(maps, anomaly, mean, *refs):
    outs, results = refs[:8], refs[8]
    both = [maps[0], maps[1]]
    for q in range(8):
        apply_maps(anomaly, mean, both, results, q, 184, (0, 1))
    send_back(results, outs)


def analyse_kernel(line, below, above, anomaly, mean, *refs):
    outs, (kept, results, ordered) = refs[:8], refs[8:]
    size = 256
    eye = identity(size, F32)
    norms, pulls, roots, inverses = [], [], [], []
    for t in range(2):
        beside = below[t].astype(F32) + above[t].astype(F32)
        block, pull = unpacked(line[t] + neighbour_weight * beside)
        system = (size - 1) * eye + block
        square = jnp.sum(jnp.sum(system * system, axis=0, keepdims=True), axis=1, keepdims=True)
        norms.append(jnp.sqrt(square))
        pulls.append(pull)
        roots.append(system / norms[t])
    for sweep in range(SWEEPS):
        rights = [right_3(split(root)) for root in roots]
        if sweep == 0:
            inverses = [1.5 * eye - 0.5 * root for root in roots]
            lefts = [left_3(split(inverse)) for inverse in inverses]
            roots = [dot_nn(left, right) for left, right in zip(lefts, rights)]
            continue
        parts = [split(inverse) for inverse in inverses]
        products = [dot_nn(left_3(part), right) for part, right in zip(parts, rights)]
        middles = [left_3(split(1.5 * eye - 0.5 * product)) for product in products]
        if sweep < SWEEPS - 1:
            roots = [dot_nn(middle, right) for middle, right in zip(middles, rights)]
        inverses = [dot_nn(middle, right_3(part)) for middle, part in zip(middles, parts)]
    maps = []
    for t in range(2):
        right = right_3(split(inverses[t]))
        half_pull = dot_nn(left_3(split(pulls[t])), right)
        shift = dot_nn(left_3(split(half_pull)), right) / norms[t]
        scale = math.sqrt(size - 1) / jnp.sqrt(norms[t])
        ordered[t] = (inverses[t] * scale + shift[0:1]).astype(BF16).reshape(8, 32, size)
    me = lax.axis_index("mem")
    for t in range(2):
        maps.append(jnp.concatenate([ordered[t, me ^ d] for d in range(8)], axis=0))
        kept[t] = maps[t]
    for q in range(8):
        apply_maps(anomaly, mean, maps, results, q, 180 if q < 6 else FIRST, (1, 0))
    send_back(results, outs)


def spread_strips(got, wide):
    me = lax.axis_index("mem")
    for k, d in enumerate(ORDER):
        wide[me ^ d] = got[k][...].astype(F32)


def take_group(wide, turned, eye, g, shape, skipped=0):
    rows = shape[2] // 8
    at = row_of(g) - row_of(skipped)
    g = g - skipped
    for s in range(8):
        turned[g, rows * s : rows * (s + 1), :] = wide[s, at : at + rows, :]
    return dot_nt(eye, turned[g].astype(BF16)).astype(BF16).reshape(shape)


def first_return_kernel(*refs):
    got, (out, wide, turned, planes, sent) = refs[:8], refs[8:]
    shape = (8,) + planes.shape[2:]
    spread_strips(got, wide)
    eye = identity(256, BF16)
    copies = []
    for v in range(3):
        for index in range(3, 7):
            at = 8 * (index - 3)
            planes[v, at : at + 8] = take_group(wide, turned, eye, group_of(v, index), shape)
        copies.append(pltpu.make_async_copy(planes.at[v], out.at[v, pl.ds(24, 32)], sent.at[v]))
        copies[v].start()
    for copy in copies:
        copy.wait()


def second_return_kernel(*refs):
    got, (_, out, wide, turned, planes, sent) = refs[:8], refs[8:]
    shape = (8,) + planes.shape[2:]
    spread_strips(got, wide)
    eye = identity(256, BF16)
    mixed = take_group(wide, turned, eye, 21, shape, 12)
    planes[0, 24:28] = mixed[0:4]
    planes[1, 24:28] = mixed[4:8]
    at = row_of(22) - row_of(12)
    turned[10] = jnp.zeros(turned.shape[1:], F32)
    for s in range(8):
        for k in range(2):
            to = 20 * s + 10 * k
            half = wide[s, at : at + 10, k * LANES : (k + 1) * LANES]
            turned[10, to : to + 10, 0:LANES] = half
    block = dot_nt(eye, turned[10].astype(BF16)).astype(BF16).reshape(shape)
    planes[2, 24:28] = block[0:4]
    copies = []
    for v in range(3):
        for index in range(3):
            at = 8 * index
            block = take_group(wide, turned, eye, group_of(v, index), shape, 12)
            planes[v, at : at + 8] = block
        for k, (at, to, count) in enumerate(((0, 0, 24), (24, 56, 4))):
            source, target = planes.at[v, pl.ds(at, count)], out.at[v, pl.ds(to, count)]
            copies.append(pltpu.make_async_copy(source, target, sent.at[2 * v + k]))
            copies[-1].start()
    for copy in copies:
        copy.wait()


def swapped_pairs(values, axis, pairs):
    moved = []
    for value, some in zip(values, pairs):
        both = some + [(j, i) for i, j in some]
        moved.append(lax.ppermute(value, axis, both))
    return moved


def band_swaps(first, second):
    count = lax.axis_size("band")
    starts = range(0, count, 2)
    pairs = [[(i, i + 1) for i in starts], [(i + 1, (i + 2) % count) for i in starts]]
    return swapped_pairs((first, second), "band", pairs)


def mem_swaps(value):
    count = lax.axis_size("mem")
    pairs = [[(i, i + 1) for i in range(k, count - 1, 2)] for k in range(2)]
    return swapped_pairs((value, value), "mem", pairs)


def across(value, difference):
    return lax.ppermute(value, "mem", [(i, i ^ difference) for i in range(8)])


def partners(values):
    return [across(value, d) if d else value for d, value in zip(ORDER, values)]


def swap(value):
    return lax.all_to_all(value, "mem", split_axis=0, concat_axis=0, tiled=True)


def cell_rows(cell):
    variable = cell // 600
    tile = jnp.arange(2, dtype=jnp.int32)[:, None]
    column = tile * 30 + cell // 20 % 30
    index = column // 8
    place = column % 8
    group = variable + jnp.where(index > 3, variable * 2 + index - 4, 18 - 3 * index)
    is_last = column >= 56
    group = jnp.where(is_last, 21 + variable // 2, group)
    place = jnp.where(is_last, column - 56 + 4 * (variable % 2), place)
    row = cell % 20
    place = jnp.where(group == 22, place + 4 * (row // 10), place)
    row = jnp.where(group == 22, row % 10, row)
    first = place * INNER + group * 20
    last = 8 * INNER + place * OUTER + (group - 15) * 20
    return jnp.where(group < 15, first, last) + row


def on_device_fast(
    ensemble, layer_depth, observed_cell, observed_value, error_variance, observed_count
):
    members, _, columns, latitudes = ensemble.shape
    slots = observed_cell.shape[2]
    planes = jnp.transpose(ensemble, (1, 2, 0, 3))
    edge = jax.ShapeDtypeStruct((4, members, latitudes), BF16)
    far = pl.BlockSpec(memory_space=pltpu.HBM)
    sent, to_first, to_second = pl.pallas_call(
        inner_kernel,
        out_shape=(jax.ShapeDtypeStruct((8, INNER, 256), BF16), edge, edge),
        in_specs=[far, far],
        scratch_shapes=[
            pltpu.VMEM(planes.shape, BF16),
            pltpu.VMEM((columns, latitudes), F32),
            pltpu.VMEM((columns, members, latitudes), F32),
            pltpu.VMEM((columns, members, latitudes), BF16),
            pltpu.VMEM((8, INNER, 256), F32),
            pltpu.VMEM((2, 4, members, latitudes), BF16),
            pltpu.SemaphoreType.DMA((6,)),
        ],
        compiler_params=params(60),
        name="inner",
    )(planes, layer_depth)
    got = swap(sent)
    swaps = band_swaps(to_first, to_second)
    flat = pl.BlockSpec((4, members, latitudes), lambda i: (0, 0, 0))
    straight, cross = pl.pallas_call(
        outer_kernel,
        grid=(1,),
        out_shape=(jax.ShapeDtypeStruct((4, OUTER, 256), BF16),) * 2,
        in_specs=[
            pl.BlockSpec((3, 20, members, latitudes), lambda i: (0, 0, 0, 0)),
            pl.BlockSpec((3, 6, members, latitudes), lambda i: (0, 9, 0, 0)),
            flat,
            flat,
            pl.BlockSpec((columns, latitudes), lambda i: (0, 0)),
        ],
        out_specs=(pl.BlockSpec((4, OUTER, 256), lambda i: (0, 0, 0)),) * 2,
        scratch_shapes=[
            pltpu.VMEM((20, members, latitudes), F32),
            pltpu.VMEM((18, members, latitudes), BF16),
            pltpu.VMEM((8, OUTER, 256), F32),
            pltpu.VMEM((2, 4, members, latitudes), BF16),
        ],
        compiler_params=params(24),
        name="outer",
    )(planes, planes, *swaps, layer_depth)
    cross = across(cross, 1)
    got_edges = [across(jnp.stack([straight[k], cross[k]]), CHIPS[k]) for k in (3, 1, 2)]
    got_edges = got_edges[1:] + got_edges[:1]

    rows = cell_rows(observed_cell[0])
    live = jnp.arange(slots, dtype=jnp.int32)[None, :] < observed_count[0][:, None]
    root = jnp.sqrt(jnp.where(live, 1.0 / error_variance[0], 0.0))
    vmem = pl.BlockSpec(memory_space=pltpu.VMEM)
    slot = jnp.arange(slots, dtype=jnp.int32)
    place = jnp.arange(slots + LANES, dtype=jnp.int32)
    is_outer = rows >= 8 * INNER
    near = jnp.where(is_outer, 0, rows)
    rank = jnp.sum(is_outer[:, None, :] & (slot[None, :] < slot[:, None])[None], axis=2)
    count = jnp.sum(is_outer, axis=1, keepdims=True)
    found = is_outer[:, None, :] & (rank[:, None, :] == place[None, :, None])
    outer = jnp.sum(jnp.where(found, slot, 0), axis=2)
    outer = jnp.where(place[None] < count, outer, slots)
    outer = jnp.where(place[None] == slots + LANES - 1, count, outer).astype(jnp.int32)
    beyond = (rows - 8 * INNER)[:, None, :]
    rows = jnp.sum(jnp.where(found, beyond, 0), axis=2).astype(jnp.int32)
    smem = pl.BlockSpec(memory_space=pltpu.SMEM)
    held_inner, seen = pl.pallas_call(
        spread_kernel,
        out_shape=(
            jax.ShapeDtypeStruct((8, INNER, 256), BF16),
            jax.ShapeDtypeStruct((2, 2, slots, LANES), F32),
        ),
        in_specs=[smem, vmem],
        scratch_shapes=[pltpu.VMEM((2, 8 * INNER, LANES), F32)],
        compiler_params=params(12),
        cost_estimate=cost(1, 8 * MIB),
        name="spread",
    )(near, got)
    one_tile = jax.ShapeDtypeStruct((PACKED, 256), BF16)
    held_outer, gram, to_first, to_second = pl.pallas_call(
        observe_kernel,
        out_shape=(
            jax.ShapeDtypeStruct((8, OUTER, 256), BF16),
            jax.ShapeDtypeStruct((2, PACKED, 256), F32),
            one_tile,
            one_tile,
        ),
        in_specs=[smem, smem] + [vmem] * 8,
        scratch_shapes=[
            pltpu.VMEM((8, OUTER, 256), BF16),
            pltpu.VMEM((2, 8 * OUTER, LANES), F32),
            pltpu.VMEM((2, 2, slots + 8, LANES), F32),
        ],
        compiler_params=params(16),
        name="observe",
    )(rows, outer, root, observed_value[0], seen, straight, cross, *got_edges)
    anomaly_1, mean_1, anomaly_2, mean_2 = pl.pallas_call(
        prepare_kernel,
        out_shape=(
            jax.ShapeDtypeStruct((8, FIRST, 256), BF16),
            jax.ShapeDtypeStruct((8, FIRST, LANES), F32),
            jax.ShapeDtypeStruct((8, SECOND, 256), BF16),
            jax.ShapeDtypeStruct((8, SECOND, LANES), F32),
        ),
        compiler_params=params(12),
        cost_estimate=cost(1, 6 * MIB),
        name="prepare",
    )(held_inner, held_outer)

    line, short = pl.pallas_call(
        combine_kernel,
        out_shape=(
            jax.ShapeDtypeStruct(gram.shape, F32),
            jax.ShapeDtypeStruct(gram.shape, BF16),
        ),
        compiler_params=params(8),
        name="combine",
    )(gram, *band_swaps(to_first, to_second))
    below, above = mem_swaps(short)
    *back, maps = pl.pallas_call(
        analyse_kernel,
        out_shape=(jax.ShapeDtypeStruct((FIRST, 256), BF16),) * 8
        + (jax.ShapeDtypeStruct((2, 256, 256), BF16),),
        scratch_shapes=[pltpu.VMEM((8, FIRST, 256), BF16), pltpu.VMEM((2, 8, 32, 256), BF16)],
        compiler_params=params(20),
        name="analyse",
    )(line, below, above, anomaly_1, mean_1)
    first = partners(back)
    maps, first[4] = lax.optimization_barrier((maps, first[4]))
    back = pl.pallas_call(
        second_kernel,
        out_shape=(jax.ShapeDtypeStruct((SECOND, 256), BF16),) * 8,
        scratch_shapes=[pltpu.VMEM((8, SECOND, 256), BF16)],
        compiler_params=params(16),
        cost_estimate=cost(1, 6 * MIB),
        name="second",
    )(maps, anomaly_2, mean_2)
    second = partners(back)
    result = jax.ShapeDtypeStruct(planes.shape, BF16)
    half = pl.pallas_call(
        first_return_kernel,
        out_shape=result,
        out_specs=far,
        scratch_shapes=[
            pltpu.VMEM((8, FIRST, 256), F32),
            pltpu.VMEM((12, latitudes, 256), F32),
            pltpu.VMEM((3, 32, members, latitudes), BF16),
            pltpu.SemaphoreType.DMA((3,)),
        ],
        compiler_params=params(20),
        cost_estimate=cost(1, 4 * MIB),
        name="first_return",
    )(*first)
    planes = pl.pallas_call(
        second_return_kernel,
        out_shape=result,
        in_specs=[vmem] * 8 + [far],
        out_specs=far,
        scratch_shapes=[
            pltpu.VMEM((8, SECOND, 256), F32),
            pltpu.VMEM((11, latitudes, 256), F32),
            pltpu.VMEM((3, 28, members, latitudes), BF16),
            pltpu.SemaphoreType.DMA((6,)),
        ],
        input_output_aliases={8: 0},
        compiler_params=params(20),
        name="second_return",
    )(*second, half)
    return jnp.transpose(planes, (2, 0, 1, 3))


def choose(ensemble, layer_depth, observed_cell, *rest):
    mesh_shape = (lax.axis_size("mem"), lax.axis_size("band"))
    shape = (mesh_shape, ensemble.shape, observed_cell.shape[1])
    fits = shape == ((8, 4), (32, 3, 60, 160), 2) and observed_cell.shape[2] % 16 == 0
    chosen = on_device_fast if fits else on_device
    return chosen(ensemble, layer_depth, observed_cell, *rest)


def solution(mesh):
    in_specs = (
        P("mem", None, "band", None),
        P("band", None),
        P("mem", "band", None),
        P("mem", "band", None),
        P("mem", "band", None),
        P("mem", "band"),
    )
    out_specs = P("mem", None, "band", None)
    return jax.shard_map(
        choose, mesh=mesh, in_specs=in_specs, out_specs=out_specs, check_vma=False
    )
```

```python
import math

import jax
import jax.numpy as jnp
import numpy as np
from jax import lax
from jax.experimental import pallas as pl
from jax.experimental.pallas import tpu as pltpu
from jax.sharding import PartitionSpec as P

SWEEPS = 5


half_step = 0.1
coriolis_scale = 0.3
neighbour_weight = 0.75


def padded_2(cells, sides, width):
    for axis, dim in sides:
        count = lax.axis_size(axis)
        head = lax.slice_in_dim(cells, 0, width, axis=dim)
        tail = lax.slice_in_dim(cells, cells.shape[dim] - width, cells.shape[dim], axis=dim)
        cells = jnp.concatenate(
            [
                lax.ppermute(tail, axis, [(i, (i + 1) % count) for i in range(count)]),
                cells,
                lax.ppermute(head, axis, [((i + 1) % count, i) for i in range(count)]),
            ],
            axis=dim,
        )
    return cells


def north_south(source):
    widths = [(0, 0)] * (source.ndim - 1) + [(1, 1)]
    padded = jnp.pad(source, widths)
    return padded[..., 2:] - padded[..., :-2]


def coriolis(latitudes):
    position = jnp.arange(latitudes, dtype=jnp.float32)
    return coriolis_scale * jnp.sin(math.pi * ((position + 0.5) / latitudes - 0.5))


def newton_schulz(starting):
    identity = jnp.eye(starting.shape[-1], dtype=starting.dtype)
    root_part = starting
    inverse_root = jnp.broadcast_to(identity, starting.shape)
    for sweep_index in range(SWEEPS):
        product = jnp.einsum(
            "tij,tjk->tik", inverse_root, root_part, precision=lax.Precision.HIGHEST
        )
        middle = 1.5 * identity - 0.5 * product
        root_part = jnp.einsum("tij,tjk->tik", root_part, middle, precision=lax.Precision.HIGHEST)
        inverse_root = jnp.einsum(
            "tij,tjk->tik", middle, inverse_root, precision=lax.Precision.HIGHEST
        )
    return inverse_root


def on_device(ensemble, layer_depth, observed_cell, observed_value, error_variance, observed_count):
    block_members = ensemble.shape[0]
    columns = ensemble.shape[2]
    latitudes = ensemble.shape[3]
    strips = lax.axis_size("mem")
    members = block_members * strips
    strip_rows = latitudes // strips
    tile_count = observed_cell.shape[1]
    tile_columns = columns // tile_count
    slot_count = observed_cell.shape[2]
    tile_cells = 3 * tile_columns * strip_rows
    height = ensemble[:, 0].astype(jnp.float32)
    eastward = ensemble[:, 1].astype(jnp.float32)
    northward = ensemble[:, 2].astype(jnp.float32)
    turning = coriolis(latitudes)
    flux_east = (layer_depth * eastward).astype(jnp.bfloat16)
    flux_north = (layer_depth * northward).astype(jnp.bfloat16)
    east_margin = padded_2(flux_east, (("band", 1),), 1)
    east_west = east_margin[:, 2:].astype(jnp.float32) - east_margin[:, :-2].astype(jnp.float32)
    north_local = lax.optimization_barrier(flux_north).astype(jnp.float32)
    raised = height - half_step * (east_west + north_south(north_local))
    surface_elevation_cast = raised.astype(jnp.bfloat16)
    height_margin = padded_2(surface_elevation_cast, (("band", 1),), 1)
    margin_wide = height_margin.astype(jnp.float32)
    height_inner = margin_wide[:, 1:-1]
    revised_zonal_velocity = (
        eastward + turning * northward - half_step * (margin_wide[:, 2:] - margin_wide[:, :-2])
    )
    revised_meridional_velocity = (
        northward - turning * eastward - half_step * north_south(height_inner)
    )
    advance_dynamics = jnp.stack(
        [
            surface_elevation_cast,
            revised_zonal_velocity.astype(jnp.bfloat16),
            revised_meridional_velocity.astype(jnp.bfloat16),
        ],
        axis=1,
    )
    reordered = advance_dynamics.reshape(
        block_members, 3, tile_count, tile_columns, strips, strip_rows
    )
    reordered = jnp.transpose(reordered, (4, 2, 0, 1, 3, 5)).reshape(
        strips, tile_count, block_members, tile_cells
    )
    tile_block = lax.all_to_all(reordered, "mem", split_axis=0, concat_axis=2, tiled=True)[0]
    cells_here = observed_cell[0]
    values = jnp.take_along_axis(tile_block, cells_here[:, None, :], axis=2)
    observed_mean = jnp.sum(values, axis=1, dtype=jnp.float32) / members
    slot_index = jnp.arange(slot_count, dtype=jnp.int32)[None, :]
    live_slots = slot_index < observed_count[0][:, None]
    root_weight = jnp.sqrt(jnp.where(live_slots, 1.0 / error_variance[0], 0.0))
    spread = (
        root_weight[:, None, :] * (values.astype(jnp.float32) - observed_mean[:, None, :])
    ).astype(jnp.bfloat16)
    misfit = (root_weight * (observed_value[0] - observed_mean)).astype(jnp.bfloat16)
    spread_margin, misfit_margin = (
        padded_2(spread[None], (("mem", 0), ("band", 1)), 1),
        padded_2(misfit[None], (("mem", 0), ("band", 1)), 1),
    )
    gram_margin = jnp.einsum(
        "atko,atlo->atkl", spread_margin, spread_margin, preferred_element_type=jnp.float32
    )
    pull_margin = jnp.einsum(
        "atko,ato->atk", spread_margin, misfit_margin, preferred_element_type=jnp.float32
    )
    strip_here = lax.axis_index("mem")
    lower_valid = (strip_here > 0).astype(jnp.float32)
    upper_valid = (strip_here < strips - 1).astype(jnp.float32)
    strip_mask = (lower_valid, 1.0, upper_valid)
    total_gram = jnp.zeros((tile_count, members, members), jnp.float32)
    total_pull = jnp.zeros((tile_count, members), jnp.float32)
    for offset_lat in range(3):
        for offset_lon in range(3):
            factor = (
                neighbour_weight ** (abs(offset_lat - 1) + abs(offset_lon - 1))
                * strip_mask[offset_lat]
            )
            total_gram = (
                total_gram + factor * gram_margin[offset_lat, offset_lon : offset_lon + tile_count]
            )
            total_pull = (
                total_pull + factor * pull_margin[offset_lat, offset_lon : offset_lon + tile_count]
            )
    system = (members - 1) * jnp.eye(members, dtype=jnp.float32)[None] + total_gram
    frobenius = jnp.sqrt(jnp.sum(system * system, axis=(1, 2)))
    inverse_root = newton_schulz(system / frobenius[:, None, None])
    spread_map = inverse_root * (math.sqrt(members - 1) / jnp.sqrt(frobenius))[:, None, None]
    half_pull = jnp.einsum("tij,tj->ti", inverse_root, total_pull, precision=lax.Precision.HIGHEST)
    shift_weights = (
        jnp.einsum("tij,tj->ti", inverse_root, half_pull, precision=lax.Precision.HIGHEST)
        / frobenius[:, None]
    )
    weights = (spread_map + shift_weights[:, :, None]).astype(jnp.bfloat16)
    state_mean = jnp.sum(tile_block, axis=1, dtype=jnp.float32) / members
    anomaly = (tile_block.astype(jnp.float32) - state_mean[:, None, :]).astype(jnp.bfloat16)
    update = jnp.einsum("tjk,tjc->tkc", weights, anomaly, preferred_element_type=jnp.float32)
    analysed = (state_mean[:, None, :] + update).astype(jnp.bfloat16)
    returned = lax.all_to_all(analysed[None], "mem", split_axis=2, concat_axis=0, tiled=True)
    returned = returned.reshape(strips, tile_count, block_members, 3, tile_columns, strip_rows)
    return jnp.transpose(returned, (2, 3, 1, 4, 0, 5)).reshape(block_members, 3, columns, latitudes)


LANES = 128
GROUPS = 23
INNER = 304
OUTER = 152
FIRST = 240
SECOND = 216
F32 = jnp.float32
BF16 = jnp.bfloat16
PACKED = 136
CHIPS = (0, 2, 4, 6)
ORDER = (6, 7, 2, 4, 3, 5, 1, 0)
MIB = 1024 * 1024


def params(size):
    return pltpu.CompilerParams(vmem_limit_bytes=size * MIB)


def cost(flops, moved):
    return pl.CostEstimate(flops=flops, bytes_accessed=moved, transcendentals=0)


def identity(size, dtype):
    row = lax.broadcasted_iota(jnp.int32, (size, size), 0)
    column = lax.broadcasted_iota(jnp.int32, (size, size), 1)
    return (row == column).astype(F32).astype(dtype)


def dot_nt(left, right):
    return lax.dot_general(left, right, (((1,), (1,)), ((), ())), preferred_element_type=F32)


def dot_nn(left, right):
    return lax.dot_general(left, right, (((1,), (0,)), ((), ())), preferred_element_type=F32)


def split(value):
    high = value.astype(BF16)
    return high, (value - high.astype(F32)).astype(BF16)


def left_3(parts):
    return jnp.concatenate([parts[0], parts[0], parts[1]], axis=1)


def right_3(parts):
    return jnp.concatenate([parts[0], parts[1], parts[0]], axis=0)


def triangle(size):
    row = lax.broadcasted_iota(jnp.int32, (size, size), 0)
    column = lax.broadcasted_iota(jnp.int32, (size, size), 1)
    return row, column


def packed(block, pull):
    row, column = triangle(128)
    last = block[128:256, 128:256]
    corner = jnp.where(row >= column, block[0:128, 0:128], last)
    middle = jnp.sum(jnp.where(row == column, last, 0.0), axis=0, keepdims=True)
    middle = jnp.concatenate([jnp.zeros_like(middle), middle], axis=1)
    top = jnp.concatenate([block[128:256, 0:128], corner], axis=1)
    tail = jnp.where(lax.broadcasted_iota(jnp.int32, (8, 256), 0) == 0, pull, middle)
    return jnp.concatenate([top, tail], axis=0)


def unpacked(value):
    row, column = triangle(128)
    low, corner = value[0:128, 0:128], value[0:128, 128:256]
    other = jnp.transpose(corner)
    first = jnp.where(row >= column, corner, other)
    last = jnp.where(row < column, corner, other)
    last = jnp.where(row == column, value[129:130, 128:256], last)
    top = jnp.concatenate([first, jnp.transpose(low)], axis=1)
    return jnp.concatenate([top, jnp.concatenate([low, last], axis=1)], axis=0), value[128:136]


def exchange_lanes(blocks, lane):
    blocks = [list(pair) for pair in blocks]
    for q in range(4):
        low, high = blocks[q], blocks[q + 4]
        blocks[q], blocks[q + 4] = [low[0], high[0]], [low[1], high[1]]
    for bit in range(2):
        step = 32 << bit
        odd = (lane & step) != 0
        for q in range(8):
            if q & (1 << bit):
                continue
            for h in range(2):
                low, high = blocks[q][h], blocks[q | (1 << bit)][h]
                blocks[q][h] = jnp.where(odd, pltpu.roll(high, step, 1), low)
                blocks[q | (1 << bit)][h] = jnp.where(odd, high, pltpu.roll(low, LANES - step, 1))
    return blocks


def group_of(variable, index):
    return variable + (variable * 2 + index - 4 if index > 3 else 18 - 3 * index)


def row_of(group):
    return 20 * group + (4 if group >= 15 else 0)


def difference(latitudes):
    source = lax.broadcasted_iota(jnp.int32, (latitudes, latitudes), 0)
    target = lax.broadcasted_iota(jnp.int32, (latitudes, latitudes), 1)
    shift = (source == target + 1).astype(F32) - (source == target - 1).astype(F32)
    return shift.astype(BF16)


def rows_apart(value, shift):
    flat = value.reshape(-1, value.shape[-1])
    return dot_nn(flat, shift).reshape(value.shape)


def fluxes(east, deep):
    return (deep * east.astype(F32)).astype(BF16).astype(F32)


def heights(field, north, deep, ahead, behind, shift):
    flux_north = (deep * north.astype(F32)).astype(BF16)
    raised = field.astype(F32) - half_step * ((ahead - behind) + rows_apart(flux_north, shift))
    return raised.astype(BF16)


def velocities(east, north, here, ahead, behind, turning, shift):
    east, north = east.astype(F32), north.astype(F32)
    apart = ahead.astype(F32) - behind.astype(F32)
    new_east = east + turning * north - half_step * apart
    new_north = north - turning * east - half_step * rows_apart(here, shift)
    return new_east.astype(BF16), new_north.astype(BF16)


def put_group(staged, block, eye, first):
    latitudes = eye.shape[0]
    rows = latitudes // 8
    turned = dot_nt(eye, block.reshape(256, latitudes))
    for s in range(8):
        staged[s, first : first + rows, :] = turned[rows * s : rows * (s + 1)]


def turning_row(latitudes):
    position = lax.broadcasted_iota(jnp.int32, (8, latitudes), 1).astype(F32)
    turning = coriolis_scale * jnp.sin(math.pi * ((position + 0.5) / latitudes - 0.5))
    return turning[0:1, :][None]


def inner_kernel(
    ens, depth, out, to_first, to_second, here, deep, flux, height, staged, edges, arrived
):
    columns, members, latitudes = here.shape[1:]
    batch = columns // 5
    pieces = [pltpu.make_async_copy(depth, deep, arrived.at[5])]
    for k in range(5):
        span = pl.ds(k * batch, batch)
        piece = pltpu.make_async_copy(ens.at[:, span], here.at[:, span], arrived.at[k])
        pieces.append(piece)
    for piece in pieces:
        piece.start()
    shift = difference(latitudes)
    turning = turning_row(latitudes)
    eye = identity(latitudes, BF16)
    pieces[0].wait()

    def depths(first, count):
        rows = [deep[c : c + 1, :] for c in range(first, first + count)]
        return jnp.stack([jnp.broadcast_to(row, (members, latitudes)) for row in rows])

    def edge(side, near, far):
        edges[side, 0] = here[0, near]
        edges[side, 1] = (deep[near : near + 1, :] * here[2, near].astype(F32)).astype(BF16)
        edges[side, 2] = flux[near].astype(BF16)
        edges[side, 3] = flux[far].astype(BF16)

    staged[:, 300:INNER, :] = jnp.zeros((8, INNER - 300, 256), F32)
    done = 2
    for k in range(5):
        pieces[k + 1].wait()
        first, count = k * batch, batch if k else 2
        flux[first : first + count] = fluxes(here[1, first : first + count], depths(first, count))
        if k == 0:
            edge(0, 0, 1)
            continue
        if k == 4:
            edge(1, columns - 1, columns - 2)
        low, high = max(first - 1, batch + 1), first + batch - 1
        at = slice(low, high)
        ahead, behind = flux[low + 1 : high + 1], flux[low - 1 : high - 1]
        height[at] = heights(
            here[0, at], here[2, at], depths(low, high - low), ahead, behind, shift
        )
        while done < 7 and 8 * done + 9 <= high:
            first = 8 * done
            at = slice(first, first + 8)
            ahead, behind = height[first + 1 : first + 9], height[first - 1 : first + 7]
            new = velocities(here[1, at], here[2, at], height[at], ahead, behind, turning, shift)
            for v, field in enumerate((height[at],) + new):
                put_group(staged, field, eye, row_of(group_of(v, done)))
            done += 1
    odd = lax.axis_index("band") & 1
    to_first[...] = edges[1 - odd]
    to_second[...] = edges[odd]
    out[...] = staged[...].astype(BF16)


def outer_kernel(
    west_block, east_block, first_swap, second_swap, depth, *refs
):
    straight, cross, flux, height, staged, swapped = refs
    odd = lax.axis_index("band") & 1
    for side, block in enumerate((first_swap, second_swap)):
        swapped[side] = block[...]
    left, right = swapped.at[1 - odd], swapped.at[odd]
    members, latitudes = west_block.shape[2:]
    shift = difference(latitudes)
    turning = turning_row(latitudes)
    eye = identity(latitudes, BF16)

    def depths(first, count):
        return jnp.stack(
            [
                jnp.broadcast_to(depth[c : c + 1, :], (members, latitudes))
                for c in range(first, first + count)
            ]
        )

    def window(ens, edge, first, count, low, high):
        is_left = low == 0
        base = 2 if is_left else 0
        flux[base : base + count] = fluxes(ens[1, 0:count], depths(first, count))
        at = 0 if is_left else count
        near, far = (1, 0) if is_left else (at, at + 1)
        flux[near] = edge[2].astype(F32)
        flux[far] = edge[3].astype(F32)
        wide = high - low + 1
        skip = 0 if is_left else 1
        columns = slice(skip, skip + wide)
        new = heights(
            ens[0, columns],
            ens[2, columns],
            depths(first + skip, wide),
            flux[base + skip + 1 : base + skip + 1 + wide],
            flux[base + skip - 1 : base + skip - 1 + wide],
            shift,
        )
        start = 1 if is_left else 0
        height[start : start + wide] = new
        place = 0 if is_left else wide
        middle = near
        east_west = flux[middle + 1] - flux[middle - 1]
        raised = edge[0].astype(F32) - half_step * (east_west + rows_apart(edge[1], shift))
        height[place] = raised.astype(BF16)
        count = high - low
        here = height[1 : 1 + count]
        ahead, behind = height[2 : 2 + count], height[0:count]
        at = slice(low - first, high - first)
        return (here,) + velocities(ens[1, at], ens[2, at], here, ahead, behind, turning, shift)

    for v, field in enumerate(window(west_block, left, 0, 18, 0, 16)):
        for index in range(2):
            at = row_of(group_of(v, index)) - INNER
            put_group(staged, field[8 * index : 8 * index + 8], eye, at)
    ends = window(east_block, right, 54, 6, 56, 60)
    put_group(staged, jnp.concatenate([ends[0], ends[1]], axis=0), eye, 120)
    block = jnp.concatenate([ends[2], ends[2]], axis=0).reshape(256, latitudes)
    turned = dot_nt(eye, block)
    lower = lax.broadcasted_iota(jnp.int32, (10, 256), 1) < LANES
    for s in range(8):
        rows = [turned[20 * s + 10 * k : 20 * s + 10 * k + 10] for k in range(2)]
        staged[s, 140:150, :] = jnp.where(lower, rows[0], rows[1])
    staged[:, 150:OUTER, :] = jnp.zeros((8, OUTER - 150, 256), F32)
    me = lax.axis_index("mem")
    for k, d in enumerate(CHIPS):
        straight[k] = staged[me ^ d].astype(BF16)
        cross[k] = staged[me ^ d ^ 1].astype(BF16)


def spread_block(source, held, wide, start, lane):
    spans = [slice(h * LANES, (h + 1) * LANES) for h in range(2)]
    count = source.shape[1]
    here = pl.ds(start, 16)
    blocks = exchange_lanes([[source[q, here, span] for span in spans] for q in range(8)], lane)
    for q in range(8):
        to = pl.ds(pl.multiple_of(q * count + start, 8), 16)
        for h in range(2):
            wide[h, to, :] = blocks[q][h].astype(F32)
            held[q, here, spans[h]] = blocks[q][h]


def spread_kernel(cells, got, held, seen, wide):
    lane = lax.broadcasted_iota(jnp.int32, (16, LANES), 1)

    def step(index, carry):
        spread_block(got, held, wide, pl.multiple_of(index * 16, 16), lane)
        return carry

    lax.fori_loop(0, INNER // 16, step, 0, unroll=4)
    slots = seen.shape[2]
    unroll = 16

    def pick(index, carry):
        for t in range(2):
            for k in range(unroll):
                slot = index * unroll + k
                row = cells[t, slot]
                for h in range(2):
                    seen[t, h, pl.ds(slot, 1), :] = wide[h, pl.ds(row, 1), :]
        return carry

    lax.fori_loop(0, slots // unroll, pick, 0)


def observe_kernel(cells, outer, weight, target, first, straight, cross, *refs):
    edges, (held, gram, to_first, to_second, joined, wide, seen) = refs[:3], refs[3:]
    wholes = []
    lane = lax.broadcasted_iota(jnp.int32, (16, LANES), 1)
    me = lax.axis_index("mem")
    for k, d in enumerate(CHIPS):
        joined[me ^ d, 0:OUTER, :] = straight[0] if k == 0 else edges[k - 1][0]
        joined[me ^ d ^ 1, 0:OUTER, :] = cross[0] if k == 0 else edges[k - 1][1]
    for start in (*range(0, OUTER - 16, 16), OUTER - 16):
        spread_block(joined, held, wide, start, lane)
    slots = first.shape[2]
    seen[:, :, 0:slots, :] = first[...]
    for t in range(2):

        def pick(index, carry):
            for k in range(8):
                slot = outer[t, index * 8 + k]
                row = cells[t, slot] - 8 * INNER
                for h in range(2):
                    seen[t, h, pl.ds(slot, 1), :] = wide[h, pl.ds(row, 1), :]
            return carry

        lax.fori_loop(0, (outer[t, slots + LANES - 1] + 7) // 8, pick, 0)
    eye = identity(256, BF16)
    for t in range(2):
        values = jnp.concatenate([seen[t, h, 0:slots] for h in range(2)], axis=1).astype(BF16)
        turned = dot_nt(eye, values)
        mean = jnp.sum(turned, axis=0, keepdims=True) * (1.0 / 256)
        root = weight[t : t + 1, :]
        spread = (root * (turned - mean)).astype(BF16)
        misfit = (root * (target[t : t + 1, :] - mean)).astype(BF16)
        block = dot_nt(spread, spread)
        pull = dot_nt(jnp.broadcast_to(misfit, (16, slots)), spread)
        whole = packed(block, pull[0:8])
        gram[t] = whole
        wholes.append(whole.astype(BF16))
    odd = (lax.axis_index("band") & 1) == 1
    to_first[...] = jnp.where(odd, wholes[0], wholes[1])
    to_second[...] = jnp.where(odd, wholes[1], wholes[0])


def combine_kernel(gram, first_swap, second_swap, line, short):
    odd = (lax.axis_index("band") & 1) == 1
    first, second = first_swap[...].astype(F32), second_swap[...].astype(F32)
    west, east = jnp.where(odd, first, second), jnp.where(odd, second, first)
    for t, beside in enumerate((west + gram[1], gram[0] + east)):
        total = gram[t] + neighbour_weight * beside
        line[t] = total
        short[t] = total.astype(BF16)


def prepare_kernel(inner, outer, *refs):
    average = jnp.full((256, LANES), 1.0 / 256, BF16)
    for q in range(8):
        pieces = (inner[q, 0:FIRST], jnp.concatenate([inner[q, FIRST:INNER], outer[q, 0:OUTER]], axis=0))
        for k, piece in enumerate(pieces):
            mean = dot_nn(piece, average)
            refs[2 * k + 1][q] = mean
            mean = jnp.concatenate([mean, mean], axis=1)
            refs[2 * k][q] = (piece.astype(F32) - mean).astype(BF16)


def send_back(results, outs):
    lane = lax.broadcasted_iota(jnp.int32, (16, LANES), 1)
    spans = [slice(h * LANES, (h + 1) * LANES) for h in range(2)]

    def move(start):
        here = pl.ds(start, 16)
        blocks = [[results[q, here, span] for span in spans] for q in range(8)]
        blocks = exchange_lanes(blocks, lane)
        for q in range(8):
            for h in range(2):
                outs[ORDER.index(q)][here, spans[h]] = blocks[q][h]

    def step(index, carry):
        move(pl.multiple_of(index * 16, 16))
        return carry

    count = results.shape[1]
    lax.fori_loop(0, count // 16, step, 0, unroll=4)
    if count % 16:
        move(count - 16)


def apply_maps(anomaly, mean, maps, results, q, edge, order):
    count = results.shape[1]
    low, high = edge // 16 * 16, (edge + 15) // 16 * 16
    first = dot_nt(anomaly[q, 0:high], maps[order[0]])
    centre = jnp.concatenate([mean[q], mean[q]], axis=1)
    results[q, 0:low] = (centre[0:low] + first[0:low]).astype(BF16)
    if low == count:
        return
    second = dot_nt(anomaly[q, low:count], maps[order[1]])
    if low < high:
        near = lax.broadcasted_iota(jnp.int32, (16, 256), 0) < edge - low
        both = jnp.where(near, first[low:high], second[0:16])
        results[q, low:high] = (centre[low:high] + both).astype(BF16)
    results[q, high:count] = (centre[high:count] + second[high - low : count - low]).astype(BF16)


def second_kernel(maps, anomaly, mean, *refs):
    outs, results = refs[:8], refs[8]
    both = [maps[0], maps[1]]
    for q in range(8):
        apply_maps(anomaly, mean, both, results, q, 184, (0, 1))
    send_back(results, outs)


def analyse_kernel(line, below, above, anomaly, mean, *refs):
    outs, (kept, results, ordered) = refs[:8], refs[8:]
    size = 256
    eye = identity(size, F32)
    norms, pulls, roots, inverses = [], [], [], []
    for t in range(2):
        beside = below[t].astype(F32) + above[t].astype(F32)
        block, pull = unpacked(line[t] + neighbour_weight * beside)
        system = (size - 1) * eye + block
        square = jnp.sum(jnp.sum(system * system, axis=0, keepdims=True), axis=1, keepdims=True)
        norms.append(jnp.sqrt(square))
        pulls.append(pull)
        roots.append(system / norms[t])
    for sweep in range(SWEEPS):
        rights = [right_3(split(root)) for root in roots]
        if sweep == 0:
            inverses = [1.5 * eye - 0.5 * root for root in roots]
            lefts = [left_3(split(inverse)) for inverse in inverses]
            roots = [dot_nn(left, right) for left, right in zip(lefts, rights)]
            continue
        parts = [split(inverse) for inverse in inverses]
        products = [dot_nn(left_3(part), right) for part, right in zip(parts, rights)]
        middles = [left_3(split(1.5 * eye - 0.5 * product)) for product in products]
        if sweep < SWEEPS - 1:
            roots = [dot_nn(middle, right) for middle, right in zip(middles, rights)]
        inverses = [dot_nn(middle, right_3(part)) for middle, part in zip(middles, parts)]
    maps = []
    for t in range(2):
        right = right_3(split(inverses[t]))
        half_pull = dot_nn(left_3(split(pulls[t])), right)
        shift = dot_nn(left_3(split(half_pull)), right) / norms[t]
        scale = math.sqrt(size - 1) / jnp.sqrt(norms[t])
        ordered[t] = (inverses[t] * scale + shift[0:1]).astype(BF16).reshape(8, 32, size)
    me = lax.axis_index("mem")
    for t in range(2):
        maps.append(jnp.concatenate([ordered[t, me ^ d] for d in range(8)], axis=0))
        kept[t] = maps[t]
    for q in range(8):
        apply_maps(anomaly, mean, maps, results, q, 180 if q < 6 else FIRST, (1, 0))
    send_back(results, outs)


def spread_strips(got, wide):
    me = lax.axis_index("mem")
    for k, d in enumerate(ORDER):
        wide[me ^ d] = got[k][...].astype(F32)


def take_group(wide, turned, eye, g, shape, skipped=0):
    rows = shape[2] // 8
    at = row_of(g) - row_of(skipped)
    g = g - skipped
    for s in range(8):
        turned[g, rows * s : rows * (s + 1), :] = wide[s, at : at + rows, :]
    return dot_nt(eye, turned[g].astype(BF16)).astype(BF16).reshape(shape)


def first_return_kernel(*refs):
    got, (out, wide, turned, planes, sent) = refs[:8], refs[8:]
    shape = (8,) + planes.shape[2:]
    spread_strips(got, wide)
    eye = identity(256, BF16)
    copies = []
    for v in range(3):
        for index in range(3, 7):
            at = 8 * (index - 3)
            planes[v, at : at + 8] = take_group(wide, turned, eye, group_of(v, index), shape)
        copies.append(pltpu.make_async_copy(planes.at[v], out.at[v, pl.ds(24, 32)], sent.at[v]))
        copies[v].start()
    for copy in copies:
        copy.wait()


def second_return_kernel(*refs):
    got, (_, out, wide, turned, planes, sent) = refs[:8], refs[8:]
    shape = (8,) + planes.shape[2:]
    spread_strips(got, wide)
    eye = identity(256, BF16)
    mixed = take_group(wide, turned, eye, 21, shape, 12)
    planes[0, 24:28] = mixed[0:4]
    planes[1, 24:28] = mixed[4:8]
    at = row_of(22) - row_of(12)
    turned[10] = jnp.zeros(turned.shape[1:], F32)
    for s in range(8):
        for k in range(2):
            to = 20 * s + 10 * k
            half = wide[s, at : at + 10, k * LANES : (k + 1) * LANES]
            turned[10, to : to + 10, 0:LANES] = half
    block = dot_nt(eye, turned[10].astype(BF16)).astype(BF16).reshape(shape)
    planes[2, 24:28] = block[0:4]
    copies = []
    for v in range(3):
        for index in range(3):
            at = 8 * index
            block = take_group(wide, turned, eye, group_of(v, index), shape, 12)
            planes[v, at : at + 8] = block
        for k, (at, to, count) in enumerate(((0, 0, 24), (24, 56, 4))):
            source, target = planes.at[v, pl.ds(at, count)], out.at[v, pl.ds(to, count)]
            copies.append(pltpu.make_async_copy(source, target, sent.at[2 * v + k]))
            copies[-1].start()
    for copy in copies:
        copy.wait()


def swapped_pairs(values, axis, pairs):
    moved = []
    for value, some in zip(values, pairs):
        both = some + [(j, i) for i, j in some]
        moved.append(lax.ppermute(value, axis, both))
    return moved


def band_swaps(first, second):
    count = lax.axis_size("band")
    starts = range(0, count, 2)
    pairs = [[(i, i + 1) for i in starts], [(i + 1, (i + 2) % count) for i in starts]]
    return swapped_pairs((first, second), "band", pairs)


def mem_swaps(value):
    count = lax.axis_size("mem")
    pairs = [[(i, i + 1) for i in range(k, count - 1, 2)] for k in range(2)]
    return swapped_pairs((value, value), "mem", pairs)


def across(value, difference):
    return lax.ppermute(value, "mem", [(i, i ^ difference) for i in range(8)])


def partners(values):
    return [across(value, d) if d else value for d, value in zip(ORDER, values)]


def swap(value):
    return lax.all_to_all(value, "mem", split_axis=0, concat_axis=0, tiled=True)


def cell_rows(cell):
    variable = cell // 600
    tile = jnp.arange(2, dtype=jnp.int32)[:, None]
    column = tile * 30 + cell // 20 % 30
    index = column // 8
    place = column % 8
    group = variable + jnp.where(index > 3, variable * 2 + index - 4, 18 - 3 * index)
    is_last = column >= 56
    group = jnp.where(is_last, 21 + variable // 2, group)
    place = jnp.where(is_last, column - 56 + 4 * (variable % 2), place)
    row = cell % 20
    place = jnp.where(group == 22, place + 4 * (row // 10), place)
    row = jnp.where(group == 22, row % 10, row)
    first = place * INNER + group * 20
    last = 8 * INNER + place * OUTER + (group - 15) * 20
    return jnp.where(group < 15, first, last) + row


def on_device_fast(
    ensemble, layer_depth, observed_cell, observed_value, error_variance, observed_count
):
    members, _, columns, latitudes = ensemble.shape
    slots = observed_cell.shape[2]
    planes = jnp.transpose(ensemble, (1, 2, 0, 3))
    edge = jax.ShapeDtypeStruct((4, members, latitudes), BF16)
    far = pl.BlockSpec(memory_space=pltpu.HBM)
    sent, to_first, to_second = pl.pallas_call(
        inner_kernel,
        out_shape=(jax.ShapeDtypeStruct((8, INNER, 256), BF16), edge, edge),
        in_specs=[far, far],
        scratch_shapes=[
            pltpu.VMEM(planes.shape, BF16),
            pltpu.VMEM((columns, latitudes), F32),
            pltpu.VMEM((columns, members, latitudes), F32),
            pltpu.VMEM((columns, members, latitudes), BF16),
            pltpu.VMEM((8, INNER, 256), F32),
            pltpu.VMEM((2, 4, members, latitudes), BF16),
            pltpu.SemaphoreType.DMA((6,)),
        ],
        compiler_params=params(60),
        name="inner",
    )(planes, layer_depth)
    got = swap(sent)
    swaps = band_swaps(to_first, to_second)
    flat = pl.BlockSpec((4, members, latitudes), lambda i: (0, 0, 0))
    straight, cross = pl.pallas_call(
        outer_kernel,
        grid=(1,),
        out_shape=(jax.ShapeDtypeStruct((4, OUTER, 256), BF16),) * 2,
        in_specs=[
            pl.BlockSpec((3, 20, members, latitudes), lambda i: (0, 0, 0, 0)),
            pl.BlockSpec((3, 6, members, latitudes), lambda i: (0, 9, 0, 0)),
            flat,
            flat,
            pl.BlockSpec((columns, latitudes), lambda i: (0, 0)),
        ],
        out_specs=(pl.BlockSpec((4, OUTER, 256), lambda i: (0, 0, 0)),) * 2,
        scratch_shapes=[
            pltpu.VMEM((20, members, latitudes), F32),
            pltpu.VMEM((18, members, latitudes), BF16),
            pltpu.VMEM((8, OUTER, 256), F32),
            pltpu.VMEM((2, 4, members, latitudes), BF16),
        ],
        compiler_params=params(24),
        name="outer",
    )(planes, planes, *swaps, layer_depth)
    cross = across(cross, 1)
    got_edges = [across(jnp.stack([straight[k], cross[k]]), CHIPS[k]) for k in (3, 1, 2)]
    got_edges = got_edges[1:] + got_edges[:1]

    rows = cell_rows(observed_cell[0])
    live = jnp.arange(slots, dtype=jnp.int32)[None, :] < observed_count[0][:, None]
    root = jnp.sqrt(jnp.where(live, 1.0 / error_variance[0], 0.0))
    vmem = pl.BlockSpec(memory_space=pltpu.VMEM)
    slot = jnp.arange(slots, dtype=jnp.int32)
    place = jnp.arange(slots + LANES, dtype=jnp.int32)
    is_outer = rows >= 8 * INNER
    near = jnp.where(is_outer, 0, rows)
    rank = jnp.sum(is_outer[:, None, :] & (slot[None, :] < slot[:, None])[None], axis=2)
    count = jnp.sum(is_outer, axis=1, keepdims=True)
    found = is_outer[:, None, :] & (rank[:, None, :] == place[None, :, None])
    outer = jnp.sum(jnp.where(found, slot, 0), axis=2)
    outer = jnp.where(place[None] < count, outer, slots)
    outer = jnp.where(place[None] == slots + LANES - 1, count, outer).astype(jnp.int32)
    rows = jnp.pad(rows, ((0, 0), (0, LANES)), constant_values=8 * INNER)
    smem = pl.BlockSpec(memory_space=pltpu.SMEM)
    held_inner, seen = pl.pallas_call(
        spread_kernel,
        out_shape=(
            jax.ShapeDtypeStruct((8, INNER, 256), BF16),
            jax.ShapeDtypeStruct((2, 2, slots, LANES), F32),
        ),
        in_specs=[smem, vmem],
        scratch_shapes=[pltpu.VMEM((2, 8 * INNER, LANES), F32)],
        compiler_params=params(12),
        cost_estimate=cost(1, 8 * MIB),
        name="spread",
    )(near, got)
    one_tile = jax.ShapeDtypeStruct((PACKED, 256), BF16)
    held_outer, gram, to_first, to_second = pl.pallas_call(
        observe_kernel,
        out_shape=(
            jax.ShapeDtypeStruct((8, OUTER, 256), BF16),
            jax.ShapeDtypeStruct((2, PACKED, 256), F32),
            one_tile,
            one_tile,
        ),
        in_specs=[smem, smem] + [vmem] * 8,
        scratch_shapes=[
            pltpu.VMEM((8, OUTER, 256), BF16),
            pltpu.VMEM((2, 8 * OUTER, LANES), F32),
            pltpu.VMEM((2, 2, slots + 8, LANES), F32),
        ],
        compiler_params=params(16),
        name="observe",
    )(rows, outer, root, observed_value[0], seen, straight, cross, *got_edges)
    anomaly_1, mean_1, anomaly_2, mean_2 = pl.pallas_call(
        prepare_kernel,
        out_shape=(
            jax.ShapeDtypeStruct((8, FIRST, 256), BF16),
            jax.ShapeDtypeStruct((8, FIRST, LANES), F32),
            jax.ShapeDtypeStruct((8, SECOND, 256), BF16),
            jax.ShapeDtypeStruct((8, SECOND, LANES), F32),
        ),
        compiler_params=params(12),
        cost_estimate=cost(1, 6 * MIB),
        name="prepare",
    )(held_inner, held_outer)

    line, short = pl.pallas_call(
        combine_kernel,
        out_shape=(
            jax.ShapeDtypeStruct(gram.shape, F32),
            jax.ShapeDtypeStruct(gram.shape, BF16),
        ),
        compiler_params=params(8),
        name="combine",
    )(gram, *band_swaps(to_first, to_second))
    below, above = mem_swaps(short)
    *back, maps = pl.pallas_call(
        analyse_kernel,
        out_shape=(jax.ShapeDtypeStruct((FIRST, 256), BF16),) * 8
        + (jax.ShapeDtypeStruct((2, 256, 256), BF16),),
        scratch_shapes=[pltpu.VMEM((8, FIRST, 256), BF16), pltpu.VMEM((2, 8, 32, 256), BF16)],
        compiler_params=params(20),
        name="analyse",
    )(line, below, above, anomaly_1, mean_1)
    first = partners(back)
    back = pl.pallas_call(
        second_kernel,
        out_shape=(jax.ShapeDtypeStruct((SECOND, 256), BF16),) * 8,
        scratch_shapes=[pltpu.VMEM((8, SECOND, 256), BF16)],
        compiler_params=params(16),
        cost_estimate=cost(1, 6 * MIB),
        name="second",
    )(maps, anomaly_2, mean_2)
    second = partners(back)
    result = jax.ShapeDtypeStruct(planes.shape, BF16)
    half = pl.pallas_call(
        first_return_kernel,
        out_shape=result,
        out_specs=far,
        scratch_shapes=[
            pltpu.VMEM((8, FIRST, 256), F32),
            pltpu.VMEM((12, latitudes, 256), F32),
            pltpu.VMEM((3, 32, members, latitudes), BF16),
            pltpu.SemaphoreType.DMA((3,)),
        ],
        compiler_params=params(20),
        cost_estimate=cost(1, 4 * MIB),
        name="first_return",
    )(*first)
    planes = pl.pallas_call(
        second_return_kernel,
        out_shape=result,
        in_specs=[vmem] * 8 + [far],
        out_specs=far,
        scratch_shapes=[
            pltpu.VMEM((8, SECOND, 256), F32),
            pltpu.VMEM((11, latitudes, 256), F32),
            pltpu.VMEM((3, 28, members, latitudes), BF16),
            pltpu.SemaphoreType.DMA((6,)),
        ],
        input_output_aliases={8: 0},
        compiler_params=params(20),
        name="second_return",
    )(*second, half)
    return jnp.transpose(planes, (2, 0, 1, 3))


def choose(ensemble, layer_depth, observed_cell, *rest):
    mesh_shape = (lax.axis_size("mem"), lax.axis_size("band"))
    shape = (mesh_shape, ensemble.shape, observed_cell.shape[1])
    fits = shape == ((8, 4), (32, 3, 60, 160), 2) and observed_cell.shape[2] % 16 == 0
    chosen = on_device_fast if fits else on_device
    return chosen(ensemble, layer_depth, observed_cell, *rest)


def solution(mesh):
    in_specs = (
        P("mem", None, "band", None),
        P("band", None),
        P("mem", "band", None),
        P("mem", "band", None),
        P("mem", "band", None),
        P("mem", "band"),
    )
    out_specs = P("mem", None, "band", None)
    return jax.shard_map(
        choose, mesh=mesh, in_specs=in_specs, out_specs=out_specs, check_vma=False
    )
```

```python
import math

import jax
import jax.numpy as jnp
import numpy as np
from jax import lax
from jax.experimental import pallas as pl
from jax.experimental.pallas import tpu as pltpu
from jax.sharding import PartitionSpec as P

SWEEPS = 5


half_step = 0.1
coriolis_scale = 0.3
neighbour_weight = 0.75


def padded_2(cells, sides, width):
    for axis, dim in sides:
        count = lax.axis_size(axis)
        head = lax.slice_in_dim(cells, 0, width, axis=dim)
        tail = lax.slice_in_dim(cells, cells.shape[dim] - width, cells.shape[dim], axis=dim)
        cells = jnp.concatenate(
            [
                lax.ppermute(tail, axis, [(i, (i + 1) % count) for i in range(count)]),
                cells,
                lax.ppermute(head, axis, [((i + 1) % count, i) for i in range(count)]),
            ],
            axis=dim,
        )
    return cells


def north_south(source):
    widths = [(0, 0)] * (source.ndim - 1) + [(1, 1)]
    padded = jnp.pad(source, widths)
    return padded[..., 2:] - padded[..., :-2]


def coriolis(latitudes):
    position = jnp.arange(latitudes, dtype=jnp.float32)
    return coriolis_scale * jnp.sin(math.pi * ((position + 0.5) / latitudes - 0.5))


def newton_schulz(starting):
    identity = jnp.eye(starting.shape[-1], dtype=starting.dtype)
    root_part = starting
    inverse_root = jnp.broadcast_to(identity, starting.shape)
    for sweep_index in range(SWEEPS):
        product = jnp.einsum(
            "tij,tjk->tik", inverse_root, root_part, precision=lax.Precision.HIGHEST
        )
        middle = 1.5 * identity - 0.5 * product
        root_part = jnp.einsum("tij,tjk->tik", root_part, middle, precision=lax.Precision.HIGHEST)
        inverse_root = jnp.einsum(
            "tij,tjk->tik", middle, inverse_root, precision=lax.Precision.HIGHEST
        )
    return inverse_root


def on_device(ensemble, layer_depth, observed_cell, observed_value, error_variance, observed_count):
    block_members = ensemble.shape[0]
    columns = ensemble.shape[2]
    latitudes = ensemble.shape[3]
    strips = lax.axis_size("mem")
    members = block_members * strips
    strip_rows = latitudes // strips
    tile_count = observed_cell.shape[1]
    tile_columns = columns // tile_count
    slot_count = observed_cell.shape[2]
    tile_cells = 3 * tile_columns * strip_rows
    height = ensemble[:, 0].astype(jnp.float32)
    eastward = ensemble[:, 1].astype(jnp.float32)
    northward = ensemble[:, 2].astype(jnp.float32)
    turning = coriolis(latitudes)
    flux_east = (layer_depth * eastward).astype(jnp.bfloat16)
    flux_north = (layer_depth * northward).astype(jnp.bfloat16)
    east_margin = padded_2(flux_east, (("band", 1),), 1)
    east_west = east_margin[:, 2:].astype(jnp.float32) - east_margin[:, :-2].astype(jnp.float32)
    north_local = lax.optimization_barrier(flux_north).astype(jnp.float32)
    raised = height - half_step * (east_west + north_south(north_local))
    surface_elevation_cast = raised.astype(jnp.bfloat16)
    height_margin = padded_2(surface_elevation_cast, (("band", 1),), 1)
    margin_wide = height_margin.astype(jnp.float32)
    height_inner = margin_wide[:, 1:-1]
    revised_zonal_velocity = (
        eastward + turning * northward - half_step * (margin_wide[:, 2:] - margin_wide[:, :-2])
    )
    revised_meridional_velocity = (
        northward - turning * eastward - half_step * north_south(height_inner)
    )
    advance_dynamics = jnp.stack(
        [
            surface_elevation_cast,
            revised_zonal_velocity.astype(jnp.bfloat16),
            revised_meridional_velocity.astype(jnp.bfloat16),
        ],
        axis=1,
    )
    reordered = advance_dynamics.reshape(
        block_members, 3, tile_count, tile_columns, strips, strip_rows
    )
    reordered = jnp.transpose(reordered, (4, 2, 0, 1, 3, 5)).reshape(
        strips, tile_count, block_members, tile_cells
    )
    tile_block = lax.all_to_all(reordered, "mem", split_axis=0, concat_axis=2, tiled=True)[0]
    cells_here = observed_cell[0]
    values = jnp.take_along_axis(tile_block, cells_here[:, None, :], axis=2)
    observed_mean = jnp.sum(values, axis=1, dtype=jnp.float32) / members
    slot_index = jnp.arange(slot_count, dtype=jnp.int32)[None, :]
    live_slots = slot_index < observed_count[0][:, None]
    root_weight = jnp.sqrt(jnp.where(live_slots, 1.0 / error_variance[0], 0.0))
    spread = (
        root_weight[:, None, :] * (values.astype(jnp.float32) - observed_mean[:, None, :])
    ).astype(jnp.bfloat16)
    misfit = (root_weight * (observed_value[0] - observed_mean)).astype(jnp.bfloat16)
    spread_margin, misfit_margin = (
        padded_2(spread[None], (("mem", 0), ("band", 1)), 1),
        padded_2(misfit[None], (("mem", 0), ("band", 1)), 1),
    )
    gram_margin = jnp.einsum(
        "atko,atlo->atkl", spread_margin, spread_margin, preferred_element_type=jnp.float32
    )
    pull_margin = jnp.einsum(
        "atko,ato->atk", spread_margin, misfit_margin, preferred_element_type=jnp.float32
    )
    strip_here = lax.axis_index("mem")
    lower_valid = (strip_here > 0).astype(jnp.float32)
    upper_valid = (strip_here < strips - 1).astype(jnp.float32)
    strip_mask = (lower_valid, 1.0, upper_valid)
    total_gram = jnp.zeros((tile_count, members, members), jnp.float32)
    total_pull = jnp.zeros((tile_count, members), jnp.float32)
    for offset_lat in range(3):
        for offset_lon in range(3):
            factor = (
                neighbour_weight ** (abs(offset_lat - 1) + abs(offset_lon - 1))
                * strip_mask[offset_lat]
            )
            total_gram = (
                total_gram + factor * gram_margin[offset_lat, offset_lon : offset_lon + tile_count]
            )
            total_pull = (
                total_pull + factor * pull_margin[offset_lat, offset_lon : offset_lon + tile_count]
            )
    system = (members - 1) * jnp.eye(members, dtype=jnp.float32)[None] + total_gram
    frobenius = jnp.sqrt(jnp.sum(system * system, axis=(1, 2)))
    inverse_root = newton_schulz(system / frobenius[:, None, None])
    spread_map = inverse_root * (math.sqrt(members - 1) / jnp.sqrt(frobenius))[:, None, None]
    half_pull = jnp.einsum("tij,tj->ti", inverse_root, total_pull, precision=lax.Precision.HIGHEST)
    shift_weights = (
        jnp.einsum("tij,tj->ti", inverse_root, half_pull, precision=lax.Precision.HIGHEST)
        / frobenius[:, None]
    )
    weights = (spread_map + shift_weights[:, :, None]).astype(jnp.bfloat16)
    state_mean = jnp.sum(tile_block, axis=1, dtype=jnp.float32) / members
    anomaly = (tile_block.astype(jnp.float32) - state_mean[:, None, :]).astype(jnp.bfloat16)
    update = jnp.einsum("tjk,tjc->tkc", weights, anomaly, preferred_element_type=jnp.float32)
    analysed = (state_mean[:, None, :] + update).astype(jnp.bfloat16)
    returned = lax.all_to_all(analysed[None], "mem", split_axis=2, concat_axis=0, tiled=True)
    returned = returned.reshape(strips, tile_count, block_members, 3, tile_columns, strip_rows)
    return jnp.transpose(returned, (2, 3, 1, 4, 0, 5)).reshape(block_members, 3, columns, latitudes)


LANES = 128
GROUPS = 23
INNER = 304
OUTER = 152
FIRST = 240
SECOND = 216
F32 = jnp.float32
BF16 = jnp.bfloat16
PACKED = 136
CHIPS = (0, 2, 4, 6)
ORDER = (6, 2, 4, 7, 1, 3, 5, 0)
MIB = 1024 * 1024


def params(size):
    return pltpu.CompilerParams(vmem_limit_bytes=size * MIB)


def cost(flops, moved):
    return pl.CostEstimate(flops=flops, bytes_accessed=moved, transcendentals=0)


def identity(size, dtype):
    row = lax.broadcasted_iota(jnp.int32, (size, size), 0)
    column = lax.broadcasted_iota(jnp.int32, (size, size), 1)
    return (row == column).astype(F32).astype(dtype)


def dot_nt(left, right):
    return lax.dot_general(left, right, (((1,), (1,)), ((), ())), preferred_element_type=F32)


def dot_nn(left, right):
    return lax.dot_general(left, right, (((1,), (0,)), ((), ())), preferred_element_type=F32)


def split(value):
    high = value.astype(BF16)
    return high, (value - high.astype(F32)).astype(BF16)


def left_3(parts):
    return jnp.concatenate([parts[0], parts[0], parts[1]], axis=1)


def right_3(parts):
    return jnp.concatenate([parts[0], parts[1], parts[0]], axis=0)


def triangle(size):
    row = lax.broadcasted_iota(jnp.int32, (size, size), 0)
    column = lax.broadcasted_iota(jnp.int32, (size, size), 1)
    return row, column


def packed(block, pull):
    row, column = triangle(128)
    last = block[128:256, 128:256]
    corner = jnp.where(row >= column, block[0:128, 0:128], last)
    middle = jnp.sum(jnp.where(row == column, last, 0.0), axis=0, keepdims=True)
    middle = jnp.concatenate([jnp.zeros_like(middle), middle], axis=1)
    top = jnp.concatenate([block[128:256, 0:128], corner], axis=1)
    tail = jnp.where(lax.broadcasted_iota(jnp.int32, (8, 256), 0) == 0, pull, middle)
    return jnp.concatenate([top, tail], axis=0)


def unpacked(value):
    row, column = triangle(128)
    low, corner = value[0:128, 0:128], value[0:128, 128:256]
    other = jnp.transpose(corner)
    first = jnp.where(row >= column, corner, other)
    last = jnp.where(row < column, corner, other)
    last = jnp.where(row == column, value[129:130, 128:256], last)
    top = jnp.concatenate([first, jnp.transpose(low)], axis=1)
    return jnp.concatenate([top, jnp.concatenate([low, last], axis=1)], axis=0), value[128:136]


def exchange_lanes(blocks, lane):
    blocks = [list(pair) for pair in blocks]
    for q in range(4):
        low, high = blocks[q], blocks[q + 4]
        blocks[q], blocks[q + 4] = [low[0], high[0]], [low[1], high[1]]
    for bit in range(2):
        step = 32 << bit
        odd = (lane & step) != 0
        for q in range(8):
            if q & (1 << bit):
                continue
            for h in range(2):
                low, high = blocks[q][h], blocks[q | (1 << bit)][h]
                blocks[q][h] = jnp.where(odd, pltpu.roll(high, step, 1), low)
                blocks[q | (1 << bit)][h] = jnp.where(odd, high, pltpu.roll(low, LANES - step, 1))
    return blocks


def group_of(variable, index):
    return variable + (variable * 2 + index - 4 if index > 3 else 18 - 3 * index)


def row_of(group):
    return 20 * group + (4 if group >= 15 else 0)


def difference(latitudes):
    source = lax.broadcasted_iota(jnp.int32, (latitudes, latitudes), 0)
    target = lax.broadcasted_iota(jnp.int32, (latitudes, latitudes), 1)
    shift = (source == target + 1).astype(F32) - (source == target - 1).astype(F32)
    return shift.astype(BF16)


def rows_apart(value, shift):
    flat = value.reshape(-1, value.shape[-1])
    return dot_nn(flat, shift).reshape(value.shape)


def fluxes(east, deep):
    return (deep * east.astype(F32)).astype(BF16).astype(F32)


def heights(field, north, deep, ahead, behind, shift):
    flux_north = (deep * north.astype(F32)).astype(BF16)
    raised = field.astype(F32) - half_step * ((ahead - behind) + rows_apart(flux_north, shift))
    return raised.astype(BF16)


def velocities(east, north, here, ahead, behind, turning, shift):
    east, north = east.astype(F32), north.astype(F32)
    apart = ahead.astype(F32) - behind.astype(F32)
    new_east = east + turning * north - half_step * apart
    new_north = north - turning * east - half_step * rows_apart(here, shift)
    return new_east.astype(BF16), new_north.astype(BF16)


def put_group(staged, block, eye, first):
    latitudes = eye.shape[0]
    rows = latitudes // 8
    turned = dot_nt(eye, block.reshape(256, latitudes))
    for s in range(8):
        staged[s, first : first + rows, :] = turned[rows * s : rows * (s + 1)]


def turning_row(latitudes):
    position = lax.broadcasted_iota(jnp.int32, (8, latitudes), 1).astype(F32)
    turning = coriolis_scale * jnp.sin(math.pi * ((position + 0.5) / latitudes - 0.5))
    return turning[0:1, :][None]


def inner_kernel(
    ens, depth, out, to_first, to_second, here, deep, flux, height, staged, edges, arrived
):
    columns, members, latitudes = here.shape[1:]
    batch = columns // 5
    pieces = [pltpu.make_async_copy(depth, deep, arrived.at[5])]
    for k in range(5):
        span = pl.ds(k * batch, batch if k else 2)
        piece = pltpu.make_async_copy(ens.at[:, span], here.at[:, span], arrived.at[k])
        pieces.append(piece)
    for k in (0, 2, 3, 4, 5, 1):
        pieces[k].start()
    shift = difference(latitudes)
    turning = turning_row(latitudes)
    eye = identity(latitudes, BF16)
    pieces[0].wait()

    def depths(first, count):
        rows = [deep[c : c + 1, :] for c in range(first, first + count)]
        return jnp.stack([jnp.broadcast_to(row, (members, latitudes)) for row in rows])

    def edge(side, near, far):
        edges[side, 0] = here[0, near]
        edges[side, 1] = (deep[near : near + 1, :] * here[2, near].astype(F32)).astype(BF16)
        edges[side, 2] = flux[near].astype(BF16)
        edges[side, 3] = flux[far].astype(BF16)

    staged[:, 300:INNER, :] = jnp.zeros((8, INNER - 300, 256), F32)
    done = 2
    for k in (1, 2, 3, 4, 0):
        pieces[k + 1].wait()
        first, count = k * batch, batch if k else 2
        flux[first : first + count] = fluxes(here[1, first : first + count], depths(first, count))
        if k == 0:
            edge(0, 0, 1)
            continue
        if k == 4:
            edge(1, columns - 1, columns - 2)
        low, high = max(first - 1, batch + 1), first + batch - 1
        at = slice(low, high)
        ahead, behind = flux[low + 1 : high + 1], flux[low - 1 : high - 1]
        height[at] = heights(
            here[0, at], here[2, at], depths(low, high - low), ahead, behind, shift
        )
        while done < 7 and 8 * done + 9 <= high:
            first = 8 * done
            at = slice(first, first + 8)
            ahead, behind = height[first + 1 : first + 9], height[first - 1 : first + 7]
            new = velocities(here[1, at], here[2, at], height[at], ahead, behind, turning, shift)
            for v, field in enumerate((height[at],) + new):
                put_group(staged, field, eye, row_of(group_of(v, done)))
            done += 1
    odd = lax.axis_index("band") & 1
    to_first[...] = edges[1 - odd]
    to_second[...] = edges[odd]
    out[...] = staged[...].astype(BF16)


def outer_kernel(
    west_block, east_block, first_swap, second_swap, depth, *refs
):
    straight, cross, flux, height, staged, swapped = refs
    odd = lax.axis_index("band") & 1
    for side, block in enumerate((first_swap, second_swap)):
        swapped[side] = block[...]
    left, right = swapped.at[1 - odd], swapped.at[odd]
    members, latitudes = west_block.shape[2:]
    shift = difference(latitudes)
    turning = turning_row(latitudes)
    eye = identity(latitudes, BF16)

    def depths(first, count):
        return jnp.stack(
            [
                jnp.broadcast_to(depth[c : c + 1, :], (members, latitudes))
                for c in range(first, first + count)
            ]
        )

    def window(ens, edge, first, count, low, high):
        is_left = low == 0
        base = 2 if is_left else 0
        flux[base : base + count] = fluxes(ens[1, 0:count], depths(first, count))
        at = 0 if is_left else count
        near, far = (1, 0) if is_left else (at, at + 1)
        flux[near] = edge[2].astype(F32)
        flux[far] = edge[3].astype(F32)
        wide = high - low + 1
        skip = 0 if is_left else 1
        columns = slice(skip, skip + wide)
        new = heights(
            ens[0, columns],
            ens[2, columns],
            depths(first + skip, wide),
            flux[base + skip + 1 : base + skip + 1 + wide],
            flux[base + skip - 1 : base + skip - 1 + wide],
            shift,
        )
        start = 1 if is_left else 0
        height[start : start + wide] = new
        place = 0 if is_left else wide
        middle = near
        east_west = flux[middle + 1] - flux[middle - 1]
        raised = edge[0].astype(F32) - half_step * (east_west + rows_apart(edge[1], shift))
        height[place] = raised.astype(BF16)
        count = high - low
        here = height[1 : 1 + count]
        ahead, behind = height[2 : 2 + count], height[0:count]
        at = slice(low - first, high - first)
        return (here,) + velocities(ens[1, at], ens[2, at], here, ahead, behind, turning, shift)

    for v, field in enumerate(window(west_block, left, 0, 18, 0, 16)):
        for index in range(2):
            at = row_of(group_of(v, index)) - INNER
            put_group(staged, field[8 * index : 8 * index + 8], eye, at)
    ends = window(east_block, right, 54, 6, 56, 60)
    put_group(staged, jnp.concatenate([ends[0], ends[1]], axis=0), eye, 120)
    block = jnp.concatenate([ends[2], ends[2]], axis=0).reshape(256, latitudes)
    turned = dot_nt(eye, block)
    lower = lax.broadcasted_iota(jnp.int32, (10, 256), 1) < LANES
    for s in range(8):
        rows = [turned[20 * s + 10 * k : 20 * s + 10 * k + 10] for k in range(2)]
        staged[s, 140:150, :] = jnp.where(lower, rows[0], rows[1])
    staged[:, 150:OUTER, :] = jnp.zeros((8, OUTER - 150, 256), F32)
    me = lax.axis_index("mem")
    for k, d in enumerate(CHIPS):
        straight[k] = staged[me ^ d].astype(BF16)
        cross[k] = staged[me ^ d ^ 1].astype(BF16)


def spread_block(source, held, wide, start, lane):
    spans = [slice(h * LANES, (h + 1) * LANES) for h in range(2)]
    count = source.shape[1]
    here = pl.ds(start, 16)
    blocks = exchange_lanes([[source[q, here, span] for span in spans] for q in range(8)], lane)
    for q in range(8):
        to = pl.ds(pl.multiple_of(q * count + start, 8), 16)
        for h in range(2):
            wide[h, to, :] = blocks[q][h].astype(F32)
            held[q, here, spans[h]] = blocks[q][h]


def spread_kernel(cells, got, held, seen, wide):
    lane = lax.broadcasted_iota(jnp.int32, (16, LANES), 1)

    def step(index, carry):
        spread_block(got, held, wide, pl.multiple_of(index * 16, 16), lane)
        return carry

    lax.fori_loop(0, INNER // 16, step, 0, unroll=4)
    slots = seen.shape[2]
    unroll = 16

    def pick(index, carry):
        for t in range(2):
            for k in range(unroll):
                slot = index * unroll + k
                row = cells[t, slot]
                for h in range(2):
                    seen[t, h, pl.ds(slot, 1), :] = wide[h, pl.ds(row, 1), :]
        return carry

    lax.fori_loop(0, slots // unroll, pick, 0)


def observe_kernel(cells, outer, weight, target, first, straight, cross, *refs):
    edges, (held, gram, to_first, to_second, joined, wide, seen) = refs[:3], refs[3:]
    wholes = []
    lane = lax.broadcasted_iota(jnp.int32, (16, LANES), 1)
    me = lax.axis_index("mem")
    for k, d in enumerate(CHIPS):
        joined[me ^ d, 0:OUTER, :] = straight[0] if k == 0 else edges[k - 1][0]
        joined[me ^ d ^ 1, 0:OUTER, :] = cross[0] if k == 0 else edges[k - 1][1]
    for start in (*range(0, OUTER - 16, 16), OUTER - 16):
        spread_block(joined, held, wide, start, lane)
    slots = first.shape[2]
    seen[:, :, 0:slots, :] = first[...]
    for t in range(2):

        def pick(index, carry):
            for k in range(8):
                slot = outer[t, index * 8 + k]
                row = cells[t, slot] - 8 * INNER
                for h in range(2):
                    seen[t, h, pl.ds(slot, 1), :] = wide[h, pl.ds(row, 1), :]
            return carry

        lax.fori_loop(0, (outer[t, slots + LANES - 1] + 7) // 8, pick, 0)
    eye = identity(256, BF16)
    for t in range(2):
        values = jnp.concatenate([seen[t, h, 0:slots] for h in range(2)], axis=1).astype(BF16)
        turned = dot_nt(eye, values)
        mean = jnp.sum(turned, axis=0, keepdims=True) * (1.0 / 256)
        root = weight[t : t + 1, :]
        spread = (root * (turned - mean)).astype(BF16)
        misfit = (root * (target[t : t + 1, :] - mean)).astype(BF16)
        block = dot_nt(spread, spread)
        pull = dot_nt(jnp.broadcast_to(misfit, (16, slots)), spread)
        whole = packed(block, pull[0:8])
        gram[t] = whole
        wholes.append(whole.astype(BF16))
    odd = (lax.axis_index("band") & 1) == 1
    to_first[...] = jnp.where(odd, wholes[0], wholes[1])
    to_second[...] = jnp.where(odd, wholes[1], wholes[0])


def combine_kernel(gram, first_swap, second_swap, line, short):
    odd = (lax.axis_index("band") & 1) == 1
    first, second = first_swap[...].astype(F32), second_swap[...].astype(F32)
    west, east = jnp.where(odd, first, second), jnp.where(odd, second, first)
    for t, beside in enumerate((west + gram[1], gram[0] + east)):
        total = gram[t] + neighbour_weight * beside
        line[t] = total
        short[t] = total.astype(BF16)


def prepare_kernel(inner, outer, *refs):
    average = jnp.full((256, LANES), 1.0 / 256, BF16)
    for q in range(8):
        pieces = (inner[q, 0:FIRST], jnp.concatenate([inner[q, FIRST:INNER], outer[q, 0:OUTER]], axis=0))
        for k, piece in enumerate(pieces):
            mean = dot_nn(piece, average)
            refs[2 * k + 1][q] = mean
            mean = jnp.concatenate([mean, mean], axis=1)
            refs[2 * k][q] = (piece.astype(F32) - mean).astype(BF16)


def send_back(results, outs):
    lane = lax.broadcasted_iota(jnp.int32, (16, LANES), 1)
    spans = [slice(h * LANES, (h + 1) * LANES) for h in range(2)]

    def move(start):
        here = pl.ds(start, 16)
        blocks = [[results[q, here, span] for span in spans] for q in range(8)]
        blocks = exchange_lanes(blocks, lane)
        for q in range(8):
            for h in range(2):
                outs[ORDER.index(q)][here, spans[h]] = blocks[q][h]

    def step(index, carry):
        move(pl.multiple_of(index * 16, 16))
        return carry

    count = results.shape[1]
    lax.fori_loop(0, count // 16, step, 0, unroll=4)
    if count % 16:
        move(count - 16)


def apply_maps(anomaly, mean, maps, results, q, edge, order):
    count = results.shape[1]
    low, high = edge // 16 * 16, (edge + 15) // 16 * 16
    first = dot_nt(anomaly[q, 0:high], maps[order[0]])
    centre = jnp.concatenate([mean[q], mean[q]], axis=1)
    results[q, 0:low] = (centre[0:low] + first[0:low]).astype(BF16)
    if low == count:
        return
    second = dot_nt(anomaly[q, low:count], maps[order[1]])
    if low < high:
        near = lax.broadcasted_iota(jnp.int32, (16, 256), 0) < edge - low
        both = jnp.where(near, first[low:high], second[0:16])
        results[q, low:high] = (centre[low:high] + both).astype(BF16)
    results[q, high:count] = (centre[high:count] + second[high - low : count - low]).astype(BF16)


def second_kernel(maps, anomaly, mean, *refs):
    outs, results = refs[:8], refs[8]
    both = [maps[0], maps[1]]
    for q in range(8):
        apply_maps(anomaly, mean, both, results, q, 184, (0, 1))
    send_back(results, outs)


def analyse_kernel(line, below, above, anomaly, mean, *refs):
    outs, (kept, results, ordered) = refs[:8], refs[8:]
    size = 256
    eye = identity(size, F32)
    norms, pulls, roots, inverses = [], [], [], []
    for t in range(2):
        beside = below[t].astype(F32) + above[t].astype(F32)
        block, pull = unpacked(line[t] + neighbour_weight * beside)
        system = (size - 1) * eye + block
        square = jnp.sum(jnp.sum(system * system, axis=0, keepdims=True), axis=1, keepdims=True)
        norms.append(jnp.sqrt(square))
        pulls.append(pull)
        roots.append(system * (1.0 / norms[t]))
    for sweep in range(SWEEPS):
        rights = [right_3(split(root)) for root in roots]
        if sweep == 0:
            inverses = [1.5 * eye - 0.5 * root for root in roots]
            lefts = [left_3(split(inverse)) for inverse in inverses]
            roots = [dot_nn(left, right) for left, right in zip(lefts, rights)]
            continue
        parts = [split(inverse) for inverse in inverses]
        products = [dot_nn(left_3(part), right) for part, right in zip(parts, rights)]
        middles = [left_3(split(1.5 * eye - 0.5 * product)) for product in products]
        if sweep < SWEEPS - 1:
            roots = [dot_nn(middle, right) for middle, right in zip(middles, rights)]
        inverses = [dot_nn(middle, right_3(part)) for middle, part in zip(middles, parts)]
    maps = []
    for t in range(2):
        right = right_3(split(inverses[t]))
        half_pull = dot_nn(left_3(split(pulls[t])), right)
        shift = dot_nn(left_3(split(half_pull)), right) / norms[t]
        scale = math.sqrt(size - 1) / jnp.sqrt(norms[t])
        ordered[t] = (inverses[t] * scale + shift[0:1]).astype(BF16).reshape(8, 32, size)
    me = lax.axis_index("mem")
    for t in range(2):
        maps.append(jnp.concatenate([ordered[t, me ^ d] for d in range(8)], axis=0))
        kept[t] = maps[t]
    for q in range(8):
        apply_maps(anomaly, mean, maps, results, q, 180 if q < 6 else FIRST, (1, 0))
    send_back(results, outs)


def spread_strips(got, wide):
    me = lax.axis_index("mem")
    for k, d in enumerate(ORDER):
        wide[me ^ d] = got[k][...].astype(F32)


def take_group(wide, turned, eye, g, shape, skipped=0):
    rows = shape[2] // 8
    at = row_of(g) - row_of(skipped)
    g = g - skipped
    for s in range(8):
        turned[g, rows * s : rows * (s + 1), :] = wide[s, at : at + rows, :]
    return dot_nt(eye, turned[g].astype(BF16)).astype(BF16).reshape(shape)


def first_return_kernel(*refs):
    got, (out, wide, turned, planes, sent) = refs[:8], refs[8:]
    shape = (8,) + planes.shape[2:]
    spread_strips(got, wide)
    eye = identity(256, BF16)
    copies = []
    for v in range(3):
        for index in range(3, 7):
            at = 8 * (index - 3)
            planes[v, at : at + 8] = take_group(wide, turned, eye, group_of(v, index), shape)
        copies.append(pltpu.make_async_copy(planes.at[v], out.at[v, pl.ds(24, 32)], sent.at[v]))
        copies[v].start()
    for copy in copies:
        copy.wait()


def second_return_kernel(*refs):
    got, (_, out, wide, turned, planes, sent) = refs[:8], refs[8:]
    shape = (8,) + planes.shape[2:]
    spread_strips(got, wide)
    eye = identity(256, BF16)
    mixed = take_group(wide, turned, eye, 21, shape, 12)
    planes[0, 24:28] = mixed[0:4]
    planes[1, 24:28] = mixed[4:8]
    at = row_of(22) - row_of(12)
    turned[10] = jnp.zeros(turned.shape[1:], F32)
    for s in range(8):
        for k in range(2):
            to = 20 * s + 10 * k
            half = wide[s, at : at + 10, k * LANES : (k + 1) * LANES]
            turned[10, to : to + 10, 0:LANES] = half
    block = dot_nt(eye, turned[10].astype(BF16)).astype(BF16).reshape(shape)
    planes[2, 24:28] = block[0:4]
    copies = []
    for v in range(3):
        for index in range(3):
            at = 8 * index
            block = take_group(wide, turned, eye, group_of(v, index), shape, 12)
            planes[v, at : at + 8] = block
        for k, (at, to, count) in enumerate(((0, 0, 24), (24, 56, 4))):
            source, target = planes.at[v, pl.ds(at, count)], out.at[v, pl.ds(to, count)]
            copies.append(pltpu.make_async_copy(source, target, sent.at[2 * v + k]))
            copies[-1].start()
    for copy in copies:
        copy.wait()


def swapped_pairs(values, axis, pairs):
    moved = []
    for value, some in zip(values, pairs):
        both = some + [(j, i) for i, j in some]
        moved.append(lax.ppermute(value, axis, both))
    return moved


def band_swaps(first, second):
    count = lax.axis_size("band")
    starts = range(0, count, 2)
    pairs = [[(i, i + 1) for i in starts], [(i + 1, (i + 2) % count) for i in starts]]
    return swapped_pairs((first, second), "band", pairs)


def mem_swaps(value):
    count = lax.axis_size("mem")
    pairs = [[(i, i + 1) for i in range(k, count - 1, 2)] for k in range(2)]
    return swapped_pairs((value, value), "mem", pairs)


def across(value, difference):
    return lax.ppermute(value, "mem", [(i, i ^ difference) for i in range(8)])


def partners(values):
    return [across(value, d) if d else value for d, value in zip(ORDER, values)]


def swap(value):
    return lax.all_to_all(value, "mem", split_axis=0, concat_axis=0, tiled=True)


def cell_rows(cell):
    variable = cell // 600
    tile = jnp.arange(2, dtype=jnp.int32)[:, None]
    column = tile * 30 + cell // 20 % 30
    index = column // 8
    place = column % 8
    group = variable + jnp.where(index > 3, variable * 2 + index - 4, 18 - 3 * index)
    is_last = column >= 56
    group = jnp.where(is_last, 21 + variable // 2, group)
    place = jnp.where(is_last, column - 56 + 4 * (variable % 2), place)
    row = cell % 20
    place = jnp.where(group == 22, place + 4 * (row // 10), place)
    row = jnp.where(group == 22, row % 10, row)
    first = place * INNER + group * 20
    last = 8 * INNER + place * OUTER + (group - 15) * 20
    return jnp.where(group < 15, first, last) + row


def on_device_fast(
    ensemble, layer_depth, observed_cell, observed_value, error_variance, observed_count
):
    members, _, columns, latitudes = ensemble.shape
    slots = observed_cell.shape[2]
    planes = jnp.transpose(ensemble, (1, 2, 0, 3))
    edge = jax.ShapeDtypeStruct((4, members, latitudes), BF16)
    far = pl.BlockSpec(memory_space=pltpu.HBM)
    sent, to_first, to_second = pl.pallas_call(
        inner_kernel,
        out_shape=(jax.ShapeDtypeStruct((8, INNER, 256), BF16), edge, edge),
        in_specs=[far, far],
        scratch_shapes=[
            pltpu.VMEM(planes.shape, BF16),
            pltpu.VMEM((columns, latitudes), F32),
            pltpu.VMEM((columns, members, latitudes), F32),
            pltpu.VMEM((columns, members, latitudes), BF16),
            pltpu.VMEM((8, INNER, 256), F32),
            pltpu.VMEM((2, 4, members, latitudes), BF16),
            pltpu.SemaphoreType.DMA((6,)),
        ],
        compiler_params=params(60),
        name="inner",
    )(planes, layer_depth)
    got = swap(sent)
    swaps = band_swaps(to_first, to_second)
    flat = pl.BlockSpec((4, members, latitudes), lambda i: (0, 0, 0))
    straight, cross = pl.pallas_call(
        outer_kernel,
        grid=(1,),
        out_shape=(jax.ShapeDtypeStruct((4, OUTER, 256), BF16),) * 2,
        in_specs=[
            pl.BlockSpec((3, 20, members, latitudes), lambda i: (0, 0, 0, 0)),
            pl.BlockSpec((3, 6, members, latitudes), lambda i: (0, 9, 0, 0)),
            flat,
            flat,
            pl.BlockSpec((columns, latitudes), lambda i: (0, 0)),
        ],
        out_specs=(pl.BlockSpec((4, OUTER, 256), lambda i: (0, 0, 0)),) * 2,
        scratch_shapes=[
            pltpu.VMEM((20, members, latitudes), F32),
            pltpu.VMEM((18, members, latitudes), BF16),
            pltpu.VMEM((8, OUTER, 256), F32),
            pltpu.VMEM((2, 4, members, latitudes), BF16),
        ],
        compiler_params=params(24),
        name="outer",
    )(planes, planes, *swaps, layer_depth)
    cross = across(cross, 1)
    got_edges = [across(jnp.stack([straight[k], cross[k]]), CHIPS[k]) for k in (3, 1, 2)]
    got_edges = got_edges[1:] + got_edges[:1]

    rows = cell_rows(observed_cell[0])
    live = jnp.arange(slots, dtype=jnp.int32)[None, :] < observed_count[0][:, None]
    root = jnp.sqrt(jnp.where(live, 1.0 / error_variance[0], 0.0))
    vmem = pl.BlockSpec(memory_space=pltpu.VMEM)
    slot = jnp.arange(slots, dtype=jnp.int32)
    place = jnp.arange(slots + LANES, dtype=jnp.int32)
    is_outer = rows >= 8 * INNER
    near = jnp.where(is_outer, 0, rows)
    rank = jnp.sum(is_outer[:, None, :] & (slot[None, :] < slot[:, None])[None], axis=2)
    count = jnp.sum(is_outer, axis=1, keepdims=True)
    found = is_outer[:, None, :] & (rank[:, None, :] == place[None, :, None])
    outer = jnp.sum(jnp.where(found, slot, 0), axis=2)
    outer = jnp.where(place[None] < count, outer, slots)
    outer = jnp.where(place[None] == slots + LANES - 1, count, outer).astype(jnp.int32)
    rows = jnp.pad(rows, ((0, 0), (0, LANES)), constant_values=8 * INNER)
    smem = pl.BlockSpec(memory_space=pltpu.SMEM)
    held_inner, seen = pl.pallas_call(
        spread_kernel,
        out_shape=(
            jax.ShapeDtypeStruct((8, INNER, 256), BF16),
            jax.ShapeDtypeStruct((2, 2, slots, LANES), F32),
        ),
        in_specs=[smem, vmem],
        scratch_shapes=[pltpu.VMEM((2, 8 * INNER, LANES), F32)],
        compiler_params=params(12),
        cost_estimate=cost(1, 8 * MIB),
        name="spread",
    )(near, got)
    one_tile = jax.ShapeDtypeStruct((PACKED, 256), BF16)
    held_outer, gram, to_first, to_second = pl.pallas_call(
        observe_kernel,
        out_shape=(
            jax.ShapeDtypeStruct((8, OUTER, 256), BF16),
            jax.ShapeDtypeStruct((2, PACKED, 256), F32),
            one_tile,
            one_tile,
        ),
        in_specs=[smem, smem] + [vmem] * 8,
        scratch_shapes=[
            pltpu.VMEM((8, OUTER, 256), BF16),
            pltpu.VMEM((2, 8 * OUTER, LANES), F32),
            pltpu.VMEM((2, 2, slots + 8, LANES), F32),
        ],
        compiler_params=params(16),
        name="observe",
    )(rows, outer, root, observed_value[0], seen, straight, cross, *got_edges)
    anomaly_1, mean_1, anomaly_2, mean_2 = pl.pallas_call(
        prepare_kernel,
        out_shape=(
            jax.ShapeDtypeStruct((8, FIRST, 256), BF16),
            jax.ShapeDtypeStruct((8, FIRST, LANES), F32),
            jax.ShapeDtypeStruct((8, SECOND, 256), BF16),
            jax.ShapeDtypeStruct((8, SECOND, LANES), F32),
        ),
        compiler_params=params(12),
        cost_estimate=cost(1, 6 * MIB),
        name="prepare",
    )(held_inner, held_outer)

    line, short = pl.pallas_call(
        combine_kernel,
        out_shape=(
            jax.ShapeDtypeStruct(gram.shape, F32),
            jax.ShapeDtypeStruct(gram.shape, BF16),
        ),
        compiler_params=params(8),
        name="combine",
    )(gram, *band_swaps(to_first, to_second))
    below, above = mem_swaps(short)
    *back, maps = pl.pallas_call(
        analyse_kernel,
        out_shape=(jax.ShapeDtypeStruct((FIRST, 256), BF16),) * 8
        + (jax.ShapeDtypeStruct((2, 256, 256), BF16),),
        scratch_shapes=[pltpu.VMEM((8, FIRST, 256), BF16), pltpu.VMEM((2, 8, 32, 256), BF16)],
        compiler_params=params(20),
        name="analyse",
    )(line, below, above, anomaly_1, mean_1)
    first = partners(back)
    maps, first[4] = lax.optimization_barrier((maps, first[4]))
    back = pl.pallas_call(
        second_kernel,
        out_shape=(jax.ShapeDtypeStruct((SECOND, 256), BF16),) * 8,
        scratch_shapes=[pltpu.VMEM((8, SECOND, 256), BF16)],
        compiler_params=params(16),
        cost_estimate=cost(1, 6 * MIB),
        name="second",
    )(maps, anomaly_2, mean_2)
    second = partners(back)
    result = jax.ShapeDtypeStruct(planes.shape, BF16)
    half = pl.pallas_call(
        first_return_kernel,
        out_shape=result,
        out_specs=far,
        scratch_shapes=[
            pltpu.VMEM((8, FIRST, 256), F32),
            pltpu.VMEM((12, latitudes, 256), F32),
            pltpu.VMEM((3, 32, members, latitudes), BF16),
            pltpu.SemaphoreType.DMA((3,)),
        ],
        compiler_params=params(20),
        cost_estimate=cost(1, 4 * MIB),
        name="first_return",
    )(*first)
    planes = pl.pallas_call(
        second_return_kernel,
        out_shape=result,
        in_specs=[vmem] * 8 + [far],
        out_specs=far,
        scratch_shapes=[
            pltpu.VMEM((8, SECOND, 256), F32),
            pltpu.VMEM((11, latitudes, 256), F32),
            pltpu.VMEM((3, 28, members, latitudes), BF16),
            pltpu.SemaphoreType.DMA((6,)),
        ],
        input_output_aliases={8: 0},
        compiler_params=params(20),
        name="second_return",
    )(*second, half)
    return jnp.transpose(planes, (2, 0, 1, 3))


def choose(ensemble, layer_depth, observed_cell, *rest):
    mesh_shape = (lax.axis_size("mem"), lax.axis_size("band"))
    shape = (mesh_shape, ensemble.shape, observed_cell.shape[1])
    fits = shape == ((8, 4), (32, 3, 60, 160), 2) and observed_cell.shape[2] % 16 == 0
    chosen = on_device_fast if fits else on_device
    return chosen(ensemble, layer_depth, observed_cell, *rest)


def solution(mesh):
    in_specs = (
        P("mem", None, "band", None),
        P("band", None),
        P("mem", "band", None),
        P("mem", "band", None),
        P("mem", "band", None),
        P("mem", "band"),
    )
    out_specs = P("mem", None, "band", None)
    return jax.shard_map(
        choose, mesh=mesh, in_specs=in_specs, out_specs=out_specs, check_vma=False
    )
```

```python
import math

import jax
import jax.numpy as jnp
import numpy as np
from jax import lax
from jax.experimental import pallas as pl
from jax.experimental.pallas import tpu as pltpu
from jax.sharding import PartitionSpec as P

SWEEPS = 5


half_step = 0.1
coriolis_scale = 0.3
neighbour_weight = 0.75


def padded_2(cells, sides, width):
    for axis, dim in sides:
        count = lax.axis_size(axis)
        head = lax.slice_in_dim(cells, 0, width, axis=dim)
        tail = lax.slice_in_dim(cells, cells.shape[dim] - width, cells.shape[dim], axis=dim)
        cells = jnp.concatenate(
            [
                lax.ppermute(tail, axis, [(i, (i + 1) % count) for i in range(count)]),
                cells,
                lax.ppermute(head, axis, [((i + 1) % count, i) for i in range(count)]),
            ],
            axis=dim,
        )
    return cells


def north_south(source):
    widths = [(0, 0)] * (source.ndim - 1) + [(1, 1)]
    padded = jnp.pad(source, widths)
    return padded[..., 2:] - padded[..., :-2]


def coriolis(latitudes):
    position = jnp.arange(latitudes, dtype=jnp.float32)
    return coriolis_scale * jnp.sin(math.pi * ((position + 0.5) / latitudes - 0.5))


def newton_schulz(starting):
    identity = jnp.eye(starting.shape[-1], dtype=starting.dtype)
    root_part = starting
    inverse_root = jnp.broadcast_to(identity, starting.shape)
    for sweep_index in range(SWEEPS):
        product = jnp.einsum(
            "tij,tjk->tik", inverse_root, root_part, precision=lax.Precision.HIGHEST
        )
        middle = 1.5 * identity - 0.5 * product
        root_part = jnp.einsum("tij,tjk->tik", root_part, middle, precision=lax.Precision.HIGHEST)
        inverse_root = jnp.einsum(
            "tij,tjk->tik", middle, inverse_root, precision=lax.Precision.HIGHEST
        )
    return inverse_root


def on_device(ensemble, layer_depth, observed_cell, observed_value, error_variance, observed_count):
    block_members = ensemble.shape[0]
    columns = ensemble.shape[2]
    latitudes = ensemble.shape[3]
    strips = lax.axis_size("mem")
    members = block_members * strips
    strip_rows = latitudes // strips
    tile_count = observed_cell.shape[1]
    tile_columns = columns // tile_count
    slot_count = observed_cell.shape[2]
    tile_cells = 3 * tile_columns * strip_rows
    height = ensemble[:, 0].astype(jnp.float32)
    eastward = ensemble[:, 1].astype(jnp.float32)
    northward = ensemble[:, 2].astype(jnp.float32)
    turning = coriolis(latitudes)
    flux_east = (layer_depth * eastward).astype(jnp.bfloat16)
    flux_north = (layer_depth * northward).astype(jnp.bfloat16)
    east_margin = padded_2(flux_east, (("band", 1),), 1)
    east_west = east_margin[:, 2:].astype(jnp.float32) - east_margin[:, :-2].astype(jnp.float32)
    north_local = lax.optimization_barrier(flux_north).astype(jnp.float32)
    raised = height - half_step * (east_west + north_south(north_local))
    surface_elevation_cast = raised.astype(jnp.bfloat16)
    height_margin = padded_2(surface_elevation_cast, (("band", 1),), 1)
    margin_wide = height_margin.astype(jnp.float32)
    height_inner = margin_wide[:, 1:-1]
    revised_zonal_velocity = (
        eastward + turning * northward - half_step * (margin_wide[:, 2:] - margin_wide[:, :-2])
    )
    revised_meridional_velocity = (
        northward - turning * eastward - half_step * north_south(height_inner)
    )
    advance_dynamics = jnp.stack(
        [
            surface_elevation_cast,
            revised_zonal_velocity.astype(jnp.bfloat16),
            revised_meridional_velocity.astype(jnp.bfloat16),
        ],
        axis=1,
    )
    reordered = advance_dynamics.reshape(
        block_members, 3, tile_count, tile_columns, strips, strip_rows
    )
    reordered = jnp.transpose(reordered, (4, 2, 0, 1, 3, 5)).reshape(
        strips, tile_count, block_members, tile_cells
    )
    tile_block = lax.all_to_all(reordered, "mem", split_axis=0, concat_axis=2, tiled=True)[0]
    cells_here = observed_cell[0]
    values = jnp.take_along_axis(tile_block, cells_here[:, None, :], axis=2)
    observed_mean = jnp.sum(values, axis=1, dtype=jnp.float32) / members
    slot_index = jnp.arange(slot_count, dtype=jnp.int32)[None, :]
    live_slots = slot_index < observed_count[0][:, None]
    root_weight = jnp.sqrt(jnp.where(live_slots, 1.0 / error_variance[0], 0.0))
    spread = (
        root_weight[:, None, :] * (values.astype(jnp.float32) - observed_mean[:, None, :])
    ).astype(jnp.bfloat16)
    misfit = (root_weight * (observed_value[0] - observed_mean)).astype(jnp.bfloat16)
    spread_margin, misfit_margin = (
        padded_2(spread[None], (("mem", 0), ("band", 1)), 1),
        padded_2(misfit[None], (("mem", 0), ("band", 1)), 1),
    )
    gram_margin = jnp.einsum(
        "atko,atlo->atkl", spread_margin, spread_margin, preferred_element_type=jnp.float32
    )
    pull_margin = jnp.einsum(
        "atko,ato->atk", spread_margin, misfit_margin, preferred_element_type=jnp.float32
    )
    strip_here = lax.axis_index("mem")
    lower_valid = (strip_here > 0).astype(jnp.float32)
    upper_valid = (strip_here < strips - 1).astype(jnp.float32)
    strip_mask = (lower_valid, 1.0, upper_valid)
    total_gram = jnp.zeros((tile_count, members, members), jnp.float32)
    total_pull = jnp.zeros((tile_count, members), jnp.float32)
    for offset_lat in range(3):
        for offset_lon in range(3):
            factor = (
                neighbour_weight ** (abs(offset_lat - 1) + abs(offset_lon - 1))
                * strip_mask[offset_lat]
            )
            total_gram = (
                total_gram + factor * gram_margin[offset_lat, offset_lon : offset_lon + tile_count]
            )
            total_pull = (
                total_pull + factor * pull_margin[offset_lat, offset_lon : offset_lon + tile_count]
            )
    system = (members - 1) * jnp.eye(members, dtype=jnp.float32)[None] + total_gram
    frobenius = jnp.sqrt(jnp.sum(system * system, axis=(1, 2)))
    inverse_root = newton_schulz(system / frobenius[:, None, None])
    spread_map = inverse_root * (math.sqrt(members - 1) / jnp.sqrt(frobenius))[:, None, None]
    half_pull = jnp.einsum("tij,tj->ti", inverse_root, total_pull, precision=lax.Precision.HIGHEST)
    shift_weights = (
        jnp.einsum("tij,tj->ti", inverse_root, half_pull, precision=lax.Precision.HIGHEST)
        / frobenius[:, None]
    )
    weights = (spread_map + shift_weights[:, :, None]).astype(jnp.bfloat16)
    state_mean = jnp.sum(tile_block, axis=1, dtype=jnp.float32) / members
    anomaly = (tile_block.astype(jnp.float32) - state_mean[:, None, :]).astype(jnp.bfloat16)
    update = jnp.einsum("tjk,tjc->tkc", weights, anomaly, preferred_element_type=jnp.float32)
    analysed = (state_mean[:, None, :] + update).astype(jnp.bfloat16)
    returned = lax.all_to_all(analysed[None], "mem", split_axis=2, concat_axis=0, tiled=True)
    returned = returned.reshape(strips, tile_count, block_members, 3, tile_columns, strip_rows)
    return jnp.transpose(returned, (2, 3, 1, 4, 0, 5)).reshape(block_members, 3, columns, latitudes)


LANES = 128
GROUPS = 23
INNER = 304
OUTER = 152
FIRST = 240
SECOND = 216
F32 = jnp.float32
BF16 = jnp.bfloat16
PACKED = 136
CHIPS = (0, 2, 4, 6)
ORDER = (6, 2, 4, 7, 1, 3, 5, 0)
MIB = 1024 * 1024


def params(size):
    return pltpu.CompilerParams(vmem_limit_bytes=size * MIB)


def cost(flops, moved):
    return pl.CostEstimate(flops=flops, bytes_accessed=moved, transcendentals=0)


def identity(size, dtype):
    row = lax.broadcasted_iota(jnp.int32, (size, size), 0)
    column = lax.broadcasted_iota(jnp.int32, (size, size), 1)
    return (row == column).astype(F32).astype(dtype)


def dot_nt(left, right):
    return lax.dot_general(left, right, (((1,), (1,)), ((), ())), preferred_element_type=F32)


def dot_nn(left, right):
    return lax.dot_general(left, right, (((1,), (0,)), ((), ())), preferred_element_type=F32)


def split(value):
    high = value.astype(BF16)
    return high, (value - high.astype(F32)).astype(BF16)


def left_3(parts):
    return jnp.concatenate([parts[0], parts[0], parts[1]], axis=1)


def right_3(parts):
    return jnp.concatenate([parts[0], parts[1], parts[0]], axis=0)


def triangle(size):
    row = lax.broadcasted_iota(jnp.int32, (size, size), 0)
    column = lax.broadcasted_iota(jnp.int32, (size, size), 1)
    return row, column


def packed(block, pull):
    row, column = triangle(128)
    last = block[128:256, 128:256]
    corner = jnp.where(row >= column, block[0:128, 0:128], last)
    middle = jnp.sum(jnp.where(row == column, last, 0.0), axis=0, keepdims=True)
    middle = jnp.concatenate([jnp.zeros_like(middle), middle], axis=1)
    top = jnp.concatenate([block[128:256, 0:128], corner], axis=1)
    tail = jnp.where(lax.broadcasted_iota(jnp.int32, (8, 256), 0) == 0, pull, middle)
    return jnp.concatenate([top, tail], axis=0)


def unpacked(value):
    row, column = triangle(128)
    low, corner = value[0:128, 0:128], value[0:128, 128:256]
    other = jnp.transpose(corner)
    first = jnp.where(row >= column, corner, other)
    last = jnp.where(row < column, corner, other)
    last = jnp.where(row == column, value[129:130, 128:256], last)
    top = jnp.concatenate([first, jnp.transpose(low)], axis=1)
    return jnp.concatenate([top, jnp.concatenate([low, last], axis=1)], axis=0), value[128:136]


def exchange_lanes(blocks, lane):
    blocks = [list(pair) for pair in blocks]
    for q in range(4):
        low, high = blocks[q], blocks[q + 4]
        blocks[q], blocks[q + 4] = [low[0], high[0]], [low[1], high[1]]
    for bit in range(2):
        step = 32 << bit
        odd = (lane & step) != 0
        for q in range(8):
            if q & (1 << bit):
                continue
            for h in range(2):
                low, high = blocks[q][h], blocks[q | (1 << bit)][h]
                blocks[q][h] = jnp.where(odd, pltpu.roll(high, step, 1), low)
                blocks[q | (1 << bit)][h] = jnp.where(odd, high, pltpu.roll(low, LANES - step, 1))
    return blocks


def group_of(variable, index):
    return variable + (variable * 2 + index - 4 if index > 3 else 18 - 3 * index)


def row_of(group):
    return 20 * group + (4 if group >= 15 else 0)


def difference(latitudes):
    source = lax.broadcasted_iota(jnp.int32, (latitudes, latitudes), 0)
    target = lax.broadcasted_iota(jnp.int32, (latitudes, latitudes), 1)
    shift = (source == target + 1).astype(F32) - (source == target - 1).astype(F32)
    return shift.astype(BF16)


def rows_apart(value, shift):
    flat = value.reshape(-1, value.shape[-1])
    return dot_nn(flat, shift).reshape(value.shape)


def fluxes(east, deep):
    return (deep * east.astype(F32)).astype(BF16).astype(F32)


def heights(field, north, deep, ahead, behind, shift):
    flux_north = (deep * north.astype(F32)).astype(BF16)
    raised = field.astype(F32) - half_step * ((ahead - behind) + rows_apart(flux_north, shift))
    return raised.astype(BF16)


def velocities(east, north, here, ahead, behind, turning, shift):
    east, north = east.astype(F32), north.astype(F32)
    apart = ahead.astype(F32) - behind.astype(F32)
    new_east = east + turning * north - half_step * apart
    new_north = north - turning * east - half_step * rows_apart(here, shift)
    return new_east.astype(BF16), new_north.astype(BF16)


def put_group(staged, block, eye, first):
    latitudes = eye.shape[0]
    rows = latitudes // 8
    turned = dot_nt(eye, block.reshape(256, latitudes))
    for s in range(8):
        staged[s, first : first + rows, :] = turned[rows * s : rows * (s + 1)]


def turning_row(latitudes):
    position = lax.broadcasted_iota(jnp.int32, (8, latitudes), 1).astype(F32)
    turning = coriolis_scale * jnp.sin(math.pi * ((position + 0.5) / latitudes - 0.5))
    return turning[0:1, :][None]


def inner_kernel(
    ens, depth, out, to_first, to_second, here, deep, flux, height, staged, edges, arrived
):
    columns, members, latitudes = here.shape[1:]
    batch = columns // 5
    pieces = [pltpu.make_async_copy(depth, deep, arrived.at[5])]
    for k in range(5):
        span = pl.ds(k * batch, batch if k else 2)
        piece = pltpu.make_async_copy(ens.at[:, span], here.at[:, span], arrived.at[k])
        pieces.append(piece)
    for k in (0, 2, 3, 4, 5, 1):
        pieces[k].start()
    shift = difference(latitudes)
    turning = turning_row(latitudes)
    eye = identity(latitudes, BF16)
    pieces[0].wait()

    def depths(first, count):
        rows = [deep[c : c + 1, :] for c in range(first, first + count)]
        return jnp.stack([jnp.broadcast_to(row, (members, latitudes)) for row in rows])

    def edge(side, near, far):
        edges[side, 0] = here[0, near]
        edges[side, 1] = (deep[near : near + 1, :] * here[2, near].astype(F32)).astype(BF16)
        edges[side, 2] = flux[near].astype(BF16)
        edges[side, 3] = flux[far].astype(BF16)

    staged[:, 300:INNER, :] = jnp.zeros((8, INNER - 300, 256), F32)
    done = 2
    for k in (1, 2, 3, 4, 0):
        pieces[k + 1].wait()
        first, count = k * batch, batch if k else 2
        flux[first : first + count] = fluxes(here[1, first : first + count], depths(first, count))
        if k == 0:
            edge(0, 0, 1)
            continue
        if k == 4:
            edge(1, columns - 1, columns - 2)
        low, high = max(first - 1, batch + 1), first + batch - 1
        at = slice(low, high)
        ahead, behind = flux[low + 1 : high + 1], flux[low - 1 : high - 1]
        height[at] = heights(
            here[0, at], here[2, at], depths(low, high - low), ahead, behind, shift
        )
        while done < 7 and 8 * done + 9 <= high:
            first = 8 * done
            at = slice(first, first + 8)
            ahead, behind = height[first + 1 : first + 9], height[first - 1 : first + 7]
            new = velocities(here[1, at], here[2, at], height[at], ahead, behind, turning, shift)
            for v, field in enumerate((height[at],) + new):
                put_group(staged, field, eye, row_of(group_of(v, done)))
            done += 1
    odd = lax.axis_index("band") & 1
    to_first[...] = edges[1 - odd]
    to_second[...] = edges[odd]
    out[...] = staged[...].astype(BF16)


def outer_kernel(
    west_block, east_block, first_swap, second_swap, depth, *refs
):
    straight, cross, flux, height, staged, swapped = refs
    odd = lax.axis_index("band") & 1
    for side, block in enumerate((first_swap, second_swap)):
        swapped[side] = block[...]
    left, right = swapped.at[1 - odd], swapped.at[odd]
    members, latitudes = west_block.shape[2:]
    shift = difference(latitudes)
    turning = turning_row(latitudes)
    eye = identity(latitudes, BF16)

    def depths(first, count):
        return jnp.stack(
            [
                jnp.broadcast_to(depth[c : c + 1, :], (members, latitudes))
                for c in range(first, first + count)
            ]
        )

    def window(ens, edge, first, count, low, high):
        is_left = low == 0
        base = 2 if is_left else 0
        flux[base : base + count] = fluxes(ens[1, 0:count], depths(first, count))
        at = 0 if is_left else count
        near, far = (1, 0) if is_left else (at, at + 1)
        flux[near] = edge[2].astype(F32)
        flux[far] = edge[3].astype(F32)
        wide = high - low + 1
        skip = 0 if is_left else 1
        columns = slice(skip, skip + wide)
        new = heights(
            ens[0, columns],
            ens[2, columns],
            depths(first + skip, wide),
            flux[base + skip + 1 : base + skip + 1 + wide],
            flux[base + skip - 1 : base + skip - 1 + wide],
            shift,
        )
        start = 1 if is_left else 0
        height[start : start + wide] = new
        place = 0 if is_left else wide
        middle = near
        east_west = flux[middle + 1] - flux[middle - 1]
        raised = edge[0].astype(F32) - half_step * (east_west + rows_apart(edge[1], shift))
        height[place] = raised.astype(BF16)
        count = high - low
        here = height[1 : 1 + count]
        ahead, behind = height[2 : 2 + count], height[0:count]
        at = slice(low - first, high - first)
        return (here,) + velocities(ens[1, at], ens[2, at], here, ahead, behind, turning, shift)

    for v, field in enumerate(window(west_block, left, 0, 18, 0, 16)):
        for index in range(2):
            at = row_of(group_of(v, index)) - INNER
            put_group(staged, field[8 * index : 8 * index + 8], eye, at)
    ends = window(east_block, right, 54, 6, 56, 60)
    put_group(staged, jnp.concatenate([ends[0], ends[1]], axis=0), eye, 120)
    block = jnp.concatenate([ends[2], ends[2]], axis=0).reshape(256, latitudes)
    turned = dot_nt(eye, block)
    lower = lax.broadcasted_iota(jnp.int32, (10, 256), 1) < LANES
    for s in range(8):
        rows = [turned[20 * s + 10 * k : 20 * s + 10 * k + 10] for k in range(2)]
        staged[s, 140:150, :] = jnp.where(lower, rows[0], rows[1])
    staged[:, 150:OUTER, :] = jnp.zeros((8, OUTER - 150, 256), F32)
    me = lax.axis_index("mem")
    for k, d in enumerate(CHIPS):
        straight[k] = staged[me ^ d].astype(BF16)
        cross[k] = staged[me ^ d ^ 1].astype(BF16)


def spread_block(source, held, wide, start, lane):
    spans = [slice(h * LANES, (h + 1) * LANES) for h in range(2)]
    count = source.shape[1]
    here = pl.ds(start, 16)
    blocks = exchange_lanes([[source[q, here, span] for span in spans] for q in range(8)], lane)
    for q in range(8):
        to = pl.ds(pl.multiple_of(q * count + start, 8), 16)
        for h in range(2):
            wide[h, to, :] = blocks[q][h].astype(F32)
            held[q, here, spans[h]] = blocks[q][h]


def spread_kernel(cells, got, held, seen, wide):
    lane = lax.broadcasted_iota(jnp.int32, (16, LANES), 1)

    def step(index, carry):
        spread_block(got, held, wide, pl.multiple_of(index * 16, 16), lane)
        return carry

    lax.fori_loop(0, INNER // 16, step, 0, unroll=4)
    slots = seen.shape[2]
    unroll = 16

    def pick(index, carry):
        for t in range(2):
            for k in range(unroll):
                slot = index * unroll + k
                row = cells[t, slot]
                for h in range(2):
                    seen[t, h, pl.ds(slot, 1), :] = wide[h, pl.ds(row, 1), :]
        return carry

    lax.fori_loop(0, slots // unroll, pick, 0)


def observe_kernel(cells, outer, weight, target, first, straight, cross, *refs):
    edges, (held, gram, to_first, to_second, joined, wide, seen) = refs[:3], refs[3:]
    wholes = []
    lane = lax.broadcasted_iota(jnp.int32, (16, LANES), 1)
    me = lax.axis_index("mem")
    for k, d in enumerate(CHIPS):
        joined[me ^ d, 0:OUTER, :] = straight[0] if k == 0 else edges[k - 1][0]
        joined[me ^ d ^ 1, 0:OUTER, :] = cross[0] if k == 0 else edges[k - 1][1]
    for start in (*range(0, OUTER - 16, 16), OUTER - 16):
        spread_block(joined, held, wide, start, lane)
    slots = first.shape[2]
    seen[:, :, 0:slots, :] = first[...]

    def pick(index, carry):
        picked = []
        for k in range(4):
            for t in range(2):
                slot = outer[t, index * 4 + k]
                row = cells[t, slot] - 8 * INNER
                picked.append((t, slot, [wide[h, pl.ds(row, 1), :] for h in range(2)]))
        for t, slot, halves in picked:
            for h in range(2):
                seen[t, h, pl.ds(slot, 1), :] = halves[h]
        return carry

    last = slots + LANES - 1
    most = jnp.maximum(outer[0, last], outer[1, last])
    lax.fori_loop(0, (most + 3) // 4, pick, 0)
    eye = identity(256, BF16)
    for t in range(2):
        values = jnp.concatenate([seen[t, h, 0:slots] for h in range(2)], axis=1).astype(BF16)
        turned = dot_nt(eye, values)
        mean = jnp.sum(turned, axis=0, keepdims=True) * (1.0 / 256)
        root = weight[t : t + 1, :]
        spread = (root * (turned - mean)).astype(BF16)
        misfit = (root * (target[t : t + 1, :] - mean)).astype(BF16)
        block = dot_nt(spread, spread)
        pull = dot_nt(jnp.broadcast_to(misfit, (16, slots)), spread)
        whole = packed(block, pull[0:8])
        gram[t] = whole
        wholes.append(whole.astype(BF16))
    odd = (lax.axis_index("band") & 1) == 1
    to_first[...] = jnp.where(odd, wholes[0], wholes[1])
    to_second[...] = jnp.where(odd, wholes[1], wholes[0])


def combine_kernel(gram, first_swap, second_swap, line, short):
    odd = (lax.axis_index("band") & 1) == 1
    first, second = first_swap[...].astype(F32), second_swap[...].astype(F32)
    west, east = jnp.where(odd, first, second), jnp.where(odd, second, first)
    for t, beside in enumerate((west + gram[1], gram[0] + east)):
        total = gram[t] + neighbour_weight * beside
        line[t] = total
        short[t] = total.astype(BF16)


def prepare_kernel(inner, outer, *refs):
    average = jnp.full((256, LANES), 1.0 / 256, BF16)
    for q in range(8):
        pieces = (inner[q, 0:FIRST], jnp.concatenate([inner[q, FIRST:INNER], outer[q, 0:OUTER]], axis=0))
        for k, piece in enumerate(pieces):
            mean = dot_nn(piece, average)
            refs[2 * k + 1][q] = mean
            mean = jnp.concatenate([mean, mean], axis=1)
            refs[2 * k][q] = (piece.astype(F32) - mean).astype(BF16)


def send_back(results, outs):
    lane = lax.broadcasted_iota(jnp.int32, (16, LANES), 1)
    spans = [slice(h * LANES, (h + 1) * LANES) for h in range(2)]

    def move(start):
        here = pl.ds(start, 16)
        blocks = [[results[q, here, span] for span in spans] for q in range(8)]
        blocks = exchange_lanes(blocks, lane)
        for q in range(8):
            for h in range(2):
                outs[ORDER.index(q)][here, spans[h]] = blocks[q][h]

    def step(index, carry):
        move(pl.multiple_of(index * 16, 16))
        return carry

    count = results.shape[1]
    lax.fori_loop(0, count // 16, step, 0, unroll=4)
    if count % 16:
        move(count - 16)


def apply_maps(anomaly, mean, maps, results, q, edge, order):
    count = results.shape[1]
    low, high = edge // 16 * 16, (edge + 15) // 16 * 16
    first = dot_nt(anomaly[q, 0:high], maps[order[0]])
    centre = jnp.concatenate([mean[q], mean[q]], axis=1)
    results[q, 0:low] = (centre[0:low] + first[0:low]).astype(BF16)
    if low == count:
        return
    second = dot_nt(anomaly[q, low:count], maps[order[1]])
    if low < high:
        near = lax.broadcasted_iota(jnp.int32, (16, 256), 0) < edge - low
        both = jnp.where(near, first[low:high], second[0:16])
        results[q, low:high] = (centre[low:high] + both).astype(BF16)
    results[q, high:count] = (centre[high:count] + second[high - low : count - low]).astype(BF16)


def second_kernel(maps, anomaly, mean, *refs):
    outs, results = refs[:8], refs[8]
    both = [maps[0], maps[1]]
    for q in range(8):
        apply_maps(anomaly, mean, both, results, q, 184, (0, 1))
    send_back(results, outs)


def analyse_kernel(line, below, above, anomaly, mean, *refs):
    outs, (kept, results, ordered) = refs[:8], refs[8:]
    size = 256
    eye = identity(size, F32)
    norms, pulls, roots, inverses = [], [], [], []
    for t in range(2):
        beside = below[t].astype(F32) + above[t].astype(F32)
        block, pull = unpacked(line[t] + neighbour_weight * beside)
        system = (size - 1) * eye + block
        square = jnp.sum(jnp.sum(system * system, axis=0, keepdims=True), axis=1, keepdims=True)
        norms.append(jnp.sqrt(square))
        pulls.append(pull)
        roots.append(system * (1.0 / norms[t]))
    for sweep in range(SWEEPS):
        rights = [right_3(split(root)) for root in roots]
        if sweep == 0:
            inverses = [1.5 * eye - 0.5 * root for root in roots]
            lefts = [left_3(split(inverse)) for inverse in inverses]
            roots = [dot_nn(left, right) for left, right in zip(lefts, rights)]
            continue
        parts = [split(inverse) for inverse in inverses]
        products = [dot_nn(left_3(part), right) for part, right in zip(parts, rights)]
        middles = [left_3(split(1.5 * eye - 0.5 * product)) for product in products]
        if sweep < SWEEPS - 1:
            roots = [dot_nn(middle, right) for middle, right in zip(middles, rights)]
        inverses = [dot_nn(middle, right_3(part)) for middle, part in zip(middles, parts)]
    maps = []
    for t in range(2):
        right = right_3(split(inverses[t]))
        half_pull = dot_nn(left_3(split(pulls[t])), right)
        shift = dot_nn(left_3(split(half_pull)), right) / norms[t]
        scale = math.sqrt(size - 1) / jnp.sqrt(norms[t])
        ordered[t] = (inverses[t] * scale + shift[0:1]).astype(BF16).reshape(8, 32, size)
    me = lax.axis_index("mem")
    for t in range(2):
        maps.append(jnp.concatenate([ordered[t, me ^ d] for d in range(8)], axis=0))
        kept[t] = maps[t]
    for q in range(8):
        apply_maps(anomaly, mean, maps, results, q, 180 if q < 6 else FIRST, (1, 0))
    send_back(results, outs)


def spread_strips(got, wide):
    me = lax.axis_index("mem")
    for k, d in enumerate(ORDER):
        wide[me ^ d] = got[k][...].astype(F32)


def take_group(wide, turned, eye, g, shape, skipped=0):
    rows = shape[2] // 8
    at = row_of(g) - row_of(skipped)
    g = g - skipped
    for s in range(8):
        turned[g, rows * s : rows * (s + 1), :] = wide[s, at : at + rows, :]
    return dot_nt(eye, turned[g].astype(BF16)).astype(BF16).reshape(shape)


def first_return_kernel(*refs):
    got, (out, wide, turned, planes, sent) = refs[:8], refs[8:]
    shape = (8,) + planes.shape[2:]
    spread_strips(got, wide)
    eye = identity(256, BF16)
    copies = []
    for v in range(3):
        for index in range(3, 7):
            at = 8 * (index - 3)
            planes[v, at : at + 8] = take_group(wide, turned, eye, group_of(v, index), shape)
        copies.append(pltpu.make_async_copy(planes.at[v], out.at[v, pl.ds(24, 32)], sent.at[v]))
        copies[v].start()
    for copy in copies:
        copy.wait()


def second_return_kernel(*refs):
    got, (_, out, wide, turned, planes, sent) = refs[:8], refs[8:]
    shape = (8,) + planes.shape[2:]
    spread_strips(got, wide)
    eye = identity(256, BF16)
    mixed = take_group(wide, turned, eye, 21, shape, 12)
    planes[0, 24:28] = mixed[0:4]
    planes[1, 24:28] = mixed[4:8]
    at = row_of(22) - row_of(12)
    turned[10] = jnp.zeros(turned.shape[1:], F32)
    for s in range(8):
        for k in range(2):
            to = 20 * s + 10 * k
            half = wide[s, at : at + 10, k * LANES : (k + 1) * LANES]
            turned[10, to : to + 10, 0:LANES] = half
    block = dot_nt(eye, turned[10].astype(BF16)).astype(BF16).reshape(shape)
    planes[2, 24:28] = block[0:4]
    copies = []

    def leave(v, at, to, count):
        source, target = planes.at[v, pl.ds(at, count)], out.at[v, pl.ds(to, count)]
        copies.append(pltpu.make_async_copy(source, target, sent.at[len(copies)]))
        copies[-1].start()

    for v in range(3):
        leave(v, 24, 56, 4)
    for v in range(3):
        for index in range(3):
            at = 8 * index
            block = take_group(wide, turned, eye, group_of(v, index), shape, 12)
            planes[v, at : at + 8] = block
            leave(v, at, at, 8)
    for copy in copies:
        copy.wait()


def swapped_pairs(values, axis, pairs):
    moved = []
    for value, some in zip(values, pairs):
        both = some + [(j, i) for i, j in some]
        moved.append(lax.ppermute(value, axis, both))
    return moved


def band_swaps(first, second):
    count = lax.axis_size("band")
    starts = range(0, count, 2)
    pairs = [[(i, i + 1) for i in starts], [(i + 1, (i + 2) % count) for i in starts]]
    return swapped_pairs((first, second), "band", pairs)


def mem_swaps(value):
    count = lax.axis_size("mem")
    pairs = [[(i, i + 1) for i in range(k, count - 1, 2)] for k in range(2)]
    return swapped_pairs((value, value), "mem", pairs)


def across(value, difference):
    return lax.ppermute(value, "mem", [(i, i ^ difference) for i in range(8)])


def partners(values):
    return [across(value, d) if d else value for d, value in zip(ORDER, values)]


def swap(value):
    return lax.all_to_all(value, "mem", split_axis=0, concat_axis=0, tiled=True)


def cell_rows(cell):
    variable = cell // 600
    tile = jnp.arange(2, dtype=jnp.int32)[:, None]
    column = tile * 30 + cell // 20 % 30
    index = column // 8
    place = column % 8
    group = variable + jnp.where(index > 3, variable * 2 + index - 4, 18 - 3 * index)
    is_last = column >= 56
    group = jnp.where(is_last, 21 + variable // 2, group)
    place = jnp.where(is_last, column - 56 + 4 * (variable % 2), place)
    row = cell % 20
    place = jnp.where(group == 22, place + 4 * (row // 10), place)
    row = jnp.where(group == 22, row % 10, row)
    first = place * INNER + group * 20
    last = 8 * INNER + place * OUTER + (group - 15) * 20
    return jnp.where(group < 15, first, last) + row


def on_device_fast(
    ensemble, layer_depth, observed_cell, observed_value, error_variance, observed_count
):
    members, _, columns, latitudes = ensemble.shape
    slots = observed_cell.shape[2]
    planes = jnp.transpose(ensemble, (1, 2, 0, 3))
    edge = jax.ShapeDtypeStruct((4, members, latitudes), BF16)
    far = pl.BlockSpec(memory_space=pltpu.HBM)
    sent, to_first, to_second = pl.pallas_call(
        inner_kernel,
        out_shape=(jax.ShapeDtypeStruct((8, INNER, 256), BF16), edge, edge),
        in_specs=[far, far],
        scratch_shapes=[
            pltpu.VMEM(planes.shape, BF16),
            pltpu.VMEM((columns, latitudes), F32),
            pltpu.VMEM((columns, members, latitudes), F32),
            pltpu.VMEM((columns, members, latitudes), BF16),
            pltpu.VMEM((8, INNER, 256), F32),
            pltpu.VMEM((2, 4, members, latitudes), BF16),
            pltpu.SemaphoreType.DMA((6,)),
        ],
        compiler_params=params(60),
        name="inner",
    )(planes, layer_depth)
    got = swap(sent)
    swaps = band_swaps(to_first, to_second)
    flat = pl.BlockSpec((4, members, latitudes), lambda i: (0, 0, 0))
    straight, cross = pl.pallas_call(
        outer_kernel,
        grid=(1,),
        out_shape=(jax.ShapeDtypeStruct((4, OUTER, 256), BF16),) * 2,
        in_specs=[
            pl.BlockSpec((3, 20, members, latitudes), lambda i: (0, 0, 0, 0)),
            pl.BlockSpec((3, 6, members, latitudes), lambda i: (0, 9, 0, 0)),
            flat,
            flat,
            pl.BlockSpec((columns, latitudes), lambda i: (0, 0)),
        ],
        out_specs=(pl.BlockSpec((4, OUTER, 256), lambda i: (0, 0, 0)),) * 2,
        scratch_shapes=[
            pltpu.VMEM((20, members, latitudes), F32),
            pltpu.VMEM((18, members, latitudes), BF16),
            pltpu.VMEM((8, OUTER, 256), F32),
            pltpu.VMEM((2, 4, members, latitudes), BF16),
        ],
        compiler_params=params(24),
        name="outer",
    )(planes, planes, *swaps, layer_depth)
    cross = across(cross, 1)
    got_edges = [across(jnp.stack([straight[k], cross[k]]), CHIPS[k]) for k in (3, 1, 2)]
    got_edges = got_edges[1:] + got_edges[:1]

    rows = cell_rows(observed_cell[0])
    live = jnp.arange(slots, dtype=jnp.int32)[None, :] < observed_count[0][:, None]
    root = jnp.sqrt(jnp.where(live, 1.0 / error_variance[0], 0.0))
    vmem = pl.BlockSpec(memory_space=pltpu.VMEM)
    slot = jnp.arange(slots, dtype=jnp.int32)
    place = jnp.arange(slots + LANES, dtype=jnp.int32)
    is_outer = rows >= 8 * INNER
    near = jnp.where(is_outer, 0, rows)
    rank = jnp.sum(is_outer[:, None, :] & (slot[None, :] < slot[:, None])[None], axis=2)
    count = jnp.sum(is_outer, axis=1, keepdims=True)
    found = is_outer[:, None, :] & (rank[:, None, :] == place[None, :, None])
    outer = jnp.sum(jnp.where(found, slot, 0), axis=2)
    outer = jnp.where(place[None] < count, outer, slots)
    outer = jnp.where(place[None] == slots + LANES - 1, count, outer).astype(jnp.int32)
    rows = jnp.pad(rows, ((0, 0), (0, LANES)), constant_values=8 * INNER)
    smem = pl.BlockSpec(memory_space=pltpu.SMEM)
    held_inner, seen = pl.pallas_call(
        spread_kernel,
        out_shape=(
            jax.ShapeDtypeStruct((8, INNER, 256), BF16),
            jax.ShapeDtypeStruct((2, 2, slots, LANES), F32),
        ),
        in_specs=[smem, vmem],
        scratch_shapes=[pltpu.VMEM((2, 8 * INNER, LANES), F32)],
        compiler_params=params(12),
        cost_estimate=cost(1, 8 * MIB),
        name="spread",
    )(near, got)
    one_tile = jax.ShapeDtypeStruct((PACKED, 256), BF16)
    held_outer, gram, to_first, to_second = pl.pallas_call(
        observe_kernel,
        out_shape=(
            jax.ShapeDtypeStruct((8, OUTER, 256), BF16),
            jax.ShapeDtypeStruct((2, PACKED, 256), F32),
            one_tile,
            one_tile,
        ),
        in_specs=[smem, smem] + [vmem] * 8,
        scratch_shapes=[
            pltpu.VMEM((8, OUTER, 256), BF16),
            pltpu.VMEM((2, 8 * OUTER, LANES), F32),
            pltpu.VMEM((2, 2, slots + 8, LANES), F32),
        ],
        compiler_params=params(16),
        name="observe",
    )(rows, outer, root, observed_value[0], seen, straight, cross, *got_edges)
    anomaly_1, mean_1, anomaly_2, mean_2 = pl.pallas_call(
        prepare_kernel,
        out_shape=(
            jax.ShapeDtypeStruct((8, FIRST, 256), BF16),
            jax.ShapeDtypeStruct((8, FIRST, LANES), F32),
            jax.ShapeDtypeStruct((8, SECOND, 256), BF16),
            jax.ShapeDtypeStruct((8, SECOND, LANES), F32),
        ),
        compiler_params=params(12),
        cost_estimate=cost(1, 6 * MIB),
        name="prepare",
    )(held_inner, held_outer)

    line, short = pl.pallas_call(
        combine_kernel,
        out_shape=(
            jax.ShapeDtypeStruct(gram.shape, F32),
            jax.ShapeDtypeStruct(gram.shape, BF16),
        ),
        compiler_params=params(8),
        name="combine",
    )(gram, *band_swaps(to_first, to_second))
    below, above = mem_swaps(short)
    *back, maps = pl.pallas_call(
        analyse_kernel,
        out_shape=(jax.ShapeDtypeStruct((FIRST, 256), BF16),) * 8
        + (jax.ShapeDtypeStruct((2, 256, 256), BF16),),
        scratch_shapes=[pltpu.VMEM((8, FIRST, 256), BF16), pltpu.VMEM((2, 8, 32, 256), BF16)],
        compiler_params=params(20),
        name="analyse",
    )(line, below, above, anomaly_1, mean_1)
    first = partners(back)
    maps, first[4] = lax.optimization_barrier((maps, first[4]))
    back = pl.pallas_call(
        second_kernel,
        out_shape=(jax.ShapeDtypeStruct((SECOND, 256), BF16),) * 8,
        scratch_shapes=[pltpu.VMEM((8, SECOND, 256), BF16)],
        compiler_params=params(16),
        cost_estimate=cost(1, 6 * MIB),
        name="second",
    )(maps, anomaly_2, mean_2)
    second = partners(back)
    result = jax.ShapeDtypeStruct(planes.shape, BF16)
    half = pl.pallas_call(
        first_return_kernel,
        out_shape=result,
        out_specs=far,
        scratch_shapes=[
            pltpu.VMEM((8, FIRST, 256), F32),
            pltpu.VMEM((12, latitudes, 256), F32),
            pltpu.VMEM((3, 32, members, latitudes), BF16),
            pltpu.SemaphoreType.DMA((3,)),
        ],
        compiler_params=params(20),
        cost_estimate=cost(1, 4 * MIB),
        name="first_return",
    )(*first)
    planes = pl.pallas_call(
        second_return_kernel,
        out_shape=result,
        in_specs=[vmem] * 8 + [far],
        out_specs=far,
        scratch_shapes=[
            pltpu.VMEM((8, SECOND, 256), F32),
            pltpu.VMEM((11, latitudes, 256), F32),
            pltpu.VMEM((3, 28, members, latitudes), BF16),
            pltpu.SemaphoreType.DMA((12,)),
        ],
        input_output_aliases={8: 0},
        compiler_params=params(20),
        name="second_return",
    )(*second, half)
    return jnp.transpose(planes, (2, 0, 1, 3))


def choose(ensemble, layer_depth, observed_cell, *rest):
    mesh_shape = (lax.axis_size("mem"), lax.axis_size("band"))
    shape = (mesh_shape, ensemble.shape, observed_cell.shape[1])
    fits = shape == ((8, 4), (32, 3, 60, 160), 2) and observed_cell.shape[2] % 16 == 0
    chosen = on_device_fast if fits else on_device
    return chosen(ensemble, layer_depth, observed_cell, *rest)


def solution(mesh):
    in_specs = (
        P("mem", None, "band", None),
        P("band", None),
        P("mem", "band", None),
        P("mem", "band", None),
        P("mem", "band", None),
        P("mem", "band"),
    )
    out_specs = P("mem", None, "band", None)
    return jax.shard_map(
        choose, mesh=mesh, in_specs=in_specs, out_specs=out_specs, check_vma=False
    )
```

```python
import math

import jax
import jax.numpy as jnp
import numpy as np
from jax import lax
from jax.experimental import pallas as pl
from jax.experimental.pallas import tpu as pltpu
from jax.sharding import PartitionSpec as P

SWEEPS = 5


half_step = 0.1
coriolis_scale = 0.3
neighbour_weight = 0.75


def padded_2(cells, sides, width):
    for axis, dim in sides:
        count = lax.axis_size(axis)
        head = lax.slice_in_dim(cells, 0, width, axis=dim)
        tail = lax.slice_in_dim(cells, cells.shape[dim] - width, cells.shape[dim], axis=dim)
        cells = jnp.concatenate(
            [
                lax.ppermute(tail, axis, [(i, (i + 1) % count) for i in range(count)]),
                cells,
                lax.ppermute(head, axis, [((i + 1) % count, i) for i in range(count)]),
            ],
            axis=dim,
        )
    return cells


def north_south(source):
    widths = [(0, 0)] * (source.ndim - 1) + [(1, 1)]
    padded = jnp.pad(source, widths)
    return padded[..., 2:] - padded[..., :-2]


def coriolis(latitudes):
    position = jnp.arange(latitudes, dtype=jnp.float32)
    return coriolis_scale * jnp.sin(math.pi * ((position + 0.5) / latitudes - 0.5))


def newton_schulz(starting):
    identity = jnp.eye(starting.shape[-1], dtype=starting.dtype)
    root_part = starting
    inverse_root = jnp.broadcast_to(identity, starting.shape)
    for sweep_index in range(SWEEPS):
        product = jnp.einsum(
            "tij,tjk->tik", inverse_root, root_part, precision=lax.Precision.HIGHEST
        )
        middle = 1.5 * identity - 0.5 * product
        root_part = jnp.einsum("tij,tjk->tik", root_part, middle, precision=lax.Precision.HIGHEST)
        inverse_root = jnp.einsum(
            "tij,tjk->tik", middle, inverse_root, precision=lax.Precision.HIGHEST
        )
    return inverse_root


def on_device(ensemble, layer_depth, observed_cell, observed_value, error_variance, observed_count):
    block_members = ensemble.shape[0]
    columns = ensemble.shape[2]
    latitudes = ensemble.shape[3]
    strips = lax.axis_size("mem")
    members = block_members * strips
    strip_rows = latitudes // strips
    tile_count = observed_cell.shape[1]
    tile_columns = columns // tile_count
    slot_count = observed_cell.shape[2]
    tile_cells = 3 * tile_columns * strip_rows
    height = ensemble[:, 0].astype(jnp.float32)
    eastward = ensemble[:, 1].astype(jnp.float32)
    northward = ensemble[:, 2].astype(jnp.float32)
    turning = coriolis(latitudes)
    flux_east = (layer_depth * eastward).astype(jnp.bfloat16)
    flux_north = (layer_depth * northward).astype(jnp.bfloat16)
    east_margin = padded_2(flux_east, (("band", 1),), 1)
    east_west = east_margin[:, 2:].astype(jnp.float32) - east_margin[:, :-2].astype(jnp.float32)
    north_local = lax.optimization_barrier(flux_north).astype(jnp.float32)
    raised = height - half_step * (east_west + north_south(north_local))
    surface_elevation_cast = raised.astype(jnp.bfloat16)
    height_margin = padded_2(surface_elevation_cast, (("band", 1),), 1)
    margin_wide = height_margin.astype(jnp.float32)
    height_inner = margin_wide[:, 1:-1]
    revised_zonal_velocity = (
        eastward + turning * northward - half_step * (margin_wide[:, 2:] - margin_wide[:, :-2])
    )
    revised_meridional_velocity = (
        northward - turning * eastward - half_step * north_south(height_inner)
    )
    advance_dynamics = jnp.stack(
        [
            surface_elevation_cast,
            revised_zonal_velocity.astype(jnp.bfloat16),
            revised_meridional_velocity.astype(jnp.bfloat16),
        ],
        axis=1,
    )
    reordered = advance_dynamics.reshape(
        block_members, 3, tile_count, tile_columns, strips, strip_rows
    )
    reordered = jnp.transpose(reordered, (4, 2, 0, 1, 3, 5)).reshape(
        strips, tile_count, block_members, tile_cells
    )
    tile_block = lax.all_to_all(reordered, "mem", split_axis=0, concat_axis=2, tiled=True)[0]
    cells_here = observed_cell[0]
    values = jnp.take_along_axis(tile_block, cells_here[:, None, :], axis=2)
    observed_mean = jnp.sum(values, axis=1, dtype=jnp.float32) / members
    slot_index = jnp.arange(slot_count, dtype=jnp.int32)[None, :]
    live_slots = slot_index < observed_count[0][:, None]
    root_weight = jnp.sqrt(jnp.where(live_slots, 1.0 / error_variance[0], 0.0))
    spread = (
        root_weight[:, None, :] * (values.astype(jnp.float32) - observed_mean[:, None, :])
    ).astype(jnp.bfloat16)
    misfit = (root_weight * (observed_value[0] - observed_mean)).astype(jnp.bfloat16)
    spread_margin, misfit_margin = (
        padded_2(spread[None], (("mem", 0), ("band", 1)), 1),
        padded_2(misfit[None], (("mem", 0), ("band", 1)), 1),
    )
    gram_margin = jnp.einsum(
        "atko,atlo->atkl", spread_margin, spread_margin, preferred_element_type=jnp.float32
    )
    pull_margin = jnp.einsum(
        "atko,ato->atk", spread_margin, misfit_margin, preferred_element_type=jnp.float32
    )
    strip_here = lax.axis_index("mem")
    lower_valid = (strip_here > 0).astype(jnp.float32)
    upper_valid = (strip_here < strips - 1).astype(jnp.float32)
    strip_mask = (lower_valid, 1.0, upper_valid)
    total_gram = jnp.zeros((tile_count, members, members), jnp.float32)
    total_pull = jnp.zeros((tile_count, members), jnp.float32)
    for offset_lat in range(3):
        for offset_lon in range(3):
            factor = (
                neighbour_weight ** (abs(offset_lat - 1) + abs(offset_lon - 1))
                * strip_mask[offset_lat]
            )
            total_gram = (
                total_gram + factor * gram_margin[offset_lat, offset_lon : offset_lon + tile_count]
            )
            total_pull = (
                total_pull + factor * pull_margin[offset_lat, offset_lon : offset_lon + tile_count]
            )
    system = (members - 1) * jnp.eye(members, dtype=jnp.float32)[None] + total_gram
    frobenius = jnp.sqrt(jnp.sum(system * system, axis=(1, 2)))
    inverse_root = newton_schulz(system / frobenius[:, None, None])
    spread_map = inverse_root * (math.sqrt(members - 1) / jnp.sqrt(frobenius))[:, None, None]
    half_pull = jnp.einsum("tij,tj->ti", inverse_root, total_pull, precision=lax.Precision.HIGHEST)
    shift_weights = (
        jnp.einsum("tij,tj->ti", inverse_root, half_pull, precision=lax.Precision.HIGHEST)
        / frobenius[:, None]
    )
    weights = (spread_map + shift_weights[:, :, None]).astype(jnp.bfloat16)
    state_mean = jnp.sum(tile_block, axis=1, dtype=jnp.float32) / members
    anomaly = (tile_block.astype(jnp.float32) - state_mean[:, None, :]).astype(jnp.bfloat16)
    update = jnp.einsum("tjk,tjc->tkc", weights, anomaly, preferred_element_type=jnp.float32)
    analysed = (state_mean[:, None, :] + update).astype(jnp.bfloat16)
    returned = lax.all_to_all(analysed[None], "mem", split_axis=2, concat_axis=0, tiled=True)
    returned = returned.reshape(strips, tile_count, block_members, 3, tile_columns, strip_rows)
    return jnp.transpose(returned, (2, 3, 1, 4, 0, 5)).reshape(block_members, 3, columns, latitudes)


LANES = 128
GROUPS = 23
INNER = 304
OUTER = 152
FIRST = 240
SECOND = 216
F32 = jnp.float32
BF16 = jnp.bfloat16
PACKED = 136
CHIPS = (0, 2, 4, 6)
ORDER = (6, 2, 4, 7, 1, 3, 5, 0)
MIB = 1024 * 1024


def params(size):
    return pltpu.CompilerParams(vmem_limit_bytes=size * MIB)


def cost(flops, moved):
    return pl.CostEstimate(flops=flops, bytes_accessed=moved, transcendentals=0)


def identity(size, dtype):
    row = lax.broadcasted_iota(jnp.int32, (size, size), 0)
    column = lax.broadcasted_iota(jnp.int32, (size, size), 1)
    return (row == column).astype(F32).astype(dtype)


def dot_nt(left, right):
    return lax.dot_general(left, right, (((1,), (1,)), ((), ())), preferred_element_type=F32)


def dot_nn(left, right):
    return lax.dot_general(left, right, (((1,), (0,)), ((), ())), preferred_element_type=F32)


def split(value):
    high = value.astype(BF16)
    return high, (value - high.astype(F32)).astype(BF16)


def left_3(parts):
    return jnp.concatenate([parts[0], parts[0], parts[1]], axis=1)


def right_3(parts):
    return jnp.concatenate([parts[0], parts[1], parts[0]], axis=0)


def triangle(size):
    row = lax.broadcasted_iota(jnp.int32, (size, size), 0)
    column = lax.broadcasted_iota(jnp.int32, (size, size), 1)
    return row, column


def packed(block, pull):
    row, column = triangle(128)
    last = block[128:256, 128:256]
    corner = jnp.where(row >= column, block[0:128, 0:128], last)
    middle = jnp.sum(jnp.where(row == column, last, 0.0), axis=0, keepdims=True)
    middle = jnp.concatenate([jnp.zeros_like(middle), middle], axis=1)
    top = jnp.concatenate([block[128:256, 0:128], corner], axis=1)
    tail = jnp.where(lax.broadcasted_iota(jnp.int32, (8, 256), 0) == 0, pull, middle)
    return jnp.concatenate([top, tail], axis=0)


def unpacked(value):
    row, column = triangle(128)
    low, corner = value[0:128, 0:128], value[0:128, 128:256]
    other = jnp.transpose(corner)
    first = jnp.where(row >= column, corner, other)
    last = jnp.where(row < column, corner, other)
    last = jnp.where(row == column, value[129:130, 128:256], last)
    top = jnp.concatenate([first, jnp.transpose(low)], axis=1)
    return jnp.concatenate([top, jnp.concatenate([low, last], axis=1)], axis=0), value[128:136]


def exchange_lanes(blocks, lane):
    blocks = [list(pair) for pair in blocks]
    for q in range(4):
        low, high = blocks[q], blocks[q + 4]
        blocks[q], blocks[q + 4] = [low[0], high[0]], [low[1], high[1]]
    for bit in range(2):
        step = 32 << bit
        odd = (lane & step) != 0
        for q in range(8):
            if q & (1 << bit):
                continue
            for h in range(2):
                low, high = blocks[q][h], blocks[q | (1 << bit)][h]
                blocks[q][h] = jnp.where(odd, pltpu.roll(high, step, 1), low)
                blocks[q | (1 << bit)][h] = jnp.where(odd, high, pltpu.roll(low, LANES - step, 1))
    return blocks


def group_of(variable, index):
    return variable + (variable * 2 + index - 4 if index > 3 else 18 - 3 * index)


def row_of(group):
    return 20 * group + (4 if group >= 15 else 0)


def difference(latitudes):
    source = lax.broadcasted_iota(jnp.int32, (latitudes, latitudes), 0)
    target = lax.broadcasted_iota(jnp.int32, (latitudes, latitudes), 1)
    shift = (source == target + 1).astype(F32) - (source == target - 1).astype(F32)
    return shift.astype(BF16)


def rows_apart(value, shift):
    flat = value.reshape(-1, value.shape[-1])
    return dot_nn(flat, shift).reshape(value.shape)


def fluxes(east, deep):
    return (deep * east.astype(F32)).astype(BF16).astype(F32)


def heights(field, north, deep, ahead, behind, shift):
    flux_north = (deep * north.astype(F32)).astype(BF16)
    raised = field.astype(F32) - half_step * ((ahead - behind) + rows_apart(flux_north, shift))
    return raised.astype(BF16)


def velocities(east, north, here, ahead, behind, turning, shift):
    east, north = east.astype(F32), north.astype(F32)
    apart = ahead.astype(F32) - behind.astype(F32)
    new_east = east + turning * north - half_step * apart
    new_north = north - turning * east - half_step * rows_apart(here, shift)
    return new_east.astype(BF16), new_north.astype(BF16)


def put_group(staged, block, eye, first):
    latitudes = eye.shape[0]
    rows = latitudes // 8
    turned = dot_nt(eye, block.reshape(256, latitudes))
    for s in range(8):
        staged[s, first : first + rows, :] = turned[rows * s : rows * (s + 1)]


def turning_row(latitudes):
    position = lax.broadcasted_iota(jnp.int32, (8, latitudes), 1).astype(F32)
    turning = coriolis_scale * jnp.sin(math.pi * ((position + 0.5) / latitudes - 0.5))
    return turning[0:1, :][None]


def inner_kernel(
    ens, depth, out, to_first, to_second, here, deep, flux, height, staged, edges, arrived
):
    columns, members, latitudes = here.shape[1:]
    batch = columns // 5
    pieces = [pltpu.make_async_copy(depth, deep, arrived.at[5])]
    for k in range(5):
        span = pl.ds(k * batch, batch if k else 2)
        piece = pltpu.make_async_copy(ens.at[:, span], here.at[:, span], arrived.at[k])
        pieces.append(piece)
    for k in (0, 2, 3, 4, 5, 1):
        pieces[k].start()
    shift = difference(latitudes)
    turning = turning_row(latitudes)
    eye = identity(latitudes, BF16)
    pieces[0].wait()

    def depths(first, count):
        rows = [deep[c : c + 1, :] for c in range(first, first + count)]
        return jnp.stack([jnp.broadcast_to(row, (members, latitudes)) for row in rows])

    def edge(side, near, far):
        edges[side, 0] = here[0, near]
        edges[side, 1] = (deep[near : near + 1, :] * here[2, near].astype(F32)).astype(BF16)
        edges[side, 2] = flux[near].astype(BF16)
        edges[side, 3] = flux[far].astype(BF16)

    staged[:, 300:INNER, :] = jnp.zeros((8, INNER - 300, 256), F32)
    done = 2
    for k in (1, 2, 3, 4, 0):
        pieces[k + 1].wait()
        first, count = k * batch, batch if k else 2
        flux[first : first + count] = fluxes(here[1, first : first + count], depths(first, count))
        if k == 0:
            edge(0, 0, 1)
            continue
        if k == 4:
            edge(1, columns - 1, columns - 2)
        low, high = max(first - 1, batch + 1), first + batch - 1
        at = slice(low, high)
        ahead, behind = flux[low + 1 : high + 1], flux[low - 1 : high - 1]
        height[at] = heights(
            here[0, at], here[2, at], depths(low, high - low), ahead, behind, shift
        )
        while done < 7 and 8 * done + 9 <= high:
            first = 8 * done
            at = slice(first, first + 8)
            ahead, behind = height[first + 1 : first + 9], height[first - 1 : first + 7]
            new = velocities(here[1, at], here[2, at], height[at], ahead, behind, turning, shift)
            for v, field in enumerate((height[at],) + new):
                put_group(staged, field, eye, row_of(group_of(v, done)))
            done += 1
    odd = lax.axis_index("band") & 1
    to_first[...] = edges[1 - odd]
    to_second[...] = edges[odd]
    out[...] = staged[...].astype(BF16)


def outer_kernel(
    west_block, east_block, first_swap, second_swap, depth, *refs
):
    straight, cross, flux, height, staged, swapped = refs
    odd = lax.axis_index("band") & 1
    for side, block in enumerate((first_swap, second_swap)):
        swapped[side] = block[...]
    left, right = swapped.at[1 - odd], swapped.at[odd]
    members, latitudes = west_block.shape[2:]
    shift = difference(latitudes)
    turning = turning_row(latitudes)
    eye = identity(latitudes, BF16)

    def depths(first, count):
        return jnp.stack(
            [
                jnp.broadcast_to(depth[c : c + 1, :], (members, latitudes))
                for c in range(first, first + count)
            ]
        )

    def window(ens, edge, first, count, low, high):
        is_left = low == 0
        base = 2 if is_left else 0
        flux[base : base + count] = fluxes(ens[1, 0:count], depths(first, count))
        at = 0 if is_left else count
        near, far = (1, 0) if is_left else (at, at + 1)
        flux[near] = edge[2].astype(F32)
        flux[far] = edge[3].astype(F32)
        wide = high - low + 1
        skip = 0 if is_left else 1
        columns = slice(skip, skip + wide)
        new = heights(
            ens[0, columns],
            ens[2, columns],
            depths(first + skip, wide),
            flux[base + skip + 1 : base + skip + 1 + wide],
            flux[base + skip - 1 : base + skip - 1 + wide],
            shift,
        )
        start = 1 if is_left else 0
        height[start : start + wide] = new
        place = 0 if is_left else wide
        middle = near
        east_west = flux[middle + 1] - flux[middle - 1]
        raised = edge[0].astype(F32) - half_step * (east_west + rows_apart(edge[1], shift))
        height[place] = raised.astype(BF16)
        count = high - low
        here = height[1 : 1 + count]
        ahead, behind = height[2 : 2 + count], height[0:count]
        at = slice(low - first, high - first)
        return (here,) + velocities(ens[1, at], ens[2, at], here, ahead, behind, turning, shift)

    for v, field in enumerate(window(west_block, left, 0, 18, 0, 16)):
        for index in range(2):
            at = row_of(group_of(v, index)) - INNER
            put_group(staged, field[8 * index : 8 * index + 8], eye, at)
    ends = window(east_block, right, 54, 6, 56, 60)
    put_group(staged, jnp.concatenate([ends[0], ends[1]], axis=0), eye, 120)
    block = jnp.concatenate([ends[2], ends[2]], axis=0).reshape(256, latitudes)
    turned = dot_nt(eye, block)
    lower = lax.broadcasted_iota(jnp.int32, (10, 256), 1) < LANES
    for s in range(8):
        rows = [turned[20 * s + 10 * k : 20 * s + 10 * k + 10] for k in range(2)]
        staged[s, 140:150, :] = jnp.where(lower, rows[0], rows[1])
    staged[:, 150:OUTER, :] = jnp.zeros((8, OUTER - 150, 256), F32)
    me = lax.axis_index("mem")
    for k, d in enumerate(CHIPS):
        straight[k] = staged[me ^ d].astype(BF16)
        cross[k] = staged[me ^ d ^ 1].astype(BF16)


def spread_block(source, held, wide, start, lane):
    spans = [slice(h * LANES, (h + 1) * LANES) for h in range(2)]
    count = source.shape[1]
    here = pl.ds(start, 16)
    blocks = exchange_lanes([[source[q, here, span] for span in spans] for q in range(8)], lane)
    for q in range(8):
        to = pl.ds(pl.multiple_of(q * count + start, 8), 16)
        for h in range(2):
            wide[h, to, :] = blocks[q][h].astype(F32)
            held[q, here, spans[h]] = blocks[q][h]


def spread_kernel(cells, got, held, seen, wide):
    lane = lax.broadcasted_iota(jnp.int32, (16, LANES), 1)

    def step(index, carry):
        spread_block(got, held, wide, pl.multiple_of(index * 16, 16), lane)
        return carry

    lax.fori_loop(0, INNER // 16, step, 0, unroll=4)
    slots = seen.shape[2]
    unroll = 16

    def pick(index, carry):
        for t in range(2):
            for k in range(unroll):
                slot = index * unroll + k
                row = cells[t, slot]
                for h in range(2):
                    seen[t, h, pl.ds(slot, 1), :] = wide[h, pl.ds(row, 1), :]
        return carry

    lax.fori_loop(0, slots // unroll, pick, 0)


def observe_kernel(cells, outer, weight, target, first, straight, cross, *refs):
    edges, (held, gram, to_first, to_second, joined, wide, seen) = refs[:3], refs[3:]
    wholes = []
    lane = lax.broadcasted_iota(jnp.int32, (16, LANES), 1)
    me = lax.axis_index("mem")
    for k, d in enumerate(CHIPS):
        joined[me ^ d, 0:OUTER, :] = straight[0] if k == 0 else edges[k - 1][0]
        joined[me ^ d ^ 1, 0:OUTER, :] = cross[0] if k == 0 else edges[k - 1][1]
    for start in (*range(0, OUTER - 16, 16), OUTER - 16):
        spread_block(joined, held, wide, start, lane)
    slots = first.shape[2]
    seen[:, :, 0:slots, :] = first[...]
    for t in range(2):

        def pick(index, carry):
            for k in range(8):
                slot = outer[t, index * 8 + k]
                row = cells[t, slot] - 8 * INNER
                for h in range(2):
                    seen[t, h, pl.ds(slot, 1), :] = wide[h, pl.ds(row, 1), :]
            return carry

        lax.fori_loop(0, (outer[t, slots + LANES - 1] + 7) // 8, pick, 0)
    eye = identity(256, BF16)
    for t in range(2):
        values = jnp.concatenate([seen[t, h, 0:slots] for h in range(2)], axis=1).astype(BF16)
        turned = dot_nt(eye, values)
        mean = jnp.sum(turned, axis=0, keepdims=True) * (1.0 / 256)
        root = weight[t : t + 1, :]
        spread = (root * (turned - mean)).astype(BF16)
        misfit = (root * (target[t : t + 1, :] - mean)).astype(BF16)
        block = dot_nt(spread, spread)
        pull = dot_nt(jnp.broadcast_to(misfit, (16, slots)), spread)
        whole = packed(block, pull[0:8])
        gram[t] = whole
        wholes.append(whole.astype(BF16))
    odd = (lax.axis_index("band") & 1) == 1
    to_first[...] = jnp.where(odd, wholes[0], wholes[1])
    to_second[...] = jnp.where(odd, wholes[1], wholes[0])


def combine_kernel(gram, first_swap, second_swap, line, short):
    odd = (lax.axis_index("band") & 1) == 1
    first, second = first_swap[...].astype(F32), second_swap[...].astype(F32)
    west, east = jnp.where(odd, first, second), jnp.where(odd, second, first)
    for t, beside in enumerate((west + gram[1], gram[0] + east)):
        total = gram[t] + neighbour_weight * beside
        line[t] = total
        short[t] = total.astype(BF16)


def prepare_kernel(inner, outer, *refs):
    average = jnp.full((256, LANES), 1.0 / 256, BF16)
    for q in range(8):
        pieces = (inner[q, 0:FIRST], jnp.concatenate([inner[q, FIRST:INNER], outer[q, 0:OUTER]], axis=0))
        for k, piece in enumerate(pieces):
            mean = dot_nn(piece, average)
            refs[2 * k + 1][q] = mean
            mean = jnp.concatenate([mean, mean], axis=1)
            refs[2 * k][q] = (piece.astype(F32) - mean).astype(BF16)


def send_back(results, outs):
    lane = lax.broadcasted_iota(jnp.int32, (16, LANES), 1)
    spans = [slice(h * LANES, (h + 1) * LANES) for h in range(2)]

    def move(start):
        here = pl.ds(start, 16)
        blocks = [[results[q, here, span] for span in spans] for q in range(8)]
        blocks = exchange_lanes(blocks, lane)
        for q in range(8):
            for h in range(2):
                outs[ORDER.index(q)][here, spans[h]] = blocks[q][h]

    def step(index, carry):
        move(pl.multiple_of(index * 16, 16))
        return carry

    count = results.shape[1]
    lax.fori_loop(0, count // 16, step, 0, unroll=4)
    if count % 16:
        move(count - 16)


def apply_maps(anomaly, mean, maps, results, q, edge, order):
    count = results.shape[1]
    low, high = edge // 16 * 16, (edge + 15) // 16 * 16
    first = dot_nt(anomaly[q, 0:high], maps[order[0]])
    centre = jnp.concatenate([mean[q], mean[q]], axis=1)
    results[q, 0:low] = (centre[0:low] + first[0:low]).astype(BF16)
    if low == count:
        return
    second = dot_nt(anomaly[q, low:count], maps[order[1]])
    if low < high:
        near = lax.broadcasted_iota(jnp.int32, (16, 256), 0) < edge - low
        both = jnp.where(near, first[low:high], second[0:16])
        results[q, low:high] = (centre[low:high] + both).astype(BF16)
    results[q, high:count] = (centre[high:count] + second[high - low : count - low]).astype(BF16)


def second_kernel(maps, anomaly, mean, *refs):
    outs, results = refs[:8], refs[8]
    both = [maps[0], maps[1]]
    for q in range(8):
        apply_maps(anomaly, mean, both, results, q, 184, (0, 1))
    send_back(results, outs)


def analyse_kernel(line, below, above, anomaly, mean, *refs):
    outs, (kept, results, ordered) = refs[:8], refs[8:]
    size = 256
    eye = identity(size, F32)
    norms, pulls, roots, inverses = [], [], [], []
    for t in range(2):
        beside = below[t].astype(F32) + above[t].astype(F32)
        block, pull = unpacked(line[t] + neighbour_weight * beside)
        system = (size - 1) * eye + block
        square = jnp.sum(jnp.sum(system * system, axis=0, keepdims=True), axis=1, keepdims=True)
        norms.append(jnp.sqrt(square))
        pulls.append(pull)
        roots.append(system * (1.0 / norms[t]))
    for sweep in range(SWEEPS):
        rights = [right_3(split(root)) for root in roots]
        if sweep == 0:
            inverses = [1.5 * eye - 0.5 * root for root in roots]
            lefts = [left_3(split(inverse)) for inverse in inverses]
            roots = [dot_nn(left, right) for left, right in zip(lefts, rights)]
            continue
        parts = [split(inverse) for inverse in inverses]
        products = [dot_nn(left_3(part), right) for part, right in zip(parts, rights)]
        middles = [left_3(split(1.5 * eye - 0.5 * product)) for product in products]
        if sweep < SWEEPS - 1:
            roots = [dot_nn(middle, right) for middle, right in zip(middles, rights)]
        inverses = [dot_nn(middle, right_3(part)) for middle, part in zip(middles, parts)]
    maps = []
    for t in range(2):
        right = right_3(split(inverses[t]))
        half_pull = dot_nn(left_3(split(pulls[t])), right)
        shift = dot_nn(left_3(split(half_pull)), right) / norms[t]
        scale = math.sqrt(size - 1) / jnp.sqrt(norms[t])
        ordered[t] = (inverses[t] * scale + shift[0:1]).astype(BF16).reshape(8, 32, size)
    me = lax.axis_index("mem")
    for t in range(2):
        maps.append(jnp.concatenate([ordered[t, me ^ d] for d in range(8)], axis=0))
        kept[t] = maps[t]
    for q in range(8):
        apply_maps(anomaly, mean, maps, results, q, 180 if q < 6 else FIRST, (1, 0))
    send_back(results, outs)


def spread_strips(got, wide):
    me = lax.axis_index("mem")
    for k, d in enumerate(ORDER):
        wide[me ^ d] = got[k][...].astype(F32)


def take_group(wide, turned, eye, g, shape, skipped=0):
    rows = shape[2] // 8
    at = row_of(g) - row_of(skipped)
    g = g - skipped
    for s in range(8):
        turned[g, rows * s : rows * (s + 1), :] = wide[s, at : at + rows, :]
    return dot_nt(eye, turned[g].astype(BF16)).astype(BF16).reshape(shape)


def first_return_kernel(*refs):
    got, (out, wide, turned, planes, sent) = refs[:8], refs[8:]
    shape = (8,) + planes.shape[2:]
    spread_strips(got, wide)
    eye = identity(256, BF16)
    copies = []
    for v in range(3):
        for index in range(3, 7):
            at = 8 * (index - 3)
            planes[v, at : at + 8] = take_group(wide, turned, eye, group_of(v, index), shape)
        copies.append(pltpu.make_async_copy(planes.at[v], out.at[v, pl.ds(24, 32)], sent.at[v]))
        copies[v].start()
    for copy in copies:
        copy.wait()


def second_return_kernel(*refs):
    got, (_, out, wide, turned, planes, sent) = refs[:8], refs[8:]
    shape = (8,) + planes.shape[2:]
    spread_strips(got, wide)
    eye = identity(256, BF16)
    mixed = take_group(wide, turned, eye, 21, shape, 12)
    planes[0, 24:28] = mixed[0:4]
    planes[1, 24:28] = mixed[4:8]
    at = row_of(22) - row_of(12)
    turned[10] = jnp.zeros(turned.shape[1:], F32)
    for s in range(8):
        for k in range(2):
            to = 20 * s + 10 * k
            half = wide[s, at : at + 10, k * LANES : (k + 1) * LANES]
            turned[10, to : to + 10, 0:LANES] = half
    block = dot_nt(eye, turned[10].astype(BF16)).astype(BF16).reshape(shape)
    planes[2, 24:28] = block[0:4]
    copies = []

    def leave(v, at, to, count):
        source, target = planes.at[v, pl.ds(at, count)], out.at[v, pl.ds(to, count)]
        copies.append(pltpu.make_async_copy(source, target, sent.at[len(copies)]))
        copies[-1].start()

    for v in range(3):
        leave(v, 24, 56, 4)
    for v in range(3):
        for index in range(3):
            at = 8 * index
            block = take_group(wide, turned, eye, group_of(v, index), shape, 12)
            planes[v, at : at + 8] = block
            leave(v, at, at, 8)
    for copy in copies:
        copy.wait()


def swapped_pairs(values, axis, pairs):
    moved = []
    for value, some in zip(values, pairs):
        both = some + [(j, i) for i, j in some]
        moved.append(lax.ppermute(value, axis, both))
    return moved


def band_swaps(first, second):
    count = lax.axis_size("band")
    starts = range(0, count, 2)
    pairs = [[(i, i + 1) for i in starts], [(i + 1, (i + 2) % count) for i in starts]]
    return swapped_pairs((first, second), "band", pairs)


def mem_swaps(value):
    count = lax.axis_size("mem")
    pairs = [[(i, i + 1) for i in range(k, count - 1, 2)] for k in range(2)]
    return swapped_pairs((value, value), "mem", pairs)


def across(value, difference):
    return lax.ppermute(value, "mem", [(i, i ^ difference) for i in range(8)])


def partners(values):
    return [across(value, d) if d else value for d, value in zip(ORDER, values)]


def swap(value):
    return lax.all_to_all(value, "mem", split_axis=0, concat_axis=0, tiled=True)


def cell_rows(cell):
    variable = cell // 600
    tile = jnp.arange(2, dtype=jnp.int32)[:, None]
    column = tile * 30 + cell // 20 % 30
    index = column // 8
    place = column % 8
    group = variable + jnp.where(index > 3, variable * 2 + index - 4, 18 - 3 * index)
    is_last = column >= 56
    group = jnp.where(is_last, 21 + variable // 2, group)
    place = jnp.where(is_last, column - 56 + 4 * (variable % 2), place)
    row = cell % 20
    place = jnp.where(group == 22, place + 4 * (row // 10), place)
    row = jnp.where(group == 22, row % 10, row)
    first = place * INNER + group * 20
    last = 8 * INNER + place * OUTER + (group - 15) * 20
    return jnp.where(group < 15, first, last) + row


def on_device_fast(
    ensemble, layer_depth, observed_cell, observed_value, error_variance, observed_count
):
    members, _, columns, latitudes = ensemble.shape
    slots = observed_cell.shape[2]
    planes = jnp.transpose(ensemble, (1, 2, 0, 3))
    edge = jax.ShapeDtypeStruct((4, members, latitudes), BF16)
    far = pl.BlockSpec(memory_space=pltpu.HBM)
    sent, to_first, to_second = pl.pallas_call(
        inner_kernel,
        out_shape=(jax.ShapeDtypeStruct((8, INNER, 256), BF16), edge, edge),
        in_specs=[far, far],
        scratch_shapes=[
            pltpu.VMEM(planes.shape, BF16),
            pltpu.VMEM((columns, latitudes), F32),
            pltpu.VMEM((columns, members, latitudes), F32),
            pltpu.VMEM((columns, members, latitudes), BF16),
            pltpu.VMEM((8, INNER, 256), F32),
            pltpu.VMEM((2, 4, members, latitudes), BF16),
            pltpu.SemaphoreType.DMA((6,)),
        ],
        compiler_params=params(60),
        name="inner",
    )(planes, layer_depth)
    got = swap(sent)
    swaps = band_swaps(to_first, to_second)
    flat = pl.BlockSpec((4, members, latitudes), lambda i: (0, 0, 0))
    straight, cross = pl.pallas_call(
        outer_kernel,
        grid=(1,),
        out_shape=(jax.ShapeDtypeStruct((4, OUTER, 256), BF16),) * 2,
        in_specs=[
            pl.BlockSpec((3, 20, members, latitudes), lambda i: (0, 0, 0, 0)),
            pl.BlockSpec((3, 6, members, latitudes), lambda i: (0, 9, 0, 0)),
            flat,
            flat,
            pl.BlockSpec((columns, latitudes), lambda i: (0, 0)),
        ],
        out_specs=(pl.BlockSpec((4, OUTER, 256), lambda i: (0, 0, 0)),) * 2,
        scratch_shapes=[
            pltpu.VMEM((20, members, latitudes), F32),
            pltpu.VMEM((18, members, latitudes), BF16),
            pltpu.VMEM((8, OUTER, 256), F32),
            pltpu.VMEM((2, 4, members, latitudes), BF16),
        ],
        compiler_params=params(24),
        name="outer",
    )(planes, planes, *swaps, layer_depth)
    cross = across(cross, 1)
    got_edges = [across(jnp.stack([straight[k], cross[k]]), CHIPS[k]) for k in (3, 1, 2)]
    got_edges = got_edges[1:] + got_edges[:1]

    rows = cell_rows(observed_cell[0])
    live = jnp.arange(slots, dtype=jnp.int32)[None, :] < observed_count[0][:, None]
    root = jnp.sqrt(jnp.where(live, 1.0 / error_variance[0], 0.0))
    vmem = pl.BlockSpec(memory_space=pltpu.VMEM)
    slot = jnp.arange(slots, dtype=jnp.int32)
    place = jnp.arange(slots + LANES, dtype=jnp.int32)
    is_outer = rows >= 8 * INNER
    near = jnp.where(is_outer, 0, rows)
    rank = jnp.sum(is_outer[:, None, :] & (slot[None, :] < slot[:, None])[None], axis=2)
    count = jnp.sum(is_outer, axis=1, keepdims=True)
    found = is_outer[:, None, :] & (rank[:, None, :] == place[None, :, None])
    outer = jnp.sum(jnp.where(found, slot, 0), axis=2)
    outer = jnp.where(place[None] < count, outer, slots)
    outer = jnp.where(place[None] == slots + LANES - 1, count, outer).astype(jnp.int32)
    rows = jnp.pad(rows, ((0, 0), (0, LANES)), constant_values=8 * INNER)
    smem = pl.BlockSpec(memory_space=pltpu.SMEM)
    held_inner, seen = pl.pallas_call(
        spread_kernel,
        out_shape=(
            jax.ShapeDtypeStruct((8, INNER, 256), BF16),
            jax.ShapeDtypeStruct((2, 2, slots, LANES), F32),
        ),
        in_specs=[smem, vmem],
        scratch_shapes=[pltpu.VMEM((2, 8 * INNER, LANES), F32)],
        compiler_params=params(12),
        cost_estimate=cost(1, 8 * MIB),
        name="spread",
    )(near, got)
    one_tile = jax.ShapeDtypeStruct((PACKED, 256), BF16)
    held_outer, gram, to_first, to_second = pl.pallas_call(
        observe_kernel,
        out_shape=(
            jax.ShapeDtypeStruct((8, OUTER, 256), BF16),
            jax.ShapeDtypeStruct((2, PACKED, 256), F32),
            one_tile,
            one_tile,
        ),
        in_specs=[smem, smem] + [vmem] * 8,
        scratch_shapes=[
            pltpu.VMEM((8, OUTER, 256), BF16),
            pltpu.VMEM((2, 8 * OUTER, LANES), F32),
            pltpu.VMEM((2, 2, slots + 8, LANES), F32),
        ],
        compiler_params=params(16),
        name="observe",
    )(rows, outer, root, observed_value[0], seen, straight, cross, *got_edges)
    anomaly_1, mean_1, anomaly_2, mean_2 = pl.pallas_call(
        prepare_kernel,
        out_shape=(
            jax.ShapeDtypeStruct((8, FIRST, 256), BF16),
            jax.ShapeDtypeStruct((8, FIRST, LANES), F32),
            jax.ShapeDtypeStruct((8, SECOND, 256), BF16),
            jax.ShapeDtypeStruct((8, SECOND, LANES), F32),
        ),
        compiler_params=params(12),
        cost_estimate=cost(1, 6 * MIB),
        name="prepare",
    )(held_inner, held_outer)

    line, short = pl.pallas_call(
        combine_kernel,
        out_shape=(
            jax.ShapeDtypeStruct(gram.shape, F32),
            jax.ShapeDtypeStruct(gram.shape, BF16),
        ),
        compiler_params=params(8),
        name="combine",
    )(gram, *band_swaps(to_first, to_second))
    below, above = mem_swaps(short)
    *back, maps = pl.pallas_call(
        analyse_kernel,
        out_shape=(jax.ShapeDtypeStruct((FIRST, 256), BF16),) * 8
        + (jax.ShapeDtypeStruct((2, 256, 256), BF16),),
        scratch_shapes=[pltpu.VMEM((8, FIRST, 256), BF16), pltpu.VMEM((2, 8, 32, 256), BF16)],
        compiler_params=params(20),
        name="analyse",
    )(line, below, above, anomaly_1, mean_1)
    first = partners(back)
    maps, first[4] = lax.optimization_barrier((maps, first[4]))
    back = pl.pallas_call(
        second_kernel,
        out_shape=(jax.ShapeDtypeStruct((SECOND, 256), BF16),) * 8,
        scratch_shapes=[pltpu.VMEM((8, SECOND, 256), BF16)],
        compiler_params=params(16),
        cost_estimate=cost(1, 6 * MIB),
        name="second",
    )(maps, anomaly_2, mean_2)
    second = partners(back)
    result = jax.ShapeDtypeStruct(planes.shape, BF16)
    half = pl.pallas_call(
        first_return_kernel,
        out_shape=result,
        out_specs=far,
        scratch_shapes=[
            pltpu.VMEM((8, FIRST, 256), F32),
            pltpu.VMEM((12, latitudes, 256), F32),
            pltpu.VMEM((3, 32, members, latitudes), BF16),
            pltpu.SemaphoreType.DMA((3,)),
        ],
        compiler_params=params(20),
        cost_estimate=cost(1, 4 * MIB),
        name="first_return",
    )(*first)
    planes = pl.pallas_call(
        second_return_kernel,
        out_shape=result,
        in_specs=[vmem] * 8 + [far],
        out_specs=far,
        scratch_shapes=[
            pltpu.VMEM((8, SECOND, 256), F32),
            pltpu.VMEM((11, latitudes, 256), F32),
            pltpu.VMEM((3, 28, members, latitudes), BF16),
            pltpu.SemaphoreType.DMA((12,)),
        ],
        input_output_aliases={8: 0},
        compiler_params=params(20),
        name="second_return",
    )(*second, half)
    return jnp.transpose(planes, (2, 0, 1, 3))


def choose(ensemble, layer_depth, observed_cell, *rest):
    mesh_shape = (lax.axis_size("mem"), lax.axis_size("band"))
    shape = (mesh_shape, ensemble.shape, observed_cell.shape[1])
    fits = shape == ((8, 4), (32, 3, 60, 160), 2) and observed_cell.shape[2] % 16 == 0
    chosen = on_device_fast if fits else on_device
    return chosen(ensemble, layer_depth, observed_cell, *rest)


def solution(mesh):
    in_specs = (
        P("mem", None, "band", None),
        P("band", None),
        P("mem", "band", None),
        P("mem", "band", None),
        P("mem", "band", None),
        P("mem", "band"),
    )
    out_specs = P("mem", None, "band", None)
    return jax.shard_map(
        choose, mesh=mesh, in_specs=in_specs, out_specs=out_specs, check_vma=False
    )
```

```python
import math

import jax
import jax.numpy as jnp
import numpy as np
from jax import lax
from jax.experimental import pallas as pl
from jax.experimental.pallas import tpu as pltpu
from jax.sharding import PartitionSpec as P

SWEEPS = 5


half_step = 0.1
coriolis_scale = 0.3
neighbour_weight = 0.75


def padded_2(cells, sides, width):
    for axis, dim in sides:
        count = lax.axis_size(axis)
        head = lax.slice_in_dim(cells, 0, width, axis=dim)
        tail = lax.slice_in_dim(cells, cells.shape[dim] - width, cells.shape[dim], axis=dim)
        cells = jnp.concatenate(
            [
                lax.ppermute(tail, axis, [(i, (i + 1) % count) for i in range(count)]),
                cells,
                lax.ppermute(head, axis, [((i + 1) % count, i) for i in range(count)]),
            ],
            axis=dim,
        )
    return cells


def north_south(source):
    widths = [(0, 0)] * (source.ndim - 1) + [(1, 1)]
    padded = jnp.pad(source, widths)
    return padded[..., 2:] - padded[..., :-2]


def coriolis(latitudes):
    position = jnp.arange(latitudes, dtype=jnp.float32)
    return coriolis_scale * jnp.sin(math.pi * ((position + 0.5) / latitudes - 0.5))


def newton_schulz(starting):
    identity = jnp.eye(starting.shape[-1], dtype=starting.dtype)
    root_part = starting
    inverse_root = jnp.broadcast_to(identity, starting.shape)
    for sweep_index in range(SWEEPS):
        product = jnp.einsum(
            "tij,tjk->tik", inverse_root, root_part, precision=lax.Precision.HIGHEST
        )
        middle = 1.5 * identity - 0.5 * product
        root_part = jnp.einsum("tij,tjk->tik", root_part, middle, precision=lax.Precision.HIGHEST)
        inverse_root = jnp.einsum(
            "tij,tjk->tik", middle, inverse_root, precision=lax.Precision.HIGHEST
        )
    return inverse_root


def on_device(ensemble, layer_depth, observed_cell, observed_value, error_variance, observed_count):
    block_members = ensemble.shape[0]
    columns = ensemble.shape[2]
    latitudes = ensemble.shape[3]
    strips = lax.axis_size("mem")
    members = block_members * strips
    strip_rows = latitudes // strips
    tile_count = observed_cell.shape[1]
    tile_columns = columns // tile_count
    slot_count = observed_cell.shape[2]
    tile_cells = 3 * tile_columns * strip_rows
    height = ensemble[:, 0].astype(jnp.float32)
    eastward = ensemble[:, 1].astype(jnp.float32)
    northward = ensemble[:, 2].astype(jnp.float32)
    turning = coriolis(latitudes)
    flux_east = (layer_depth * eastward).astype(jnp.bfloat16)
    flux_north = (layer_depth * northward).astype(jnp.bfloat16)
    east_margin = padded_2(flux_east, (("band", 1),), 1)
    east_west = east_margin[:, 2:].astype(jnp.float32) - east_margin[:, :-2].astype(jnp.float32)
    north_local = lax.optimization_barrier(flux_north).astype(jnp.float32)
    raised = height - half_step * (east_west + north_south(north_local))
    surface_elevation_cast = raised.astype(jnp.bfloat16)
    height_margin = padded_2(surface_elevation_cast, (("band", 1),), 1)
    margin_wide = height_margin.astype(jnp.float32)
    height_inner = margin_wide[:, 1:-1]
    revised_zonal_velocity = (
        eastward + turning * northward - half_step * (margin_wide[:, 2:] - margin_wide[:, :-2])
    )
    revised_meridional_velocity = (
        northward - turning * eastward - half_step * north_south(height_inner)
    )
    advance_dynamics = jnp.stack(
        [
            surface_elevation_cast,
            revised_zonal_velocity.astype(jnp.bfloat16),
            revised_meridional_velocity.astype(jnp.bfloat16),
        ],
        axis=1,
    )
    reordered = advance_dynamics.reshape(
        block_members, 3, tile_count, tile_columns, strips, strip_rows
    )
    reordered = jnp.transpose(reordered, (4, 2, 0, 1, 3, 5)).reshape(
        strips, tile_count, block_members, tile_cells
    )
    tile_block = lax.all_to_all(reordered, "mem", split_axis=0, concat_axis=2, tiled=True)[0]
    cells_here = observed_cell[0]
    values = jnp.take_along_axis(tile_block, cells_here[:, None, :], axis=2)
    observed_mean = jnp.sum(values, axis=1, dtype=jnp.float32) / members
    slot_index = jnp.arange(slot_count, dtype=jnp.int32)[None, :]
    live_slots = slot_index < observed_count[0][:, None]
    root_weight = jnp.sqrt(jnp.where(live_slots, 1.0 / error_variance[0], 0.0))
    spread = (
        root_weight[:, None, :] * (values.astype(jnp.float32) - observed_mean[:, None, :])
    ).astype(jnp.bfloat16)
    misfit = (root_weight * (observed_value[0] - observed_mean)).astype(jnp.bfloat16)
    spread_margin, misfit_margin = (
        padded_2(spread[None], (("mem", 0), ("band", 1)), 1),
        padded_2(misfit[None], (("mem", 0), ("band", 1)), 1),
    )
    gram_margin = jnp.einsum(
        "atko,atlo->atkl", spread_margin, spread_margin, preferred_element_type=jnp.float32
    )
    pull_margin = jnp.einsum(
        "atko,ato->atk", spread_margin, misfit_margin, preferred_element_type=jnp.float32
    )
    strip_here = lax.axis_index("mem")
    lower_valid = (strip_here > 0).astype(jnp.float32)
    upper_valid = (strip_here < strips - 1).astype(jnp.float32)
    strip_mask = (lower_valid, 1.0, upper_valid)
    total_gram = jnp.zeros((tile_count, members, members), jnp.float32)
    total_pull = jnp.zeros((tile_count, members), jnp.float32)
    for offset_lat in range(3):
        for offset_lon in range(3):
            factor = (
                neighbour_weight ** (abs(offset_lat - 1) + abs(offset_lon - 1))
                * strip_mask[offset_lat]
            )
            total_gram = (
                total_gram + factor * gram_margin[offset_lat, offset_lon : offset_lon + tile_count]
            )
            total_pull = (
                total_pull + factor * pull_margin[offset_lat, offset_lon : offset_lon + tile_count]
            )
    system = (members - 1) * jnp.eye(members, dtype=jnp.float32)[None] + total_gram
    frobenius = jnp.sqrt(jnp.sum(system * system, axis=(1, 2)))
    inverse_root = newton_schulz(system / frobenius[:, None, None])
    spread_map = inverse_root * (math.sqrt(members - 1) / jnp.sqrt(frobenius))[:, None, None]
    half_pull = jnp.einsum("tij,tj->ti", inverse_root, total_pull, precision=lax.Precision.HIGHEST)
    shift_weights = (
        jnp.einsum("tij,tj->ti", inverse_root, half_pull, precision=lax.Precision.HIGHEST)
        / frobenius[:, None]
    )
    weights = (spread_map + shift_weights[:, :, None]).astype(jnp.bfloat16)
    state_mean = jnp.sum(tile_block, axis=1, dtype=jnp.float32) / members
    anomaly = (tile_block.astype(jnp.float32) - state_mean[:, None, :]).astype(jnp.bfloat16)
    update = jnp.einsum("tjk,tjc->tkc", weights, anomaly, preferred_element_type=jnp.float32)
    analysed = (state_mean[:, None, :] + update).astype(jnp.bfloat16)
    returned = lax.all_to_all(analysed[None], "mem", split_axis=2, concat_axis=0, tiled=True)
    returned = returned.reshape(strips, tile_count, block_members, 3, tile_columns, strip_rows)
    return jnp.transpose(returned, (2, 3, 1, 4, 0, 5)).reshape(block_members, 3, columns, latitudes)


LANES = 128
GROUPS = 23
INNER = 304
OUTER = 152
FIRST = 240
SECOND = 216
F32 = jnp.float32
BF16 = jnp.bfloat16
PACKED = 136
CHIPS = (0, 2, 4, 6)
ORDER = (6, 2, 4, 7, 1, 3, 5, 0)
MIB = 1024 * 1024


def params(size):
    return pltpu.CompilerParams(vmem_limit_bytes=size * MIB)


def cost(flops, moved):
    return pl.CostEstimate(flops=flops, bytes_accessed=moved, transcendentals=0)


def identity(size, dtype):
    row = lax.broadcasted_iota(jnp.int32, (size, size), 0)
    column = lax.broadcasted_iota(jnp.int32, (size, size), 1)
    return (row == column).astype(F32).astype(dtype)


def dot_nt(left, right):
    return lax.dot_general(left, right, (((1,), (1,)), ((), ())), preferred_element_type=F32)


def dot_nn(left, right):
    return lax.dot_general(left, right, (((1,), (0,)), ((), ())), preferred_element_type=F32)


def split(value):
    high = value.astype(BF16)
    return high, (value - high.astype(F32)).astype(BF16)


def left_3(parts):
    return jnp.concatenate([parts[0], parts[0], parts[1]], axis=1)


def right_3(parts):
    return jnp.concatenate([parts[0], parts[1], parts[0]], axis=0)


def triangle(size):
    row = lax.broadcasted_iota(jnp.int32, (size, size), 0)
    column = lax.broadcasted_iota(jnp.int32, (size, size), 1)
    return row, column


def packed(block, pull):
    row, column = triangle(128)
    last = block[128:256, 128:256]
    corner = jnp.where(row >= column, block[0:128, 0:128], last)
    middle = jnp.sum(jnp.where(row == column, last, 0.0), axis=0, keepdims=True)
    middle = jnp.concatenate([jnp.zeros_like(middle), middle], axis=1)
    top = jnp.concatenate([block[128:256, 0:128], corner], axis=1)
    tail = jnp.where(lax.broadcasted_iota(jnp.int32, (8, 256), 0) == 0, pull, middle)
    return jnp.concatenate([top, tail], axis=0)


def unpacked(value):
    row, column = triangle(128)
    low, corner = value[0:128, 0:128], value[0:128, 128:256]
    other = jnp.transpose(corner)
    first = jnp.where(row >= column, corner, other)
    last = jnp.where(row < column, corner, other)
    last = jnp.where(row == column, value[129:130, 128:256], last)
    top = jnp.concatenate([first, jnp.transpose(low)], axis=1)
    return jnp.concatenate([top, jnp.concatenate([low, last], axis=1)], axis=0), value[128:136]


def exchange_lanes(blocks, lane):
    blocks = [list(pair) for pair in blocks]
    for q in range(4):
        low, high = blocks[q], blocks[q + 4]
        blocks[q], blocks[q + 4] = [low[0], high[0]], [low[1], high[1]]
    for bit in range(2):
        step = 32 << bit
        odd = (lane & step) != 0
        for q in range(8):
            if q & (1 << bit):
                continue
            for h in range(2):
                low, high = blocks[q][h], blocks[q | (1 << bit)][h]
                blocks[q][h] = jnp.where(odd, pltpu.roll(high, step, 1), low)
                blocks[q | (1 << bit)][h] = jnp.where(odd, high, pltpu.roll(low, LANES - step, 1))
    return blocks


def group_of(variable, index):
    return variable + (variable * 2 + index - 4 if index > 3 else 18 - 3 * index)


def row_of(group):
    return 20 * group + (4 if group >= 15 else 0)


def difference(latitudes):
    source = lax.broadcasted_iota(jnp.int32, (latitudes, latitudes), 0)
    target = lax.broadcasted_iota(jnp.int32, (latitudes, latitudes), 1)
    shift = (source == target + 1).astype(F32) - (source == target - 1).astype(F32)
    return shift.astype(BF16)


def rows_apart(value, shift):
    flat = value.reshape(-1, value.shape[-1])
    return dot_nn(flat, shift).reshape(value.shape)


def fluxes(east, deep):
    return (deep * east.astype(F32)).astype(BF16).astype(F32)


def heights(field, north, deep, ahead, behind, shift):
    flux_north = (deep * north.astype(F32)).astype(BF16)
    raised = field.astype(F32) - half_step * ((ahead - behind) + rows_apart(flux_north, shift))
    return raised.astype(BF16)


def velocities(east, north, here, ahead, behind, turning, shift):
    east, north = east.astype(F32), north.astype(F32)
    apart = ahead.astype(F32) - behind.astype(F32)
    new_east = east + turning * north - half_step * apart
    new_north = north - turning * east - half_step * rows_apart(here, shift)
    return new_east.astype(BF16), new_north.astype(BF16)


def put_group(staged, block, eye, first):
    latitudes = eye.shape[0]
    rows = latitudes // 8
    turned = dot_nt(eye, block.reshape(256, latitudes))
    for s in range(8):
        staged[s, first : first + rows, :] = turned[rows * s : rows * (s + 1)]


def turning_row(latitudes):
    position = lax.broadcasted_iota(jnp.int32, (8, latitudes), 1).astype(F32)
    turning = coriolis_scale * jnp.sin(math.pi * ((position + 0.5) / latitudes - 0.5))
    return turning[0:1, :][None]


def inner_kernel(
    ens, depth, out, to_first, to_second, here, deep, flux, height, staged, edges, arrived
):
    columns, members, latitudes = here.shape[1:]
    batch = columns // 5
    pieces = [pltpu.make_async_copy(depth, deep, arrived.at[5])]
    for k in range(5):
        span = pl.ds(k * batch, batch if k else 2)
        piece = pltpu.make_async_copy(ens.at[:, span], here.at[:, span], arrived.at[k])
        pieces.append(piece)
    for k in (0, 2, 3, 4, 5, 1):
        pieces[k].start()
    shift = difference(latitudes)
    turning = turning_row(latitudes)
    eye = identity(latitudes, BF16)
    pieces[0].wait()

    def depths(first, count):
        rows = [deep[c : c + 1, :] for c in range(first, first + count)]
        return jnp.stack([jnp.broadcast_to(row, (members, latitudes)) for row in rows])

    def edge(side, near, far):
        edges[side, 0] = here[0, near]
        edges[side, 1] = (deep[near : near + 1, :] * here[2, near].astype(F32)).astype(BF16)
        edges[side, 2] = flux[near].astype(BF16)
        edges[side, 3] = flux[far].astype(BF16)

    staged[:, 300:INNER, :] = jnp.zeros((8, INNER - 300, 256), F32)
    done = 2
    for k in (1, 2, 3, 4, 0):
        pieces[k + 1].wait()
        first, count = k * batch, batch if k else 2
        flux[first : first + count] = fluxes(here[1, first : first + count], depths(first, count))
        if k == 0:
            edge(0, 0, 1)
            continue
        if k == 4:
            edge(1, columns - 1, columns - 2)
        low, high = max(first - 1, batch + 1), first + batch - 1
        at = slice(low, high)
        ahead, behind = flux[low + 1 : high + 1], flux[low - 1 : high - 1]
        height[at] = heights(
            here[0, at], here[2, at], depths(low, high - low), ahead, behind, shift
        )
        while done < 7 and 8 * done + 9 <= high:
            first = 8 * done
            at = slice(first, first + 8)
            ahead, behind = height[first + 1 : first + 9], height[first - 1 : first + 7]
            new = velocities(here[1, at], here[2, at], height[at], ahead, behind, turning, shift)
            for v, field in enumerate((height[at],) + new):
                put_group(staged, field, eye, row_of(group_of(v, done)))
            done += 1
    odd = lax.axis_index("band") & 1
    to_first[...] = edges[1 - odd]
    to_second[...] = edges[odd]
    out[...] = staged[...].astype(BF16)


def outer_kernel(
    west_block, east_block, first_swap, second_swap, depth, *refs
):
    straight, cross, flux, height, staged, swapped = refs
    odd = lax.axis_index("band") & 1
    for side, block in enumerate((first_swap, second_swap)):
        swapped[side] = block[...]
    left, right = swapped.at[1 - odd], swapped.at[odd]
    members, latitudes = west_block.shape[2:]
    shift = difference(latitudes)
    turning = turning_row(latitudes)
    eye = identity(latitudes, BF16)

    def depths(first, count):
        return jnp.stack(
            [
                jnp.broadcast_to(depth[c : c + 1, :], (members, latitudes))
                for c in range(first, first + count)
            ]
        )

    def window(ens, edge, first, count, low, high):
        is_left = low == 0
        base = 2 if is_left else 0
        flux[base : base + count] = fluxes(ens[1, 0:count], depths(first, count))
        at = 0 if is_left else count
        near, far = (1, 0) if is_left else (at, at + 1)
        flux[near] = edge[2].astype(F32)
        flux[far] = edge[3].astype(F32)
        wide = high - low + 1
        skip = 0 if is_left else 1
        columns = slice(skip, skip + wide)
        new = heights(
            ens[0, columns],
            ens[2, columns],
            depths(first + skip, wide),
            flux[base + skip + 1 : base + skip + 1 + wide],
            flux[base + skip - 1 : base + skip - 1 + wide],
            shift,
        )
        start = 1 if is_left else 0
        height[start : start + wide] = new
        place = 0 if is_left else wide
        middle = near
        east_west = flux[middle + 1] - flux[middle - 1]
        raised = edge[0].astype(F32) - half_step * (east_west + rows_apart(edge[1], shift))
        height[place] = raised.astype(BF16)
        count = high - low
        here = height[1 : 1 + count]
        ahead, behind = height[2 : 2 + count], height[0:count]
        at = slice(low - first, high - first)
        return (here,) + velocities(ens[1, at], ens[2, at], here, ahead, behind, turning, shift)

    for v, field in enumerate(window(west_block, left, 0, 18, 0, 16)):
        for index in range(2):
            at = row_of(group_of(v, index)) - INNER
            put_group(staged, field[8 * index : 8 * index + 8], eye, at)
    ends = window(east_block, right, 54, 6, 56, 60)
    put_group(staged, jnp.concatenate([ends[0], ends[1]], axis=0), eye, 120)
    block = jnp.concatenate([ends[2], ends[2]], axis=0).reshape(256, latitudes)
    turned = dot_nt(eye, block)
    lower = lax.broadcasted_iota(jnp.int32, (10, 256), 1) < LANES
    for s in range(8):
        rows = [turned[20 * s + 10 * k : 20 * s + 10 * k + 10] for k in range(2)]
        staged[s, 140:150, :] = jnp.where(lower, rows[0], rows[1])
    staged[:, 150:OUTER, :] = jnp.zeros((8, OUTER - 150, 256), F32)
    me = lax.axis_index("mem")
    for k, d in enumerate(CHIPS):
        straight[k] = staged[me ^ d].astype(BF16)
        cross[k] = staged[me ^ d ^ 1].astype(BF16)


def spread_block(source, held, wide, start, lane):
    spans = [slice(h * LANES, (h + 1) * LANES) for h in range(2)]
    count = source.shape[1]
    here = pl.ds(start, 16)
    blocks = exchange_lanes([[source[q, here, span] for span in spans] for q in range(8)], lane)
    for q in range(8):
        to = pl.ds(pl.multiple_of(q * count + start, 8), 16)
        for h in range(2):
            wide[h, to, :] = blocks[q][h].astype(F32)
            held[q, here, spans[h]] = blocks[q][h]


def spread_kernel(cells, got, held, seen, wide):
    lane = lax.broadcasted_iota(jnp.int32, (16, LANES), 1)

    def step(index, carry):
        spread_block(got, held, wide, pl.multiple_of(index * 16, 16), lane)
        return carry

    lax.fori_loop(0, INNER // 16, step, 0, unroll=4)
    slots = seen.shape[2]
    unroll = 16

    def pick(index, carry):
        for t in range(2):
            for k in range(unroll):
                slot = index * unroll + k
                row = cells[t, slot]
                for h in range(2):
                    seen[t, h, pl.ds(slot, 1), :] = wide[h, pl.ds(row, 1), :]
        return carry

    lax.fori_loop(0, slots // unroll, pick, 0)


def observe_kernel(cells, outer, weight, target, first, straight, cross, *refs):
    edges, (held, gram, to_first, to_second, joined, wide, seen) = refs[:3], refs[3:]
    wholes = []
    lane = lax.broadcasted_iota(jnp.int32, (16, LANES), 1)
    me = lax.axis_index("mem")
    for k, d in enumerate(CHIPS):
        joined[me ^ d, 0:OUTER, :] = straight[0] if k == 0 else edges[k - 1][0]
        joined[me ^ d ^ 1, 0:OUTER, :] = cross[0] if k == 0 else edges[k - 1][1]
    for start in (*range(0, OUTER - 16, 16), OUTER - 16):
        spread_block(joined, held, wide, start, lane)
    slots = first.shape[2]
    seen[:, :, 0:slots, :] = first[...]
    for t in range(2):

        def pick(index, carry):
            for k in range(8):
                slot = outer[t, index * 8 + k]
                row = cells[t, slot] - 8 * INNER
                for h in range(2):
                    seen[t, h, pl.ds(slot, 1), :] = wide[h, pl.ds(row, 1), :]
            return carry

        lax.fori_loop(0, (outer[t, slots + LANES - 1] + 7) // 8, pick, 0)
    eye = identity(256, BF16)
    for t in range(2):
        values = jnp.concatenate([seen[t, h, 0:slots] for h in range(2)], axis=1).astype(BF16)
        turned = dot_nt(eye, values)
        mean = jnp.sum(turned, axis=0, keepdims=True) * (1.0 / 256)
        root = weight[t : t + 1, :]
        spread = (root * (turned - mean)).astype(BF16)
        misfit = (root * (target[t : t + 1, :] - mean)).astype(BF16)
        block = dot_nt(spread, spread)
        pull = dot_nt(jnp.broadcast_to(misfit, (16, slots)), spread)
        whole = packed(block, pull[0:8])
        gram[t] = whole
        wholes.append(whole.astype(BF16))
    odd = (lax.axis_index("band") & 1) == 1
    to_first[...] = jnp.where(odd, wholes[0], wholes[1])
    to_second[...] = jnp.where(odd, wholes[1], wholes[0])


def combine_kernel(gram, first_swap, second_swap, line, short):
    odd = (lax.axis_index("band") & 1) == 1
    first, second = first_swap[...].astype(F32), second_swap[...].astype(F32)
    west, east = jnp.where(odd, first, second), jnp.where(odd, second, first)
    for t, beside in enumerate((west + gram[1], gram[0] + east)):
        total = gram[t] + neighbour_weight * beside
        line[t] = total
        short[t] = total.astype(BF16)


def prepare_kernel(inner, outer, *refs):
    average = jnp.full((256, LANES), 1.0 / 256, BF16)
    for q in range(8):
        pieces = (inner[q, 0:FIRST], jnp.concatenate([inner[q, FIRST:INNER], outer[q, 0:OUTER]], axis=0))
        for k, piece in enumerate(pieces):
            mean = dot_nn(piece, average)
            refs[2 * k + 1][q] = mean
            mean = jnp.concatenate([mean, mean], axis=1)
            refs[2 * k][q] = (piece.astype(F32) - mean).astype(BF16)


def send_back(results, outs):
    lane = lax.broadcasted_iota(jnp.int32, (16, LANES), 1)
    spans = [slice(h * LANES, (h + 1) * LANES) for h in range(2)]

    def move(start):
        here = pl.ds(start, 16)
        blocks = [[results[q, here, span] for span in spans] for q in range(8)]
        blocks = exchange_lanes(blocks, lane)
        for q in range(8):
            for h in range(2):
                outs[ORDER.index(q)][here, spans[h]] = blocks[q][h]

    def step(index, carry):
        move(pl.multiple_of(index * 16, 16))
        return carry

    count = results.shape[1]
    lax.fori_loop(0, count // 16, step, 0, unroll=4)
    if count % 16:
        move(count - 16)


def apply_maps(anomaly, mean, maps, results, q, edge, order):
    count = results.shape[1]
    low, high = edge // 16 * 16, (edge + 15) // 16 * 16
    first = dot_nt(anomaly[q, 0:high], maps[order[0]])
    centre = jnp.concatenate([mean[q], mean[q]], axis=1)
    results[q, 0:low] = (centre[0:low] + first[0:low]).astype(BF16)
    if low == count:
        return
    second = dot_nt(anomaly[q, low:count], maps[order[1]])
    if low < high:
        near = lax.broadcasted_iota(jnp.int32, (16, 256), 0) < edge - low
        both = jnp.where(near, first[low:high], second[0:16])
        results[q, low:high] = (centre[low:high] + both).astype(BF16)
    results[q, high:count] = (centre[high:count] + second[high - low : count - low]).astype(BF16)


def second_kernel(maps, anomaly, mean, *refs):
    outs, results = refs[:8], refs[8]
    both = [maps[0], maps[1]]
    for q in range(8):
        apply_maps(anomaly, mean, both, results, q, 184, (0, 1))
    send_back(results, outs)


def analyse_kernel(line, below, above, anomaly, mean, *refs):
    outs, (kept, results, ordered) = refs[:8], refs[8:]
    size = 256
    eye = identity(size, F32)
    norms, pulls, roots, inverses = [], [], [], []
    for t in range(2):
        beside = below[t].astype(F32) + above[t].astype(F32)
        block, pull = unpacked(line[t] + neighbour_weight * beside)
        system = (size - 1) * eye + block
        square = jnp.sum(jnp.sum(system * system, axis=0, keepdims=True), axis=1, keepdims=True)
        norms.append(jnp.sqrt(square))
        pulls.append(pull)
        roots.append(system * (1.0 / norms[t]))
    for sweep in range(SWEEPS):
        rights = [right_3(split(root)) for root in roots]
        if sweep == 0:
            inverses = [1.5 * eye - 0.5 * root for root in roots]
            lefts = [left_3(split(inverse)) for inverse in inverses]
            roots = [dot_nn(left, right) for left, right in zip(lefts, rights)]
            continue
        parts = [split(inverse) for inverse in inverses]
        products = [dot_nn(left_3(part), right) for part, right in zip(parts, rights)]
        middle_parts = [split(1.5 * eye - 0.5 * product) for product in products]
        middles = [left_3(part) for part in middle_parts]
        if sweep < SWEEPS - 1:
            roots = [dot_nn(middle, right) for middle, right in zip(middles, rights)]
        else:
            pulls = [dot_nn(left_3(split(pull)), right_3(part)) for pull, part in zip(pulls, parts)]
            rights = [right_3(part) for part in middle_parts]
            pulls = [dot_nn(left_3(split(pull)), right) for pull, right in zip(pulls, rights)]
        inverses = [dot_nn(middle, right_3(part)) for middle, part in zip(middles, parts)]
    maps = []
    for t in range(2):
        right = right_3(split(inverses[t]))
        shift = dot_nn(left_3(split(pulls[t])), right) / norms[t]
        scale = math.sqrt(size - 1) / jnp.sqrt(norms[t])
        ordered[t] = (inverses[t] * scale + shift[0:1]).astype(BF16).reshape(8, 32, size)
    me = lax.axis_index("mem")
    for t in range(2):
        maps.append(jnp.concatenate([ordered[t, me ^ d] for d in range(8)], axis=0))
        kept[t] = maps[t]
    for q in range(8):
        apply_maps(anomaly, mean, maps, results, q, 180 if q < 6 else FIRST, (1, 0))
    send_back(results, outs)


def spread_strips(got, wide):
    me = lax.axis_index("mem")
    for k, d in enumerate(ORDER):
        wide[me ^ d] = got[k][...].astype(F32)


def take_group(wide, turned, eye, g, shape, skipped=0):
    rows = shape[2] // 8
    at = row_of(g) - row_of(skipped)
    g = g - skipped
    for s in range(8):
        turned[g, rows * s : rows * (s + 1), :] = wide[s, at : at + rows, :]
    return dot_nt(eye, turned[g].astype(BF16)).astype(BF16).reshape(shape)


def first_return_kernel(*refs):
    got, (out, wide, turned, planes, sent) = refs[:8], refs[8:]
    shape = (8,) + planes.shape[2:]
    spread_strips(got, wide)
    eye = identity(256, BF16)
    copies = []
    for v in range(3):
        for index in range(3, 7):
            at = 8 * (index - 3)
            planes[v, at : at + 8] = take_group(wide, turned, eye, group_of(v, index), shape)
        copies.append(pltpu.make_async_copy(planes.at[v], out.at[v, pl.ds(24, 32)], sent.at[v]))
        copies[v].start()
    for copy in copies:
        copy.wait()


def second_return_kernel(*refs):
    got, (_, out, wide, turned, planes, sent) = refs[:8], refs[8:]
    shape = (8,) + planes.shape[2:]
    spread_strips(got, wide)
    eye = identity(256, BF16)
    mixed = take_group(wide, turned, eye, 21, shape, 12)
    planes[0, 24:28] = mixed[0:4]
    planes[1, 24:28] = mixed[4:8]
    at = row_of(22) - row_of(12)
    turned[10] = jnp.zeros(turned.shape[1:], F32)
    for s in range(8):
        for k in range(2):
            to = 20 * s + 10 * k
            half = wide[s, at : at + 10, k * LANES : (k + 1) * LANES]
            turned[10, to : to + 10, 0:LANES] = half
    block = dot_nt(eye, turned[10].astype(BF16)).astype(BF16).reshape(shape)
    planes[2, 24:28] = block[0:4]
    copies = []

    def leave(v, at, to, count):
        source, target = planes.at[v, pl.ds(at, count)], out.at[v, pl.ds(to, count)]
        copies.append(pltpu.make_async_copy(source, target, sent.at[len(copies)]))
        copies[-1].start()

    for v in range(3):
        leave(v, 24, 56, 4)
    for v in range(3):
        for index in range(3):
            at = 8 * index
            block = take_group(wide, turned, eye, group_of(v, index), shape, 12)
            planes[v, at : at + 8] = block
            leave(v, at, at, 8)
    for copy in copies:
        copy.wait()


def swapped_pairs(values, axis, pairs):
    moved = []
    for value, some in zip(values, pairs):
        both = some + [(j, i) for i, j in some]
        moved.append(lax.ppermute(value, axis, both))
    return moved


def band_swaps(first, second):
    count = lax.axis_size("band")
    starts = range(0, count, 2)
    pairs = [[(i, i + 1) for i in starts], [(i + 1, (i + 2) % count) for i in starts]]
    return swapped_pairs((first, second), "band", pairs)


def mem_swaps(value):
    count = lax.axis_size("mem")
    pairs = [[(i, i + 1) for i in range(k, count - 1, 2)] for k in range(2)]
    return swapped_pairs((value, value), "mem", pairs)


def across(value, difference):
    return lax.ppermute(value, "mem", [(i, i ^ difference) for i in range(8)])


def partners(values):
    return [across(value, d) if d else value for d, value in zip(ORDER, values)]


def swap(value):
    return lax.all_to_all(value, "mem", split_axis=0, concat_axis=0, tiled=True)


def cell_rows(cell):
    variable = cell // 600
    tile = jnp.arange(2, dtype=jnp.int32)[:, None]
    column = tile * 30 + cell // 20 % 30
    index = column // 8
    place = column % 8
    group = variable + jnp.where(index > 3, variable * 2 + index - 4, 18 - 3 * index)
    is_last = column >= 56
    group = jnp.where(is_last, 21 + variable // 2, group)
    place = jnp.where(is_last, column - 56 + 4 * (variable % 2), place)
    row = cell % 20
    place = jnp.where(group == 22, place + 4 * (row // 10), place)
    row = jnp.where(group == 22, row % 10, row)
    first = place * INNER + group * 20
    last = 8 * INNER + place * OUTER + (group - 15) * 20
    return jnp.where(group < 15, first, last) + row


def on_device_fast(
    ensemble, layer_depth, observed_cell, observed_value, error_variance, observed_count
):
    members, _, columns, latitudes = ensemble.shape
    slots = observed_cell.shape[2]
    planes = jnp.transpose(ensemble, (1, 2, 0, 3))
    edge = jax.ShapeDtypeStruct((4, members, latitudes), BF16)
    far = pl.BlockSpec(memory_space=pltpu.HBM)
    sent, to_first, to_second = pl.pallas_call(
        inner_kernel,
        out_shape=(jax.ShapeDtypeStruct((8, INNER, 256), BF16), edge, edge),
        in_specs=[far, far],
        scratch_shapes=[
            pltpu.VMEM(planes.shape, BF16),
            pltpu.VMEM((columns, latitudes), F32),
            pltpu.VMEM((columns, members, latitudes), F32),
            pltpu.VMEM((columns, members, latitudes), BF16),
            pltpu.VMEM((8, INNER, 256), F32),
            pltpu.VMEM((2, 4, members, latitudes), BF16),
            pltpu.SemaphoreType.DMA((6,)),
        ],
        compiler_params=params(60),
        name="inner",
    )(planes, layer_depth)
    got = swap(sent)
    swaps = band_swaps(to_first, to_second)
    flat = pl.BlockSpec((4, members, latitudes), lambda i: (0, 0, 0))
    straight, cross = pl.pallas_call(
        outer_kernel,
        grid=(1,),
        out_shape=(jax.ShapeDtypeStruct((4, OUTER, 256), BF16),) * 2,
        in_specs=[
            pl.BlockSpec((3, 20, members, latitudes), lambda i: (0, 0, 0, 0)),
            pl.BlockSpec((3, 6, members, latitudes), lambda i: (0, 9, 0, 0)),
            flat,
            flat,
            pl.BlockSpec((columns, latitudes), lambda i: (0, 0)),
        ],
        out_specs=(pl.BlockSpec((4, OUTER, 256), lambda i: (0, 0, 0)),) * 2,
        scratch_shapes=[
            pltpu.VMEM((20, members, latitudes), F32),
            pltpu.VMEM((18, members, latitudes), BF16),
            pltpu.VMEM((8, OUTER, 256), F32),
            pltpu.VMEM((2, 4, members, latitudes), BF16),
        ],
        compiler_params=params(24),
        name="outer",
    )(planes, planes, *swaps, layer_depth)
    cross = across(cross, 1)
    got_edges = [across(jnp.stack([straight[k], cross[k]]), CHIPS[k]) for k in (3, 1, 2)]
    got_edges = got_edges[1:] + got_edges[:1]

    rows = cell_rows(observed_cell[0])
    live = jnp.arange(slots, dtype=jnp.int32)[None, :] < observed_count[0][:, None]
    root = jnp.sqrt(jnp.where(live, 1.0 / error_variance[0], 0.0))
    vmem = pl.BlockSpec(memory_space=pltpu.VMEM)
    slot = jnp.arange(slots, dtype=jnp.int32)
    place = jnp.arange(slots + LANES, dtype=jnp.int32)
    is_outer = rows >= 8 * INNER
    near = jnp.where(is_outer, 0, rows)
    rank = jnp.sum(is_outer[:, None, :] & (slot[None, :] < slot[:, None])[None], axis=2)
    count = jnp.sum(is_outer, axis=1, keepdims=True)
    found = is_outer[:, None, :] & (rank[:, None, :] == place[None, :, None])
    outer = jnp.sum(jnp.where(found, slot, 0), axis=2)
    outer = jnp.where(place[None] < count, outer, slots)
    outer = jnp.where(place[None] == slots + LANES - 1, count, outer).astype(jnp.int32)
    rows = jnp.pad(rows, ((0, 0), (0, LANES)), constant_values=8 * INNER)
    smem = pl.BlockSpec(memory_space=pltpu.SMEM)
    held_inner, seen = pl.pallas_call(
        spread_kernel,
        out_shape=(
            jax.ShapeDtypeStruct((8, INNER, 256), BF16),
            jax.ShapeDtypeStruct((2, 2, slots, LANES), F32),
        ),
        in_specs=[smem, vmem],
        scratch_shapes=[pltpu.VMEM((2, 8 * INNER, LANES), F32)],
        compiler_params=params(12),
        cost_estimate=cost(1, 8 * MIB),
        name="spread",
    )(near, got)
    one_tile = jax.ShapeDtypeStruct((PACKED, 256), BF16)
    held_outer, gram, to_first, to_second = pl.pallas_call(
        observe_kernel,
        out_shape=(
            jax.ShapeDtypeStruct((8, OUTER, 256), BF16),
            jax.ShapeDtypeStruct((2, PACKED, 256), F32),
            one_tile,
            one_tile,
        ),
        in_specs=[smem, smem] + [vmem] * 8,
        scratch_shapes=[
            pltpu.VMEM((8, OUTER, 256), BF16),
            pltpu.VMEM((2, 8 * OUTER, LANES), F32),
            pltpu.VMEM((2, 2, slots + 8, LANES), F32),
        ],
        compiler_params=params(16),
        name="observe",
    )(rows, outer, root, observed_value[0], seen, straight, cross, *got_edges)
    anomaly_1, mean_1, anomaly_2, mean_2 = pl.pallas_call(
        prepare_kernel,
        out_shape=(
            jax.ShapeDtypeStruct((8, FIRST, 256), BF16),
            jax.ShapeDtypeStruct((8, FIRST, LANES), F32),
            jax.ShapeDtypeStruct((8, SECOND, 256), BF16),
            jax.ShapeDtypeStruct((8, SECOND, LANES), F32),
        ),
        compiler_params=params(12),
        cost_estimate=cost(1, 6 * MIB),
        name="prepare",
    )(held_inner, held_outer)

    line, short = pl.pallas_call(
        combine_kernel,
        out_shape=(
            jax.ShapeDtypeStruct(gram.shape, F32),
            jax.ShapeDtypeStruct(gram.shape, BF16),
        ),
        compiler_params=params(8),
        name="combine",
    )(gram, *band_swaps(to_first, to_second))
    below, above = mem_swaps(short)
    *back, maps = pl.pallas_call(
        analyse_kernel,
        out_shape=(jax.ShapeDtypeStruct((FIRST, 256), BF16),) * 8
        + (jax.ShapeDtypeStruct((2, 256, 256), BF16),),
        scratch_shapes=[pltpu.VMEM((8, FIRST, 256), BF16), pltpu.VMEM((2, 8, 32, 256), BF16)],
        compiler_params=params(20),
        name="analyse",
    )(line, below, above, anomaly_1, mean_1)
    first = partners(back)
    maps, first[4] = lax.optimization_barrier((maps, first[4]))
    back = pl.pallas_call(
        second_kernel,
        out_shape=(jax.ShapeDtypeStruct((SECOND, 256), BF16),) * 8,
        scratch_shapes=[pltpu.VMEM((8, SECOND, 256), BF16)],
        compiler_params=params(16),
        cost_estimate=cost(1, 6 * MIB),
        name="second",
    )(maps, anomaly_2, mean_2)
    second = partners(back)
    result = jax.ShapeDtypeStruct(planes.shape, BF16)
    half = pl.pallas_call(
        first_return_kernel,
        out_shape=result,
        out_specs=far,
        scratch_shapes=[
            pltpu.VMEM((8, FIRST, 256), F32),
            pltpu.VMEM((12, latitudes, 256), F32),
            pltpu.VMEM((3, 32, members, latitudes), BF16),
            pltpu.SemaphoreType.DMA((3,)),
        ],
        compiler_params=params(20),
        cost_estimate=cost(1, 4 * MIB),
        name="first_return",
    )(*first)
    planes = pl.pallas_call(
        second_return_kernel,
        out_shape=result,
        in_specs=[vmem] * 8 + [far],
        out_specs=far,
        scratch_shapes=[
            pltpu.VMEM((8, SECOND, 256), F32),
            pltpu.VMEM((11, latitudes, 256), F32),
            pltpu.VMEM((3, 28, members, latitudes), BF16),
            pltpu.SemaphoreType.DMA((12,)),
        ],
        input_output_aliases={8: 0},
        compiler_params=params(20),
        name="second_return",
    )(*second, half)
    return jnp.transpose(planes, (2, 0, 1, 3))


def choose(ensemble, layer_depth, observed_cell, *rest):
    mesh_shape = (lax.axis_size("mem"), lax.axis_size("band"))
    shape = (mesh_shape, ensemble.shape, observed_cell.shape[1])
    fits = shape == ((8, 4), (32, 3, 60, 160), 2) and observed_cell.shape[2] % 16 == 0
    chosen = on_device_fast if fits else on_device
    return chosen(ensemble, layer_depth, observed_cell, *rest)


def solution(mesh):
    in_specs = (
        P("mem", None, "band", None),
        P("band", None),
        P("mem", "band", None),
        P("mem", "band", None),
        P("mem", "band", None),
        P("mem", "band"),
    )
    out_specs = P("mem", None, "band", None)
    return jax.shard_map(
        choose, mesh=mesh, in_specs=in_specs, out_specs=out_specs, check_vma=False
    )
```
